32 devices in a mesh: wide: 8 (over z, y), narrow: 4 (over x, core).
Axes of the slice: x: 2, y: 2, z: 4, core: 2. Of those that a mesh axis runs over, the one named last changes fastest.
Arguments:
- tokens: bfloat16 [4096, 2048], P('wide'), may hold values from -6 to 6
- cotangent: bfloat16 [4096, 2048], P('wide'), may hold values from -6 to 6
- keep_mask: int32 [4096], P('wide'), may hold values 0 or 1
- doc_lengths: int32 [1, 16], replicated, may hold values from 1 to 2048, 4096 in all within a row
- block_order: int32 [1, 16], replicated, may hold values from 0 to 15, each once within a row
- gain_attn: bfloat16 [2048], replicated, may hold values from 0.25 to 1.75
- w_query: bfloat16 [2048, 2048], P(None, 'narrow'), may hold values from -0.125 to 0.125
- w_key: bfloat16 [2048, 1024], P(None, 'narrow'), may hold values from -0.125 to 0.125
- w_value: bfloat16 [2048, 1024], P(None, 'narrow'), may hold values from -0.125 to 0.125
- w_out: bfloat16 [2048, 2048], P('narrow'), may hold values from -0.5 to 0.5
- gain_dense: bfloat16 [2048], replicated, may hold values from 0.25 to 1.75
- w_gate: bfloat16 [2048, 5632], P(None, 'narrow'), may hold values from -0.125 to 0.125
- w_up: bfloat16 [2048, 5632], P(None, 'narrow'), may hold values from -0.125 to 0.125
- w_down: bfloat16 [5632, 2048], P('narrow'), may hold values from -0.078125 to 0.078125
Outputs:
- output: bfloat16 [4096, 2048], P('wide')
- grad_tokens: bfloat16 [4096, 2048], P('wide')
- grad_gain_attn: float32 [2048], P('wide')
- grad_w_query: float32 [2048, 2048], P('wide', 'narrow')
- grad_w_key: float32 [2048, 1024], P('wide', 'narrow')
- grad_w_value: float32 [2048, 1024], P('wide', 'narrow')
- grad_w_out: float32 [2048, 2048], P('narrow', 'wide')
- grad_gain_dense: float32 [2048], P('wide')
- grad_w_gate: float32 [2048, 5632], P('wide', 'narrow')
- grad_w_up: float32 [2048, 5632], P('wide', 'narrow')
- grad_w_down: float32 [5632, 2048], P('narrow', 'wide')
The draws below stay inside these ranges and needn't reach their ends.
All inputs are finite; a program needn't handle non-finite values. No bound on the sum of `keep_mask` on one device may be relied on, other than what follows from the above.
Results may differ from the reference program's by a relative error of at most 0.025.
Values may be sent and summed in bfloat16 or wider, within the bound.
No kernel may reach another device: no remote copies, remote signals or barrier semaphores. Data moves between devices by JAX's collectives and lax.ppermute only.
A program may use at most 192 MiB of HBM per device.

```python
import math
import jax
import jax.numpy as jnp
import numpy as np
from jax import lax

D = 2048
HQ = 16
HK = 8
HD = 128
FF = 5632
TOK_DEV = 512
SEQ_LEN = 4096
SEQS = 1
TOKENS = 4096
BLOCKS = 16
DOCS = 16
MAXDOC = 2048


def plant(entries, stream_key, low, top_value):
    shape = entries.shape
    spot = [jax.random.randint(jax.random.fold_in(stream_key, axis), (), 0, shape[axis]) for axis in range(len(shape))]
    entries = entries.at[tuple(spot)].set(low)
    longest = shape.index(max(shape))
    spot[longest] = (spot[longest] + 1) % shape[longest]
    return entries.at[tuple(spot)].set(top_value)


def strengthened(entries, key, source, target, shards_of, factor):
    owner, partner = [(jnp.arange(entries.shape[position]) // (entries.shape[position] // shards_of)).reshape([-1 if axis == position else 1 for axis in range(entries.ndim)]) for position in (source, target)]
    chosen = jax.random.permutation(key, shards_of)[partner]
    strong = (owner == chosen) | (owner == (partner + shards_of // 2) % shards_of)
    return jnp.where(strong, factor * entries, entries)


def steps_of(stream_key, shape, shards, low, high):
    def one(dim, parts):
        draws = jax.random.uniform(jax.random.fold_in(jax.random.fold_in(stream_key, 6), dim), (parts,), jnp.float32, low / len(shards), high / len(shards))
        return jnp.repeat(jnp.exp(draws), shape[dim] // parts).reshape((-1,) + (1,) * (len(shape) - dim - 1))

    loudness = one(*shards[0])
    for cut in shards[1:]:
        loudness = loudness * one(*cut)
    return loudness


def split_up(amount, total, bound, lean):
    portions = [(1 << 20) // math.isqrt(standing ** lean) + 1 for standing in range(2, amount + 1)]
    spare, counts = total - bound - (amount - 1), [1] * (amount - 1)
    while spare > 0:
        candidates = [i for i in range(amount - 1) if counts[i] < bound]
        pool, left = sum([portions[i] for i in candidates]), spare
        for i in candidates:
            more = min(bound - counts[i], max(1, left * portions[i] // pool), spare)
            counts[i] = counts[i] + more
            spare = spare - more
    return np.array([bound] + counts)


def uneven(own_key, number_of, total, limit, lean):
    if number_of == 2:
        one = jax.random.randint(own_key, (), max(1, total - limit), min(limit, total - 1) + 1)
        return jnp.stack([one, total - one])
    tallies = jnp.asarray(split_up(number_of, total, limit, lean), jnp.int32)
    twos = (number_of - 1) // 2
    giver, sink = tallies[1:1 + 2 * twos:2], tallies[2:2 + 2 * twos:2]
    slack = jnp.minimum(giver - 1, limit - sink)
    moved = jax.random.randint(jax.random.fold_in(own_key, 1), (twos,), 0, 1 << 20) % (slack + 1)
    tallies = tallies.at[1:1 + 2 * twos:2].set(giver - moved).at[2:2 + 2 * twos:2].set(sink + moved)
    return tallies[jax.random.permutation(jax.random.fold_in(own_key, 2), number_of)]


def gaussian(rng, extent, scale, limit, cuts=(), kind=jnp.bfloat16):
    loudness = steps_of(rng, extent, cuts, -0.22, 0.18) if cuts else 1.0
    entries = jax.random.normal(rng, extent, jnp.float32) * scale * loudness
    return jnp.minimum(jnp.maximum(entries, -limit), limit).astype(kind)


def bell_draw_with(key, shape, spread, bound, cuts, heavy, held_as=jnp.bfloat16):
    drawn = spread * jax.random.normal(key, shape, jnp.float32)
    if cuts:
        drawn = drawn * steps_of(key, shape, cuts, -0.22, 0.18)
    return jnp.clip(strengthened(drawn, jax.random.fold_in(key, 3), *heavy), -bound, bound).astype(held_as)


def setup_inputs(seed: int = 0) -> dict:
    key_of = jax.random.split(jax.random.key(seed), 15)
    tokens = bell_draw_with(key_of[0], (TOKENS, D), 1.0, 6.0, ((0, 8),), (0, 1, 8, 2.0))
    cotangent = bell_draw_with(key_of[1], (TOKENS, D), 1.0, 6.0, ((0, 8),), (0, 1, 8, 2.0))
    keep_mask = plant((jax.random.randint(key_of[2], (TOKENS,), 0, 4) < 3).astype(jnp.int32), jax.random.fold_in(key_of[2], 1), 0, 1)
    doc_lengths = jax.vmap(lambda own: uneven(own, DOCS, SEQ_LEN, MAXDOC, 2))(jax.random.split(key_of[3], SEQS)).reshape((SEQS, DOCS)).astype(jnp.int32)
    block_order = jax.vmap(lambda own: jax.random.permutation(own, BLOCKS))(jax.random.split(key_of[4], SEQS)).reshape((SEQS, BLOCKS)).astype(jnp.int32)
    gain_attn = jnp.clip(1.0 + 0.15 * jax.random.normal(key_of[5], (D,), jnp.float32), 0.25, 1.75).astype(jnp.bfloat16)
    w_query = gaussian(key_of[6], (D, HQ * HD), D ** -0.5, 0.125, ((1, 4),))
    w_key = gaussian(key_of[7], (D, HK * HD), D ** -0.5, 0.125, ((1, 4),))
    w_value = gaussian(key_of[8], (D, HK * HD), D ** -0.5, 0.125, ((1, 4),))
    w_out = gaussian(key_of[9], (HQ * HD, D), HD ** -0.5, 0.5, ((0, 4),))
    gain_dense = jnp.clip(1.0 + 0.15 * jax.random.normal(key_of[10], (D,), jnp.float32), 0.25, 1.75).astype(jnp.bfloat16)
    w_gate = gaussian(key_of[11], (D, FF), D ** -0.5, 0.125, ((1, 4),))
    w_up = gaussian(key_of[12], (D, FF), D ** -0.5, 0.125, ((1, 4),))
    w_down = gaussian(key_of[13], (FF, D), FF ** -0.5, 0.078125, ((0, 4),))
    return {"tokens": tokens, "cotangent": cotangent, "keep_mask": keep_mask, "doc_lengths": doc_lengths, "block_order": block_order, "gain_attn": gain_attn, "w_query": w_query, "w_key": w_key, "w_value": w_value, "w_out": w_out, "gain_dense": gain_dense, "w_gate": w_gate, "w_up": w_up, "w_down": w_down}


EPSILON = 1e-05
NEGATIVE = -1e+30
BASE = 10000.0
HIGHEST = lax.Precision.HIGHEST

@jax.custom_vjp
def low(v):
    return lax.optimization_barrier(v.astype(jnp.bfloat16)).astype(jnp.float32)

@jax.custom_vjp
def low_back(v):
    return v

def low_keep(v):
    return (low(v), None)

def low_pass(kept, grad):
    return (grad,)

def back_keep(v):
    return (v, None)

def back_low(kept, grad):
    return (low(grad),)
low.defvjp(low_keep, low_pass)
low_back.defvjp(back_keep, back_low)

def matmul(left, right):
    return jnp.dot(left, right, precision=HIGHEST)

def normalize(values, gain):
    scale_rows = lax.rsqrt(lax.optimization_barrier(jnp.mean(values * values, axis=1, keepdims=True)) + EPSILON)
    return values * scale_rows * gain

def rotary_tables(positions, head_size):
    halfway = head_size // 2
    frequency = BASE ** (-(jnp.arange(halfway, dtype=jnp.float32) * 2.0) / head_size)
    angles = positions.astype(jnp.float32)[:, None] * frequency[None, :]
    return (jnp.cos(angles), jnp.sin(angles))

def rotate(values, cosine, sine_table):
    halfway = values.shape[-1] // 2
    leading = values[..., :halfway]
    trailing = values[..., halfway:]
    cosine = cosine[:, None, :]
    sine_table = sine_table[:, None, :]
    return jnp.concatenate([leading * cosine - trailing * sine_table, trailing * cosine + leading * sine_table], axis=-1)

def attention(query_rot, keys_rot, values_in, positions, documents):
    block_rows = min(512, SEQ_LEN)
    block_count = SEQ_LEN // block_rows
    factor = HD ** (-0.5)
    query_seqs = query_rot.reshape(SEQS, SEQ_LEN, HK, HQ // HK, HD)
    key_seqs = keys_rot.reshape(SEQS, SEQ_LEN, HK, HD)
    value_seqs = values_in.reshape(SEQS, SEQ_LEN, HK, HD)

    def one_sequence(seq_item):
        query_seq, key_seq, value_seq, seq_pos, seq_doc = seq_item
        query_blocks = query_seq.reshape(block_count, block_rows, HK, HQ // HK, HD)
        position_blocks = seq_pos.reshape(block_count, block_rows)
        document_blocks = seq_doc.reshape(block_count, block_rows)

        @jax.checkpoint
        def one_block(block_item):
            query_block, query_pos, query_doc = block_item
            raw_scores = jnp.einsum('tgrd,kgd->grtk', query_block, key_seq, precision=HIGHEST)
            scaled = low_back(raw_scores * factor)
            allowed = (seq_pos[None, :] <= query_pos[:, None]) & (seq_doc[None, :] == query_doc[:, None])
            masked = jnp.where(allowed[None, None], scaled, NEGATIVE)
            log_total = jax.nn.logsumexp(masked, axis=-1, keepdims=True)
            weights_low = low(jnp.exp(masked - log_total))
            return jnp.einsum('grtk,kgd->tgrd', weights_low, value_seq, precision=HIGHEST)
        return lax.map(one_block, (query_blocks, position_blocks, document_blocks))
    mixed = lax.map(one_sequence, (query_seqs, key_seqs, value_seqs, positions, documents))
    return mixed.reshape(TOKENS, HQ * HD)

def reference(tokens, cotangent, keep_mask, doc_lengths, block_order, gain_attn, w_query, w_key, w_value, w_out, gain_dense, w_gate, w_up, w_down):
    half_rows = TOK_DEV // 2
    positions = (block_order[:, :, None] * half_rows + jnp.arange(half_rows, dtype=jnp.int32)[None, None, :]).reshape(SEQS, SEQ_LEN).astype(jnp.int32)
    doc_ends = jnp.cumsum(doc_lengths, axis=1).astype(jnp.int32)
    documents = lax.optimization_barrier(jnp.sum((doc_ends[:, None, :] <= positions[:, :, None]).astype(jnp.int32), axis=2)).astype(jnp.int32)
    cosine, sine_table = rotary_tables(positions.reshape(-1), HD)
    keep_rows = keep_mask.astype(jnp.float32)[:, None]

    def forward(source, gain_one, query_weight, key_weight, value_weight, out_weight, gain_two, gate_weight, up_weight, down_weight):
        normed_one = low(normalize(source, gain_one))
        query_raw = low_back(matmul(normed_one, query_weight)).reshape(TOKENS, HQ, HD)
        query_rot = low(rotate(query_raw, cosine, sine_table)).reshape(TOKENS, HK, HQ // HK, HD)
        key_raw = low_back(matmul(normed_one, key_weight)).reshape(TOKENS, HK, HD)
        keys_rot = low(rotate(key_raw, cosine, sine_table))
        values_in = low(low_back(matmul(normed_one, value_weight))).reshape(TOKENS, HK, HD)
        mixed_heads = low(low_back(attention(query_rot, keys_rot, values_in, positions, documents)))
        attn_out = low_back(matmul(mixed_heads, out_weight))
        hidden_one = source + keep_rows * attn_out
        normed_two = low(normalize(hidden_one, gain_two))
        gate_proj = low_back(matmul(normed_two, gate_weight))
        up_proj = low_back(matmul(normed_two, up_weight))
        inner_act = low(jax.nn.silu(gate_proj) * up_proj)
        dense_out = low_back(matmul(inner_act, down_weight))
        return hidden_one + keep_rows * dense_out
    primals = (tokens.astype(jnp.float32), gain_attn.astype(jnp.float32), w_query.astype(jnp.float32), w_key.astype(jnp.float32), w_value.astype(jnp.float32), w_out.astype(jnp.float32), gain_dense.astype(jnp.float32), w_gate.astype(jnp.float32), w_up.astype(jnp.float32), w_down.astype(jnp.float32))
    result, pullback = jax.vjp(forward, *primals)
    grads = pullback(cotangent.astype(jnp.float32))
    return (result.astype(jnp.bfloat16), grads[0].astype(jnp.bfloat16), grads[1], grads[2], grads[3], grads[4], grads[5], grads[6], grads[7], grads[8], grads[9])
```

```python
import functools

import jax
import jax.numpy as jnp
from jax import lax
from jax.experimental import pallas as pl
from jax.experimental.pallas import tpu as pltpu
from jax.sharding import PartitionSpec as P

HD = 128
EPSILON = 1e-05
NEGATIVE = -1e30
BASE = 10000.0
LOG2E = 1.4426950408889634
SCORE = HD ** (-0.5) * LOG2E
FACTOR = HD ** (-0.5)
BF = jnp.bfloat16
F32 = jnp.float32
NT = (((1,), (1,)), ((), ()))
TN = (((0,), (0,)), ((), ()))
VM = pl.BlockSpec(memory_space=pltpu.VMEM)
SM = pl.BlockSpec(memory_space=pltpu.SMEM)
ANY = pl.BlockSpec(memory_space=pl.ANY)


def dot(a, b, dims=(((1,), (0,)), ((), ()))):
    return lax.dot_general(a, b, dims, preferred_element_type=F32)


def narrow_swap(value, mask):
    pairs = [(n, n ^ mask) for n in range(lax.axis_size("narrow"))]
    return lax.ppermute(value, "narrow", pairs)


def wide_swap(value):
    return lax.ppermute(value, "wide", [(w, w ^ 1) for w in range(lax.axis_size("wide"))])


def wide_ring(value, group):
    ring = group // 2
    pairs = []
    for w in range(lax.axis_size("wide")):
        base, member = w // group * group, w % group
        pairs.append((w, base + (member // 2 + 1) % ring * 2 + member % 2))
    return lax.ppermute(value, "wide", pairs)


def rope(value, cosine, sine):
    return value * cosine + pltpu.roll(value, HD // 2, 1) * sine


def norm_kv_kernel(core, x_ref, gain_ref, wk_ref, wv_ref, cos_ref, sin_ref, normed_ref, kv_ref):
    x = x_ref[...].astype(F32)
    scale = lax.rsqrt(jnp.mean(x * x, axis=1, keepdims=True) + EPSILON)
    normed = (x * scale * gain_ref[...].astype(F32)).astype(BF)
    normed_ref[...] = normed
    width = wk_ref.shape[1]
    keys = dot(normed, wk_ref[...])
    for h in range(width // HD):
        cols = slice(h * HD, (h + 1) * HD)
        kv_ref[:, cols] = rope(keys[:, cols], cos_ref[...], sin_ref[...]).astype(BF)
    kv_ref[:, width:] = dot(normed, wv_ref[...]).astype(BF)


def norm_kv(core, tokens, gain, wk, wv, cosine, sine):
    rows, width = tokens.shape
    half = rows // 2
    full = lambda w: pl.BlockSpec(w.shape, lambda i, c: (0, 0))
    return pl.pallas_call(
        norm_kv_kernel,
        out_shape=(
            jax.ShapeDtypeStruct((rows, width), BF),
            jax.ShapeDtypeStruct((rows, 2 * wk.shape[1]), BF),
        ),
        grid_spec=pltpu.PrefetchScalarGridSpec(
            num_scalar_prefetch=1,
            grid=(2,),
            in_specs=[
                pl.BlockSpec((half, width), lambda i, c: (i ^ c[0], 0)),
                full(gain),
                full(wk),
                full(wv),
                pl.BlockSpec((half, HD), lambda i, c: (i, 0)),
                pl.BlockSpec((half, HD), lambda i, c: (i, 0)),
            ],
            out_specs=[
                pl.BlockSpec((half, width), lambda i, c: (i, 0)),
                pl.BlockSpec((half, 2 * wk.shape[1]), lambda i, c: (i, 0)),
            ],
        ),
        name="norm_kv",
    )(core, tokens, gain, wk, wv, cosine, sine)


def query_kernel(x_ref, w_ref, cos_ref, sin_ref, out_ref):
    raw = dot(x_ref[...], w_ref[...])
    for h in range(raw.shape[1] // HD):
        cols = slice(h * HD, (h + 1) * HD)
        out_ref[:, cols] = rope(raw[:, cols], cos_ref[...], sin_ref[...]).astype(BF)


def query_proj(x, w, cosine, sine):
    rows, width = x.shape
    half = rows // 2
    return pl.pallas_call(
        query_kernel,
        out_shape=jax.ShapeDtypeStruct((rows, w.shape[1]), BF),
        grid=(2,),
        in_specs=[
            pl.BlockSpec((half, width), lambda i: (i, 0)),
            pl.BlockSpec(w.shape, lambda i: (0, 0)),
            pl.BlockSpec((half, HD), lambda i: (i, 0)),
            pl.BlockSpec((half, HD), lambda i: (i, 0)),
        ],
        out_specs=pl.BlockSpec((half, w.shape[1]), lambda i: (i, 0)),
        cost_estimate=pl.CostEstimate(
            flops=2 * rows * width * w.shape[1], bytes_accessed=6 << 20, transcendentals=0
        ),
        name="query_proj",
    )(x, w, cosine, sine)


def fetch_slots(slot_refs, kv_ref, sems):
    rows = slot_refs[0].shape[0]
    copies = [
        pltpu.make_async_copy(ref, kv_ref.at[pl.ds(j * rows, rows), :], sems.at[j])
        for j, ref in enumerate(slot_refs)
    ]
    for copy in copies:
        copy.start()
    for copy in copies:
        copy.wait()


def allowed(pk, size, span, pos, low):
    key_pos = pk * size + lax.broadcasted_iota(jnp.int32, (size, span), 0)
    return (key_pos <= pos) & (key_pos >= low)


def attn_fwd_kernel(slots, *refs):
    meta, q_ref, pos_ref, low_ref = refs[:4]
    slot_refs = refs[4 : 4 + slots]
    mixed_ref, lse_ref, kv_ref, acc_ref, sems = refs[4 + slots :]
    fetch_slots(slot_refs, kv_ref, sems)
    size = q_ref.shape[0] // 2
    kv_width = kv_ref.shape[1] // 2
    groups = kv_width // HD
    for i in range(2):
        rows = slice(i * size, (i + 1) * size)
        pos = jnp.tile(pos_ref[0:1, rows], (1, 2))
        low = jnp.tile(low_ref[0:1, rows], (1, 2))
        for g in range(groups):
            queries = [
                q_ref[rows, (2 * g + r) * HD : (2 * g + r + 1) * HD] for r in range(2)
            ]
            acc_ref[...] = jnp.zeros_like(acc_ref)

            def body(pk, carry):
                peak, total = carry
                spot = pl.multiple_of(meta[4 + pk] * size, size)
                keys = kv_ref[pl.ds(spot, size), g * HD : (g + 1) * HD]
                values = kv_ref[pl.ds(spot, size), kv_width + g * HD : kv_width + (g + 1) * HD]
                scores = jnp.concatenate([dot(keys, q, NT) for q in queries], axis=1) * SCORE
                scores = jnp.where(allowed(pk, size, 2 * size, pos, low), scores, NEGATIVE)
                peak_new = jnp.maximum(peak, jnp.max(scores, axis=0, keepdims=True))
                alpha = jnp.exp2(peak - peak_new)
                probs = jnp.exp2(scores - peak_new)
                total = total * alpha + jnp.sum(probs, axis=0, keepdims=True)
                acc_ref[...] = acc_ref[...] * alpha + dot(values, probs.astype(BF), TN)
                return peak_new, total

            start = (jnp.full((1, 2 * size), NEGATIVE, F32), jnp.zeros((1, 2 * size), F32))
            peak, total = lax.fori_loop(meta[i], meta[2 + i] + 1, body, start)
            lse_ref[pl.ds(i * groups + g, 1), :] = peak + jnp.log2(total)
            out = acc_ref[...] * (1.0 / total)
            for r in range(2):
                mixed_ref[rows, (2 * g + r) * HD : (2 * g + r + 1) * HD] = (
                    out[:, r * size : (r + 1) * size].T.astype(BF)
                )


def attn_fwd(meta, q, pos, low, slots):
    rows, q_width = q.shape
    kv_width = slots[0].shape[1]
    return pl.pallas_call(
        functools.partial(attn_fwd_kernel, len(slots)),
        out_shape=(
            jax.ShapeDtypeStruct((rows, q_width), BF),
            jax.ShapeDtypeStruct((q_width // HD, rows), F32),
        ),
        in_specs=[SM, VM, VM, VM] + [ANY] * len(slots),
        out_specs=[VM, VM],
        scratch_shapes=[
            pltpu.VMEM((len(slots) * rows, kv_width), BF),
            pltpu.VMEM((HD, rows), F32),
            pltpu.SemaphoreType.DMA((len(slots),)),
        ],
        name="attn_fwd",
    )(meta, q, pos, low, *slots)


def attn_bwd_kernel(slots, *refs):
    meta, q_ref, pos_ref, low_ref, lse_ref, mixed_ref, dmix_ref, cos_ref, sin_ref = refs[:9]
    slot_refs = refs[9 : 9 + slots]
    dq_ref = refs[9 + slots]
    dkv_refs = refs[10 + slots : 10 + 2 * slots]
    kv_ref, dkv_ref, dq_acc, sems = refs[10 + 2 * slots :]
    fetch_slots(slot_refs, kv_ref, sems)
    dkv_ref[...] = jnp.zeros_like(dkv_ref)
    rows_all = q_ref.shape[0]
    size = rows_all // 2
    kv_width = kv_ref.shape[1] // 2
    groups = kv_width // HD
    for i in range(2):
        rows = slice(i * size, (i + 1) * size)
        pos = jnp.tile(pos_ref[0:1, rows], (1, 2))
        low = jnp.tile(low_ref[0:1, rows], (1, 2))
        for g in range(groups):
            cols = [slice((2 * g + r) * HD, (2 * g + r + 1) * HD) for r in range(2)]
            queries = jnp.concatenate([q_ref[rows, c] for c in cols], axis=0)
            grads = jnp.concatenate([dmix_ref[rows, c] for c in cols], axis=0)
            outs = jnp.concatenate([mixed_ref[rows, c] for c in cols], axis=0)
            delta = jnp.sum((grads.astype(F32) * outs.astype(F32)).T, axis=0, keepdims=True)
            lse = lse_ref[pl.ds(i * groups + g, 1), :]
            dq_acc[...] = jnp.zeros_like(dq_acc)

            def body(pk, carry):
                spot = pl.multiple_of(meta[4 + pk] * size, size)
                key_cols = slice(g * HD, (g + 1) * HD)
                value_cols = slice(kv_width + g * HD, kv_width + (g + 1) * HD)
                keys = kv_ref[pl.ds(spot, size), key_cols]
                values = kv_ref[pl.ds(spot, size), value_cols]
                scores = dot(keys, queries, NT) * SCORE
                probs = jnp.where(
                    allowed(pk, size, 2 * size, pos, low), jnp.exp2(scores - lse), 0.0
                )
                d_probs = dot(values, grads, NT)
                d_scores = (probs * (d_probs - delta)).astype(BF)
                dkv_ref[pl.ds(spot, size), value_cols] += dot(probs.astype(BF), grads)
                dkv_ref[pl.ds(spot, size), key_cols] += dot(d_scores, queries) * FACTOR
                dq_acc[...] += dot(d_scores, keys, TN)
                return carry

            lax.fori_loop(meta[i], meta[2 + i] + 1, body, 0)
            for r in range(2):
                part = dq_acc[r * size : (r + 1) * size, :] * FACTOR
                dq_ref[rows, cols[r]] = rope(part, cos_ref[rows, :], -sin_ref[rows, :]).astype(BF)
    for j, ref in enumerate(dkv_refs):
        ref[...] = dkv_ref[j * rows_all : (j + 1) * rows_all, :].astype(BF)


def attn_bwd(meta, q, pos, low, lse, mixed, dmix, cosine, sine, slots):
    rows, q_width = q.shape
    kv_width = slots[0].shape[1]
    count = len(slots)
    outs = pl.pallas_call(
        functools.partial(attn_bwd_kernel, count),
        out_shape=[jax.ShapeDtypeStruct((rows, q_width), BF)]
        + [jax.ShapeDtypeStruct((rows, kv_width), BF)] * count,
        in_specs=[SM] + [VM] * 8 + [ANY] * count,
        out_specs=[VM] * (1 + count),
        scratch_shapes=[
            pltpu.VMEM((count * rows, kv_width), BF),
            pltpu.VMEM((count * rows, kv_width), F32),
            pltpu.VMEM((rows, HD), F32),
            pltpu.SemaphoreType.DMA((count,)),
        ],
        name="attn_bwd",
    )(meta, q, pos, low, lse, mixed, dmix, cosine, sine, *slots)
    return outs[0], outs[1:]


def norm_backward(source, scale_rows, gain, upstream):
    weighted = upstream * gain
    average = jnp.mean(weighted * source, axis=1, keepdims=True)
    return scale_rows * weighted - source * scale_rows**3 * average


def shards(
    tokens,
    cotangent,
    keep_mask,
    doc_lengths,
    block_order,
    gain_attn,
    w_query,
    w_key,
    w_value,
    w_out,
    gain_dense,
    w_gate,
    w_up,
    w_down,
):
    rows, width = tokens.shape
    half = rows // 2
    wide = lax.axis_size("wide")
    group = wide // block_order.shape[0]
    ring = group // 2
    wide_index = lax.axis_index("wide")
    member = wide_index % group
    seq_index = wide_index // group
    side = wide_index % 2
    core = lax.axis_index("narrow") % 2
    strip = width // wide
    turns = wide // 2

    def ordered(mine, other):
        return jnp.where(
            core == 0,
            jnp.concatenate([mine, other], axis=0),
            jnp.concatenate([other, mine], axis=0),
        )

    def own_half(value):
        return lax.dynamic_slice_in_dim(value, core * half, half)

    def other_half(value):
        return lax.dynamic_slice_in_dim(value, (1 - core) * half, half)

    order_row = lax.dynamic_index_in_dim(block_order, seq_index, 0, keepdims=False)
    length_row = lax.dynamic_index_in_dim(doc_lengths, seq_index, 0, keepdims=False)
    doc_ends = jnp.cumsum(length_row)
    places = jnp.stack([member * 2 + core, member * 2 + 1 - core])
    chosen = jnp.sum(
        jnp.where(places[:, None] == jnp.arange(2 * group)[None, :], order_row[None, :], 0), axis=1
    )
    pos = (chosen[:, None] * half + jnp.arange(half, dtype=jnp.int32)[None, :]).reshape(-1)
    low = jnp.max(jnp.where(doc_ends[None, :] <= pos[:, None], doc_ends[None, :], 0), axis=1)
    block_low = low.reshape(2, half)[:, 0] // half
    stored = jnp.sum(
        jnp.where(
            order_row[None, :] == jnp.arange(2 * group)[:, None], jnp.arange(2 * group)[None, :], 0
        ),
        axis=1,
    )
    owner = stored // 2
    slot = (member // 2 - owner // 2) % ring + ring * (owner % 2 != side).astype(jnp.int32)
    spots = slot * 2 + (stored % 2 != core).astype(jnp.int32)
    meta = jnp.concatenate([block_low, chosen, spots]).astype(jnp.int32)
    frequency = BASE ** (-(jnp.arange(HD // 2, dtype=F32) * 2.0) / HD)
    angles = pos.astype(F32)[:, None] * frequency[None, :]
    cosine = jnp.cos(angles)
    sine = jnp.sin(angles)
    cosine = jnp.concatenate([cosine, cosine], axis=1)
    sine = jnp.concatenate([-sine, sine], axis=1)
    pos_row = pos[None, :]
    low_row = low[None, :]

    core_arr = core.astype(jnp.int32)[None]
    normed_one, both = norm_kv(core_arr, tokens, gain_attn[None, :], w_key, w_value, cosine, sine)
    near = [both]
    far = [wide_swap(both)]
    for step in range(1, ring):
        near.append(wide_ring(near[-1], group))
        far.append(wide_swap(near[-1]))
    slots = near + far
    query = query_proj(normed_one, w_query, cosine, sine)
    mixed, lse = attn_fwd(meta, query, pos_row, low_row, slots)

    def reduce_narrow(other_part, own_part):
        got = narrow_swap(other_part, 1)
        held = (own_part + got.astype(F32)).astype(BF)
        return held.astype(F32) + narrow_swap(held, 2).astype(F32)

    def cut(value):
        return value[:half], value[half:]

    mixed_own, mixed_other = cut(mixed)
    attn_out = reduce_narrow(dot(mixed_other, w_out).astype(BF), dot(mixed_own, w_out))
    source = own_half(tokens).astype(F32)
    keep_own = own_half(keep_mask).astype(F32)[:, None]
    hidden_one = source + keep_own * attn_out
    gain_two = gain_dense.astype(F32)
    scale_two = lax.rsqrt(jnp.mean(hidden_one * hidden_one, axis=1, keepdims=True) + EPSILON)
    normed_two_own = (hidden_one * scale_two * gain_two).astype(BF)
    normed_two = jnp.concatenate([normed_two_own, narrow_swap(normed_two_own, 1)], axis=0)

    keep_rel = jnp.concatenate([own_half(keep_mask), other_half(keep_mask)])[:, None]
    cot_rel = jnp.concatenate([own_half(cotangent), other_half(cotangent)])
    d_dense = jnp.where(keep_rel > 0, cot_rel, jnp.zeros_like(cot_rel))
    d_inner = dot(d_dense, w_down, NT)
    gate = dot(normed_two, w_gate)
    up = dot(normed_two, w_up)
    sigma = jax.nn.sigmoid(gate)
    silu = gate * sigma
    inner = (silu * up).astype(BF)
    d_gate = (d_inner * up * sigma * (1.0 + gate * (1.0 - sigma))).astype(BF)
    d_up = (d_inner * silu).astype(BF)

    dg_own, dg_other = cut(d_gate)
    du_own, du_other = cut(d_up)

    def back_dense(dg, du):
        return dot(dg, w_gate, NT) + dot(du, w_up, NT)

    d_normed_two = reduce_narrow(back_dense(dg_other, du_other).astype(BF), back_dense(dg_own, du_own))
    inner_own, inner_other = cut(inner)
    dense_out = reduce_narrow(dot(inner_other, w_down).astype(BF), dot(inner_own, w_down))
    output_own = (hidden_one + keep_own * dense_out).astype(BF)
    output = ordered(output_own, narrow_swap(output_own, 1))

    upstream = own_half(cotangent).astype(F32)
    d_hidden = upstream + norm_backward(hidden_one, scale_two, gain_two, d_normed_two)
    d_attn_own = (keep_own * d_hidden).astype(BF)
    d_attn = jnp.concatenate([d_attn_own, narrow_swap(d_attn_own, 1)], axis=0)

    def strips(value):
        cells = value.reshape(value.shape[0], turns, 2, strip)
        mine = lax.dynamic_index_in_dim(cells, side, 2, keepdims=False)
        theirs = lax.dynamic_index_in_dim(cells, 1 - side, 2, keepdims=False)
        flat = (value.shape[0], turns * strip)
        return jnp.concatenate([mine.reshape(flat), wide_swap(theirs.reshape(flat))], axis=0)

    def paired(value):
        return jnp.concatenate([value, wide_swap(value)], axis=0)

    def ring_sum(part):
        carried = None
        for step in range(1, turns + 1):
            piece = part((wide_index // 2 - step) % turns)
            if carried is not None:
                piece = piece + carried.astype(F32)
            if step == turns:
                return piece
            carried = wide_ring(piece.astype(BF), wide)

    def strip_of(value, turn):
        return lax.dynamic_slice_in_dim(value, turn * strip, strip, axis=1)

    d_dense_strips = strips(d_dense)
    normed_two_strips = strips(normed_two)
    normed_one_strips = strips(normed_one)
    d_attn_strips = strips(d_attn)
    inner_two = paired(inner)
    d_gate_two = paired(d_gate)
    d_up_two = paired(d_up)
    grad_down = ring_sum(lambda t: dot(inner_two, strip_of(d_dense_strips, t), TN))
    grad_gate = ring_sum(lambda t: dot(strip_of(normed_two_strips, t), d_gate_two, TN))
    grad_up = ring_sum(lambda t: dot(strip_of(normed_two_strips, t), d_up_two, TN))

    d_mixed = dot(d_attn, w_out, NT).astype(BF)
    d_query, d_slots = attn_bwd(
        meta, query, pos_row, low_row, lse, mixed, d_mixed, cosine, sine, slots
    )
    mixed_two = paired(mixed)
    grad_out = ring_sum(lambda t: dot(mixed_two, strip_of(d_attn_strips, t), TN))

    carried = None
    for step in [*range(1, ring), 0]:
        piece = d_slots[step].astype(F32) + wide_swap(d_slots[ring + step]).astype(F32)
        if carried is not None:
            piece = piece + carried.astype(F32)
        if step:
            carried = wide_ring(piece.astype(BF), group)
    kv_width = w_key.shape[1]
    d_keys = piece[:, :kv_width].reshape(rows, kv_width // HD, HD)
    turned = jnp.concatenate([d_keys[..., HD // 2 :], d_keys[..., : HD // 2]], axis=-1)
    d_keys = d_keys * cosine[:, None, :] - turned * sine[:, None, :]
    d_kv = jnp.concatenate([d_keys.reshape(rows, kv_width), piece[:, kv_width:]], axis=1).astype(BF)
    d_key, d_value = d_kv[:, :kv_width], d_kv[:, kv_width:]

    def back_attn(part):
        return (
            dot(part(d_query), w_query, NT)
            + dot(part(d_key), w_key, NT)
            + dot(part(d_value), w_value, NT)
        )

    d_normed_one = reduce_narrow(
        back_attn(lambda v: v[half:]).astype(BF), back_attn(lambda v: v[:half])
    )
    gain_one = gain_attn.astype(F32)
    scale_one = lax.rsqrt(jnp.mean(source * source, axis=1, keepdims=True) + EPSILON)
    grad_own = (d_hidden + norm_backward(source, scale_one, gain_one, d_normed_one)).astype(BF)
    grad_tokens = ordered(grad_own, narrow_swap(grad_own, 1))

    d_query_two = paired(d_query)
    d_kv_two = paired(d_kv)
    grad_query = ring_sum(lambda t: dot(strip_of(normed_one_strips, t), d_query_two, TN))
    grad_kv = ring_sum(lambda t: dot(strip_of(normed_one_strips, t), d_kv_two, TN))
    grad_key, grad_value = grad_kv[:, :kv_width], grad_kv[:, kv_width:]

    def strip_rows(weight):
        return lax.dynamic_slice_in_dim(weight, wide_index * strip, strip).astype(F32)

    def gain_grad(pairs, gain):
        local = sum(jnp.sum(strip_rows(w) * g, axis=1) for w, g in pairs)[None, :]
        local = local + narrow_swap(local, 1)
        local = local + narrow_swap(local, 2)
        return local[0] / lax.dynamic_slice_in_dim(gain, wide_index * strip, strip)

    grad_gain_two = gain_grad([(w_gate, grad_gate), (w_up, grad_up)], gain_two)
    grad_gain_one = gain_grad(
        [(w_query, grad_query), (w_key, grad_key), (w_value, grad_value)], gain_one
    )
    return (
        output,
        grad_tokens,
        grad_gain_one,
        grad_query,
        grad_key,
        grad_value,
        grad_out,
        grad_gain_two,
        grad_gate,
        grad_up,
        grad_down,
    )


def solution(mesh):
    placed = (
        P("wide", None),
        P("wide", None),
        P("wide"),
        P(),
        P(),
        P(),
        P(None, "narrow"),
        P(None, "narrow"),
        P(None, "narrow"),
        P("narrow", None),
        P(),
        P(None, "narrow"),
        P(None, "narrow"),
        P("narrow", None),
    )
    return jax.shard_map(
        shards,
        mesh=mesh,
        in_specs=placed,
        out_specs=(
            P("wide", None),
            P("wide", None),
            P("wide"),
            P("wide", "narrow"),
            P("wide", "narrow"),
            P("wide", "narrow"),
            P("narrow", "wide"),
            P("wide"),
            P("wide", "narrow"),
            P("wide", "narrow"),
            P("narrow", "wide"),
        ),
        check_vma=False,
    )
```

```python
import functools

import jax
import jax.numpy as jnp
from jax import lax
from jax.experimental import pallas as pl
from jax.experimental.pallas import tpu as pltpu
from jax.sharding import PartitionSpec as P

HD = 128
EPSILON = 1e-05
NEGATIVE = -1e30
BASE = 10000.0
LOG2E = 1.4426950408889634
SCORE = HD ** (-0.5) * LOG2E
FACTOR = HD ** (-0.5)
BF = jnp.bfloat16
F32 = jnp.float32
NT = (((1,), (1,)), ((), ()))
TN = (((0,), (0,)), ((), ()))
NN = (((1,), (0,)), ((), ()))
VM = pl.BlockSpec(memory_space=pltpu.VMEM)
SM = pl.BlockSpec(memory_space=pltpu.SMEM)
ANY = pl.BlockSpec(memory_space=pl.ANY)


def dot(a, b, dims=(((1,), (0,)), ((), ()))):
    return lax.dot_general(a, b, dims, preferred_element_type=F32)


def narrow_swap(value, mask):
    pairs = [(n, n ^ mask) for n in range(lax.axis_size("narrow"))]
    return lax.ppermute(value, "narrow", pairs)


def wide_swap(value):
    return lax.ppermute(value, "wide", [(w, w ^ 1) for w in range(lax.axis_size("wide"))])


def wide_ring(value, group):
    ring = group // 2
    pairs = []
    for w in range(lax.axis_size("wide")):
        base, member = w // group * group, w % group
        pairs.append((w, base + (member // 2 + 1) % ring * 2 + member % 2))
    return lax.ppermute(value, "wide", pairs)


def rope(value, cosine, sine):
    return value * cosine + pltpu.roll(value, HD // 2, 1) * sine


def norm_kv_kernel(core, x_ref, gain_ref, wk_ref, wv_ref, cos_ref, sin_ref, normed_ref, kv_ref):
    x = x_ref[...].astype(F32)
    scale = lax.rsqrt(jnp.mean(x * x, axis=1, keepdims=True) + EPSILON)
    normed = (x * scale * gain_ref[...].astype(F32)).astype(BF)
    normed_ref[...] = normed
    width = wk_ref.shape[1]
    keys = dot(normed, wk_ref[...])
    for h in range(width // HD):
        cols = slice(h * HD, (h + 1) * HD)
        kv_ref[:, cols] = rope(keys[:, cols], cos_ref[...], sin_ref[...]).astype(BF)
    kv_ref[:, width:] = dot(normed, wv_ref[...]).astype(BF)


def norm_kv(core, tokens, gain, wk, wv, cosine, sine):
    rows, width = tokens.shape
    half = rows // 2
    full = lambda w: pl.BlockSpec(w.shape, lambda i, c: (0, 0))
    return pl.pallas_call(
        norm_kv_kernel,
        out_shape=(
            jax.ShapeDtypeStruct((rows, width), BF),
            jax.ShapeDtypeStruct((rows, 2 * wk.shape[1]), BF),
        ),
        grid_spec=pltpu.PrefetchScalarGridSpec(
            num_scalar_prefetch=1,
            grid=(2,),
            in_specs=[
                pl.BlockSpec((half, width), lambda i, c: (i ^ c[0], 0)),
                full(gain),
                full(wk),
                full(wv),
                pl.BlockSpec((half, HD), lambda i, c: (i, 0)),
                pl.BlockSpec((half, HD), lambda i, c: (i, 0)),
            ],
            out_specs=[
                pl.BlockSpec((half, width), lambda i, c: (i, 0)),
                pl.BlockSpec((half, 2 * wk.shape[1]), lambda i, c: (i, 0)),
            ],
        ),
        cost_estimate=pl.CostEstimate(flops=int(2.9e9), bytes_accessed=0, transcendentals=0),
        name="norm_kv",
    )(core, tokens, gain, wk, wv, cosine, sine)


def query_kernel(x_ref, w_ref, cos_ref, sin_ref, out_ref):
    raw = dot(x_ref[...], w_ref[...])
    for h in range(raw.shape[1] // HD):
        cols = slice(h * HD, (h + 1) * HD)
        out_ref[:, cols] = rope(raw[:, cols], cos_ref[...], sin_ref[...]).astype(BF)


def query_proj(x, w, cosine, sine):
    rows, width = x.shape
    half = rows // 2
    return pl.pallas_call(
        query_kernel,
        out_shape=jax.ShapeDtypeStruct((rows, w.shape[1]), BF),
        grid=(2,),
        in_specs=[
            pl.BlockSpec((half, width), lambda i: (i, 0)),
            pl.BlockSpec(w.shape, lambda i: (0, 0)),
            pl.BlockSpec((half, HD), lambda i: (i, 0)),
            pl.BlockSpec((half, HD), lambda i: (i, 0)),
        ],
        out_specs=pl.BlockSpec((half, w.shape[1]), lambda i: (i, 0)),
        cost_estimate=pl.CostEstimate(flops=int(2.9e9), bytes_accessed=0, transcendentals=0),
        name="query_proj",
    )(x, w, cosine, sine)


def fetch_slots(slot_refs, kv_ref, sems):
    rows = slot_refs[0].shape[0]
    copies = [
        pltpu.make_async_copy(ref, kv_ref.at[pl.ds(j * rows, rows), :], sems.at[j])
        for j, ref in enumerate(slot_refs)
    ]
    for copy in copies:
        copy.start()
    for copy in copies:
        copy.wait()


def allowed(pk, size, span, pos, low):
    key_pos = pk * size + lax.broadcasted_iota(jnp.int32, (size, span), 0)
    return (key_pos <= pos) & (key_pos >= low)


def attn_fwd_kernel(slots, *refs):
    meta, q_ref, pos_ref, low_ref = refs[:4]
    slot_refs = refs[4 : 4 + slots]
    mixed_ref, lse_ref, kv_ref, acc_ref, sems = refs[4 + slots :]
    fetch_slots(slot_refs, kv_ref, sems)
    size = q_ref.shape[0] // 2
    kv_width = kv_ref.shape[1] // 2
    groups = kv_width // HD
    for i in range(2):
        rows = slice(i * size, (i + 1) * size)
        pos = jnp.tile(pos_ref[0:1, rows], (1, 2))
        low = jnp.tile(low_ref[0:1, rows], (1, 2))
        for g in range(groups):
            queries = [
                q_ref[rows, (2 * g + r) * HD : (2 * g + r + 1) * HD] for r in range(2)
            ]
            acc_ref[...] = jnp.zeros_like(acc_ref)

            def body(pk, carry):
                peak, total = carry
                spot = pl.multiple_of(meta[4 + pk] * size, size)
                keys = kv_ref[pl.ds(spot, size), g * HD : (g + 1) * HD]
                values = kv_ref[pl.ds(spot, size), kv_width + g * HD : kv_width + (g + 1) * HD]
                scores = jnp.concatenate([dot(keys, q, NT) for q in queries], axis=1) * SCORE
                scores = jnp.where(allowed(pk, size, 2 * size, pos, low), scores, NEGATIVE)
                peak_new = jnp.maximum(peak, jnp.max(scores, axis=0, keepdims=True))
                alpha = jnp.exp2(peak - peak_new)
                probs = jnp.exp2(scores - peak_new)
                total = total * alpha + jnp.sum(probs, axis=0, keepdims=True)
                acc_ref[...] = acc_ref[...] * alpha + dot(values, probs.astype(BF), TN)
                return peak_new, total

            start = (jnp.full((1, 2 * size), NEGATIVE, F32), jnp.zeros((1, 2 * size), F32))
            peak, total = lax.fori_loop(meta[i], meta[2 + i] + 1, body, start)
            lse_ref[pl.ds(i * groups + g, 1), :] = peak + jnp.log2(total)
            out = acc_ref[...] * (1.0 / total)
            for r in range(2):
                mixed_ref[rows, (2 * g + r) * HD : (2 * g + r + 1) * HD] = (
                    out[:, r * size : (r + 1) * size].T.astype(BF)
                )


def attn_fwd(meta, q, pos, low, slots):
    rows, q_width = q.shape
    kv_width = slots[0].shape[1]
    return pl.pallas_call(
        functools.partial(attn_fwd_kernel, len(slots)),
        out_shape=(
            jax.ShapeDtypeStruct((rows, q_width), BF),
            jax.ShapeDtypeStruct((q_width // HD, rows), F32),
        ),
        in_specs=[SM, VM, VM, VM] + [ANY] * len(slots),
        out_specs=[VM, VM],
        scratch_shapes=[
            pltpu.VMEM((len(slots) * rows, kv_width), BF),
            pltpu.VMEM((HD, rows), F32),
            pltpu.SemaphoreType.DMA((len(slots),)),
        ],
        cost_estimate=pl.CostEstimate(flops=int(5.2e9), bytes_accessed=0, transcendentals=0),
        name="attn_fwd",
    )(meta, q, pos, low, *slots)


def attn_bwd_kernel(slots, *refs):
    meta, q_ref, pos_ref, low_ref, lse_ref, mixed_ref, dmix_ref, cos_ref, sin_ref = refs[:9]
    slot_refs = refs[9 : 9 + slots]
    dq_ref = refs[9 + slots]
    dkv_refs = refs[10 + slots : 10 + 2 * slots]
    kv_ref, dkv_ref, dq_acc, sems = refs[10 + 2 * slots :]
    fetch_slots(slot_refs, kv_ref, sems)
    dkv_ref[...] = jnp.zeros_like(dkv_ref)
    rows_all = q_ref.shape[0]
    size = rows_all // 2
    kv_width = kv_ref.shape[1] // 2
    groups = kv_width // HD
    for i in range(2):
        rows = slice(i * size, (i + 1) * size)
        pos = jnp.tile(pos_ref[0:1, rows], (1, 2))
        low = jnp.tile(low_ref[0:1, rows], (1, 2))
        for g in range(groups):
            cols = [slice((2 * g + r) * HD, (2 * g + r + 1) * HD) for r in range(2)]
            queries = jnp.concatenate([q_ref[rows, c] for c in cols], axis=0)
            grads = jnp.concatenate([dmix_ref[rows, c] for c in cols], axis=0)
            outs = jnp.concatenate([mixed_ref[rows, c] for c in cols], axis=0)
            delta = jnp.sum((grads.astype(F32) * outs.astype(F32)).T, axis=0, keepdims=True)
            lse = lse_ref[pl.ds(i * groups + g, 1), :]
            dq_acc[...] = jnp.zeros_like(dq_acc)

            def body(pk, carry):
                spot = pl.multiple_of(meta[4 + pk] * size, size)
                key_cols = slice(g * HD, (g + 1) * HD)
                value_cols = slice(kv_width + g * HD, kv_width + (g + 1) * HD)
                keys = kv_ref[pl.ds(spot, size), key_cols]
                values = kv_ref[pl.ds(spot, size), value_cols]
                scores = dot(keys, queries, NT) * SCORE
                probs = jnp.where(
                    allowed(pk, size, 2 * size, pos, low), jnp.exp2(scores - lse), 0.0
                )
                d_probs = dot(values, grads, NT)
                d_scores = (probs * (d_probs - delta)).astype(BF)
                dkv_ref[pl.ds(spot, size), value_cols] += dot(probs.astype(BF), grads)
                dkv_ref[pl.ds(spot, size), key_cols] += dot(d_scores, queries) * FACTOR
                dq_acc[...] += dot(d_scores, keys, TN)
                return carry

            lax.fori_loop(meta[i], meta[2 + i] + 1, body, 0)
            for r in range(2):
                part = dq_acc[r * size : (r + 1) * size, :] * FACTOR
                dq_ref[rows, cols[r]] = rope(part, cos_ref[rows, :], -sin_ref[rows, :]).astype(BF)
    for j, ref in enumerate(dkv_refs):
        ref[...] = dkv_ref[j * rows_all : (j + 1) * rows_all, :].astype(BF)


def attn_bwd(meta, q, pos, low, lse, mixed, dmix, cosine, sine, slots):
    rows, q_width = q.shape
    kv_width = slots[0].shape[1]
    count = len(slots)
    outs = pl.pallas_call(
        functools.partial(attn_bwd_kernel, count),
        out_shape=[jax.ShapeDtypeStruct((rows, q_width), BF)]
        + [jax.ShapeDtypeStruct((rows, kv_width), BF)] * count,
        in_specs=[SM] + [VM] * 8 + [ANY] * count,
        out_specs=[VM] * (1 + count),
        scratch_shapes=[
            pltpu.VMEM((count * rows, kv_width), BF),
            pltpu.VMEM((count * rows, kv_width), F32),
            pltpu.VMEM((rows, HD), F32),
            pltpu.SemaphoreType.DMA((count,)),
        ],
        cost_estimate=pl.CostEstimate(flops=int(7.2e9), bytes_accessed=0, transcendentals=0),
        name="attn_bwd",
    )(meta, q, pos, low, lse, mixed, dmix, cosine, sine, *slots)
    return outs[0], outs[1:]


def cost(micros):
    return pl.CostEstimate(flops=int(micros * 0.575e9), bytes_accessed=0, transcendentals=0)


def split_rows(total, own_ref, other_ref):
    half = own_ref.shape[0]
    own_ref[...] = total[:half].astype(BF)
    other_ref[...] = total[half:].astype(BF)


def project_kernel(spec, *refs):
    total = None
    for a, b, offset, dims in spec:
        left = refs[a][...] if dims is not None else None
        if dims == "nt":
            right, form = refs[b][:, offset : offset + left.shape[1]], NT
        else:
            right, form = refs[b][offset : offset + left.shape[1], :], NN
        term = dot(left, right, form)
        total = term if total is None else total + term
    split_rows(total, refs[-2], refs[-1])


def project(pairs, dims, tile, micros):
    operands, specs, plan, weights = [], [], [], []
    for a, b, offset in pairs:
        operands.append(a)
        specs.append(pl.BlockSpec(a.shape, lambda i: (0, 0)))
        spot = next((at for at, seen in weights if seen is b), None)
        left = len(operands) - 1
        if spot is None:
            spot = len(operands)
            operands.append(b)
            weights.append((spot, b))
            if dims == "nt":
                specs.append(pl.BlockSpec((tile, b.shape[1]), lambda i: (i, 0)))
            else:
                specs.append(pl.BlockSpec((b.shape[0], tile), lambda i: (0, i)))
        plan.append((left, spot, offset, dims))
    rows = pairs[0][0].shape[0]
    width = pairs[0][1].shape[0 if dims == "nt" else 1]
    return pl.pallas_call(
        functools.partial(project_kernel, plan),
        out_shape=[jax.ShapeDtypeStruct((rows // 2, width), BF)] * 2,
        grid=(width // tile,),
        in_specs=specs,
        out_specs=[pl.BlockSpec((rows // 2, tile), lambda i: (0, i))] * 2,
        cost_estimate=cost(micros),
        name="project",
    )(*operands)


def back_dense_kernel(first_ref, second_ref, wg_ref, wu_ref, own_ref, other_ref):
    total = None
    offset = 0
    for ref in (first_ref, second_ref):
        count = ref.shape[2]
        for k, w_ref in enumerate((wg_ref, wu_ref)):
            term = dot(ref[k], w_ref[:, offset : offset + count], NT)
            total = term if total is None else total + term
        offset += count
    split_rows(total, own_ref, other_ref)


def back_dense(first, second, w_gate, w_up, tile):
    width, hidden = w_gate.shape
    rows = first.shape[1]
    whole = lambda v: pl.BlockSpec(v.shape, lambda i: (0, 0, 0))
    weight = pl.BlockSpec((tile, hidden), lambda i: (i, 0))
    return pl.pallas_call(
        back_dense_kernel,
        out_shape=[jax.ShapeDtypeStruct((rows // 2, width), BF)] * 2,
        grid=(width // tile,),
        in_specs=[whole(first), whole(second), weight, weight],
        out_specs=[pl.BlockSpec((rows // 2, tile), lambda i: (0, i))] * 2,
        cost_estimate=cost(11),
        name="back_dense",
    )(first, second, w_gate, w_up)


def gated_kernel(own_ref, other_ref, wg_ref, wu_ref, di_ref, inner_ref, dgu_ref, all_ref):
    @pl.when(pl.program_id(0) == 0)
    def _():
        half = own_ref.shape[0]
        all_ref[:half, :] = own_ref[...]
        all_ref[half:, :] = other_ref[...]

    gate = dot(all_ref[...], wg_ref[...])
    up = dot(all_ref[...], wu_ref[...])
    sigma = 1.0 / (1.0 + jnp.exp(-gate))
    silu = gate * sigma
    d_inner = di_ref[...]
    inner_ref[...] = (silu * up).astype(BF)
    dgu_ref[0] = (d_inner * up * sigma * (1.0 + gate * (1.0 - sigma))).astype(BF)
    dgu_ref[1] = (d_inner * silu).astype(BF)


def gated(own, other, wg, wu, d_inner, first, columns, tile):
    half, width = own.shape
    weight = pl.BlockSpec((width, tile), lambda i: (0, first // tile + i))
    whole = pl.BlockSpec((half, width), lambda i: (0, 0))
    return pl.pallas_call(
        gated_kernel,
        out_shape=[
            jax.ShapeDtypeStruct((2 * half, columns), BF),
            jax.ShapeDtypeStruct((2, 2 * half, columns), BF),
        ],
        grid=(pl.cdiv(columns, tile),),
        in_specs=[
            whole,
            whole,
            weight,
            weight,
            pl.BlockSpec((2 * half, tile), lambda i: (0, first // tile + i)),
        ],
        out_specs=[
            pl.BlockSpec((2 * half, tile), lambda i: (0, i)),
            pl.BlockSpec((2, 2 * half, tile), lambda i: (0, 0, i)),
        ],
        scratch_shapes=[pltpu.VMEM((2 * half, width), BF)],
        cost_estimate=cost(7.5),
        name="gated",
    )(own, other, wg, wu, d_inner)


def mixed_grad_kernel(own_ref, other_ref, w_ref, out_ref):
    both = jnp.concatenate([own_ref[...], other_ref[...]], axis=0)
    out_ref[...] = dot(both, w_ref[...], NT).astype(BF)


def mixed_grad(own, other, w):
    return pl.pallas_call(
        mixed_grad_kernel,
        out_shape=jax.ShapeDtypeStruct((2 * own.shape[0], w.shape[0]), BF),
        in_specs=[VM] * 3,
        out_specs=VM,
        cost_estimate=cost(4),
        name="mixed_grad",
    )(own, other, w)


def d_inner_kernel(x_ref, w_ref, out_ref):
    out_ref[...] = dot(x_ref[...], w_ref[...], NT)


def inner_grad(x, w, tile):
    rows, width = x.shape
    hidden = w.shape[0]
    return pl.pallas_call(
        d_inner_kernel,
        out_shape=jax.ShapeDtypeStruct((rows, hidden), F32),
        grid=(pl.cdiv(hidden, tile),),
        in_specs=[
            pl.BlockSpec((rows, width), lambda i: (0, 0)),
            pl.BlockSpec((tile, width), lambda i: (i, 0)),
        ],
        out_specs=pl.BlockSpec((rows, tile), lambda i: (0, i)),
        cost_estimate=cost(8),
        name="inner_grad",
    )(x, w)


def pack_kernel(count, plan, strip, tbl, *refs):
    ins, outs = refs[:count], refs[count:]
    for out_ref, pieces in zip(outs, plan):
        column = 0
        for at, rows, row in pieces:
            for k in range(tbl.shape[1]):
                first = pl.multiple_of(tbl[row, k] * strip, 128)
                out_ref[:, column : column + strip] = ins[at][rows, pl.ds(first, strip)]
                column += strip


def pack(values, plan, tbl, strip):
    turns = tbl.shape[1]
    if strip % 128:
        cut = lambda v, rows, at: lax.dynamic_slice_in_dim(v[rows], at * strip, strip, axis=1)
        return [
            jnp.concatenate(
                [cut(values[at], rows, tbl[row, k]) for at, rows, row in pieces for k in range(turns)],
                axis=1,
            )
            for pieces in plan
        ]
    return pl.pallas_call(
        functools.partial(pack_kernel, len(values), plan, strip),
        out_shape=[
            jax.ShapeDtypeStruct(
                (p[0][1].stop - p[0][1].start, len(p) * turns * strip), values[0].dtype
            )
            for p in plan
        ],
        in_specs=[SM] + [VM] * len(values),
        out_specs=[VM] * len(plan),
        cost_estimate=cost(1.5),
        name="pack",
    )(tbl, *values)


def strip_rows_kernel(halves, near, rights, nears, tbl, *refs):
    left = refs[:halves]
    left_near = refs[halves : halves + near]
    right = refs[halves + near : halves + near + rights]
    right_near = refs[halves + near + rights : halves + near + rights + nears]
    outs = refs[halves + near + rights + nears :]
    step = pl.program_id(0)
    join = lambda group: (
        group[0][...] if len(group) == 1 else jnp.concatenate([r[...] for r in group], axis=0)
    )
    mine, theirs = join(left), join(left_near)
    pieces = []
    for r, n in zip(right, right_near):
        planes = range(r.shape[0]) if len(r.shape) == 3 else [None]
        for k in planes:
            a = r[...] if k is None else r[k]
            b = n[...] if k is None else n[k]
            pieces.append((dot(mine, a, TN) + dot(theirs, b, TN)).astype(BF))
    for k, out in enumerate(outs):

        @pl.when(step == k)
        def _():
            column = 0
            for piece in pieces:
                out[:, column : column + piece.shape[1]] = piece
                column += piece.shape[1]


def strip_rows_grad(left, left_near, right, right_near, tbl, strip, micros):
    turns = tbl.shape[1]
    columns = sum(r.shape[-1] * (r.shape[0] if r.ndim == 3 else 1) for r in right)
    if strip % 128:
        near = jnp.concatenate(left_near, axis=0)
        mine = jnp.concatenate(left, axis=0)
        flat = lambda r: [r] if r.ndim == 2 else [r[k] for k in range(r.shape[0])]
        outs = []
        for k in range(turns):
            a = lax.dynamic_slice_in_dim(mine, tbl[0, k] * strip, strip, axis=1)
            b = near[:, k * strip : (k + 1) * strip]
            outs.append(
                jnp.concatenate(
                    [
                        dot(a, x, TN) + dot(b, y, TN)
                        for r, n in zip(right, right_near)
                        for x, y in zip(flat(r), flat(n))
                    ],
                    axis=1,
                ).astype(BF)
            )
        return outs
    whole = lambda v: pl.BlockSpec(v.shape, lambda i, t: (0,) * v.ndim)
    return pl.pallas_call(
        functools.partial(
            strip_rows_kernel, len(left), len(left_near), len(right), len(right_near)
        ),
        out_shape=[jax.ShapeDtypeStruct((strip, columns), BF)] * turns,
        grid_spec=pltpu.PrefetchScalarGridSpec(
            num_scalar_prefetch=1,
            grid=(turns,),
            in_specs=[pl.BlockSpec((v.shape[0], strip), lambda i, t: (0, t[0, i])) for v in left]
            + [pl.BlockSpec((v.shape[0], strip), lambda i, t: (0, i)) for v in left_near]
            + [whole(v) for v in [*right, *right_near]],
            out_specs=[pl.BlockSpec((strip, columns), lambda i, t: (0, 0))] * turns,
        ),
        cost_estimate=cost(micros),
        name="strip_rows",
    )(tbl, *left, *left_near, *right, *right_near)


def strip_columns_kernel(halves, near, strip, *refs):
    left_ref, left_near_ref = refs[:2]
    right = refs[2 : 2 + halves]
    right_near = refs[2 + halves : 2 + halves + near]
    outs = refs[2 + halves + near :]
    total = None
    for ref, group in ((left_ref, right), (left_near_ref, right_near)):
        row = 0
        for r in group:
            term = dot(ref[row : row + r.shape[0], :], r[...], TN)
            total = term if total is None else total + term
            row += r.shape[0]
    for k, out in enumerate(outs):
        out[...] = total[:, k * strip : (k + 1) * strip].astype(BF)


def strip_columns_grad(left, left_near, right, right_near, turns, strip, tile, micros):
    rows, count = left.shape
    whole = lambda v: pl.BlockSpec(v.shape, lambda i: (0, 0))
    return pl.pallas_call(
        functools.partial(strip_columns_kernel, len(right), len(right_near), strip),
        out_shape=[jax.ShapeDtypeStruct((count, strip), BF)] * turns,
        grid=(pl.cdiv(count, tile),),
        in_specs=[pl.BlockSpec((rows, tile), lambda i: (0, i))] * 2
        + [whole(v) for v in [*right, *right_near]],
        out_specs=[pl.BlockSpec((tile, strip), lambda i: (i, 0))] * turns,
        cost_estimate=cost(micros),
        name="strip_columns",
    )(left, left_near, *right, *right_near)


def close_kv_kernel(a_ref, b_ref, c_ref, cos_ref, sin_ref, dk_ref, dv_ref):
    total = a_ref[...].astype(F32) + b_ref[...].astype(F32) + c_ref[...].astype(F32)
    width = dk_ref.shape[1]
    for h in range(width // HD):
        cols = slice(h * HD, (h + 1) * HD)
        dk_ref[:, cols] = rope(total[:, cols], cos_ref[...], -sin_ref[...]).astype(BF)
    dv_ref[...] = total[:, width:].astype(BF)


def close_kv(a, b, c, cosine, sine):
    rows, width = a.shape
    return pl.pallas_call(
        close_kv_kernel,
        out_shape=[jax.ShapeDtypeStruct((rows, width // 2), BF)] * 2,
        in_specs=[VM] * 5,
        out_specs=[VM] * 2,
        cost_estimate=cost(1.5),
        name="close_kv",
    )(a, b, c, cosine, sine)


def norm_backward(source, scale_rows, gain, upstream):
    weighted = upstream * gain
    average = jnp.mean(weighted * source, axis=1, keepdims=True)
    return scale_rows * weighted - source * scale_rows**3 * average


def after(value, *done):
    return lax.optimization_barrier((value, *done))[0]


def shards(
    tokens,
    cotangent,
    keep_mask,
    doc_lengths,
    block_order,
    gain_attn,
    w_query,
    w_key,
    w_value,
    w_out,
    gain_dense,
    w_gate,
    w_up,
    w_down,
):
    rows, width = tokens.shape
    half = rows // 2
    wide = lax.axis_size("wide")
    group = wide // block_order.shape[0]
    ring = group // 2
    wide_index = lax.axis_index("wide")
    member = wide_index % group
    seq_index = wide_index // group
    side = (wide_index % 2).astype(jnp.int32)
    core = lax.axis_index("narrow") % 2
    strip = width // wide
    turns = wide // 2

    def ordered(mine, other):
        return jnp.where(
            core == 0,
            jnp.concatenate([mine, other], axis=0),
            jnp.concatenate([other, mine], axis=0),
        )

    def own_half(value):
        return lax.dynamic_slice_in_dim(value, core * half, half)

    def other_half(value):
        return lax.dynamic_slice_in_dim(value, (1 - core) * half, half)

    order_row = lax.dynamic_index_in_dim(block_order, seq_index, 0, keepdims=False)
    length_row = lax.dynamic_index_in_dim(doc_lengths, seq_index, 0, keepdims=False)
    doc_ends = jnp.cumsum(length_row)
    places = jnp.stack([member * 2 + core, member * 2 + 1 - core])
    chosen = jnp.sum(
        jnp.where(places[:, None] == jnp.arange(2 * group)[None, :], order_row[None, :], 0), axis=1
    )
    pos = (chosen[:, None] * half + jnp.arange(half, dtype=jnp.int32)[None, :]).reshape(-1)
    low = jnp.max(jnp.where(doc_ends[None, :] <= pos[:, None], doc_ends[None, :], 0), axis=1)
    block_low = low.reshape(2, half)[:, 0] // half
    stored = jnp.sum(
        jnp.where(
            order_row[None, :] == jnp.arange(2 * group)[:, None], jnp.arange(2 * group)[None, :], 0
        ),
        axis=1,
    )
    owner = stored // 2
    slot = (member // 2 - owner // 2) % ring + ring * (owner % 2 != side).astype(jnp.int32)
    spots = slot * 2 + (stored % 2 != core).astype(jnp.int32)
    meta = jnp.concatenate([block_low, chosen, spots]).astype(jnp.int32)
    frequency = BASE ** (-(jnp.arange(HD // 2, dtype=F32) * 2.0) / HD)
    angles = pos.astype(F32)[:, None] * frequency[None, :]
    cosine = jnp.cos(angles)
    sine = jnp.sin(angles)
    cosine = jnp.concatenate([cosine, cosine], axis=1)
    sine = jnp.concatenate([-sine, sine], axis=1)
    pos_row = pos[None, :]
    low_row = low[None, :]

    turn_row = (wide_index // 2 - 1 - jnp.arange(turns, dtype=jnp.int32)) % turns
    tbl = jnp.stack([2 * turn_row + side, 2 * turn_row + 1 - side]).astype(jnp.int32)
    core_arr = core.astype(jnp.int32)[None]
    normed_one, both = norm_kv(core_arr, tokens, gain_attn[None, :], w_key, w_value, cosine, sine)
    near, far = [both], []
    low_rows, all_rows = slice(0, half), slice(0, rows)

    def together(*values):
        return list(lax.optimization_barrier(values))

    query = d_dense = d_inner = input_near = d_dense_strips = None
    for step in range(ring):
        held = near[step]
        group_out = [wide_swap(held)]
        if step + 1 < ring:
            group_out.append(wide_ring(held, group))
        if step == 0:
            query = query_proj(normed_one, w_query, cosine, sine)
            keep_rel = jnp.concatenate([own_half(keep_mask), other_half(keep_mask)])[:, None]
            cot_rel = jnp.concatenate([own_half(cotangent), other_half(cotangent)])
            d_dense = jnp.where(keep_rel > 0, cot_rel, jnp.zeros_like(cot_rel))
            group_out += [query, d_dense]
        if step == 1:
            d_inner = inner_grad(d_dense, w_down, 256)
            group_out += [d_inner]
        if step == 2:
            input_near, d_dense_strips = pack(
                [normed_one, d_dense],
                [[(0, low_rows, 1), (1, low_rows, 1)], [(1, all_rows, 0)]],
                tbl,
                strip,
            )
            group_out += [input_near, d_dense_strips]
        group_out = together(*group_out)
        far.append(group_out[0])
        if step + 1 < ring:
            near.append(group_out[1])
        if step == 0:
            query, d_dense = group_out[-2:]
        if step == 1:
            d_inner = group_out[-1]
        if step == 2:
            input_near, d_dense_strips = group_out[-2:]
    slots = near + far
    mixed, lse = attn_fwd(meta, query, pos_row, low_row, slots)

    def reduce_narrow(halves, hold=()):
        own_part, other_part = halves
        got = narrow_swap(other_part, 1)
        held = (own_part.astype(F32) + got.astype(F32)).astype(BF)
        return held, narrow_swap(held, 2)

    def total_of(held, got):
        return held.astype(F32) + got.astype(F32)

    input_near = wide_swap(after(input_near, far[-1], mixed))
    held, got = reduce_narrow(project([(mixed, w_out, 0)], "nn", 1024, 4))
    got, input_near = together(got, input_near)
    input_near_other = narrow_swap(input_near, 1)
    mixed_near = wide_swap(after(mixed, input_near))
    source = own_half(tokens).astype(F32)
    keep_own = own_half(keep_mask).astype(F32)[:, None]
    hidden_one = source + keep_own * total_of(held, got)
    gain_two = gain_dense.astype(F32)
    scale_two = lax.rsqrt(jnp.mean(hidden_one * hidden_one, axis=1, keepdims=True) + EPSILON)
    normed_two = (hidden_one * scale_two * gain_two).astype(BF)
    normed_two_other = narrow_swap(normed_two, 1)
    (normed_two_near,) = pack([normed_two], [[(0, low_rows, 1)]], tbl, strip)
    normed_two_near = wide_swap(after(normed_two_near, mixed_near))
    normed_two_near_other = narrow_swap(normed_two_near, 1)

    hidden = w_gate.shape[1]
    tile = 256
    first_count = 3 * tile
    inner_a, dgu_a = gated(
        normed_two, normed_two_other, w_gate, w_up, d_inner, 0, first_count, tile
    )
    inner_a_near = wide_swap(after(inner_a, normed_two_near))
    inner_b, dgu_b = gated(
        after(normed_two, inner_a),
        normed_two_other,
        w_gate,
        w_up,
        d_inner,
        first_count,
        hidden - first_count,
        tile,
    )
    back = back_dense(dgu_a, dgu_b, w_gate, w_up, 512)
    held, got = reduce_narrow(back)

    def ring_sum(parts, start=None):
        carried = parts[0] if start is None else after(parts[0], start)
        for k, part in enumerate(parts[1:]):
            carried = wide_ring(carried, wide)
            total = part.astype(F32) + carried.astype(F32)
            carried = total.astype(BF)
        return total

    d_dense_near = [input_near[:, turns * strip :], input_near_other[:, turns * strip :]]
    normed_one_near = [input_near[:, : turns * strip], input_near_other[:, : turns * strip]]
    down_a = strip_columns_grad(
        inner_a, inner_a_near, [d_dense_strips], d_dense_near, turns, strip, tile, 4
    )
    inner_b_near = wide_swap(after(inner_b, inner_a_near))
    grad_down_a = ring_sum(down_a)
    dgu_a_near = wide_swap(after(dgu_a, inner_b_near))
    down_b = strip_columns_grad(
        inner_b, inner_b_near, [d_dense_strips], d_dense_near, turns, strip, tile, 4
    )
    grad_down_b = ring_sum(down_b)

    upstream = own_half(cotangent).astype(F32)
    d_hidden = upstream + norm_backward(hidden_one, scale_two, gain_two, total_of(held, got))
    d_attn = (keep_own * d_hidden).astype(BF)
    d_attn_other = narrow_swap(d_attn, 1)

    d_mixed = mixed_grad(d_attn, d_attn_other, w_out)
    d_query, d_slots = attn_bwd(
        meta, query, pos_row, low_row, lse, mixed, d_mixed, cosine, sine, slots
    )
    dense_parts = project([(inner_a, w_down, 0), (inner_b, w_down, first_count)], "nn", 512, 6)
    held_out, got_out = reduce_narrow((dense_parts[0], after(dense_parts[1], d_mixed)))
    output_own = (hidden_one + keep_own * total_of(held_out, got_out)).astype(BF)
    output = ordered(output_own, narrow_swap(output_own, 1))

    carried = theirs = None
    for step in [*range(1, ring), 0]:
        sent = d_slots[ring + step]
        theirs = wide_swap(sent if theirs is None else after(sent, theirs))
        if step:
            piece = d_slots[step].astype(F32) + theirs.astype(F32)
            if carried is not None:
                piece = piece + carried.astype(F32)
            carried = wide_ring(piece.astype(BF), group)
    d_key, d_value = close_kv(d_slots[0], theirs, carried, cosine, sine)

    normed_two_sides = [normed_two_near, normed_two_near_other]
    gate_up_a = strip_rows_grad(
        [normed_two, normed_two_other], normed_two_sides, [dgu_a], [dgu_a_near], tbl, strip, 8
    )
    grad_gate_up_a = ring_sum(gate_up_a)
    d_query_near = wide_swap(d_query)
    dgu_b_near = wide_swap(after(dgu_b, dgu_a_near))
    gate_up_b = strip_rows_grad(
        [normed_two, normed_two_other], normed_two_sides, [dgu_b], [dgu_b_near], tbl, strip, 7
    )
    grad_gate_up_b = ring_sum(gate_up_b)
    d_attn_near, d_attn_strips, d_attn_other_strips = pack(
        [d_attn, d_attn_other],
        [[(0, low_rows, 1)], [(0, low_rows, 0)], [(1, low_rows, 0)]],
        tbl,
        strip,
    )
    d_attn_near = wide_swap(after(d_attn_near, dgu_b_near))
    d_attn_near_other = narrow_swap(d_attn_near, 1)
    grad_out = ring_sum(
        strip_columns_grad(
            mixed,
            mixed_near,
            [d_attn_strips, d_attn_other_strips],
            [d_attn_near, d_attn_near_other],
            turns,
            strip,
            tile,
            4,
        )
    )
    grad_query = ring_sum(
        strip_rows_grad([normed_one], normed_one_near, [d_query], [d_query_near], tbl, strip, 4)
    )

    kv_width = w_key.shape[1]
    held, got = reduce_narrow(
        project([(d_query, w_query, 0), (d_key, w_key, 0), (d_value, w_value, 0)], "nt", 512, 6)
    )
    gain_one = gain_attn.astype(F32)
    scale_one = lax.rsqrt(jnp.mean(source * source, axis=1, keepdims=True) + EPSILON)
    d_normed_one = total_of(held, got)
    grad_own = (d_hidden + norm_backward(source, scale_one, gain_one, d_normed_one)).astype(BF)
    grad_tokens = ordered(grad_own, narrow_swap(grad_own, 1))

    d_key_near = wide_swap(d_key)
    d_value_near = wide_swap(d_value)
    grad_kv = ring_sum(
        strip_rows_grad(
            [normed_one],
            normed_one_near,
            [d_key, d_value],
            [d_key_near, d_value_near],
            tbl,
            strip,
            4,
        )
    )
    grad_key, grad_value = grad_kv[:, :kv_width], grad_kv[:, kv_width:]
    grad_down = jnp.concatenate([grad_down_a, grad_down_b], axis=0)
    second_count = hidden - first_count
    grad_gate = jnp.concatenate(
        [grad_gate_up_a[:, :first_count], grad_gate_up_b[:, :second_count]], axis=1
    )
    grad_up = jnp.concatenate(
        [grad_gate_up_a[:, first_count:], grad_gate_up_b[:, second_count:]], axis=1
    )

    def strip_rows(weight):
        return lax.dynamic_slice_in_dim(weight, wide_index * strip, strip).astype(F32)

    def gain_grad(pairs, gain):
        local = sum(jnp.sum(strip_rows(w) * g, axis=1) for w, g in pairs)
        return local / lax.dynamic_slice_in_dim(gain, wide_index * strip, strip)

    local = jnp.stack(
        [
            gain_grad([(w_query, grad_query), (w_key, grad_key), (w_value, grad_value)], gain_one),
            gain_grad([(w_gate, grad_gate), (w_up, grad_up)], gain_two),
        ]
    )
    local = local + narrow_swap(local, 1)
    local = local + narrow_swap(local, 2)
    grad_gain_one, grad_gain_two = local[0], local[1]
    return (
        output,
        grad_tokens,
        grad_gain_one,
        grad_query,
        grad_key,
        grad_value,
        grad_out,
        grad_gain_two,
        grad_gate,
        grad_up,
        grad_down,
    )


def solution(mesh):
    placed = (
        P("wide", None),
        P("wide", None),
        P("wide"),
        P(),
        P(),
        P(),
        P(None, "narrow"),
        P(None, "narrow"),
        P(None, "narrow"),
        P("narrow", None),
        P(),
        P(None, "narrow"),
        P(None, "narrow"),
        P("narrow", None),
    )
    return jax.shard_map(
        shards,
        mesh=mesh,
        in_specs=placed,
        out_specs=(
            P("wide", None),
            P("wide", None),
            P("wide"),
            P("wide", "narrow"),
            P("wide", "narrow"),
            P("wide", "narrow"),
            P("narrow", "wide"),
            P("wide"),
            P("wide", "narrow"),
            P("wide", "narrow"),
            P("narrow", "wide"),
        ),
        check_vma=False,
    )
```

```python
import functools

import jax
import jax.numpy as jnp
from jax import lax
from jax.experimental import pallas as pl
from jax.experimental.pallas import tpu as pltpu
from jax.sharding import PartitionSpec as P

HD = 128
EPSILON = 1e-05
NEGATIVE = -1e30
BASE = 10000.0
LOG2E = 1.4426950408889634
SCORE = HD ** (-0.5) * LOG2E
FACTOR = HD ** (-0.5)
BF = jnp.bfloat16
F32 = jnp.float32
NT = (((1,), (1,)), ((), ()))
TN = (((0,), (0,)), ((), ()))
NN = (((1,), (0,)), ((), ()))
VM = pl.BlockSpec(memory_space=pltpu.VMEM)
SM = pl.BlockSpec(memory_space=pltpu.SMEM)
ANY = pl.BlockSpec(memory_space=pl.ANY)


def dot(a, b, dims=(((1,), (0,)), ((), ()))):
    return lax.dot_general(a, b, dims, preferred_element_type=F32)


def narrow_swap(value, mask):
    pairs = [(n, n ^ mask) for n in range(lax.axis_size("narrow"))]
    return lax.ppermute(value, "narrow", pairs)


def wide_swap(value):
    return lax.ppermute(value, "wide", [(w, w ^ 1) for w in range(lax.axis_size("wide"))])


def wide_ring(value, group, hop=1):
    ring = group // 2
    pairs = []
    for w in range(lax.axis_size("wide")):
        base, member = w // group * group, w % group
        pairs.append((w, base + (member // 2 + hop) % ring * 2 + member % 2))
    return lax.ppermute(value, "wide", pairs)


def rope(value, cosine, sine):
    return value * cosine + pltpu.roll(value, HD // 2, 1) * sine


def norm_kv_kernel(core, x_ref, gain_ref, wk_ref, wv_ref, cos_ref, sin_ref, normed_ref, *kv_refs):
    x = x_ref[...].astype(F32)
    scale = lax.rsqrt(jnp.mean(x * x, axis=1, keepdims=True) + EPSILON)
    normed = (x * scale * gain_ref[...].astype(F32)).astype(BF)
    normed_ref[...] = normed
    keys = dot(normed, wk_ref[...])
    values = dot(normed, wv_ref[...])
    for h, ref in enumerate(kv_refs):
        cols = slice(h * HD, (h + 1) * HD)
        ref[:, :HD] = rope(keys[:, cols], cos_ref[...], sin_ref[...]).astype(BF)
        ref[:, HD:] = values[:, cols].astype(BF)


def norm_kv(core, tokens, gain, wk, wv, cosine, sine):
    rows, width = tokens.shape
    half = rows // 2
    heads = wk.shape[1] // HD
    full = lambda w: pl.BlockSpec(w.shape, lambda i, c: (0, 0))
    outs = pl.pallas_call(
        norm_kv_kernel,
        out_shape=[jax.ShapeDtypeStruct((rows, width), BF)]
        + [jax.ShapeDtypeStruct((rows, 2 * HD), BF)] * heads,
        grid_spec=pltpu.PrefetchScalarGridSpec(
            num_scalar_prefetch=1,
            grid=(2,),
            in_specs=[
                pl.BlockSpec((half, width), lambda i, c: (i ^ c[0], 0)),
                full(gain),
                full(wk),
                full(wv),
                pl.BlockSpec((half, HD), lambda i, c: (i, 0)),
                pl.BlockSpec((half, HD), lambda i, c: (i, 0)),
            ],
            out_specs=[pl.BlockSpec((half, width), lambda i, c: (i, 0))]
            + [pl.BlockSpec((half, 2 * HD), lambda i, c: (i, 0))] * heads,
        ),
        cost_estimate=pl.CostEstimate(flops=int(2.9e9), bytes_accessed=0, transcendentals=0),
        name="norm_kv",
    )(core, tokens, gain, wk, wv, cosine, sine)
    return outs[0], outs[1:]


def query_kernel(x_ref, w_ref, cos_ref, sin_ref, out_ref):
    raw = dot(x_ref[...], w_ref[...])
    for h in range(raw.shape[1] // HD):
        cols = slice(h * HD, (h + 1) * HD)
        out_ref[:, cols] = rope(raw[:, cols], cos_ref[...], sin_ref[...]).astype(BF)


def query_proj(x, w, cosine, sine):
    rows, width = x.shape
    half = rows // 2
    return pl.pallas_call(
        query_kernel,
        out_shape=jax.ShapeDtypeStruct((rows, w.shape[1]), BF),
        grid=(2,),
        in_specs=[
            pl.BlockSpec((half, width), lambda i: (i, 0)),
            pl.BlockSpec(w.shape, lambda i: (0, 0)),
            pl.BlockSpec((half, HD), lambda i: (i, 0)),
            pl.BlockSpec((half, HD), lambda i: (i, 0)),
        ],
        out_specs=pl.BlockSpec((half, w.shape[1]), lambda i: (i, 0)),
        cost_estimate=pl.CostEstimate(flops=int(2.9e9), bytes_accessed=0, transcendentals=0),
        name="query_proj",
    )(x, w, cosine, sine)


def fetch_slots(slot_refs, slots, kv_ref, sems):
    rows, width = slot_refs[0].shape
    copies = []
    for at, ref in enumerate(slot_refs):
        head, slot = divmod(at, slots)
        spot = kv_ref.at[pl.ds(slot * rows, rows), pl.ds(head * width, width)]
        copies.append(pltpu.make_async_copy(ref, spot, sems.at[at]))
    for copy in copies:
        copy.start()
    for copy in copies:
        copy.wait()


def allowed(pk, size, span, pos, low):
    key_pos = pk * size + lax.broadcasted_iota(jnp.int32, (size, span), 0)
    return (key_pos <= pos) & (key_pos >= low)


def attn_fwd_kernel(slots, *refs):
    meta, q_ref, pos_ref, low_ref = refs[:4]
    slot_refs = refs[4 : 4 + slots]
    mixed_ref, lse_ref, kv_ref, acc_ref, sems = refs[-5:]
    fetch_slots(slot_refs, slots, kv_ref, sems)
    size = q_ref.shape[0] // 2
    for i in range(2):
        rows = slice(i * size, (i + 1) * size)
        pos = jnp.tile(pos_ref[0:1, rows], (1, 2))
        low = jnp.tile(low_ref[0:1, rows], (1, 2))
        queries = [q_ref[rows, r * HD : (r + 1) * HD] for r in range(2)]
        acc_ref[...] = jnp.zeros_like(acc_ref)

        def body(pk, carry):
            peak, total = carry
            spot = pl.multiple_of(meta[4 + pk] * size, size)
            keys = kv_ref[pl.ds(spot, size), :HD]
            values = kv_ref[pl.ds(spot, size), HD:]
            scores = jnp.concatenate([dot(keys, q, NT) for q in queries], axis=1) * SCORE
            scores = jnp.where(allowed(pk, size, 2 * size, pos, low), scores, NEGATIVE)
            peak_new = jnp.maximum(peak, jnp.max(scores, axis=0, keepdims=True))
            alpha = jnp.exp2(peak - peak_new)
            probs = jnp.exp2(scores - peak_new)
            total = total * alpha + jnp.sum(probs, axis=0, keepdims=True)
            acc_ref[...] = acc_ref[...] * alpha + dot(values, probs.astype(BF), TN)
            return peak_new, total

        start = (jnp.full((1, 2 * size), NEGATIVE, F32), jnp.zeros((1, 2 * size), F32))
        peak, total = lax.fori_loop(meta[i], meta[2 + i] + 1, body, start)
        lse_ref[i : i + 1, :] = peak + jnp.log2(total)
        out = acc_ref[...] * (1.0 / total)
        for r in range(2):
            mixed_ref[rows, r * HD : (r + 1) * HD] = out[:, r * size : (r + 1) * size].T.astype(BF)


def attn_fwd(head, meta, q, pos, low, slots, mixed):
    rows = q.shape[0]
    count = len(slots)
    earlier = [] if mixed is None else [mixed]
    return pl.pallas_call(
        functools.partial(attn_fwd_kernel, count),
        out_shape=(
            jax.ShapeDtypeStruct(q.shape, BF),
            jax.ShapeDtypeStruct((2, rows), F32),
        ),
        grid=(1,),
        in_specs=[
            SM,
            pl.BlockSpec((rows, 2 * HD), lambda i: (0, head)),
            pl.BlockSpec(pos.shape, lambda i: (0, 0)),
            pl.BlockSpec(low.shape, lambda i: (0, 0)),
        ]
        + [ANY] * (count + len(earlier)),
        out_specs=[
            pl.BlockSpec((rows, 2 * HD), lambda i: (0, head)),
            pl.BlockSpec((2, rows), lambda i: (0, 0)),
        ],
        input_output_aliases={4 + count: 0} if earlier else {},
        scratch_shapes=[
            pltpu.VMEM((count * rows, 2 * HD), BF),
            pltpu.VMEM((HD, rows), F32),
            pltpu.SemaphoreType.DMA((count,)),
        ],
        cost_estimate=pl.CostEstimate(flops=int(2.9e9), bytes_accessed=0, transcendentals=0),
        name="attn_fwd",
    )(meta, q, pos, low, *slots, *earlier)


def attn_bwd_kernel(heads, slots, *refs):
    meta, q_ref, pos_ref, low_ref, dmix_ref, mixed_ref, cos_ref, sin_ref = refs[:8]
    lse_refs = refs[8 : 8 + heads]
    at = 8 + heads
    slot_refs = refs[at : at + heads * slots]
    at += heads * slots
    dq_ref, dkv_refs = refs[at], refs[at + 1 : at + 1 + slots]
    kv_ref, dkv_ref, dq_acc, sems = refs[at + 1 + slots :]
    fetch_slots(slot_refs, slots, kv_ref, sems)
    dkv_ref[...] = jnp.zeros_like(dkv_ref)
    rows_all = q_ref.shape[0]
    size = rows_all // 2
    for i in range(2):
        rows = slice(i * size, (i + 1) * size)
        pos = jnp.tile(pos_ref[0:1, rows], (1, 2))
        low = jnp.tile(low_ref[0:1, rows], (1, 2))
        for g in range(heads):
            cols = [slice((2 * g + r) * HD, (2 * g + r + 1) * HD) for r in range(2)]
            queries = jnp.concatenate([q_ref[rows, c] for c in cols], axis=0)
            grads = jnp.concatenate([dmix_ref[rows, c] for c in cols], axis=0)
            outs = jnp.concatenate([mixed_ref[rows, c] for c in cols], axis=0)
            delta = jnp.sum((grads.astype(F32) * outs.astype(F32)).T, axis=0, keepdims=True)
            lse = lse_refs[g][i : i + 1, :]
            dq_acc[...] = jnp.zeros_like(dq_acc)

            def body(pk, carry):
                spot = pl.multiple_of(meta[4 + pk] * size, size)
                key_cols = slice(2 * g * HD, (2 * g + 1) * HD)
                value_cols = slice((2 * g + 1) * HD, (2 * g + 2) * HD)
                keys = kv_ref[pl.ds(spot, size), key_cols]
                values = kv_ref[pl.ds(spot, size), value_cols]
                scores = dot(keys, queries, NT) * SCORE
                probs = jnp.where(
                    allowed(pk, size, 2 * size, pos, low), jnp.exp2(scores - lse), 0.0
                )
                d_probs = dot(values, grads, NT)
                d_scores = (probs * (d_probs - delta)).astype(BF)
                dkv_ref[pl.ds(spot, size), value_cols] += dot(probs.astype(BF), grads)
                dkv_ref[pl.ds(spot, size), key_cols] += dot(d_scores, queries) * FACTOR
                dq_acc[...] += dot(d_scores, keys, TN)
                return carry

            lax.fori_loop(meta[i], meta[2 + i] + 1, body, 0)
            for r in range(2):
                part = dq_acc[r * size : (r + 1) * size, :] * FACTOR
                dq_ref[rows, cols[r]] = rope(part, cos_ref[rows, :], -sin_ref[rows, :]).astype(BF)
    for j, ref in enumerate(dkv_refs):
        ref[...] = dkv_ref[j * rows_all : (j + 1) * rows_all, :].astype(BF)


def attn_bwd(meta, q, pos, low, lse, mixed, dmix, cosine, sine, slots):
    rows, q_width = q.shape
    heads, count = len(slots), len(slots[0])
    kv_width = heads * 2 * HD
    outs = pl.pallas_call(
        functools.partial(attn_bwd_kernel, heads, count),
        out_shape=[jax.ShapeDtypeStruct((rows, q_width), BF)]
        + [jax.ShapeDtypeStruct((rows, kv_width), BF)] * count,
        in_specs=[SM] + [VM] * (7 + heads) + [ANY] * (heads * count),
        out_specs=[VM] * (1 + count),
        scratch_shapes=[
            pltpu.VMEM((count * rows, kv_width), BF),
            pltpu.VMEM((count * rows, kv_width), F32),
            pltpu.VMEM((rows, HD), F32),
            pltpu.SemaphoreType.DMA((heads * count,)),
        ],
        cost_estimate=pl.CostEstimate(flops=int(2e9), bytes_accessed=0, transcendentals=0),
        name="attn_bwd",
    )(meta, q, pos, low, dmix, mixed, cosine, sine, *lse, *[v for head in slots for v in head])
    return outs[0], outs[1:]


def cost(micros):
    return pl.CostEstimate(flops=int(micros * 0.3e9), bytes_accessed=0, transcendentals=0)


def split_rows(total, own_ref, other_ref):
    half = own_ref.shape[0]
    own_ref[...] = total[:half].astype(BF)
    other_ref[...] = total[half:].astype(BF)


def project_kernel(spec, *refs):
    total = None
    for a, b, offset, dims in spec:
        left = refs[a][...] if dims is not None else None
        if dims == "nt":
            right, form = refs[b][:, offset : offset + left.shape[1]], NT
        else:
            right, form = refs[b][offset : offset + left.shape[1], :], NN
        term = dot(left, right, form)
        total = term if total is None else total + term
    split_rows(total, refs[-2], refs[-1])


def project(pairs, dims, tile, micros):
    operands, specs, plan, weights = [], [], [], []
    for a, b, offset in pairs:
        operands.append(a)
        specs.append(pl.BlockSpec(a.shape, lambda i: (0, 0)))
        spot = next((at for at, seen in weights if seen is b), None)
        left = len(operands) - 1
        if spot is None:
            spot = len(operands)
            operands.append(b)
            weights.append((spot, b))
            if dims == "nt":
                specs.append(pl.BlockSpec((tile, b.shape[1]), lambda i: (i, 0)))
            else:
                specs.append(pl.BlockSpec((b.shape[0], tile), lambda i: (0, i)))
        plan.append((left, spot, offset, dims))
    rows = pairs[0][0].shape[0]
    width = pairs[0][1].shape[0 if dims == "nt" else 1]
    return pl.pallas_call(
        functools.partial(project_kernel, plan),
        out_shape=[jax.ShapeDtypeStruct((rows // 2, width), BF)] * 2,
        grid=(width // tile,),
        in_specs=specs,
        out_specs=[pl.BlockSpec((rows // 2, tile), lambda i: (0, i))] * 2,
        cost_estimate=cost(micros),
        name="project",
    )(*operands)


def back_dense_kernel(gate_a, up_a, gate_b, up_b, wg_ref, wu_ref, own_ref, other_ref):
    total = None
    offset = 0
    for group in ((gate_a, up_a), (gate_b, up_b)):
        count = group[0].shape[1]
        for ref, w_ref in zip(group, (wg_ref, wu_ref)):
            term = dot(ref[...], w_ref[:, offset : offset + count], NT)
            total = term if total is None else total + term
        offset += count
    split_rows(total, own_ref, other_ref)


def back_dense(grads, w_gate, w_up, tile, part, parts):
    width, hidden = w_gate.shape[0] // parts, w_gate.shape[1]
    rows = grads[0].shape[0]
    ahead = part * (width // tile)
    weight = pl.BlockSpec((tile, hidden), lambda i: (ahead + i, 0))
    return pl.pallas_call(
        back_dense_kernel,
        out_shape=[jax.ShapeDtypeStruct((rows // 2, width), BF)] * 2,
        grid=(width // tile,),
        in_specs=[pl.BlockSpec(v.shape, lambda i: (0, 0)) for v in grads] + [weight, weight],
        out_specs=[pl.BlockSpec((rows // 2, tile), lambda i: (0, i))] * 2,
        cost_estimate=cost(11 / parts),
        name="back_dense",
    )(*grads, w_gate, w_up)


def gated_kernel(own_ref, other_ref, wg_ref, wu_ref, di_ref, inner_ref, dg_ref, du_ref, all_ref):
    @pl.when(pl.program_id(0) == 0)
    def _():
        half = own_ref.shape[0]
        all_ref[:half, :] = own_ref[...]
        all_ref[half:, :] = other_ref[...]

    gate = dot(all_ref[...], wg_ref[...])
    up = dot(all_ref[...], wu_ref[...])
    sigma = 1.0 / (1.0 + jnp.exp(-gate))
    silu = gate * sigma
    d_inner = di_ref[...]
    inner_ref[...] = (silu * up).astype(BF)
    dg_ref[...] = (d_inner * up * sigma * (1.0 + gate * (1.0 - sigma))).astype(BF)
    du_ref[...] = (d_inner * silu).astype(BF)


def gated(own, other, wg, wu, d_inner, first, columns, tile):
    half, width = own.shape
    weight = pl.BlockSpec((width, tile), lambda i: (0, first // tile + i))
    whole = pl.BlockSpec((half, width), lambda i: (0, 0))
    return pl.pallas_call(
        gated_kernel,
        out_shape=[jax.ShapeDtypeStruct((2 * half, columns), BF)] * 3,
        grid=(pl.cdiv(columns, tile),),
        in_specs=[
            whole,
            whole,
            weight,
            weight,
            pl.BlockSpec((2 * half, tile), lambda i: (0, first // tile + i)),
        ],
        out_specs=[pl.BlockSpec((2 * half, tile), lambda i: (0, i))] * 3,
        scratch_shapes=[pltpu.VMEM((2 * half, width), BF)],
        cost_estimate=cost(7.5),
        name="gated",
    )(own, other, wg, wu, d_inner)


def mixed_grad_kernel(own_ref, other_ref, w_ref, out_ref):
    both = jnp.concatenate([own_ref[...], other_ref[...]], axis=0)
    out_ref[...] = dot(both, w_ref[...], NT).astype(BF)


def mixed_grad(own, other, w):
    return pl.pallas_call(
        mixed_grad_kernel,
        out_shape=jax.ShapeDtypeStruct((2 * own.shape[0], w.shape[0]), BF),
        in_specs=[VM] * 3,
        out_specs=VM,
        cost_estimate=cost(4),
        name="mixed_grad",
    )(own, other, w)


def d_inner_kernel(x_ref, w_ref, out_ref):
    out_ref[...] = dot(x_ref[...], w_ref[...], NT)


def inner_grad(x, w, tile):
    rows, width = x.shape
    hidden = w.shape[0]
    return pl.pallas_call(
        d_inner_kernel,
        out_shape=jax.ShapeDtypeStruct((rows, hidden), F32),
        grid=(pl.cdiv(hidden, tile),),
        in_specs=[
            pl.BlockSpec((rows, width), lambda i: (0, 0)),
            pl.BlockSpec((tile, width), lambda i: (i, 0)),
        ],
        out_specs=pl.BlockSpec((rows, tile), lambda i: (0, i)),
        cost_estimate=cost(8),
        name="inner_grad",
    )(x, w)


def pack_kernel(count, plan, strip, tbl, *refs):
    ins, outs = refs[:count], refs[count:]
    for out_ref, pieces in zip(outs, plan):
        column = 0
        for at, rows, row in pieces:
            for k in range(tbl.shape[1]):
                first = pl.multiple_of(tbl[row, k] * strip, 128)
                out_ref[:, column : column + strip] = ins[at][rows, pl.ds(first, strip)]
                column += strip


def pack(values, plan, tbl, strip):
    turns = tbl.shape[1]
    if strip % 128:
        cut = lambda v, rows, at: lax.dynamic_slice_in_dim(v[rows], at * strip, strip, axis=1)
        return [
            jnp.concatenate(
                [cut(values[at], rows, tbl[row, k]) for at, rows, row in pieces for k in range(turns)],
                axis=1,
            )
            for pieces in plan
        ]
    return pl.pallas_call(
        functools.partial(pack_kernel, len(values), plan, strip),
        out_shape=[
            jax.ShapeDtypeStruct(
                (p[0][1].stop - p[0][1].start, len(p) * turns * strip), values[0].dtype
            )
            for p in plan
        ],
        in_specs=[SM] + [VM] * len(values),
        out_specs=[VM] * len(plan),
        cost_estimate=cost(1.5),
        name="pack",
    )(tbl, *values)


def strip_rows_kernel(halves, near, rights, nears, tbl, *refs):
    left = refs[:halves]
    left_near = refs[halves : halves + near]
    right = refs[halves + near : halves + near + rights]
    right_near = refs[halves + near + rights : halves + near + rights + nears]
    outs = refs[halves + near + rights + nears :]
    step = pl.program_id(0)
    join = lambda group: (
        group[0][...] if len(group) == 1 else jnp.concatenate([r[...] for r in group], axis=0)
    )
    mine, theirs = join(left), join(left_near)
    pieces = []
    for r, n in zip(right, right_near):
        planes = range(r.shape[0]) if len(r.shape) == 3 else [None]
        for k in planes:
            a = r[...] if k is None else r[k]
            b = n[...] if k is None else n[k]
            pieces.append((dot(mine, a, TN) + dot(theirs, b, TN)).astype(BF))
    for k, out in enumerate(outs):

        @pl.when(step == k)
        def _():
            column = 0
            for piece in pieces:
                out[:, column : column + piece.shape[1]] = piece
                column += piece.shape[1]


def strip_rows_grad(left, left_near, right, right_near, tbl, strip, micros):
    turns = tbl.shape[1]
    columns = sum(r.shape[-1] * (r.shape[0] if r.ndim == 3 else 1) for r in right)
    if strip % 128:
        near = jnp.concatenate(left_near, axis=0)
        mine = jnp.concatenate(left, axis=0)
        flat = lambda r: [r] if r.ndim == 2 else [r[k] for k in range(r.shape[0])]
        outs = []
        for k in range(turns):
            a = lax.dynamic_slice_in_dim(mine, tbl[0, k] * strip, strip, axis=1)
            b = near[:, k * strip : (k + 1) * strip]
            outs.append(
                jnp.concatenate(
                    [
                        dot(a, x, TN) + dot(b, y, TN)
                        for r, n in zip(right, right_near)
                        for x, y in zip(flat(r), flat(n))
                    ],
                    axis=1,
                ).astype(BF)
            )
        return outs
    whole = lambda v: pl.BlockSpec(v.shape, lambda i, t: (0,) * v.ndim)
    return pl.pallas_call(
        functools.partial(
            strip_rows_kernel, len(left), len(left_near), len(right), len(right_near)
        ),
        out_shape=[jax.ShapeDtypeStruct((strip, columns), BF)] * turns,
        grid_spec=pltpu.PrefetchScalarGridSpec(
            num_scalar_prefetch=1,
            grid=(turns,),
            in_specs=[pl.BlockSpec((v.shape[0], strip), lambda i, t: (0, t[0, i])) for v in left]
            + [pl.BlockSpec((v.shape[0], strip), lambda i, t: (0, i)) for v in left_near]
            + [whole(v) for v in [*right, *right_near]],
            out_specs=[pl.BlockSpec((strip, columns), lambda i, t: (0, 0))] * turns,
        ),
        cost_estimate=cost(micros),
        name="strip_rows",
    )(tbl, *left, *left_near, *right, *right_near)


def strip_columns_kernel(parts, halves, near, strip, *refs):
    at = 2 * parts
    right, right_near = refs[at : at + halves], refs[at + halves : at + halves + near]
    outs = refs[at + halves + near :]
    first = 0
    for p in range(parts):
        total = None
        for ref, group in ((refs[p], right), (refs[parts + p], right_near)):
            row = 0
            for r in group:
                term = dot(ref[row : row + r.shape[0], :], r[...], TN)
                total = term if total is None else total + term
                row += r.shape[0]
        for k, out in enumerate(outs):
            out[first : first + total.shape[0], :] = total[:, k * strip : (k + 1) * strip].astype(BF)
        first += total.shape[0]


def strip_columns_grad(left, left_near, right, right_near, turns, strip, tile, micros, near_at=0):
    rows, count = left[0].shape[0], sum(v.shape[1] for v in left)
    if strip * turns % 128:
        raise ValueError(strip)
    whole = lambda v: pl.BlockSpec(v.shape, lambda i: (0, 0))
    near = lambda v: pl.BlockSpec((v.shape[0], turns * strip), lambda i: (0, near_at))
    if len(left) == 1:
        left_specs = [pl.BlockSpec((rows, tile), lambda i: (0, i))] * 2
    else:
        tile = count
        left_specs = [whole(v) for v in [*left, *left_near]]
    return pl.pallas_call(
        functools.partial(strip_columns_kernel, len(left), len(right), len(right_near), strip),
        out_shape=[jax.ShapeDtypeStruct((count, strip), BF)] * turns,
        grid=(pl.cdiv(count, tile),),
        in_specs=left_specs + [whole(v) for v in right] + [near(v) for v in right_near],
        out_specs=[pl.BlockSpec((tile, strip), lambda i: (i, 0))] * turns,
        cost_estimate=cost(micros),
        name="strip_columns",
    )(*left, *left_near, *right, *right_near)


def close_kv_kernel(a_ref, b_ref, c_ref, cos_ref, sin_ref, dk_ref, dv_ref):
    total = a_ref[...].astype(F32) + b_ref[...].astype(F32) + c_ref[...].astype(F32)
    for h in range(dk_ref.shape[1] // HD):
        cols = slice(h * HD, (h + 1) * HD)
        keys = total[:, 2 * h * HD : (2 * h + 1) * HD]
        dk_ref[:, cols] = rope(keys, cos_ref[...], -sin_ref[...]).astype(BF)
        dv_ref[:, cols] = total[:, (2 * h + 1) * HD : (2 * h + 2) * HD].astype(BF)


def close_kv(a, b, c, cosine, sine):
    rows, width = a.shape
    return pl.pallas_call(
        close_kv_kernel,
        out_shape=[jax.ShapeDtypeStruct((rows, width // 2), BF)] * 2,
        in_specs=[VM] * 5,
        out_specs=[VM] * 2,
        cost_estimate=cost(1.5),
        name="close_kv",
    )(a, b, c, cosine, sine)


def norm_backward(source, scale_rows, gain, upstream):
    weighted = upstream * gain
    average = jnp.mean(weighted * source, axis=1, keepdims=True)
    return scale_rows * weighted - source * scale_rows**3 * average


def after(value, *done):
    return lax.optimization_barrier((value, *done))[0]


def shards(
    tokens,
    cotangent,
    keep_mask,
    doc_lengths,
    block_order,
    gain_attn,
    w_query,
    w_key,
    w_value,
    w_out,
    gain_dense,
    w_gate,
    w_up,
    w_down,
):
    rows, width = tokens.shape
    half = rows // 2
    wide = lax.axis_size("wide")
    group = wide // block_order.shape[0]
    ring = group // 2
    wide_index = lax.axis_index("wide")
    member = wide_index % group
    seq_index = wide_index // group
    side = (wide_index % 2).astype(jnp.int32)
    core = lax.axis_index("narrow") % 2
    strip = width // wide
    turns = wide // 2

    def ordered(mine, other):
        return jnp.where(
            core == 0,
            jnp.concatenate([mine, other], axis=0),
            jnp.concatenate([other, mine], axis=0),
        )

    def own_half(value):
        return lax.dynamic_slice_in_dim(value, core * half, half)

    def other_half(value):
        return lax.dynamic_slice_in_dim(value, (1 - core) * half, half)

    order_row = lax.dynamic_index_in_dim(block_order, seq_index, 0, keepdims=False)
    length_row = lax.dynamic_index_in_dim(doc_lengths, seq_index, 0, keepdims=False)
    doc_ends = jnp.cumsum(length_row)
    places = jnp.stack([member * 2 + core, member * 2 + 1 - core])
    chosen = jnp.sum(
        jnp.where(places[:, None] == jnp.arange(2 * group)[None, :], order_row[None, :], 0), axis=1
    )
    pos = (chosen[:, None] * half + jnp.arange(half, dtype=jnp.int32)[None, :]).reshape(-1)
    low = jnp.max(jnp.where(doc_ends[None, :] <= pos[:, None], doc_ends[None, :], 0), axis=1)
    block_low = low.reshape(2, half)[:, 0] // half
    stored = jnp.sum(
        jnp.where(
            order_row[None, :] == jnp.arange(2 * group)[:, None], jnp.arange(2 * group)[None, :], 0
        ),
        axis=1,
    )
    owner = stored // 2
    slot = (member // 2 - owner // 2) % ring + ring * (owner % 2 != side).astype(jnp.int32)
    spots = slot * 2 + (stored % 2 != core).astype(jnp.int32)
    meta = jnp.concatenate([block_low, chosen, spots]).astype(jnp.int32)
    frequency = BASE ** (-(jnp.arange(HD // 2, dtype=F32) * 2.0) / HD)
    angles = pos.astype(F32)[:, None] * frequency[None, :]
    cosine = jnp.cos(angles)
    sine = jnp.sin(angles)
    cosine = jnp.concatenate([cosine, cosine], axis=1)
    sine = jnp.concatenate([-sine, sine], axis=1)
    pos_row = pos[None, :]
    low_row = low[None, :]

    turn_row = (wide_index // 2 - 1 - jnp.arange(turns, dtype=jnp.int32)) % turns
    tbl = jnp.stack([2 * turn_row + side, 2 * turn_row + 1 - side]).astype(jnp.int32)
    core_arr = core.astype(jnp.int32)[None]
    normed_one, both = norm_kv(core_arr, tokens, gain_attn[None, :], w_key, w_value, cosine, sine)
    low_rows, all_rows = slice(0, half), slice(0, rows)

    def together(*values):
        return list(lax.optimization_barrier(values))

    near, far = [[v] for v in both], [[] for v in both]
    query = d_dense = d_inner = input_near = d_dense_strips = None
    for step in range(ring):
        for head in range(len(both)):
            held = near[head][step]
            if step + 1 < ring:
                sent = [wide_swap(held), wide_ring(held, group)]
            elif head == 0:
                sent = [wide_swap(held)]
            else:
                sent = [wide_ring(far[head][0], group, -1)]
            beside = []
            if step == 0 and head == 0:
                beside = [query_proj(normed_one, w_query, cosine, sine)]
            if step == 0 and head == 1:
                keep_rel = jnp.concatenate([own_half(keep_mask), other_half(keep_mask)])[:, None]
                cot_rel = jnp.concatenate([own_half(cotangent), other_half(cotangent)])
                beside = [jnp.where(keep_rel > 0, cot_rel, jnp.zeros_like(cot_rel))]
            if step == 1 and head == 0:
                beside = [inner_grad(d_dense, w_down, 256)]
            if step == 2 and head == 0:
                beside = pack(
                    [normed_one, d_dense],
                    [[(0, low_rows, 1), (1, low_rows, 1)], [(1, all_rows, 0)]],
                    tbl,
                    strip,
                )
            done = together(*sent, *beside)
            far[head].append(done[0])
            if step + 1 < ring:
                near[head].append(done[1])
            if step == 0 and head == 0:
                query = done[-1]
            if step == 0 and head == 1:
                d_dense = done[-1]
            if step == 1 and head == 0:
                d_inner = done[-1]
            if step == 2 and head == 0:
                input_near, d_dense_strips = done[-2:]
    slots = [n + f for n, f in zip(near, far)]
    input_near = wide_swap(after(input_near, far[0][-2]))
    mixed, lse = None, []
    for h, held in enumerate(slots):
        mixed, part = attn_fwd(h, meta, query, pos_row, low_row, held, mixed)
        lse.append(part)

    def reduce_narrow(halves, hold=()):
        own_part, other_part = halves
        got = narrow_swap(other_part, 1)
        held = (own_part.astype(F32) + got.astype(F32)).astype(BF)
        return held, narrow_swap(held, 2)

    def total_of(held, got):
        return held.astype(F32) + got.astype(F32)

    held, got = reduce_narrow(project([(mixed, w_out, 0)], "nn", 1024, 4))
    mixed_near = wide_swap(mixed)
    got, input_near, mixed_near = together(got, input_near, mixed_near)
    input_near_other = narrow_swap(input_near, 1)
    source = own_half(tokens).astype(F32)
    keep_own = own_half(keep_mask).astype(F32)[:, None]
    hidden_one = source + keep_own * total_of(held, got)
    gain_two = gain_dense.astype(F32)
    scale_two = lax.rsqrt(jnp.mean(hidden_one * hidden_one, axis=1, keepdims=True) + EPSILON)
    normed_two = (hidden_one * scale_two * gain_two).astype(BF)
    normed_two_other = narrow_swap(normed_two, 1)
    (normed_two_near,) = pack([normed_two], [[(0, low_rows, 1)]], tbl, strip)
    normed_two_near = wide_swap(normed_two_near)

    hidden = w_gate.shape[1]
    tile = 256
    first_count = 3 * tile
    inner_a, *dgu_a = gated(
        normed_two, normed_two_other, w_gate, w_up, d_inner, 0, first_count, tile
    )
    inner_a_near = wide_swap(inner_a)
    inner_b, *dgu_b = gated(
        after(normed_two, inner_a, normed_two_near),
        normed_two_other,
        w_gate,
        w_up,
        d_inner,
        first_count,
        hidden - first_count,
        tile,
    )
    first_half = back_dense([*dgu_a, *dgu_b], w_gate, w_up, 512, 0, 2)
    second_half = back_dense(
        [*dgu_a, dgu_b[0], after(dgu_b[1], *first_half)], w_gate, w_up, 512, 1, 2
    )
    held_one, got_one = reduce_narrow(first_half)
    held, got = reduce_narrow((second_half[0], after(second_half[1], held_one, inner_a_near)))

    def ring_sum(parts, first=None):
        carried = parts[0]
        for k, part in enumerate(parts[1:]):
            carried = first if k == 0 and first is not None else wide_ring(carried, wide)
            total = part.astype(F32) + carried.astype(F32)
            carried = total.astype(BF)
        return total

    near_sides = [input_near, input_near_other]
    down_a = strip_columns_grad(
        [after(inner_a, held)],
        [inner_a_near],
        [d_dense_strips],
        near_sides,
        turns,
        strip,
        tile,
        4,
        1,
    )
    inner_b_near = wide_swap(inner_b)
    normed_two_near_other = narrow_swap(after(normed_two_near, held), 1)
    dgu_a_near = [wide_swap(after(v, inner_b)) for v in dgu_a]
    dense_parts = project(
        [(after(inner_a, down_a[0]), w_down, 0), (inner_b, w_down, first_count)], "nn", 512, 6
    )
    first_down_a = wide_ring(down_a[0], wide)
    down_b = strip_columns_grad(
        [after(inner_b, dense_parts[0], first_down_a)], [inner_b_near], [d_dense_strips], near_sides, turns, strip, tile, 4, 1
    )

    got = after(got, dense_parts[0], down_b[0], got_one)
    grad_down_a = ring_sum(down_a, first_down_a)
    grad_down_b = ring_sum(down_b, after(wide_ring(down_b[0], wide), got))
    upstream = own_half(cotangent).astype(F32)
    d_normed_two = jnp.concatenate([total_of(held_one, got_one), total_of(held, got)], axis=1)
    d_hidden = upstream + norm_backward(hidden_one, scale_two, gain_two, d_normed_two)
    d_attn = (keep_own * d_hidden).astype(BF)
    d_attn_other = narrow_swap(after(d_attn, dgu_a_near[0]), 1)

    d_mixed = mixed_grad(d_attn, d_attn_other, w_out)
    d_query, d_slots = attn_bwd(
        meta, query, pos_row, low_row, lse, mixed, d_mixed, cosine, sine, slots
    )
    held_out, got_out = reduce_narrow((dense_parts[0], after(dense_parts[1], d_mixed)))
    output_own = (hidden_one + keep_own * total_of(held_out, got_out)).astype(BF)
    output = ordered(output_own, narrow_swap(output_own, 1))

    carried = theirs = first_piece = None
    for step in [*range(1, ring), 0]:
        sent = d_slots[ring + step]
        theirs = wide_swap(sent)
        if step:
            piece = d_slots[step].astype(F32) + theirs.astype(F32)
            if carried is not None:
                piece = piece + carried.astype(F32)
            piece = piece.astype(BF)
            if first_piece is None:
                first_piece = piece
            carried = wide_ring(piece, group)
    d_key, d_value = close_kv(d_slots[0], theirs, carried, cosine, sine)

    normed_two_sides = [normed_two_near, normed_two_near_other]
    gate_up_a = strip_rows_grad(
        [after(normed_two, d_query), normed_two_other], normed_two_sides, dgu_a, dgu_a_near, tbl, strip, 8
    )
    grad_gate_up_a = ring_sum(gate_up_a)
    d_query_near = wide_swap(after(d_query, gate_up_a[0], first_piece))
    dgu_b_near = [wide_swap(after(v, d_query)) for v in dgu_b]
    gate_up_b = strip_rows_grad(
        [normed_two, normed_two_other], normed_two_sides, dgu_b, dgu_b_near, tbl, strip, 7
    )
    grad_gate_up_b = ring_sum(gate_up_b)
    d_attn_near, d_attn_strips, d_attn_other_strips = pack(
        [d_attn, d_attn_other],
        [[(0, low_rows, 1)], [(0, low_rows, 0)], [(1, low_rows, 0)]],
        tbl,
        strip,
    )
    d_attn_near = wide_swap(d_attn_near)
    d_attn_near_other = narrow_swap(d_attn_near, 1)
    grad_out = ring_sum(
        strip_columns_grad(
            [mixed],
            [mixed_near],
            [d_attn_strips, d_attn_other_strips],
            [d_attn_near, d_attn_near_other],
            turns,
            strip,
            tile,
            4,
        )
    )
    grad_query = ring_sum(
        strip_rows_grad([normed_one], near_sides, [d_query], [d_query_near], tbl, strip, 4)
    )

    kv_width = w_key.shape[1]
    held, got = reduce_narrow(
        project([(d_query, w_query, 0), (d_key, w_key, 0), (d_value, w_value, 0)], "nt", 512, 6)
    )
    gain_one = gain_attn.astype(F32)
    scale_one = lax.rsqrt(jnp.mean(source * source, axis=1, keepdims=True) + EPSILON)
    d_normed_one = total_of(held, got)
    grad_own = (d_hidden + norm_backward(source, scale_one, gain_one, d_normed_one)).astype(BF)
    grad_tokens = ordered(grad_own, narrow_swap(grad_own, 1))

    d_key_near = wide_swap(d_key)
    d_value_near = wide_swap(d_value)
    grad_kv = ring_sum(
        strip_rows_grad(
            [normed_one],
            near_sides,
            [d_key, d_value],
            [d_key_near, d_value_near],
            tbl,
            strip,
            4,
        )
    )
    grad_key, grad_value = grad_kv[:, :kv_width], grad_kv[:, kv_width:]
    grad_down = jnp.concatenate([grad_down_a, grad_down_b], axis=0)
    second_count = hidden - first_count
    grad_gate = jnp.concatenate(
        [grad_gate_up_a[:, :first_count], grad_gate_up_b[:, :second_count]], axis=1
    )
    grad_up = jnp.concatenate(
        [grad_gate_up_a[:, first_count:], grad_gate_up_b[:, second_count:]], axis=1
    )

    def strip_rows(weight):
        return lax.dynamic_slice_in_dim(weight, wide_index * strip, strip).astype(F32)

    def gain_grad(pairs, gain):
        local = sum(jnp.sum(strip_rows(w) * g, axis=1) for w, g in pairs)
        return local / lax.dynamic_slice_in_dim(gain, wide_index * strip, strip)

    local = jnp.stack(
        [
            gain_grad([(w_query, grad_query), (w_key, grad_key), (w_value, grad_value)], gain_one),
            gain_grad([(w_gate, grad_gate), (w_up, grad_up)], gain_two),
        ]
    )
    local = local + narrow_swap(local, 1)
    local = local + narrow_swap(local, 2)
    grad_gain_one, grad_gain_two = local[0], local[1]
    return (
        output,
        grad_tokens,
        grad_gain_one,
        grad_query,
        grad_key,
        grad_value,
        grad_out,
        grad_gain_two,
        grad_gate,
        grad_up,
        grad_down,
    )


def solution(mesh):
    placed = (
        P("wide", None),
        P("wide", None),
        P("wide"),
        P(),
        P(),
        P(),
        P(None, "narrow"),
        P(None, "narrow"),
        P(None, "narrow"),
        P("narrow", None),
        P(),
        P(None, "narrow"),
        P(None, "narrow"),
        P("narrow", None),
    )
    return jax.shard_map(
        shards,
        mesh=mesh,
        in_specs=placed,
        out_specs=(
            P("wide", None),
            P("wide", None),
            P("wide"),
            P("wide", "narrow"),
            P("wide", "narrow"),
            P("wide", "narrow"),
            P("narrow", "wide"),
            P("wide"),
            P("wide", "narrow"),
            P("wide", "narrow"),
            P("narrow", "wide"),
        ),
        check_vma=False,
    )
```

```python
import functools

import jax
import jax.numpy as jnp
import numpy as np
from jax import lax
from jax.experimental import pallas as pl
from jax.experimental.pallas import tpu as pltpu
from jax.sharding import PartitionSpec as P

HD = 128
EPSILON = 1e-05
NEGATIVE = -1e30
BASE = 10000.0
LOG2E = 1.4426950408889634
SCORE = HD ** (-0.5) * LOG2E
FACTOR = HD ** (-0.5)
BF = jnp.bfloat16
F32 = jnp.float32
NT = (((1,), (1,)), ((), ()))
TN = (((0,), (0,)), ((), ()))
NN = (((1,), (0,)), ((), ()))
VM = pl.BlockSpec(memory_space=pltpu.VMEM)
SM = pl.BlockSpec(memory_space=pltpu.SMEM)
ANY = pl.BlockSpec(memory_space=pl.ANY)


def dot(a, b, dims=(((1,), (0,)), ((), ()))):
    return lax.dot_general(a, b, dims, preferred_element_type=F32)


def narrow_swap(value, mask):
    pairs = [(n, n ^ mask) for n in range(lax.axis_size("narrow"))]
    return lax.ppermute(value, "narrow", pairs)


def wide_swap(value):
    return lax.ppermute(value, "wide", [(w, w ^ 1) for w in range(lax.axis_size("wide"))])


def wide_ring(value, group, hop=1):
    ring = group // 2
    pairs = []
    for w in range(lax.axis_size("wide")):
        base, member = w // group * group, w % group
        pairs.append((w, base + (member // 2 + hop) % ring * 2 + member % 2))
    return lax.ppermute(value, "wide", pairs)


def wide_flip(value, bit):
    return lax.ppermute(value, "wide", [(w, w ^ (2 << bit)) for w in range(lax.axis_size("wide"))])


def halving(count):
    groups = []
    step = 1
    while step < count:
        groups.append([k for k in range(count) if k % (2 * step) == step])
        step *= 2
    return [*groups, [0]]


def stretches(groups):
    starts, at = [], 0
    for group in groups:
        starts.append((at, len(group)))
        at += len(group)
    return starts


def rope(value, cosine, sine):
    return value * cosine + pltpu.roll(value, HD // 2, 1) * sine


def norm_kv_kernel(core, x_ref, gain_ref, wk_ref, wv_ref, cos_ref, sin_ref, normed_ref, *kv_refs):
    x = x_ref[...].astype(F32)
    scale = lax.rsqrt(jnp.mean(x * x, axis=1, keepdims=True) + EPSILON)
    normed = (x * scale * gain_ref[...].astype(F32)).astype(BF)
    normed_ref[...] = normed
    keys = dot(normed, wk_ref[...])
    values = dot(normed, wv_ref[...])
    for h, ref in enumerate(kv_refs):
        cols = slice(h * HD, (h + 1) * HD)
        ref[:, :HD] = rope(keys[:, cols], cos_ref[...], sin_ref[...]).astype(BF)
        ref[:, HD:] = values[:, cols].astype(BF)


def norm_kv(core, tokens, gain, wk, wv, cosine, sine):
    rows, width = tokens.shape
    half = rows // 2
    heads = wk.shape[1] // HD
    full = lambda w: pl.BlockSpec(w.shape, lambda i, c: (0, 0))
    outs = pl.pallas_call(
        norm_kv_kernel,
        out_shape=[jax.ShapeDtypeStruct((rows, width), BF)]
        + [jax.ShapeDtypeStruct((rows, 2 * HD), BF)] * heads,
        grid_spec=pltpu.PrefetchScalarGridSpec(
            num_scalar_prefetch=1,
            grid=(2,),
            in_specs=[
                pl.BlockSpec((half, width), lambda i, c: (i ^ c[0], 0)),
                full(gain),
                full(wk),
                full(wv),
                pl.BlockSpec((half, HD), lambda i, c: (i, 0)),
                pl.BlockSpec((half, HD), lambda i, c: (i, 0)),
            ],
            out_specs=[pl.BlockSpec((half, width), lambda i, c: (i, 0))]
            + [pl.BlockSpec((half, 2 * HD), lambda i, c: (i, 0))] * heads,
        ),
        cost_estimate=pl.CostEstimate(flops=int(2.9e9), bytes_accessed=0, transcendentals=0),
        name="norm_kv",
    )(core, tokens, gain, wk, wv, cosine, sine)
    return outs[0], outs[1:]


def query_kernel(x_ref, w_ref, cos_ref, sin_ref, out_ref):
    raw = dot(x_ref[...], w_ref[...])
    for h in range(raw.shape[1] // HD):
        cols = slice(h * HD, (h + 1) * HD)
        out_ref[:, cols] = rope(raw[:, cols], cos_ref[...], sin_ref[...]).astype(BF)


def query_proj(x, w, cosine, sine):
    rows, width = x.shape
    half = rows // 2
    return pl.pallas_call(
        query_kernel,
        out_shape=jax.ShapeDtypeStruct((rows, w.shape[1]), BF),
        grid=(2,),
        in_specs=[
            pl.BlockSpec((half, width), lambda i: (i, 0)),
            pl.BlockSpec(w.shape, lambda i: (0, 0)),
            pl.BlockSpec((half, HD), lambda i: (i, 0)),
            pl.BlockSpec((half, HD), lambda i: (i, 0)),
        ],
        out_specs=pl.BlockSpec((half, w.shape[1]), lambda i: (i, 0)),
        cost_estimate=pl.CostEstimate(flops=int(2.9e9), bytes_accessed=0, transcendentals=0),
        name="query_proj",
    )(x, w, cosine, sine)


def fetch_slots(slot_refs, slots, kv_ref, sems):
    rows, width = slot_refs[0].shape
    copies = []
    for at, ref in enumerate(slot_refs):
        head, slot = divmod(at, slots)
        spot = kv_ref.at[pl.ds(slot * rows, rows), pl.ds(head * width, width)]
        copies.append(pltpu.make_async_copy(ref, spot, sems.at[at]))
    for copy in copies:
        copy.start()
    for copy in copies:
        copy.wait()


def allowed(pk, size, span, pos, low):
    key_pos = pk * size + lax.broadcasted_iota(jnp.int32, (size, span), 0)
    return (key_pos <= pos) & (key_pos >= low)


def attn_fwd_kernel(slots, *refs):
    meta, q_ref, pos_ref, low_ref = refs[:4]
    slot_refs = refs[4 : 4 + slots]
    mixed_ref, lse_ref, kv_ref, acc_ref, sems = refs[-5:]
    fetch_slots(slot_refs, slots, kv_ref, sems)
    size = q_ref.shape[0] // 2
    for i in range(2):
        rows = slice(i * size, (i + 1) * size)
        pos = jnp.tile(pos_ref[0:1, rows], (1, 2))
        low = jnp.tile(low_ref[0:1, rows], (1, 2))
        queries = [q_ref[rows, r * HD : (r + 1) * HD] for r in range(2)]
        acc_ref[...] = jnp.zeros_like(acc_ref)

        def body(pk, carry):
            peak, total = carry
            spot = pl.multiple_of(meta[4 + pk] * size, size)
            keys = kv_ref[pl.ds(spot, size), :HD]
            values = kv_ref[pl.ds(spot, size), HD:]
            scores = jnp.concatenate([dot(keys, q, NT) for q in queries], axis=1) * SCORE
            scores = jnp.where(allowed(pk, size, 2 * size, pos, low), scores, NEGATIVE)
            peak_new = jnp.maximum(peak, jnp.max(scores, axis=0, keepdims=True))
            alpha = jnp.exp2(peak - peak_new)
            probs = jnp.exp2(scores - peak_new)
            total = total * alpha + jnp.sum(probs, axis=0, keepdims=True)
            acc_ref[...] = acc_ref[...] * alpha + dot(values, probs.astype(BF), TN)
            return peak_new, total

        start = (jnp.full((1, 2 * size), NEGATIVE, F32), jnp.zeros((1, 2 * size), F32))
        peak, total = lax.fori_loop(meta[i], meta[2 + i] + 1, body, start)
        lse_ref[i : i + 1, :] = peak + jnp.log2(total)
        out = acc_ref[...] * (1.0 / total)
        for r in range(2):
            mixed_ref[rows, r * HD : (r + 1) * HD] = out[:, r * size : (r + 1) * size].T.astype(BF)


def attn_fwd(head, meta, q, pos, low, slots, mixed):
    rows = q.shape[0]
    count = len(slots)
    earlier = [] if mixed is None else [mixed]
    return pl.pallas_call(
        functools.partial(attn_fwd_kernel, count),
        out_shape=(
            jax.ShapeDtypeStruct(q.shape, BF),
            jax.ShapeDtypeStruct((2, rows), F32),
        ),
        grid=(1,),
        in_specs=[
            SM,
            pl.BlockSpec((rows, 2 * HD), lambda i: (0, head)),
            pl.BlockSpec(pos.shape, lambda i: (0, 0)),
            pl.BlockSpec(low.shape, lambda i: (0, 0)),
        ]
        + [ANY] * (count + len(earlier)),
        out_specs=[
            pl.BlockSpec((rows, 2 * HD), lambda i: (0, head)),
            pl.BlockSpec((2, rows), lambda i: (0, 0)),
        ],
        input_output_aliases={4 + count: 0} if earlier else {},
        scratch_shapes=[
            pltpu.VMEM((count * rows, 2 * HD), BF),
            pltpu.VMEM((HD, rows), F32),
            pltpu.SemaphoreType.DMA((count,)),
        ],
        cost_estimate=pl.CostEstimate(flops=int(1e9), bytes_accessed=0, transcendentals=0),
        name="attn_fwd",
    )(meta, q, pos, low, *slots, *earlier)


def attn_bwd_kernel(heads, slots, groups, *refs):
    meta, q_ref, pos_ref, low_ref, dmix_ref, mixed_ref, cos_ref, sin_ref = refs[:8]
    lse_refs = refs[8 : 8 + heads]
    at = 8 + heads
    slot_refs = refs[at : at + heads * slots]
    at += heads * slots
    dq_ref, dkv_refs = refs[at], refs[at + 1 : -4]
    kv_ref, dkv_ref, dq_acc, sems = refs[-4:]
    fetch_slots(slot_refs, slots, kv_ref, sems)
    dkv_ref[...] = jnp.zeros_like(dkv_ref)
    rows_all = q_ref.shape[0]
    size = rows_all // 2
    for i in range(2):
        rows = slice(i * size, (i + 1) * size)
        pos = jnp.tile(pos_ref[0:1, rows], (1, 2))
        low = jnp.tile(low_ref[0:1, rows], (1, 2))
        for g in range(heads):
            cols = [slice((2 * g + r) * HD, (2 * g + r + 1) * HD) for r in range(2)]
            queries = jnp.concatenate([q_ref[rows, c] for c in cols], axis=0)
            grads = jnp.concatenate([dmix_ref[rows, c] for c in cols], axis=0)
            outs = jnp.concatenate([mixed_ref[rows, c] for c in cols], axis=0)
            delta = jnp.sum((grads.astype(F32) * outs.astype(F32)).T, axis=0, keepdims=True)
            lse = lse_refs[g][i : i + 1, :]
            dq_acc[...] = jnp.zeros_like(dq_acc)

            def body(pk, carry):
                spot = pl.multiple_of(meta[4 + pk] * size, size)
                key_cols = slice(2 * g * HD, (2 * g + 1) * HD)
                value_cols = slice((2 * g + 1) * HD, (2 * g + 2) * HD)
                keys = kv_ref[pl.ds(spot, size), key_cols]
                values = kv_ref[pl.ds(spot, size), value_cols]
                scores = dot(keys, queries, NT) * SCORE
                probs = jnp.where(
                    allowed(pk, size, 2 * size, pos, low), jnp.exp2(scores - lse), 0.0
                )
                d_probs = dot(values, grads, NT)
                d_scores = (probs * (d_probs - delta)).astype(BF)
                dkv_ref[pl.ds(spot, size), value_cols] += dot(probs.astype(BF), grads)
                dkv_ref[pl.ds(spot, size), key_cols] += dot(d_scores, queries) * FACTOR
                dq_acc[...] += dot(d_scores, keys, TN)
                return carry

            lax.fori_loop(meta[i], meta[2 + i] + 1, body, 0)
            for r in range(2):
                part = dq_acc[r * size : (r + 1) * size, :] * FACTOR
                dq_ref[rows, cols[r]] = rope(part, cos_ref[rows, :], -sin_ref[rows, :]).astype(BF)
    ring = slots // 2
    for j, ref in enumerate(dkv_refs):
        first = ring * (j // len(groups))
        for place, k in enumerate(groups[j % len(groups)]):
            spot = pl.multiple_of((first + meta[4 + 2 * slots + k]) * rows_all, rows_all)
            ref[place * rows_all : (place + 1) * rows_all, :] = dkv_ref[
                pl.ds(spot, rows_all), :
            ].astype(BF)


def attn_bwd(meta, q, pos, low, lse, mixed, dmix, cosine, sine, slots):
    rows, q_width = q.shape
    heads, count = len(slots), len(slots[0])
    kv_width = heads * 2 * HD
    groups = halving(count // 2)
    outs = pl.pallas_call(
        functools.partial(attn_bwd_kernel, heads, count, groups),
        out_shape=[jax.ShapeDtypeStruct((rows, q_width), BF)]
        + [jax.ShapeDtypeStruct((len(g) * rows, kv_width), BF) for g in groups] * 2,
        in_specs=[SM] + [VM] * (7 + heads) + [ANY] * (heads * count),
        out_specs=[VM] * (1 + 2 * len(groups)),
        scratch_shapes=[
            pltpu.VMEM((count * rows, kv_width), BF),
            pltpu.VMEM((count * rows, kv_width), F32),
            pltpu.VMEM((rows, HD), F32),
            pltpu.SemaphoreType.DMA((heads * count,)),
        ],
        cost_estimate=pl.CostEstimate(flops=int(2e9), bytes_accessed=0, transcendentals=0),
        name="attn_bwd",
    )(meta, q, pos, low, dmix, mixed, cosine, sine, *lse, *[v for head in slots for v in head])
    return outs[0], outs[1 : 1 + len(groups)], outs[1 + len(groups) :]


def cost(micros):
    return pl.CostEstimate(flops=int(micros * 0.3e9), bytes_accessed=0, transcendentals=0)


def split_rows(total, own_ref, other_ref):
    half = own_ref.shape[0]
    own_ref[...] = total[:half].astype(BF)
    other_ref[...] = total[half:].astype(BF)


def project_kernel(spec, *refs):
    total = None
    for a, b, offset, dims in spec:
        left = refs[a][...] if dims is not None else None
        if dims == "nt":
            right, form = refs[b][:, offset : offset + left.shape[1]], NT
        else:
            right, form = refs[b][offset : offset + left.shape[1], :], NN
        term = dot(left, right, form)
        total = term if total is None else total + term
    split_rows(total, refs[-2], refs[-1])


def project(pairs, dims, tile, micros):
    operands, specs, plan, weights = [], [], [], []
    for a, b, offset in pairs:
        operands.append(a)
        specs.append(pl.BlockSpec(a.shape, lambda i: (0, 0)))
        spot = next((at for at, seen in weights if seen is b), None)
        left = len(operands) - 1
        if spot is None:
            spot = len(operands)
            operands.append(b)
            weights.append((spot, b))
            if dims == "nt":
                specs.append(pl.BlockSpec((tile, b.shape[1]), lambda i: (i, 0)))
            else:
                specs.append(pl.BlockSpec((b.shape[0], tile), lambda i: (0, i)))
        plan.append((left, spot, offset, dims))
    rows = pairs[0][0].shape[0]
    width = pairs[0][1].shape[0 if dims == "nt" else 1]
    return pl.pallas_call(
        functools.partial(project_kernel, plan),
        out_shape=[jax.ShapeDtypeStruct((rows // 2, width), BF)] * 2,
        grid=(width // tile,),
        in_specs=specs,
        out_specs=[pl.BlockSpec((rows // 2, tile), lambda i: (0, i))] * 2,
        cost_estimate=cost(micros),
        name="project",
    )(*operands)


def back_dense_kernel(gate_a, up_a, gate_b, up_b, wg_ref, wu_ref, own_ref, other_ref):
    total = None
    offset = 0
    for group in ((gate_a, up_a), (gate_b, up_b)):
        count = group[0].shape[1]
        for ref, w_ref in zip(group, (wg_ref, wu_ref)):
            term = dot(ref[...], w_ref[:, offset : offset + count], NT)
            total = term if total is None else total + term
        offset += count
    split_rows(total, own_ref, other_ref)


def back_dense(grads, w_gate, w_up, tile, part, parts):
    width, hidden = w_gate.shape[0] // parts, w_gate.shape[1]
    rows = grads[0].shape[0]
    ahead = part * (width // tile)
    weight = pl.BlockSpec((tile, hidden), lambda i: (ahead + i, 0))
    return pl.pallas_call(
        back_dense_kernel,
        out_shape=[jax.ShapeDtypeStruct((rows // 2, width), BF)] * 2,
        grid=(width // tile,),
        in_specs=[pl.BlockSpec(v.shape, lambda i: (0, 0)) for v in grads] + [weight, weight],
        out_specs=[pl.BlockSpec((rows // 2, tile), lambda i: (0, i))] * 2,
        cost_estimate=cost(11 / parts),
        name="back_dense",
    )(*grads, w_gate, w_up)


def gated_kernel(own_ref, other_ref, wg_ref, wu_ref, di_ref, inner_ref, dg_ref, du_ref, all_ref):
    @pl.when(pl.program_id(0) == 0)
    def _():
        half = own_ref.shape[0]
        all_ref[:half, :] = own_ref[...]
        all_ref[half:, :] = other_ref[...]

    gate = dot(all_ref[...], wg_ref[...])
    up = dot(all_ref[...], wu_ref[...])
    sigma = 1.0 / (1.0 + jnp.exp(-gate))
    silu = gate * sigma
    d_inner = di_ref[...]
    inner_ref[...] = (silu * up).astype(BF)
    dg_ref[...] = (d_inner * up * sigma * (1.0 + gate * (1.0 - sigma))).astype(BF)
    du_ref[...] = (d_inner * silu).astype(BF)


def gated(own, other, wg, wu, d_inner, first, columns, tile):
    half, width = own.shape
    weight = pl.BlockSpec((width, tile), lambda i: (0, first // tile + i))
    whole = pl.BlockSpec((half, width), lambda i: (0, 0))
    return pl.pallas_call(
        gated_kernel,
        out_shape=[jax.ShapeDtypeStruct((2 * half, columns), BF)] * 3,
        grid=(pl.cdiv(columns, tile),),
        in_specs=[
            whole,
            whole,
            weight,
            weight,
            pl.BlockSpec((2 * half, tile), lambda i: (0, first // tile + i)),
        ],
        out_specs=[pl.BlockSpec((2 * half, tile), lambda i: (0, i))] * 3,
        scratch_shapes=[pltpu.VMEM((2 * half, width), BF)],
        cost_estimate=cost(7.5),
        name="gated",
    )(own, other, wg, wu, d_inner)


def mixed_grad_kernel(own_ref, other_ref, w_ref, out_ref):
    both = jnp.concatenate([own_ref[...], other_ref[...]], axis=0)
    out_ref[...] = dot(both, w_ref[...], NT).astype(BF)


def mixed_grad(own, other, w):
    return pl.pallas_call(
        mixed_grad_kernel,
        out_shape=jax.ShapeDtypeStruct((2 * own.shape[0], w.shape[0]), BF),
        in_specs=[VM] * 3,
        out_specs=VM,
        cost_estimate=cost(4),
        name="mixed_grad",
    )(own, other, w)


def d_inner_kernel(x_ref, w_ref, out_ref):
    out_ref[...] = dot(x_ref[...], w_ref[...], NT)


def inner_grad(x, w, tile):
    rows, width = x.shape
    hidden = w.shape[0]
    return pl.pallas_call(
        d_inner_kernel,
        out_shape=jax.ShapeDtypeStruct((rows, hidden), F32),
        grid=(pl.cdiv(hidden, tile),),
        in_specs=[
            pl.BlockSpec((rows, width), lambda i: (0, 0)),
            pl.BlockSpec((tile, width), lambda i: (i, 0)),
        ],
        out_specs=pl.BlockSpec((rows, tile), lambda i: (0, i)),
        cost_estimate=cost(8),
        name="inner_grad",
    )(x, w)


def pack_kernel(count, plan, strip, tbl, *refs):
    ins, outs = refs[:count], refs[count:]
    for out_ref, pieces in zip(outs, plan):
        column = 0
        for at, rows, row in pieces:
            for k in range(tbl.shape[1]):
                first = pl.multiple_of(tbl[row, k] * strip, 128)
                out_ref[:, column : column + strip] = ins[at][rows, pl.ds(first, strip)]
                column += strip


def pack(values, plan, tbl, strip):
    turns = tbl.shape[1]
    if strip % 128:
        cut = lambda v, rows, at: lax.dynamic_slice_in_dim(v[rows], at * strip, strip, axis=1)
        return [
            jnp.concatenate(
                [cut(values[at], rows, tbl[row, k]) for at, rows, row in pieces for k in range(turns)],
                axis=1,
            )
            for pieces in plan
        ]
    return pl.pallas_call(
        functools.partial(pack_kernel, len(values), plan, strip),
        out_shape=[
            jax.ShapeDtypeStruct(
                (p[0][1].stop - p[0][1].start, len(p) * turns * strip), values[0].dtype
            )
            for p in plan
        ],
        in_specs=[SM] + [VM] * len(values),
        out_specs=[VM] * len(plan),
        cost_estimate=cost(1.5),
        name="pack",
    )(tbl, *values)


def strip_rows_kernel(halves, near, rights, nears, spans, tbl, *refs):
    left = refs[:halves]
    left_near = refs[halves : halves + near]
    right = refs[halves + near : halves + near + rights]
    right_near = refs[halves + near + rights : halves + near + rights + nears]
    outs = refs[halves + near + rights + nears :]
    step = pl.program_id(0)
    join = lambda group: (
        group[0][...] if len(group) == 1 else jnp.concatenate([r[...] for r in group], axis=0)
    )
    mine, theirs = join(left), join(left_near)
    pieces = []
    for r, n in zip(right, right_near):
        planes = range(r.shape[0]) if len(r.shape) == 3 else [None]
        for k in planes:
            a = r[...] if k is None else r[k]
            b = n[...] if k is None else n[k]
            pieces.append((dot(mine, a, TN) + dot(theirs, b, TN)).astype(BF))
    for (start, length), out in zip(spans, outs):

        @pl.when((step >= start) & (step < start + length))
        def _(out=out):
            column = 0
            for piece in pieces:
                out[:, column : column + piece.shape[1]] = piece
                column += piece.shape[1]


def strip_rows_grad(left, left_near, right, right_near, tbl, strip, micros):
    turns = tbl.shape[1]
    columns = sum(r.shape[-1] * (r.shape[0] if r.ndim == 3 else 1) for r in right)
    spans = stretches(halving(turns))
    if strip % 128:
        near = jnp.concatenate(left_near, axis=0)
        mine = jnp.concatenate(left, axis=0)
        flat = lambda r: [r] if r.ndim == 2 else [r[k] for k in range(r.shape[0])]
        outs = []
        for start, length in spans:
            group = []
            for k in range(start, start + length):
                a = lax.dynamic_slice_in_dim(mine, tbl[0, k] * strip, strip, axis=1)
                b = near[:, k * strip : (k + 1) * strip]
                group.append(
                    jnp.concatenate(
                        [
                            dot(a, x, TN) + dot(b, y, TN)
                            for r, n in zip(right, right_near)
                            for x, y in zip(flat(r), flat(n))
                        ],
                        axis=1,
                    ).astype(BF)
                )
            outs.append(jnp.concatenate(group, axis=0))
        return outs
    held = lambda start, length: (lambda i, t: (jnp.clip(i - start, 0, length - 1), 0))
    whole = lambda v: pl.BlockSpec(v.shape, lambda i, t: (0,) * v.ndim)
    return pl.pallas_call(
        functools.partial(
            strip_rows_kernel, len(left), len(left_near), len(right), len(right_near), spans
        ),
        out_shape=[jax.ShapeDtypeStruct((length * strip, columns), BF) for _, length in spans],
        grid_spec=pltpu.PrefetchScalarGridSpec(
            num_scalar_prefetch=1,
            grid=(turns,),
            in_specs=[pl.BlockSpec((v.shape[0], strip), lambda i, t: (0, t[0, i])) for v in left]
            + [pl.BlockSpec((v.shape[0], strip), lambda i, t: (0, i)) for v in left_near]
            + [whole(v) for v in [*right, *right_near]],
            out_specs=[pl.BlockSpec((strip, columns), held(*span)) for span in spans],
        ),
        cost_estimate=cost(micros),
        name="strip_rows",
    )(tbl, *left, *left_near, *right, *right_near)


def strip_columns_kernel(parts, halves, near, strip, spans, *refs):
    at = 2 * parts
    right, right_near = refs[at : at + halves], refs[at + halves : at + halves + near]
    outs = refs[at + halves + near :]
    first = 0
    for p in range(parts):
        total = None
        for ref, group in ((refs[p], right), (refs[parts + p], right_near)):
            row = 0
            for r in group:
                term = dot(ref[row : row + r.shape[0], :], r[...], TN)
                total = term if total is None else total + term
                row += r.shape[0]
        for (start, length), out in zip(spans, outs):
            out[first : first + total.shape[0], :] = total[
                :, start * strip : (start + length) * strip
            ].astype(BF)
        first += total.shape[0]


def strip_columns_grad(left, left_near, right, right_near, turns, strip, tile, micros, near_at=0):
    rows, count = left[0].shape[0], sum(v.shape[1] for v in left)
    if strip * turns % 128:
        raise ValueError(strip)
    spans = stretches(halving(turns))
    whole = lambda v: pl.BlockSpec(v.shape, lambda i: (0, 0))
    near = lambda v: pl.BlockSpec((v.shape[0], turns * strip), lambda i: (0, near_at))
    if len(left) == 1:
        left_specs = [pl.BlockSpec((rows, tile), lambda i: (0, i))] * 2
    else:
        tile = count
        left_specs = [whole(v) for v in [*left, *left_near]]
    return pl.pallas_call(
        functools.partial(
            strip_columns_kernel, len(left), len(right), len(right_near), strip, spans
        ),
        out_shape=[jax.ShapeDtypeStruct((count, length * strip), BF) for _, length in spans],
        grid=(pl.cdiv(count, tile),),
        in_specs=left_specs + [whole(v) for v in right] + [near(v) for v in right_near],
        out_specs=[pl.BlockSpec((tile, length * strip), lambda i: (i, 0)) for _, length in spans],
        cost_estimate=cost(micros),
        name="strip_columns",
    )(*left, *left_near, *right, *right_near)


def close_kv_kernel(count, *refs):
    cos_ref, sin_ref, dk_ref, dv_ref = refs[count:]
    total = refs[0][...].astype(F32)
    for ref in refs[1:count]:
        total = total + ref[...].astype(F32)
    heads = dk_ref.shape[1] // HD
    for h in range(heads):
        cols = slice(h * HD, (h + 1) * HD)
        keys = total[:, 2 * h * HD : (2 * h + 1) * HD]
        dk_ref[:, cols] = rope(keys, cos_ref[...], -sin_ref[...]).astype(BF)
        dv_ref[:, cols] = total[:, (2 * h + 1) * HD : (2 * h + 2) * HD].astype(BF)


def close_kv(terms, cosine, sine):
    rows, width = terms[0].shape
    first = lambda w: pl.BlockSpec((rows, w), lambda i: (0, 0))
    return pl.pallas_call(
        functools.partial(close_kv_kernel, len(terms)),
        out_shape=[jax.ShapeDtypeStruct((rows, width // 2), BF)] * 2,
        grid=(1,),
        in_specs=[first(width)] * len(terms) + [first(HD)] * 2,
        out_specs=[first(width // 2)] * 2,
        cost_estimate=cost(1.5),
        name="close_kv",
    )(*terms, cosine, sine)


def norm_backward(source, scale_rows, gain, upstream):
    weighted = upstream * gain
    average = jnp.mean(weighted * source, axis=1, keepdims=True)
    return scale_rows * weighted - source * scale_rows**3 * average


def after(value, *done):
    return lax.optimization_barrier((value, *done))[0]


def shards(
    tokens,
    cotangent,
    keep_mask,
    doc_lengths,
    block_order,
    gain_attn,
    w_query,
    w_key,
    w_value,
    w_out,
    gain_dense,
    w_gate,
    w_up,
    w_down,
):
    rows, width = tokens.shape
    half = rows // 2
    wide = lax.axis_size("wide")
    group = wide // block_order.shape[0]
    ring = group // 2
    wide_index = lax.axis_index("wide")
    member = wide_index % group
    seq_index = wide_index // group
    side = (wide_index % 2).astype(jnp.int32)
    core = lax.axis_index("narrow") % 2
    strip = width // wide
    turns = wide // 2

    def ordered(mine, other):
        return jnp.where(
            core == 0,
            jnp.concatenate([mine, other], axis=0),
            jnp.concatenate([other, mine], axis=0),
        )

    def own_half(value):
        return lax.dynamic_slice_in_dim(value, core * half, half)

    def other_half(value):
        return lax.dynamic_slice_in_dim(value, (1 - core) * half, half)

    order_row = lax.dynamic_index_in_dim(block_order, seq_index, 0, keepdims=False)
    length_row = lax.dynamic_index_in_dim(doc_lengths, seq_index, 0, keepdims=False)
    doc_ends = jnp.cumsum(length_row)
    places = jnp.stack([member * 2 + core, member * 2 + 1 - core])
    chosen = jnp.sum(
        jnp.where(places[:, None] == jnp.arange(2 * group)[None, :], order_row[None, :], 0), axis=1
    )
    pos = (chosen[:, None] * half + jnp.arange(half, dtype=jnp.int32)[None, :]).reshape(-1)
    low = jnp.max(jnp.where(doc_ends[None, :] <= pos[:, None], doc_ends[None, :], 0), axis=1)
    block_low = low.reshape(2, half)[:, 0] // half
    stored = jnp.sum(
        jnp.where(
            order_row[None, :] == jnp.arange(2 * group)[:, None], jnp.arange(2 * group)[None, :], 0
        ),
        axis=1,
    )
    owner = stored // 2
    slot = (member // 2 - owner // 2) % ring + ring * (owner % 2 != side).astype(jnp.int32)
    spots = slot * 2 + (stored % 2 != core).astype(jnp.int32)
    place = member // 2
    back = (place - (place ^ jnp.arange(ring, dtype=jnp.int32))) % ring
    meta = jnp.concatenate([block_low, chosen, spots, back]).astype(jnp.int32)
    frequency = BASE ** (-(jnp.arange(HD // 2, dtype=F32) * 2.0) / HD)
    angles = pos.astype(F32)[:, None] * frequency[None, :]
    cosine = jnp.cos(angles)
    sine = jnp.sin(angles)
    cosine = jnp.concatenate([cosine, cosine], axis=1)
    sine = jnp.concatenate([-sine, sine], axis=1)
    pos_row = pos[None, :]
    low_row = low[None, :]

    order = np.array([k for stretch in halving(turns) for k in stretch], np.int32)
    turn_row = wide_index // 2 ^ order
    tbl = jnp.stack([2 * turn_row + side, 2 * turn_row + 1 - side]).astype(jnp.int32)
    core_arr = core.astype(jnp.int32)[None]
    normed_one, both = norm_kv(core_arr, tokens, gain_attn[None, :], w_key, w_value, cosine, sine)
    low_rows, all_rows = slice(0, half), slice(0, rows)

    def together(*values):
        return list(lax.optimization_barrier(values))

    near, far = [[v] for v in both], [[] for v in both]
    query = d_dense = d_inner = input_near = d_dense_strips = None
    for step in range(ring):
        for head in range(len(both)):
            held = near[head][step]
            if step + 1 < ring:
                sent = [wide_swap(held), wide_ring(held, group)]
            elif head == 0:
                sent = [wide_swap(held)]
            else:
                sent = [wide_ring(far[head][0], group, -1)]
            beside = []
            if step == 0 and head == 0:
                beside = [query_proj(normed_one, w_query, cosine, sine)]
            if step == 0 and head == 1:
                keep_rel = jnp.concatenate([own_half(keep_mask), other_half(keep_mask)])[:, None]
                cot_rel = jnp.concatenate([own_half(cotangent), other_half(cotangent)])
                beside = [jnp.where(keep_rel > 0, cot_rel, jnp.zeros_like(cot_rel))]
            if step == 1 and head == 0:
                beside = [inner_grad(d_dense, w_down, 256)]
            if step == 2 and head == 0:
                beside = pack(
                    [normed_one, d_dense],
                    [[(0, low_rows, 1), (1, low_rows, 1)], [(1, all_rows, 0)]],
                    tbl,
                    strip,
                )
            done = together(*sent, *beside)
            far[head].append(done[0])
            if step + 1 < ring:
                near[head].append(done[1])
            if step == 0 and head == 0:
                query = done[-1]
            if step == 0 and head == 1:
                d_dense = done[-1]
            if step == 1 and head == 0:
                d_inner = done[-1]
            if step == 2 and head == 0:
                input_near, d_dense_strips = done[-2:]
    slots = [n + f for n, f in zip(near, far)]
    input_near = wide_swap(after(input_near, far[0][-2]))
    mixed, lse = None, []
    for h, held in enumerate(slots):
        mixed, part = attn_fwd(h, meta, query, pos_row, low_row, held, mixed)
        lse.append(part)

    def reduce_narrow(halves, hold=()):
        own_part, other_part = halves
        got = narrow_swap(other_part, 1)
        held = (own_part.astype(F32) + got.astype(F32)).astype(BF)
        return held, narrow_swap(held, 2)

    def total_of(held, got):
        return held.astype(F32) + got.astype(F32)

    part = project([(mixed, w_out, 0)], "nn", 1024, 4)
    held, got = reduce_narrow((part[0], after(part[1], input_near)))
    mixed_near = wide_swap(mixed)
    input_near_other = narrow_swap(input_near, 1)
    source = own_half(tokens).astype(F32)
    keep_own = own_half(keep_mask).astype(F32)[:, None]
    hidden_one = source + keep_own * total_of(held, got)
    gain_two = gain_dense.astype(F32)
    scale_two = lax.rsqrt(jnp.mean(hidden_one * hidden_one, axis=1, keepdims=True) + EPSILON)
    normed_two = (hidden_one * scale_two * gain_two).astype(BF)
    normed_two_other = narrow_swap(after(normed_two, mixed_near), 1)
    (normed_two_near,) = pack([normed_two], [[(0, low_rows, 1)]], tbl, strip)
    normed_two_near = wide_swap(normed_two_near)

    hidden = w_gate.shape[1]
    tile = 256
    first_count = 3 * tile
    inner_a, *dgu_a = gated(
        normed_two, normed_two_other, w_gate, w_up, d_inner, 0, first_count, tile
    )
    inner_a_near = wide_swap(inner_a)
    inner_b, *dgu_b = gated(
        after(normed_two, inner_a),
        normed_two_other,
        w_gate,
        w_up,
        d_inner,
        first_count,
        hidden - first_count,
        tile,
    )
    back = back_dense([*dgu_a, dgu_b[0], after(dgu_b[1], normed_two_near)], w_gate, w_up, 512, 0, 1)
    held, got = reduce_narrow((back[0], after(back[1], inner_a_near)))

    def halve(parts, axis, hold=None):
        groups = halving(1 << (len(parts) - 1))
        size = parts[-1].shape[axis]
        received, sent = [], None
        for bit, group in enumerate(groups[:-1]):
            sent = parts[bit]
            if bit:
                total = sent.astype(F32)
                for early, value in enumerate(received):
                    there = [k ^ (1 << early) for k in groups[early]]
                    pick = [
                        lax.slice_in_dim(value, size * there.index(k), size * (there.index(k) + 1), axis=axis)
                        for k in group
                    ]
                    total = total + (pick[0] if len(pick) == 1 else jnp.concatenate(pick, axis)).astype(F32)
                sent = total.astype(BF)
                if hold is not None:
                    sent = after(sent, hold)
            received.append(wide_flip(sent, bit))
        return received, sent

    def close(parts, received, axis):
        size = parts[-1].shape[axis]
        total = parts[-1].astype(F32)
        for value in received:
            total = total + lax.slice_in_dim(value, 0, size, axis=axis).astype(F32)
        return total

    near_sides = [input_near, input_near_other]
    down_a = strip_columns_grad(
        [after(inner_a, held)],
        [inner_a_near],
        [d_dense_strips],
        near_sides,
        turns,
        strip,
        tile,
        4,
        1,
    )
    inner_b_near = wide_swap(inner_b)
    normed_two_near_other = narrow_swap(after(normed_two_near, held), 1)
    down_a_got, down_a_mid = halve(down_a, 1)
    dgu_a_near = [wide_swap(after(v, inner_b)) for v in dgu_a]
    dense_parts = project(
        [(after(inner_a, down_a[0]), w_down, 0), (inner_b, w_down, first_count)], "nn", 512, 6
    )
    down_b = strip_columns_grad(
        [after(inner_b, dense_parts[0])], [inner_b_near], [d_dense_strips], near_sides, turns, strip, tile, 4, 1
    )

    got = after(got, dense_parts[0], down_b[0])
    down_b_got, down_b_mid = halve(down_b, 1, got)
    upstream = own_half(cotangent).astype(F32)
    d_hidden = upstream + norm_backward(hidden_one, scale_two, gain_two, total_of(held, got))
    d_attn = (keep_own * d_hidden).astype(BF)
    d_attn_other = narrow_swap(after(d_attn, dgu_a_near[0], down_a_mid), 1)

    d_mixed = mixed_grad(d_attn, d_attn_other, w_out)
    d_query, d_near, d_far = attn_bwd(
        meta, query, pos_row, low_row, lse, mixed, after(d_mixed, down_b_mid), cosine, sine, slots
    )
    held_out, got_out = reduce_narrow((dense_parts[0], after(dense_parts[1], d_mixed)))
    output_own = (hidden_one + keep_own * total_of(held_out, got_out)).astype(BF)
    output = ordered(output_own, narrow_swap(output_own, 1))

    d_far = [wide_swap(v) for v in d_far]
    normed_two_sides = [normed_two_near, normed_two_near_other]
    gate_up_a = strip_rows_grad(
        [after(normed_two, d_query, down_a_got[-1], down_b_got[-1]), normed_two_other], normed_two_sides, dgu_a, dgu_a_near, tbl, strip, 8
    )
    gate_up_a_got, gate_up_a_mid = halve(gate_up_a, 0, d_far[1])
    d_far[0] = after(d_far[0], gate_up_a_mid)
    pairs = [
        (n.astype(F32) + f.astype(F32)).astype(BF) for n, f in zip(d_near[:-1], d_far[:-1])
    ]
    kv_got, kv_mid = halve([*pairs, d_near[-1]], 0)
    d_key, d_value = close_kv([d_near[-1], d_far[-1], *kv_got], cosine, sine)

    dgu_b_near = [wide_swap(after(v, d_query)) for v in dgu_b]
    gate_up_b = strip_rows_grad(
        [after(normed_two, gate_up_a_mid, kv_mid), normed_two_other],
        normed_two_sides,
        dgu_b,
        dgu_b_near,
        tbl,
        strip,
        7,
    )
    d_query_near = wide_swap(after(d_query, pairs[0]))
    gate_up_b_got, gate_up_b_mid = halve(gate_up_b, 0)
    d_attn_near, d_attn_strips, d_attn_other_strips = pack(
        [after(d_attn, gate_up_a[0]), d_attn_other],
        [[(0, low_rows, 1)], [(0, low_rows, 0)], [(1, low_rows, 0)]],
        tbl,
        strip,
    )
    d_attn_near = wide_swap(after(d_attn_near, pairs[0]))
    d_attn_near_other = narrow_swap(d_attn_near, 1)
    query_part = strip_rows_grad(
        [after(normed_one, gate_up_b[0])], near_sides, [d_query], [d_query_near], tbl, strip, 4
    )
    query_got, query_mid = halve(query_part, 0)
    out_part = strip_columns_grad(
        [after(mixed, query_part[0])],
        [mixed_near],
        [d_attn_strips, d_attn_other_strips],
        [d_attn_near, d_attn_near_other],
        turns,
        strip,
        tile,
        4,
    )
    out_got, out_mid = halve(out_part, 1)

    kv_width = w_key.shape[1]
    held, got = reduce_narrow(
        project([(d_query, w_query, 0), (d_key, w_key, 0), (d_value, w_value, 0)], "nt", 512, 6)
    )
    gain_one = gain_attn.astype(F32)
    scale_one = lax.rsqrt(jnp.mean(source * source, axis=1, keepdims=True) + EPSILON)
    d_normed_one = total_of(held, got)
    grad_own = (d_hidden + norm_backward(source, scale_one, gain_one, d_normed_one)).astype(BF)
    grad_tokens = ordered(grad_own, narrow_swap(grad_own, 1))

    d_key_near = wide_swap(d_key)
    d_value_near = wide_swap(d_value)
    kv_part = strip_rows_grad(
        [after(normed_one, out_part[0])],
        near_sides,
        [d_key, d_value],
        [d_key_near, d_value_near],
        tbl,
        strip,
        4,
    )
    kv_part_got, _ = halve(kv_part, 0)
    grad_kv = close(kv_part, kv_part_got, 0)
    grad_down_a = close(down_a, down_a_got, 1)
    grad_down_b = close(down_b, down_b_got, 1)
    grad_gate_up_a = close(gate_up_a, gate_up_a_got, 0)
    grad_gate_up_b = close(gate_up_b, gate_up_b_got, 0)
    grad_query = close(query_part, query_got, 0)
    grad_out = close(out_part, out_got, 1)
    grad_key, grad_value = grad_kv[:, :kv_width], grad_kv[:, kv_width:]
    grad_down = jnp.concatenate([grad_down_a, grad_down_b], axis=0)
    second_count = hidden - first_count
    grad_gate = jnp.concatenate(
        [grad_gate_up_a[:, :first_count], grad_gate_up_b[:, :second_count]], axis=1
    )
    grad_up = jnp.concatenate(
        [grad_gate_up_a[:, first_count:], grad_gate_up_b[:, second_count:]], axis=1
    )

    def strip_rows(weight):
        return lax.dynamic_slice_in_dim(weight, wide_index * strip, strip).astype(F32)

    def gain_grad(pairs, gain):
        local = sum(jnp.sum(strip_rows(w) * g, axis=1) for w, g in pairs)
        return local / lax.dynamic_slice_in_dim(gain, wide_index * strip, strip)

    local = jnp.stack(
        [
            gain_grad([(w_query, grad_query), (w_key, grad_key), (w_value, grad_value)], gain_one),
            gain_grad([(w_gate, grad_gate), (w_up, grad_up)], gain_two),
        ]
    )
    local = local + narrow_swap(local, 1)
    local = local + narrow_swap(local, 2)
    grad_gain_one, grad_gain_two = local[0], local[1]
    return (
        output,
        grad_tokens,
        grad_gain_one,
        grad_query,
        grad_key,
        grad_value,
        grad_out,
        grad_gain_two,
        grad_gate,
        grad_up,
        grad_down,
    )


def solution(mesh):
    placed = (
        P("wide", None),
        P("wide", None),
        P("wide"),
        P(),
        P(),
        P(),
        P(None, "narrow"),
        P(None, "narrow"),
        P(None, "narrow"),
        P("narrow", None),
        P(),
        P(None, "narrow"),
        P(None, "narrow"),
        P("narrow", None),
    )
    return jax.shard_map(
        shards,
        mesh=mesh,
        in_specs=placed,
        out_specs=(
            P("wide", None),
            P("wide", None),
            P("wide"),
            P("wide", "narrow"),
            P("wide", "narrow"),
            P("wide", "narrow"),
            P("narrow", "wide"),
            P("wide"),
            P("wide", "narrow"),
            P("wide", "narrow"),
            P("narrow", "wide"),
        ),
        check_vma=False,
    )
```

```python
import functools

import jax
import jax.numpy as jnp
import numpy as np
from jax import lax
from jax.experimental import pallas as pl
from jax.experimental.pallas import tpu as pltpu
from jax.sharding import PartitionSpec as P

HD = 128
EPSILON = 1e-05
NEGATIVE = -1e30
BASE = 10000.0
LOG2E = 1.4426950408889634
SCORE = HD ** (-0.5) * LOG2E
FACTOR = HD ** (-0.5)
BF = jnp.bfloat16
F32 = jnp.float32
NT = (((1,), (1,)), ((), ()))
TN = (((0,), (0,)), ((), ()))
NN = (((1,), (0,)), ((), ()))
VM = pl.BlockSpec(memory_space=pltpu.VMEM)
SM = pl.BlockSpec(memory_space=pltpu.SMEM)
ANY = pl.BlockSpec(memory_space=pl.ANY)


def dot(a, b, dims=(((1,), (0,)), ((), ()))):
    return lax.dot_general(a, b, dims, preferred_element_type=F32)


def narrow_swap(value, mask):
    pairs = [(n, n ^ mask) for n in range(lax.axis_size("narrow"))]
    return lax.ppermute(value, "narrow", pairs)


def wide_swap(value):
    return lax.ppermute(value, "wide", [(w, w ^ 1) for w in range(lax.axis_size("wide"))])


def wide_ring(value, group, hop=1):
    ring = group // 2
    pairs = []
    for w in range(lax.axis_size("wide")):
        base, member = w // group * group, w % group
        pairs.append((w, base + (member // 2 + hop) % ring * 2 + member % 2))
    return lax.ppermute(value, "wide", pairs)


def wide_flip(value, bit):
    return lax.ppermute(value, "wide", [(w, w ^ (2 << bit)) for w in range(lax.axis_size("wide"))])


def halving(count):
    groups = []
    step = 1
    while step < count:
        groups.append([k for k in range(count) if k % (2 * step) == step])
        step *= 2
    return [*groups, [0]]


def stretches(groups):
    starts, at = [], 0
    for group in groups:
        starts.append((at, len(group)))
        at += len(group)
    return starts


def rope(value, cosine, sine):
    return value * cosine + pltpu.roll(value, HD // 2, 1) * sine


def norm_kv_kernel(core, x_ref, gain_ref, wk_ref, wv_ref, cos_ref, sin_ref, normed_ref, *kv_refs):
    x = x_ref[...].astype(F32)
    scale = lax.rsqrt(jnp.mean(x * x, axis=1, keepdims=True) + EPSILON)
    normed = (x * scale * gain_ref[...].astype(F32)).astype(BF)
    normed_ref[...] = normed
    keys = dot(normed, wk_ref[...])
    values = dot(normed, wv_ref[...])
    for h, ref in enumerate(kv_refs):
        cols = slice(h * HD, (h + 1) * HD)
        ref[:, :HD] = rope(keys[:, cols], cos_ref[...], sin_ref[...]).astype(BF)
        ref[:, HD:] = values[:, cols].astype(BF)


def norm_kv(core, tokens, gain, wk, wv, cosine, sine):
    rows, width = tokens.shape
    half = rows // 2
    heads = wk.shape[1] // HD
    full = lambda w: pl.BlockSpec(w.shape, lambda i, c: (0, 0))
    outs = pl.pallas_call(
        norm_kv_kernel,
        out_shape=[jax.ShapeDtypeStruct((rows, width), BF)]
        + [jax.ShapeDtypeStruct((rows, 2 * HD), BF)] * heads,
        grid_spec=pltpu.PrefetchScalarGridSpec(
            num_scalar_prefetch=1,
            grid=(2,),
            in_specs=[
                pl.BlockSpec((half, width), lambda i, c: (i ^ c[0], 0)),
                full(gain),
                full(wk),
                full(wv),
                pl.BlockSpec((half, HD), lambda i, c: (i, 0)),
                pl.BlockSpec((half, HD), lambda i, c: (i, 0)),
            ],
            out_specs=[pl.BlockSpec((half, width), lambda i, c: (i, 0))]
            + [pl.BlockSpec((half, 2 * HD), lambda i, c: (i, 0))] * heads,
        ),
        cost_estimate=pl.CostEstimate(flops=int(2.9e9), bytes_accessed=0, transcendentals=0),
        name="norm_kv",
    )(core, tokens, gain, wk, wv, cosine, sine)
    return outs[0], outs[1:]


def query_kernel(x_ref, w_ref, cos_ref, sin_ref, out_ref):
    raw = dot(x_ref[...], w_ref[...])
    for h in range(raw.shape[1] // HD):
        cols = slice(h * HD, (h + 1) * HD)
        out_ref[:, cols] = rope(raw[:, cols], cos_ref[...], sin_ref[...]).astype(BF)


def query_proj(x, w, cosine, sine):
    rows, width = x.shape
    half = rows // 2
    return pl.pallas_call(
        query_kernel,
        out_shape=jax.ShapeDtypeStruct((rows, w.shape[1]), BF),
        grid=(2,),
        in_specs=[
            pl.BlockSpec((half, width), lambda i: (i, 0)),
            pl.BlockSpec(w.shape, lambda i: (0, 0)),
            pl.BlockSpec((half, HD), lambda i: (i, 0)),
            pl.BlockSpec((half, HD), lambda i: (i, 0)),
        ],
        out_specs=pl.BlockSpec((half, w.shape[1]), lambda i: (i, 0)),
        cost_estimate=pl.CostEstimate(flops=int(2.9e9), bytes_accessed=0, transcendentals=0),
        name="query_proj",
    )(x, w, cosine, sine)


def fetch_slots(slot_refs, slots, kv_ref, sems):
    rows, width = slot_refs[0].shape
    copies = []
    for at, ref in enumerate(slot_refs):
        head, slot = divmod(at, slots)
        spot = kv_ref.at[pl.ds(slot * rows, rows), pl.ds(head * width, width)]
        copies.append(pltpu.make_async_copy(ref, spot, sems.at[at]))
    for copy in copies:
        copy.start()
    for copy in copies:
        copy.wait()


def allowed(pk, size, span, pos, low):
    key_pos = pk * size + lax.broadcasted_iota(jnp.int32, (size, span), 0)
    return (key_pos <= pos) & (key_pos >= low)


def attn_fwd_kernel(slots, *refs):
    meta, q_ref, pos_ref, low_ref = refs[:4]
    slot_refs = refs[4 : 4 + slots]
    mixed_ref, lse_ref, kv_ref, acc_ref, sems = refs[-5:]
    fetch_slots(slot_refs, slots, kv_ref, sems)
    size = q_ref.shape[0] // 2
    for i in range(2):
        rows = slice(i * size, (i + 1) * size)
        pos = jnp.tile(pos_ref[0:1, rows], (1, 2))
        low = jnp.tile(low_ref[0:1, rows], (1, 2))
        queries = [q_ref[rows, r * HD : (r + 1) * HD] for r in range(2)]
        acc_ref[...] = jnp.zeros_like(acc_ref)

        def body(pk, carry):
            peak, total = carry
            spot = pl.multiple_of(meta[4 + pk] * size, size)
            keys = kv_ref[pl.ds(spot, size), :HD]
            values = kv_ref[pl.ds(spot, size), HD:]
            scores = jnp.concatenate([dot(keys, q, NT) for q in queries], axis=1) * SCORE
            scores = jnp.where(allowed(pk, size, 2 * size, pos, low), scores, NEGATIVE)
            peak_new = jnp.maximum(peak, jnp.max(scores, axis=0, keepdims=True))
            alpha = jnp.exp2(peak - peak_new)
            probs = jnp.exp2(scores - peak_new)
            total = total * alpha + jnp.sum(probs, axis=0, keepdims=True)
            acc_ref[...] = acc_ref[...] * alpha + dot(values, probs.astype(BF), TN)
            return peak_new, total

        start = (jnp.full((1, 2 * size), NEGATIVE, F32), jnp.zeros((1, 2 * size), F32))
        peak, total = lax.fori_loop(meta[i], meta[2 + i] + 1, body, start)
        lse_ref[i : i + 1, :] = peak + jnp.log2(total)
        out = acc_ref[...] * (1.0 / total)
        for r in range(2):
            mixed_ref[rows, r * HD : (r + 1) * HD] = out[:, r * size : (r + 1) * size].T.astype(BF)


def attn_fwd(head, meta, q, pos, low, slots, mixed):
    rows = q.shape[0]
    count = len(slots)
    earlier = [] if mixed is None else [mixed]
    return pl.pallas_call(
        functools.partial(attn_fwd_kernel, count),
        out_shape=(
            jax.ShapeDtypeStruct(q.shape, BF),
            jax.ShapeDtypeStruct((2, rows), F32),
        ),
        grid=(1,),
        in_specs=[
            SM,
            pl.BlockSpec((rows, 2 * HD), lambda i: (0, head)),
            pl.BlockSpec(pos.shape, lambda i: (0, 0)),
            pl.BlockSpec(low.shape, lambda i: (0, 0)),
        ]
        + [ANY] * (count + len(earlier)),
        out_specs=[
            pl.BlockSpec((rows, 2 * HD), lambda i: (0, head)),
            pl.BlockSpec((2, rows), lambda i: (0, 0)),
        ],
        input_output_aliases={4 + count: 0} if earlier else {},
        scratch_shapes=[
            pltpu.VMEM((count * rows, 2 * HD), BF),
            pltpu.VMEM((HD, rows), F32),
            pltpu.SemaphoreType.DMA((count,)),
        ],
        cost_estimate=pl.CostEstimate(flops=int(1e9), bytes_accessed=0, transcendentals=0),
        name="attn_fwd",
    )(meta, q, pos, low, *slots, *earlier)


def attn_bwd_kernel(heads, slots, groups, *refs):
    meta, q_ref, pos_ref, low_ref, dmix_ref, mixed_ref, cos_ref, sin_ref = refs[:8]
    lse_refs = refs[8 : 8 + heads]
    at = 8 + heads
    slot_refs = refs[at : at + heads * slots]
    at += heads * slots
    dq_ref, dkv_refs = refs[at], refs[at + 1 : -4]
    kv_ref, dkv_ref, dq_acc, sems = refs[-4:]
    fetch_slots(slot_refs, slots, kv_ref, sems)
    dkv_ref[...] = jnp.zeros_like(dkv_ref)
    rows_all = q_ref.shape[0]
    size = rows_all // 2
    for i in range(2):
        rows = slice(i * size, (i + 1) * size)
        pos = jnp.tile(pos_ref[0:1, rows], (1, 2))
        low = jnp.tile(low_ref[0:1, rows], (1, 2))
        for g in range(heads):
            cols = [slice((2 * g + r) * HD, (2 * g + r + 1) * HD) for r in range(2)]
            queries = jnp.concatenate([q_ref[rows, c] for c in cols], axis=0)
            grads = jnp.concatenate([dmix_ref[rows, c] for c in cols], axis=0)
            outs = jnp.concatenate([mixed_ref[rows, c] for c in cols], axis=0)
            delta = jnp.sum((grads.astype(F32) * outs.astype(F32)).T, axis=0, keepdims=True)
            lse = lse_refs[g][i : i + 1, :]
            dq_acc[...] = jnp.zeros_like(dq_acc)

            def body(pk, carry):
                spot = pl.multiple_of(meta[4 + pk] * size, size)
                key_cols = slice(2 * g * HD, (2 * g + 1) * HD)
                value_cols = slice((2 * g + 1) * HD, (2 * g + 2) * HD)
                keys = kv_ref[pl.ds(spot, size), key_cols]
                values = kv_ref[pl.ds(spot, size), value_cols]
                scores = dot(keys, queries, NT) * SCORE
                probs = jnp.where(
                    allowed(pk, size, 2 * size, pos, low), jnp.exp2(scores - lse), 0.0
                )
                d_probs = dot(values, grads, NT)
                d_scores = (probs * (d_probs - delta)).astype(BF)
                dkv_ref[pl.ds(spot, size), value_cols] += dot(probs.astype(BF), grads)
                dkv_ref[pl.ds(spot, size), key_cols] += dot(d_scores, queries) * FACTOR
                dq_acc[...] += dot(d_scores, keys, TN)
                return carry

            lax.fori_loop(meta[i], meta[2 + i] + 1, body, 0)
            for r in range(2):
                part = dq_acc[r * size : (r + 1) * size, :] * FACTOR
                dq_ref[rows, cols[r]] = rope(part, cos_ref[rows, :], -sin_ref[rows, :]).astype(BF)
    ring = slots // 2
    for j, ref in enumerate(dkv_refs):
        first = ring * (j // len(groups))
        for place, k in enumerate(groups[j % len(groups)]):
            spot = pl.multiple_of((first + meta[4 + 2 * slots + k]) * rows_all, rows_all)
            ref[place * rows_all : (place + 1) * rows_all, :] = dkv_ref[
                pl.ds(spot, rows_all), :
            ].astype(BF)


def attn_bwd(meta, q, pos, low, lse, mixed, dmix, cosine, sine, slots):
    rows, q_width = q.shape
    heads, count = len(slots), len(slots[0])
    kv_width = heads * 2 * HD
    groups = halving(count // 2)
    outs = pl.pallas_call(
        functools.partial(attn_bwd_kernel, heads, count, groups),
        out_shape=[jax.ShapeDtypeStruct((rows, q_width), BF)]
        + [jax.ShapeDtypeStruct((len(g) * rows, kv_width), BF) for g in groups] * 2,
        in_specs=[SM] + [VM] * (7 + heads) + [ANY] * (heads * count),
        out_specs=[VM] * (1 + 2 * len(groups)),
        scratch_shapes=[
            pltpu.VMEM((count * rows, kv_width), BF),
            pltpu.VMEM((count * rows, kv_width), F32),
            pltpu.VMEM((rows, HD), F32),
            pltpu.SemaphoreType.DMA((heads * count,)),
        ],
        cost_estimate=pl.CostEstimate(flops=int(2e9), bytes_accessed=0, transcendentals=0),
        name="attn_bwd",
    )(meta, q, pos, low, dmix, mixed, cosine, sine, *lse, *[v for head in slots for v in head])
    return outs[0], outs[1 : 1 + len(groups)], outs[1 + len(groups) :]


def cost(micros):
    return pl.CostEstimate(flops=int(micros * 0.3e9), bytes_accessed=0, transcendentals=0)


def split_rows(total, own_ref, other_ref):
    half = own_ref.shape[0]
    own_ref[...] = total[:half].astype(BF)
    other_ref[...] = total[half:].astype(BF)


def project_kernel(spec, *refs):
    total = None
    for a, b, offset, dims in spec:
        left = refs[a][...] if dims is not None else None
        if dims == "nt":
            right, form = refs[b][:, offset : offset + left.shape[1]], NT
        else:
            right, form = refs[b][offset : offset + left.shape[1], :], NN
        term = dot(left, right, form)
        total = term if total is None else total + term
    split_rows(total, refs[-2], refs[-1])


def project(pairs, dims, tile, micros):
    operands, specs, plan, weights = [], [], [], []
    for a, b, offset in pairs:
        operands.append(a)
        specs.append(pl.BlockSpec(a.shape, lambda i: (0, 0)))
        spot = next((at for at, seen in weights if seen is b), None)
        left = len(operands) - 1
        if spot is None:
            spot = len(operands)
            operands.append(b)
            weights.append((spot, b))
            if dims == "nt":
                specs.append(pl.BlockSpec((tile, b.shape[1]), lambda i: (i, 0)))
            else:
                specs.append(pl.BlockSpec((b.shape[0], tile), lambda i: (0, i)))
        plan.append((left, spot, offset, dims))
    rows = pairs[0][0].shape[0]
    width = pairs[0][1].shape[0 if dims == "nt" else 1]
    return pl.pallas_call(
        functools.partial(project_kernel, plan),
        out_shape=[jax.ShapeDtypeStruct((rows // 2, width), BF)] * 2,
        grid=(width // tile,),
        in_specs=specs,
        out_specs=[pl.BlockSpec((rows // 2, tile), lambda i: (0, i))] * 2,
        cost_estimate=cost(micros),
        name="project",
    )(*operands)


def back_dense_kernel(gate_a, up_a, gate_b, up_b, wg_ref, wu_ref, own_ref, other_ref):
    total = None
    offset = 0
    for group in ((gate_a, up_a), (gate_b, up_b)):
        count = group[0].shape[1]
        for ref, w_ref in zip(group, (wg_ref, wu_ref)):
            term = dot(ref[...], w_ref[:, offset : offset + count], NT)
            total = term if total is None else total + term
        offset += count
    split_rows(total, own_ref, other_ref)


def back_dense(grads, w_gate, w_up, tile, part, parts):
    width, hidden = w_gate.shape[0] // parts, w_gate.shape[1]
    rows = grads[0].shape[0]
    ahead = part * (width // tile)
    weight = pl.BlockSpec((tile, hidden), lambda i: (ahead + i, 0))
    return pl.pallas_call(
        back_dense_kernel,
        out_shape=[jax.ShapeDtypeStruct((rows // 2, width), BF)] * 2,
        grid=(width // tile,),
        in_specs=[pl.BlockSpec(v.shape, lambda i: (0, 0)) for v in grads] + [weight, weight],
        out_specs=[pl.BlockSpec((rows // 2, tile), lambda i: (0, i))] * 2,
        cost_estimate=cost(11 / parts),
        name="back_dense",
    )(*grads, w_gate, w_up)


def gated_kernel(own_ref, other_ref, wg_ref, wu_ref, di_ref, inner_ref, dg_ref, du_ref, all_ref):
    @pl.when(pl.program_id(0) == 0)
    def _():
        half = own_ref.shape[0]
        all_ref[:half, :] = own_ref[...]
        all_ref[half:, :] = other_ref[...]

    gate = dot(all_ref[...], wg_ref[...])
    up = dot(all_ref[...], wu_ref[...])
    sigma = 1.0 / (1.0 + jnp.exp(-gate))
    silu = gate * sigma
    d_inner = di_ref[...]
    inner_ref[...] = (silu * up).astype(BF)
    dg_ref[...] = (d_inner * up * sigma * (1.0 + gate * (1.0 - sigma))).astype(BF)
    du_ref[...] = (d_inner * silu).astype(BF)


def gated(own, other, wg, wu, d_inner, first, columns, tile):
    half, width = own.shape
    weight = pl.BlockSpec((width, tile), lambda i: (0, first // tile + i))
    whole = pl.BlockSpec((half, width), lambda i: (0, 0))
    return pl.pallas_call(
        gated_kernel,
        out_shape=[jax.ShapeDtypeStruct((2 * half, columns), BF)] * 3,
        grid=(pl.cdiv(columns, tile),),
        in_specs=[
            whole,
            whole,
            weight,
            weight,
            pl.BlockSpec((2 * half, tile), lambda i: (0, first // tile + i)),
        ],
        out_specs=[pl.BlockSpec((2 * half, tile), lambda i: (0, i))] * 3,
        scratch_shapes=[pltpu.VMEM((2 * half, width), BF)],
        cost_estimate=cost(7.5),
        name="gated",
    )(own, other, wg, wu, d_inner)


def mixed_grad_kernel(own_ref, other_ref, w_ref, out_ref):
    both = jnp.concatenate([own_ref[...], other_ref[...]], axis=0)
    out_ref[...] = dot(both, w_ref[...], NT).astype(BF)


def mixed_grad(own, other, w):
    return pl.pallas_call(
        mixed_grad_kernel,
        out_shape=jax.ShapeDtypeStruct((2 * own.shape[0], w.shape[0]), BF),
        in_specs=[VM] * 3,
        out_specs=VM,
        cost_estimate=cost(4),
        name="mixed_grad",
    )(own, other, w)


def d_inner_kernel(x_ref, w_ref, out_ref):
    out_ref[...] = dot(x_ref[...], w_ref[...], NT)


def inner_grad(x, w, tile):
    rows, width = x.shape
    hidden = w.shape[0]
    return pl.pallas_call(
        d_inner_kernel,
        out_shape=jax.ShapeDtypeStruct((rows, hidden), F32),
        grid=(pl.cdiv(hidden, tile),),
        in_specs=[
            pl.BlockSpec((rows, width), lambda i: (0, 0)),
            pl.BlockSpec((tile, width), lambda i: (i, 0)),
        ],
        out_specs=pl.BlockSpec((rows, tile), lambda i: (0, i)),
        cost_estimate=cost(8),
        name="inner_grad",
    )(x, w)


def pack_kernel(count, plan, strip, tbl, *refs):
    ins, outs = refs[:count], refs[count:]
    for out_ref, pieces in zip(outs, plan):
        column = 0
        for at, rows, row in pieces:
            for k in range(tbl.shape[1]):
                first = pl.multiple_of(tbl[row, k] * strip, 128)
                out_ref[:, column : column + strip] = ins[at][rows, pl.ds(first, strip)]
                column += strip


def pack(values, plan, tbl, strip):
    turns = tbl.shape[1]
    if strip % 128:
        cut = lambda v, rows, at: lax.dynamic_slice_in_dim(v[rows], at * strip, strip, axis=1)
        return [
            jnp.concatenate(
                [cut(values[at], rows, tbl[row, k]) for at, rows, row in pieces for k in range(turns)],
                axis=1,
            )
            for pieces in plan
        ]
    return pl.pallas_call(
        functools.partial(pack_kernel, len(values), plan, strip),
        out_shape=[
            jax.ShapeDtypeStruct(
                (p[0][1].stop - p[0][1].start, len(p) * turns * strip), values[0].dtype
            )
            for p in plan
        ],
        in_specs=[SM] + [VM] * len(values),
        out_specs=[VM] * len(plan),
        cost_estimate=cost(1.5),
        name="pack",
    )(tbl, *values)


def strip_rows_kernel(halves, near, rights, nears, spans, tbl, *refs):
    left = refs[:halves]
    left_near = refs[halves : halves + near]
    right = refs[halves + near : halves + near + rights]
    right_near = refs[halves + near + rights : halves + near + rights + nears]
    outs = refs[halves + near + rights + nears :]
    step = pl.program_id(0)
    join = lambda group: (
        group[0][...] if len(group) == 1 else jnp.concatenate([r[...] for r in group], axis=0)
    )
    mine, theirs = join(left), join(left_near)
    pieces = []
    for r, n in zip(right, right_near):
        planes = range(r.shape[0]) if len(r.shape) == 3 else [None]
        for k in planes:
            a = r[...] if k is None else r[k]
            b = n[...] if k is None else n[k]
            pieces.append((dot(mine, a, TN) + dot(theirs, b, TN)).astype(BF))
    for (start, length), out in zip(spans, outs):

        @pl.when((step >= start) & (step < start + length))
        def _(out=out):
            column = 0
            for piece in pieces:
                out[:, column : column + piece.shape[1]] = piece
                column += piece.shape[1]


def strip_rows_grad(left, left_near, right, right_near, tbl, strip, micros):
    turns = tbl.shape[1]
    columns = sum(r.shape[-1] * (r.shape[0] if r.ndim == 3 else 1) for r in right)
    spans = stretches(halving(turns))
    if strip % 128:
        near = jnp.concatenate(left_near, axis=0)
        mine = jnp.concatenate(left, axis=0)
        flat = lambda r: [r] if r.ndim == 2 else [r[k] for k in range(r.shape[0])]
        outs = []
        for start, length in spans:
            group = []
            for k in range(start, start + length):
                a = lax.dynamic_slice_in_dim(mine, tbl[0, k] * strip, strip, axis=1)
                b = near[:, k * strip : (k + 1) * strip]
                group.append(
                    jnp.concatenate(
                        [
                            dot(a, x, TN) + dot(b, y, TN)
                            for r, n in zip(right, right_near)
                            for x, y in zip(flat(r), flat(n))
                        ],
                        axis=1,
                    ).astype(BF)
                )
            outs.append(jnp.concatenate(group, axis=0))
        return outs
    held = lambda start, length: (lambda i, t: (jnp.clip(i - start, 0, length - 1), 0))
    whole = lambda v: pl.BlockSpec(v.shape, lambda i, t: (0,) * v.ndim)
    return pl.pallas_call(
        functools.partial(
            strip_rows_kernel, len(left), len(left_near), len(right), len(right_near), spans
        ),
        out_shape=[jax.ShapeDtypeStruct((length * strip, columns), BF) for _, length in spans],
        grid_spec=pltpu.PrefetchScalarGridSpec(
            num_scalar_prefetch=1,
            grid=(turns,),
            in_specs=[pl.BlockSpec((v.shape[0], strip), lambda i, t: (0, t[0, i])) for v in left]
            + [pl.BlockSpec((v.shape[0], strip), lambda i, t: (0, i)) for v in left_near]
            + [whole(v) for v in [*right, *right_near]],
            out_specs=[pl.BlockSpec((strip, columns), held(*span)) for span in spans],
        ),
        cost_estimate=cost(micros),
        name="strip_rows",
    )(tbl, *left, *left_near, *right, *right_near)


def strip_columns_kernel(parts, halves, near, strip, spans, *refs):
    at = 2 * parts
    right, right_near = refs[at : at + halves], refs[at + halves : at + halves + near]
    outs = refs[at + halves + near :]
    first = 0
    for p in range(parts):
        total = None
        for ref, group in ((refs[p], right), (refs[parts + p], right_near)):
            row = 0
            for r in group:
                term = dot(ref[row : row + r.shape[0], :], r[...], TN)
                total = term if total is None else total + term
                row += r.shape[0]
        for (start, length), out in zip(spans, outs):
            out[first : first + total.shape[0], :] = total[
                :, start * strip : (start + length) * strip
            ].astype(BF)
        first += total.shape[0]


def strip_columns_grad(left, left_near, right, right_near, turns, strip, tile, micros, near_at=0):
    rows, count = left[0].shape[0], sum(v.shape[1] for v in left)
    if strip * turns % 128:
        raise ValueError(strip)
    spans = stretches(halving(turns))
    whole = lambda v: pl.BlockSpec(v.shape, lambda i: (0, 0))
    near = lambda v: pl.BlockSpec((v.shape[0], turns * strip), lambda i: (0, near_at))
    if len(left) == 1:
        left_specs = [pl.BlockSpec((rows, tile), lambda i: (0, i))] * 2
    else:
        tile = count
        left_specs = [whole(v) for v in [*left, *left_near]]
    return pl.pallas_call(
        functools.partial(
            strip_columns_kernel, len(left), len(right), len(right_near), strip, spans
        ),
        out_shape=[jax.ShapeDtypeStruct((count, length * strip), BF) for _, length in spans],
        grid=(pl.cdiv(count, tile),),
        in_specs=left_specs + [whole(v) for v in right] + [near(v) for v in right_near],
        out_specs=[pl.BlockSpec((tile, length * strip), lambda i: (i, 0)) for _, length in spans],
        cost_estimate=cost(micros),
        name="strip_columns",
    )(*left, *left_near, *right, *right_near)


def close_kv_kernel(count, *refs):
    cos_ref, sin_ref, dk_ref, dv_ref = refs[count:]
    total = refs[0][...].astype(F32)
    for ref in refs[1:count]:
        total = total + ref[...].astype(F32)
    heads = dk_ref.shape[1] // HD
    for h in range(heads):
        cols = slice(h * HD, (h + 1) * HD)
        keys = total[:, 2 * h * HD : (2 * h + 1) * HD]
        dk_ref[:, cols] = rope(keys, cos_ref[...], -sin_ref[...]).astype(BF)
        dv_ref[:, cols] = total[:, (2 * h + 1) * HD : (2 * h + 2) * HD].astype(BF)


def close_kv(terms, cosine, sine):
    rows, width = terms[0].shape
    first = lambda w: pl.BlockSpec((rows, w), lambda i: (0, 0))
    return pl.pallas_call(
        functools.partial(close_kv_kernel, len(terms)),
        out_shape=[jax.ShapeDtypeStruct((rows, width // 2), BF)] * 2,
        grid=(1,),
        in_specs=[first(width)] * len(terms) + [first(HD)] * 2,
        out_specs=[first(width // 2)] * 2,
        cost_estimate=cost(1.5),
        name="close_kv",
    )(*terms, cosine, sine)


def norm_backward(source, scale_rows, gain, upstream):
    weighted = upstream * gain
    average = jnp.mean(weighted * source, axis=1, keepdims=True)
    return scale_rows * weighted - source * scale_rows**3 * average


def after(value, *done):
    return lax.optimization_barrier((value, *done))[0]


def shards(
    tokens,
    cotangent,
    keep_mask,
    doc_lengths,
    block_order,
    gain_attn,
    w_query,
    w_key,
    w_value,
    w_out,
    gain_dense,
    w_gate,
    w_up,
    w_down,
):
    rows, width = tokens.shape
    half = rows // 2
    wide = lax.axis_size("wide")
    group = wide // block_order.shape[0]
    ring = group // 2
    wide_index = lax.axis_index("wide")
    member = wide_index % group
    seq_index = wide_index // group
    side = (wide_index % 2).astype(jnp.int32)
    core = lax.axis_index("narrow") % 2
    strip = width // wide
    turns = wide // 2

    def ordered(mine, other):
        return jnp.where(
            core == 0,
            jnp.concatenate([mine, other], axis=0),
            jnp.concatenate([other, mine], axis=0),
        )

    def own_half(value):
        return lax.dynamic_slice_in_dim(value, core * half, half)

    def other_half(value):
        return lax.dynamic_slice_in_dim(value, (1 - core) * half, half)

    order_row = lax.dynamic_index_in_dim(block_order, seq_index, 0, keepdims=False)
    length_row = lax.dynamic_index_in_dim(doc_lengths, seq_index, 0, keepdims=False)
    doc_ends = jnp.cumsum(length_row)
    places = jnp.stack([member * 2 + core, member * 2 + 1 - core])
    chosen = jnp.sum(
        jnp.where(places[:, None] == jnp.arange(2 * group)[None, :], order_row[None, :], 0), axis=1
    )
    pos = (chosen[:, None] * half + jnp.arange(half, dtype=jnp.int32)[None, :]).reshape(-1)
    low = jnp.max(jnp.where(doc_ends[None, :] <= pos[:, None], doc_ends[None, :], 0), axis=1)
    block_low = low.reshape(2, half)[:, 0] // half
    stored = jnp.sum(
        jnp.where(
            order_row[None, :] == jnp.arange(2 * group)[:, None], jnp.arange(2 * group)[None, :], 0
        ),
        axis=1,
    )
    owner = stored // 2
    slot = (member // 2 - owner // 2) % ring + ring * (owner % 2 != side).astype(jnp.int32)
    spots = slot * 2 + (stored % 2 != core).astype(jnp.int32)
    place = member // 2
    back = (place - (place ^ jnp.arange(ring, dtype=jnp.int32))) % ring
    meta = jnp.concatenate([block_low, chosen, spots, back]).astype(jnp.int32)
    frequency = BASE ** (-(jnp.arange(HD // 2, dtype=F32) * 2.0) / HD)
    angles = pos.astype(F32)[:, None] * frequency[None, :]
    cosine = jnp.cos(angles)
    sine = jnp.sin(angles)
    cosine = jnp.concatenate([cosine, cosine], axis=1)
    sine = jnp.concatenate([-sine, sine], axis=1)
    pos_row = pos[None, :]
    low_row = low[None, :]

    order = np.array([k for stretch in halving(turns) for k in stretch], np.int32)
    turn_row = wide_index // 2 ^ order
    tbl = jnp.stack([2 * turn_row + side, 2 * turn_row + 1 - side]).astype(jnp.int32)
    core_arr = core.astype(jnp.int32)[None]
    normed_one, both = norm_kv(core_arr, tokens, gain_attn[None, :], w_key, w_value, cosine, sine)
    low_rows, all_rows = slice(0, half), slice(0, rows)

    def together(*values):
        return list(lax.optimization_barrier(values))

    near, far = [[v] for v in both], [[] for v in both]
    query = d_dense = d_inner = input_near = d_dense_strips = None
    for step in range(ring):
        for head in range(len(both)):
            held = near[head][step]
            if step + 1 < ring:
                sent = [wide_swap(held), wide_ring(held, group)]
            elif head == 0:
                sent = [wide_swap(held)]
            else:
                sent = [wide_ring(far[head][0], group, -1)]
            beside = []
            if step == 0 and head == 0:
                beside = [query_proj(normed_one, w_query, cosine, sine)]
            if step == 0 and head == 1:
                keep_rel = jnp.concatenate([own_half(keep_mask), other_half(keep_mask)])[:, None]
                cot_rel = jnp.concatenate([own_half(cotangent), other_half(cotangent)])
                beside = [jnp.where(keep_rel > 0, cot_rel, jnp.zeros_like(cot_rel))]
            if step == 1 and head == 0:
                beside = [inner_grad(d_dense, w_down, 256)]
            if step == 2 and head == 0:
                beside = pack(
                    [normed_one, d_dense],
                    [[(0, low_rows, 1), (1, low_rows, 1)], [(1, all_rows, 0)]],
                    tbl,
                    strip,
                )
            done = together(*sent, *beside)
            far[head].append(done[0])
            if step + 1 < ring:
                near[head].append(done[1])
            if step == 0 and head == 0:
                query = done[-1]
            if step == 0 and head == 1:
                d_dense = done[-1]
            if step == 1 and head == 0:
                d_inner = done[-1]
            if step == 2 and head == 0:
                input_near, d_dense_strips = done[-2:]
    slots = [n + f for n, f in zip(near, far)]
    input_near = wide_swap(after(input_near, *slots[0], *slots[-1]))
    mixed, lse = None, []
    for h, held in enumerate(slots):
        mixed, part = attn_fwd(h, meta, query, pos_row, low_row, held, mixed)
        lse.append(part)

    def reduce_narrow(halves, hold=()):
        own_part, other_part = halves
        got = narrow_swap(other_part, 1)
        held = (own_part.astype(F32) + got.astype(F32)).astype(BF)
        return held, narrow_swap(held, 2)

    def total_of(held, got):
        return held.astype(F32) + got.astype(F32)

    part = project([(mixed, w_out, 0)], "nn", 1024, 4)
    held, got = reduce_narrow((part[0], after(part[1], input_near)))
    mixed_near = wide_swap(mixed)
    input_near_other = narrow_swap(input_near, 1)
    source = own_half(tokens).astype(F32)
    keep_own = own_half(keep_mask).astype(F32)[:, None]
    hidden_one = source + keep_own * total_of(held, got)
    gain_two = gain_dense.astype(F32)
    scale_two = lax.rsqrt(jnp.mean(hidden_one * hidden_one, axis=1, keepdims=True) + EPSILON)
    normed_two = (hidden_one * scale_two * gain_two).astype(BF)
    normed_two_other = narrow_swap(after(normed_two, mixed_near), 1)
    hidden = w_gate.shape[1]
    tile = 256
    first_count = 3 * tile
    inner_a, *dgu_a = gated(
        normed_two, normed_two_other, w_gate, w_up, d_inner, 0, first_count, tile
    )
    inner_a_near = wide_swap(inner_a)
    inner_b, *dgu_b = gated(
        after(normed_two, inner_a),
        normed_two_other,
        w_gate,
        w_up,
        d_inner,
        first_count,
        hidden - first_count,
        tile,
    )
    back = back_dense([*dgu_a, *dgu_b], w_gate, w_up, 512, 0, 1)
    held, got = reduce_narrow((back[0], after(back[1], inner_a_near)))

    def halve(parts, axis, hold=None):
        groups = halving(1 << (len(parts) - 1))
        size = parts[-1].shape[axis]
        received, sent = [], None
        for bit, group in enumerate(groups[:-1]):
            sent = parts[bit]
            if bit:
                total = sent.astype(F32)
                for early, value in enumerate(received):
                    there = [k ^ (1 << early) for k in groups[early]]
                    pick = [
                        lax.slice_in_dim(value, size * there.index(k), size * (there.index(k) + 1), axis=axis)
                        for k in group
                    ]
                    total = total + (pick[0] if len(pick) == 1 else jnp.concatenate(pick, axis)).astype(F32)
                sent = total.astype(BF)
            got = wide_flip(sent, bit)
            received.append(got if hold is None else after(got, hold))
        return received, sent

    def close(parts, received, axis):
        size = parts[-1].shape[axis]
        total = parts[-1].astype(F32)
        for value in received:
            total = total + lax.slice_in_dim(value, 0, size, axis=axis).astype(F32)
        return total

    near_sides = [input_near, input_near_other]
    down_a = strip_columns_grad(
        [after(inner_a, held)],
        [inner_a_near],
        [d_dense_strips],
        near_sides,
        turns,
        strip,
        tile,
        4,
        1,
    )
    inner_b_near = wide_swap(inner_b)
    down_a_got, down_a_mid = halve(down_a, 1)
    dgu_a_near = [wide_swap(after(v, inner_b)) for v in dgu_a]
    dense_parts = project(
        [(after(inner_a, down_a[0], inner_b_near), w_down, 0), (inner_b, w_down, first_count)], "nn", 512, 6
    )
    (normed_two_near,) = pack([after(normed_two, dense_parts[0])], [[(0, low_rows, 1)]], tbl, strip)
    normed_two_near = wide_swap(normed_two_near)
    down_b = strip_columns_grad(
        [after(inner_b, dense_parts[0])], [inner_b_near], [d_dense_strips], near_sides, turns, strip, tile, 4, 1
    )

    got = after(got, dense_parts[0], down_b[0])
    upstream = own_half(cotangent).astype(F32)
    d_hidden = upstream + norm_backward(hidden_one, scale_two, gain_two, total_of(held, got))
    d_attn = (keep_own * d_hidden).astype(BF)
    d_attn_other = narrow_swap(after(d_attn, dgu_a_near[0], down_a_mid), 1)

    d_mixed = mixed_grad(d_attn, d_attn_other, w_out)
    d_query, d_near, d_far = attn_bwd(
        meta, query, pos_row, low_row, lse, mixed, d_mixed, cosine, sine, slots
    )
    held_out, got_out = reduce_narrow((dense_parts[0], after(dense_parts[1], d_mixed)))
    output_own = (hidden_one + keep_own * total_of(held_out, got_out)).astype(BF)
    output = ordered(output_own, narrow_swap(output_own, 1))

    down_b_got, down_b_mid = halve(down_b, 1, d_query)
    normed_two_near_other = narrow_swap(after(normed_two_near, d_query), 1)
    normed_two_sides = [normed_two_near, normed_two_near_other]
    gate_up_a = strip_rows_grad(
        [after(normed_two, d_query, down_b_mid), normed_two_other], normed_two_sides, dgu_a, dgu_a_near, tbl, strip, 8
    )
    gate_up_a_got, gate_up_a_mid = halve(gate_up_a, 0)
    d_far = [wide_swap(v) for v in d_far]
    d_far[0] = after(d_far[0], gate_up_a_mid)
    pairs = [
        (n.astype(F32) + f.astype(F32)).astype(BF) for n, f in zip(d_near[:-1], d_far[:-1])
    ]
    kv_got, kv_mid = halve([*pairs, d_near[-1]], 0)
    d_key, d_value = close_kv([d_near[-1], d_far[-1], *kv_got], cosine, sine)

    dgu_b_near = [wide_swap(after(v, d_query)) for v in dgu_b]
    gate_up_b = strip_rows_grad(
        [after(normed_two, gate_up_a_mid, kv_mid), normed_two_other],
        normed_two_sides,
        dgu_b,
        dgu_b_near,
        tbl,
        strip,
        7,
    )
    d_query_near = wide_swap(after(d_query, pairs[0]))
    gate_up_b_got, gate_up_b_mid = halve(gate_up_b, 0)
    d_attn_near, d_attn_strips, d_attn_other_strips = pack(
        [after(d_attn, gate_up_a[0]), d_attn_other],
        [[(0, low_rows, 1)], [(0, low_rows, 0)], [(1, low_rows, 0)]],
        tbl,
        strip,
    )
    d_attn_near = wide_swap(after(d_attn_near, pairs[0]))
    d_attn_near_other = narrow_swap(after(d_attn_near, gate_up_b[0]), 1)
    query_part = strip_rows_grad(
        [after(normed_one, gate_up_b[0])], near_sides, [d_query], [d_query_near], tbl, strip, 4
    )
    out_part = strip_columns_grad(
        [after(mixed, query_part[0])],
        [mixed_near],
        [d_attn_strips, d_attn_other_strips],
        [d_attn_near, d_attn_near_other],
        turns,
        strip,
        tile,
        4,
    )

    kv_width = w_key.shape[1]
    held, got = reduce_narrow(
        project([(d_query, w_query, 0), (d_key, w_key, 0), (d_value, w_value, 0)], "nt", 512, 6)
    )
    gain_one = gain_attn.astype(F32)
    scale_one = lax.rsqrt(jnp.mean(source * source, axis=1, keepdims=True) + EPSILON)
    d_normed_one = total_of(held, got)
    grad_own = (d_hidden + norm_backward(source, scale_one, gain_one, d_normed_one)).astype(BF)
    grad_tokens = ordered(grad_own, narrow_swap(grad_own, 1))

    d_key_near = wide_swap(d_key)
    d_value_near = wide_swap(d_value)
    kv_part = strip_rows_grad(
        [after(normed_one, out_part[0])],
        near_sides,
        [d_key, d_value],
        [d_key_near, d_value_near],
        tbl,
        strip,
        4,
    )
    kv_part_got, _ = halve(kv_part, 0)
    query_got, query_mid = halve(query_part, 0, kv_part[0])
    out_got, out_mid = halve(out_part, 1, kv_part[0])
    kv_part_got[-1] = after(kv_part_got[-1], grad_own, output)
    grad_kv = close(kv_part, kv_part_got, 0)
    grad_down_a = close(down_a, down_a_got, 1)
    grad_down_b = close(down_b, down_b_got, 1)
    grad_gate_up_a = close(gate_up_a, gate_up_a_got, 0)
    grad_gate_up_b = close(gate_up_b, gate_up_b_got, 0)
    grad_query = close(query_part, query_got, 0)
    grad_out = close(out_part, out_got, 1)
    grad_key, grad_value = grad_kv[:, :kv_width], grad_kv[:, kv_width:]
    grad_down = jnp.concatenate([grad_down_a, grad_down_b], axis=0)
    second_count = hidden - first_count
    grad_gate = jnp.concatenate(
        [grad_gate_up_a[:, :first_count], grad_gate_up_b[:, :second_count]], axis=1
    )
    grad_up = jnp.concatenate(
        [grad_gate_up_a[:, first_count:], grad_gate_up_b[:, second_count:]], axis=1
    )

    def strip_rows(weight):
        return lax.dynamic_slice_in_dim(weight, wide_index * strip, strip).astype(F32)

    def gain_grad(pairs, gain):
        local = sum(jnp.sum(strip_rows(w) * g, axis=1) for w, g in pairs)
        return local / lax.dynamic_slice_in_dim(gain, wide_index * strip, strip)

    local = jnp.stack(
        [
            gain_grad([(w_query, grad_query), (w_key, grad_key), (w_value, grad_value)], gain_one),
            gain_grad([(w_gate, grad_gate), (w_up, grad_up)], gain_two),
        ]
    )
    local = local + narrow_swap(local, 1)
    local = local + narrow_swap(local, 2)
    grad_gain_one, grad_gain_two = local[0], local[1]
    return (
        output,
        grad_tokens,
        grad_gain_one,
        grad_query,
        grad_key,
        grad_value,
        grad_out,
        grad_gain_two,
        grad_gate,
        grad_up,
        grad_down,
    )


def solution(mesh):
    placed = (
        P("wide", None),
        P("wide", None),
        P("wide"),
        P(),
        P(),
        P(),
        P(None, "narrow"),
        P(None, "narrow"),
        P(None, "narrow"),
        P("narrow", None),
        P(),
        P(None, "narrow"),
        P(None, "narrow"),
        P("narrow", None),
    )
    return jax.shard_map(
        shards,
        mesh=mesh,
        in_specs=placed,
        out_specs=(
            P("wide", None),
            P("wide", None),
            P("wide"),
            P("wide", "narrow"),
            P("wide", "narrow"),
            P("wide", "narrow"),
            P("narrow", "wide"),
            P("wide"),
            P("wide", "narrow"),
            P("wide", "narrow"),
            P("narrow", "wide"),
        ),
        check_vma=False,
    )
```

```python
import functools

import jax
import jax.numpy as jnp
import numpy as np
from jax import lax
from jax.experimental import pallas as pl
from jax.experimental.pallas import tpu as pltpu
from jax.sharding import PartitionSpec as P

HD = 128
EPSILON = 1e-05
NEGATIVE = -1e30
BASE = 10000.0
LOG2E = 1.4426950408889634
SCORE = HD ** (-0.5) * LOG2E
FACTOR = HD ** (-0.5)
BF = jnp.bfloat16
F32 = jnp.float32
NT = (((1,), (1,)), ((), ()))
TN = (((0,), (0,)), ((), ()))
NN = (((1,), (0,)), ((), ()))
VM = pl.BlockSpec(memory_space=pltpu.VMEM)
SM = pl.BlockSpec(memory_space=pltpu.SMEM)
ANY = pl.BlockSpec(memory_space=pl.ANY)


def dot(a, b, dims=(((1,), (0,)), ((), ()))):
    return lax.dot_general(a, b, dims, preferred_element_type=F32)


def narrow_swap(value, mask):
    pairs = [(n, n ^ mask) for n in range(lax.axis_size("narrow"))]
    return lax.ppermute(value, "narrow", pairs)


def wide_swap(value):
    return lax.ppermute(value, "wide", [(w, w ^ 1) for w in range(lax.axis_size("wide"))])


def wide_ring(value, group, hop=1):
    ring = group // 2
    pairs = []
    for w in range(lax.axis_size("wide")):
        base, member = w // group * group, w % group
        pairs.append((w, base + (member // 2 + hop) % ring * 2 + member % 2))
    return lax.ppermute(value, "wide", pairs)


def wide_flip(value, bit):
    return lax.ppermute(value, "wide", [(w, w ^ (2 << bit)) for w in range(lax.axis_size("wide"))])


def halving(count):
    groups = []
    step = 1
    while step < count:
        groups.append([k for k in range(count) if k % (2 * step) == step])
        step *= 2
    return [*groups, [0]]


def stretches(groups):
    starts, at = [], 0
    for group in groups:
        starts.append((at, len(group)))
        at += len(group)
    return starts


def rope(value, cosine, sine):
    return value * cosine + pltpu.roll(value, HD // 2, 1) * sine


def norm_kv_kernel(core, x_ref, gain_ref, wk_ref, wv_ref, cos_ref, sin_ref, normed_ref, *kv_refs):
    x = x_ref[...].astype(F32)
    scale = lax.rsqrt(jnp.mean(x * x, axis=1, keepdims=True) + EPSILON)
    normed = (x * scale * gain_ref[...].astype(F32)).astype(BF)
    normed_ref[...] = normed
    keys = dot(normed, wk_ref[...])
    values = dot(normed, wv_ref[...])
    for h, ref in enumerate(kv_refs):
        cols = slice(h * HD, (h + 1) * HD)
        ref[:, :HD] = rope(keys[:, cols], cos_ref[...], sin_ref[...]).astype(BF)
        ref[:, HD:] = values[:, cols].astype(BF)


def norm_kv(core, tokens, gain, wk, wv, cosine, sine):
    rows, width = tokens.shape
    half = rows // 2
    heads = wk.shape[1] // HD
    full = lambda w: pl.BlockSpec(w.shape, lambda i, c: (0, 0))
    outs = pl.pallas_call(
        norm_kv_kernel,
        out_shape=[jax.ShapeDtypeStruct((rows, width), BF)]
        + [jax.ShapeDtypeStruct((rows, 2 * HD), BF)] * heads,
        grid_spec=pltpu.PrefetchScalarGridSpec(
            num_scalar_prefetch=1,
            grid=(2,),
            in_specs=[
                pl.BlockSpec((half, width), lambda i, c: (i ^ c[0], 0)),
                full(gain),
                full(wk),
                full(wv),
                pl.BlockSpec((half, HD), lambda i, c: (i, 0)),
                pl.BlockSpec((half, HD), lambda i, c: (i, 0)),
            ],
            out_specs=[pl.BlockSpec((half, width), lambda i, c: (i, 0))]
            + [pl.BlockSpec((half, 2 * HD), lambda i, c: (i, 0))] * heads,
        ),
        cost_estimate=pl.CostEstimate(flops=int(2.9e9), bytes_accessed=0, transcendentals=0),
        name="norm_kv",
    )(core, tokens, gain, wk, wv, cosine, sine)
    return outs[0], outs[1:]


def query_kernel(x_ref, w_ref, cos_ref, sin_ref, out_ref):
    raw = dot(x_ref[...], w_ref[...])
    for h in range(raw.shape[1] // HD):
        cols = slice(h * HD, (h + 1) * HD)
        out_ref[:, cols] = rope(raw[:, cols], cos_ref[...], sin_ref[...]).astype(BF)


def query_proj(x, w, cosine, sine):
    rows, width = x.shape
    half = rows // 2
    return pl.pallas_call(
        query_kernel,
        out_shape=jax.ShapeDtypeStruct((rows, w.shape[1]), BF),
        grid=(2,),
        in_specs=[
            pl.BlockSpec((half, width), lambda i: (i, 0)),
            pl.BlockSpec(w.shape, lambda i: (0, 0)),
            pl.BlockSpec((half, HD), lambda i: (i, 0)),
            pl.BlockSpec((half, HD), lambda i: (i, 0)),
        ],
        out_specs=pl.BlockSpec((half, w.shape[1]), lambda i: (i, 0)),
        cost_estimate=pl.CostEstimate(flops=int(2.9e9), bytes_accessed=0, transcendentals=0),
        name="query_proj",
    )(x, w, cosine, sine)


def fetch_slots(slot_refs, slots, kv_ref, sems):
    rows, width = slot_refs[0].shape
    copies = []
    for at, ref in enumerate(slot_refs):
        head, slot = divmod(at, slots)
        spot = kv_ref.at[pl.ds(slot * rows, rows), pl.ds(head * width, width)]
        copies.append(pltpu.make_async_copy(ref, spot, sems.at[at]))
    for copy in copies:
        copy.start()
    for copy in copies:
        copy.wait()


def allowed(pk, size, span, pos, low):
    key_pos = pk * size + lax.broadcasted_iota(jnp.int32, (size, span), 0)
    return (key_pos <= pos) & (key_pos >= low)


def attn_fwd_kernel(slots, *refs):
    meta, q_ref, pos_ref, low_ref = refs[:4]
    slot_refs = refs[4 : 4 + slots]
    mixed_ref, lse_ref, kv_ref, acc_ref, sems = refs[-5:]
    fetch_slots(slot_refs, slots, kv_ref, sems)
    size = q_ref.shape[0] // 2
    for i in range(2):
        rows = slice(i * size, (i + 1) * size)
        pos = jnp.tile(pos_ref[0:1, rows], (1, 2))
        low = jnp.tile(low_ref[0:1, rows], (1, 2))
        queries = [q_ref[rows, r * HD : (r + 1) * HD] for r in range(2)]
        acc_ref[...] = jnp.zeros_like(acc_ref)

        def body(pk, carry):
            peak, total = carry
            spot = pl.multiple_of(meta[4 + pk] * size, size)
            keys = kv_ref[pl.ds(spot, size), :HD]
            values = kv_ref[pl.ds(spot, size), HD:]
            scores = jnp.concatenate([dot(keys, q, NT) for q in queries], axis=1) * SCORE
            scores = jnp.where(allowed(pk, size, 2 * size, pos, low), scores, NEGATIVE)
            peak_new = jnp.maximum(peak, jnp.max(scores, axis=0, keepdims=True))
            alpha = jnp.exp2(peak - peak_new)
            probs = jnp.exp2(scores - peak_new)
            total = total * alpha + jnp.sum(probs, axis=0, keepdims=True)
            acc_ref[...] = acc_ref[...] * alpha + dot(values, probs.astype(BF), TN)
            return peak_new, total

        start = (jnp.full((1, 2 * size), NEGATIVE, F32), jnp.zeros((1, 2 * size), F32))
        peak, total = lax.fori_loop(meta[i], meta[2 + i] + 1, body, start)
        lse_ref[i : i + 1, :] = peak + jnp.log2(total)
        out = acc_ref[...] * (1.0 / total)
        for r in range(2):
            mixed_ref[rows, r * HD : (r + 1) * HD] = out[:, r * size : (r + 1) * size].T.astype(BF)


def attn_fwd(head, meta, q, pos, low, slots, mixed):
    rows = q.shape[0]
    count = len(slots)
    earlier = [] if mixed is None else [mixed]
    return pl.pallas_call(
        functools.partial(attn_fwd_kernel, count),
        out_shape=(
            jax.ShapeDtypeStruct(q.shape, BF),
            jax.ShapeDtypeStruct((2, rows), F32),
        ),
        grid=(1,),
        in_specs=[
            SM,
            pl.BlockSpec((rows, 2 * HD), lambda i: (0, head)),
            pl.BlockSpec(pos.shape, lambda i: (0, 0)),
            pl.BlockSpec(low.shape, lambda i: (0, 0)),
        ]
        + [ANY] * (count + len(earlier)),
        out_specs=[
            pl.BlockSpec((rows, 2 * HD), lambda i: (0, head)),
            pl.BlockSpec((2, rows), lambda i: (0, 0)),
        ],
        input_output_aliases={4 + count: 0} if earlier else {},
        scratch_shapes=[
            pltpu.VMEM((count * rows, 2 * HD), BF),
            pltpu.VMEM((HD, rows), F32),
            pltpu.SemaphoreType.DMA((count,)),
        ],
        cost_estimate=pl.CostEstimate(flops=int(1e9), bytes_accessed=0, transcendentals=0),
        name="attn_fwd",
    )(meta, q, pos, low, *slots, *earlier)


def attn_bwd_kernel(heads, slots, groups, *refs):
    meta, q_ref, pos_ref, low_ref, dmix_ref, mixed_ref, cos_ref, sin_ref = refs[:8]
    lse_refs = refs[8 : 8 + heads]
    at = 8 + heads
    slot_refs = refs[at : at + heads * slots]
    at += heads * slots
    dq_ref, dkv_refs = refs[at], refs[at + 1 : -4]
    kv_ref, dkv_ref, dq_acc, sems = refs[-4:]
    fetch_slots(slot_refs, slots, kv_ref, sems)
    dkv_ref[...] = jnp.zeros_like(dkv_ref)
    rows_all = q_ref.shape[0]
    size = rows_all // 2
    for i in range(2):
        rows = slice(i * size, (i + 1) * size)
        pos = jnp.tile(pos_ref[0:1, rows], (1, 2))
        low = jnp.tile(low_ref[0:1, rows], (1, 2))
        for g in range(heads):
            cols = [slice((2 * g + r) * HD, (2 * g + r + 1) * HD) for r in range(2)]
            queries = jnp.concatenate([q_ref[rows, c] for c in cols], axis=0)
            grads = jnp.concatenate([dmix_ref[rows, c] for c in cols], axis=0)
            outs = jnp.concatenate([mixed_ref[rows, c] for c in cols], axis=0)
            delta = jnp.sum((grads.astype(F32) * outs.astype(F32)).T, axis=0, keepdims=True)
            lse = lse_refs[g][i : i + 1, :]
            dq_acc[...] = jnp.zeros_like(dq_acc)

            def body(pk, carry):
                spot = pl.multiple_of(meta[4 + pk] * size, size)
                key_cols = slice(2 * g * HD, (2 * g + 1) * HD)
                value_cols = slice((2 * g + 1) * HD, (2 * g + 2) * HD)
                keys = kv_ref[pl.ds(spot, size), key_cols]
                values = kv_ref[pl.ds(spot, size), value_cols]
                scores = dot(keys, queries, NT) * SCORE
                probs = jnp.where(
                    allowed(pk, size, 2 * size, pos, low), jnp.exp2(scores - lse), 0.0
                )
                d_probs = dot(values, grads, NT)
                d_scores = (probs * (d_probs - delta)).astype(BF)
                dkv_ref[pl.ds(spot, size), value_cols] += dot(probs.astype(BF), grads)
                dkv_ref[pl.ds(spot, size), key_cols] += dot(d_scores, queries) * FACTOR
                dq_acc[...] += dot(d_scores, keys, TN)
                return carry

            lax.fori_loop(meta[i], meta[2 + i] + 1, body, 0)
            for r in range(2):
                part = dq_acc[r * size : (r + 1) * size, :] * FACTOR
                dq_ref[rows, cols[r]] = rope(part, cos_ref[rows, :], -sin_ref[rows, :]).astype(BF)
    ring = slots // 2
    for j, ref in enumerate(dkv_refs):
        first = ring * (j // len(groups))
        for place, k in enumerate(groups[j % len(groups)]):
            spot = pl.multiple_of((first + meta[4 + 2 * slots + k]) * rows_all, rows_all)
            ref[place * rows_all : (place + 1) * rows_all, :] = dkv_ref[
                pl.ds(spot, rows_all), :
            ].astype(BF)


def attn_bwd(meta, q, pos, low, lse, mixed, dmix, cosine, sine, slots):
    rows, q_width = q.shape
    heads, count = len(slots), len(slots[0])
    kv_width = heads * 2 * HD
    groups = halving(count // 2)
    outs = pl.pallas_call(
        functools.partial(attn_bwd_kernel, heads, count, groups),
        out_shape=[jax.ShapeDtypeStruct((rows, q_width), BF)]
        + [jax.ShapeDtypeStruct((len(g) * rows, kv_width), BF) for g in groups] * 2,
        in_specs=[SM] + [VM] * (7 + heads) + [ANY] * (heads * count),
        out_specs=[VM] * (1 + 2 * len(groups)),
        scratch_shapes=[
            pltpu.VMEM((count * rows, kv_width), BF),
            pltpu.VMEM((count * rows, kv_width), F32),
            pltpu.VMEM((rows, HD), F32),
            pltpu.SemaphoreType.DMA((heads * count,)),
        ],
        cost_estimate=pl.CostEstimate(flops=int(2e9), bytes_accessed=0, transcendentals=0),
        name="attn_bwd",
    )(meta, q, pos, low, dmix, mixed, cosine, sine, *lse, *[v for head in slots for v in head])
    return outs[0], outs[1 : 1 + len(groups)], outs[1 + len(groups) :]


def cost(micros):
    return pl.CostEstimate(flops=int(micros * 0.3e9), bytes_accessed=0, transcendentals=0)


def split_rows(total, own_ref, other_ref):
    half = own_ref.shape[0]
    own_ref[...] = total[:half].astype(BF)
    other_ref[...] = total[half:].astype(BF)


def project_kernel(spec, *refs):
    total = None
    for a, b, offset, dims in spec:
        left = refs[a][...] if dims is not None else None
        if dims == "nt":
            right, form = refs[b][:, offset : offset + left.shape[1]], NT
        else:
            right, form = refs[b][offset : offset + left.shape[1], :], NN
        term = dot(left, right, form)
        total = term if total is None else total + term
    split_rows(total, refs[-2], refs[-1])


def project(pairs, dims, tile, micros):
    operands, specs, plan, weights = [], [], [], []
    for a, b, offset in pairs:
        operands.append(a)
        specs.append(pl.BlockSpec(a.shape, lambda i: (0, 0)))
        spot = next((at for at, seen in weights if seen is b), None)
        left = len(operands) - 1
        if spot is None:
            spot = len(operands)
            operands.append(b)
            weights.append((spot, b))
            if dims == "nt":
                specs.append(pl.BlockSpec((tile, b.shape[1]), lambda i: (i, 0)))
            else:
                specs.append(pl.BlockSpec((b.shape[0], tile), lambda i: (0, i)))
        plan.append((left, spot, offset, dims))
    rows = pairs[0][0].shape[0]
    width = pairs[0][1].shape[0 if dims == "nt" else 1]
    return pl.pallas_call(
        functools.partial(project_kernel, plan),
        out_shape=[jax.ShapeDtypeStruct((rows // 2, width), BF)] * 2,
        grid=(width // tile,),
        in_specs=specs,
        out_specs=[pl.BlockSpec((rows // 2, tile), lambda i: (0, i))] * 2,
        cost_estimate=cost(micros),
        name="project",
    )(*operands)


def back_dense_kernel(gate_a, up_a, gate_b, up_b, wg_ref, wu_ref, own_ref, other_ref):
    total = None
    offset = 0
    for group in ((gate_a, up_a), (gate_b, up_b)):
        count = group[0].shape[1]
        for ref, w_ref in zip(group, (wg_ref, wu_ref)):
            term = dot(ref[...], w_ref[:, offset : offset + count], NT)
            total = term if total is None else total + term
        offset += count
    split_rows(total, own_ref, other_ref)


def back_dense(grads, w_gate, w_up, tile, part, parts):
    width, hidden = w_gate.shape[0] // parts, w_gate.shape[1]
    rows = grads[0].shape[0]
    ahead = part * (width // tile)
    weight = pl.BlockSpec((tile, hidden), lambda i: (ahead + i, 0))
    return pl.pallas_call(
        back_dense_kernel,
        out_shape=[jax.ShapeDtypeStruct((rows // 2, width), BF)] * 2,
        grid=(width // tile,),
        in_specs=[pl.BlockSpec(v.shape, lambda i: (0, 0)) for v in grads] + [weight, weight],
        out_specs=[pl.BlockSpec((rows // 2, tile), lambda i: (0, i))] * 2,
        cost_estimate=cost(11 / parts),
        name="back_dense",
    )(*grads, w_gate, w_up)


def gated_kernel(own_ref, other_ref, wg_ref, wu_ref, di_ref, inner_ref, dg_ref, du_ref, all_ref):
    @pl.when(pl.program_id(0) == 0)
    def _():
        half = own_ref.shape[0]
        all_ref[:half, :] = own_ref[...]
        all_ref[half:, :] = other_ref[...]

    gate = dot(all_ref[...], wg_ref[...])
    up = dot(all_ref[...], wu_ref[...])
    sigma = 1.0 / (1.0 + jnp.exp(-gate))
    silu = gate * sigma
    d_inner = di_ref[...]
    inner_ref[...] = (silu * up).astype(BF)
    dg_ref[...] = (d_inner * up * sigma * (1.0 + gate * (1.0 - sigma))).astype(BF)
    du_ref[...] = (d_inner * silu).astype(BF)


def gated(own, other, wg, wu, d_inner, first, columns, tile):
    half, width = own.shape
    weight = pl.BlockSpec((width, tile), lambda i: (0, first // tile + i))
    whole = pl.BlockSpec((half, width), lambda i: (0, 0))
    return pl.pallas_call(
        gated_kernel,
        out_shape=[jax.ShapeDtypeStruct((2 * half, columns), BF)] * 3,
        grid=(pl.cdiv(columns, tile),),
        in_specs=[
            whole,
            whole,
            weight,
            weight,
            pl.BlockSpec((2 * half, tile), lambda i: (0, first // tile + i)),
        ],
        out_specs=[pl.BlockSpec((2 * half, tile), lambda i: (0, i))] * 3,
        scratch_shapes=[pltpu.VMEM((2 * half, width), BF)],
        cost_estimate=cost(7.5),
        name="gated",
    )(own, other, wg, wu, d_inner)


def mixed_grad_kernel(own_ref, other_ref, w_ref, out_ref):
    both = jnp.concatenate([own_ref[...], other_ref[...]], axis=0)
    out_ref[...] = dot(both, w_ref[...], NT).astype(BF)


def mixed_grad(own, other, w):
    return pl.pallas_call(
        mixed_grad_kernel,
        out_shape=jax.ShapeDtypeStruct((2 * own.shape[0], w.shape[0]), BF),
        in_specs=[VM] * 3,
        out_specs=VM,
        cost_estimate=cost(4),
        name="mixed_grad",
    )(own, other, w)


def d_inner_kernel(x_ref, w_ref, out_ref):
    out_ref[...] = dot(x_ref[...], w_ref[...], NT)


def inner_grad(x, w, tile):
    rows, width = x.shape
    hidden = w.shape[0]
    return pl.pallas_call(
        d_inner_kernel,
        out_shape=jax.ShapeDtypeStruct((rows, hidden), F32),
        grid=(pl.cdiv(hidden, tile),),
        in_specs=[
            pl.BlockSpec((rows, width), lambda i: (0, 0)),
            pl.BlockSpec((tile, width), lambda i: (i, 0)),
        ],
        out_specs=pl.BlockSpec((rows, tile), lambda i: (0, i)),
        cost_estimate=cost(8),
        name="inner_grad",
    )(x, w)


def pack_kernel(count, plan, strip, tbl, *refs):
    ins, outs = refs[:count], refs[count:]
    for out_ref, pieces in zip(outs, plan):
        column = 0
        for at, rows, row in pieces:
            for k in range(tbl.shape[1]):
                first = pl.multiple_of(tbl[row, k] * strip, 128)
                out_ref[:, column : column + strip] = ins[at][rows, pl.ds(first, strip)]
                column += strip


def pack(values, plan, tbl, strip):
    turns = tbl.shape[1]
    if strip % 128:
        cut = lambda v, rows, at: lax.dynamic_slice_in_dim(v[rows], at * strip, strip, axis=1)
        return [
            jnp.concatenate(
                [cut(values[at], rows, tbl[row, k]) for at, rows, row in pieces for k in range(turns)],
                axis=1,
            )
            for pieces in plan
        ]
    return pl.pallas_call(
        functools.partial(pack_kernel, len(values), plan, strip),
        out_shape=[
            jax.ShapeDtypeStruct(
                (p[0][1].stop - p[0][1].start, len(p) * turns * strip), values[0].dtype
            )
            for p in plan
        ],
        in_specs=[SM] + [VM] * len(values),
        out_specs=[VM] * len(plan),
        cost_estimate=cost(1.5),
        name="pack",
    )(tbl, *values)


def strip_rows_kernel(halves, near, rights, nears, spans, tbl, *refs):
    left = refs[:halves]
    left_near = refs[halves : halves + near]
    right = refs[halves + near : halves + near + rights]
    right_near = refs[halves + near + rights : halves + near + rights + nears]
    outs = refs[halves + near + rights + nears :]
    step = pl.program_id(0)
    join = lambda group: (
        group[0][...] if len(group) == 1 else jnp.concatenate([r[...] for r in group], axis=0)
    )
    mine, theirs = join(left), join(left_near)
    pieces = []
    for r, n in zip(right, right_near):
        planes = range(r.shape[0]) if len(r.shape) == 3 else [None]
        for k in planes:
            a = r[...] if k is None else r[k]
            b = n[...] if k is None else n[k]
            pieces.append((dot(mine, a, TN) + dot(theirs, b, TN)).astype(BF))
    for (start, length), out in zip(spans, outs):

        @pl.when((step >= start) & (step < start + length))
        def _(out=out):
            column = 0
            for piece in pieces:
                out[:, column : column + piece.shape[1]] = piece
                column += piece.shape[1]


def strip_rows_grad(left, left_near, right, right_near, tbl, strip, micros, single=False):
    turns = tbl.shape[1]
    columns = sum(r.shape[-1] * (r.shape[0] if r.ndim == 3 else 1) for r in right)
    spans = [(k, 1) for k in range(turns)] if single else stretches(halving(turns))
    if strip % 128:
        near = jnp.concatenate(left_near, axis=0)
        mine = jnp.concatenate(left, axis=0)
        flat = lambda r: [r] if r.ndim == 2 else [r[k] for k in range(r.shape[0])]
        outs = []
        for start, length in spans:
            group = []
            for k in range(start, start + length):
                a = lax.dynamic_slice_in_dim(mine, tbl[0, k] * strip, strip, axis=1)
                b = near[:, k * strip : (k + 1) * strip]
                group.append(
                    jnp.concatenate(
                        [
                            dot(a, x, TN) + dot(b, y, TN)
                            for r, n in zip(right, right_near)
                            for x, y in zip(flat(r), flat(n))
                        ],
                        axis=1,
                    ).astype(BF)
                )
            outs.append(jnp.concatenate(group, axis=0))
        return outs
    held = lambda start, length: (lambda i, t: (jnp.clip(i - start, 0, length - 1), 0))
    whole = lambda v: pl.BlockSpec(v.shape, lambda i, t: (0,) * v.ndim)
    return pl.pallas_call(
        functools.partial(
            strip_rows_kernel, len(left), len(left_near), len(right), len(right_near), spans
        ),
        out_shape=[jax.ShapeDtypeStruct((length * strip, columns), BF) for _, length in spans],
        grid_spec=pltpu.PrefetchScalarGridSpec(
            num_scalar_prefetch=1,
            grid=(turns,),
            in_specs=[pl.BlockSpec((v.shape[0], strip), lambda i, t: (0, t[0, i])) for v in left]
            + [pl.BlockSpec((v.shape[0], strip), lambda i, t: (0, i)) for v in left_near]
            + [whole(v) for v in [*right, *right_near]],
            out_specs=[pl.BlockSpec((strip, columns), held(*span)) for span in spans],
        ),
        cost_estimate=cost(micros),
        name="strip_rows",
    )(tbl, *left, *left_near, *right, *right_near)


def strip_columns_kernel(parts, halves, near, strip, spans, *refs):
    at = 2 * parts
    right, right_near = refs[at : at + halves], refs[at + halves : at + halves + near]
    outs = refs[at + halves + near :]
    first = 0
    for p in range(parts):
        total = None
        for ref, group in ((refs[p], right), (refs[parts + p], right_near)):
            row = 0
            for r in group:
                term = dot(ref[row : row + r.shape[0], :], r[...], TN)
                total = term if total is None else total + term
                row += r.shape[0]
        for (start, length), out in zip(spans, outs):
            out[first : first + total.shape[0], :] = total[
                :, start * strip : (start + length) * strip
            ].astype(BF)
        first += total.shape[0]


def strip_columns_grad(left, left_near, right, right_near, turns, strip, tile, micros, near_at=0):
    rows, count = left[0].shape[0], sum(v.shape[1] for v in left)
    if strip * turns % 128:
        raise ValueError(strip)
    spans = stretches(halving(turns))
    whole = lambda v: pl.BlockSpec(v.shape, lambda i: (0, 0))
    near = lambda v: pl.BlockSpec((v.shape[0], turns * strip), lambda i: (0, near_at))
    if len(left) == 1:
        left_specs = [pl.BlockSpec((rows, tile), lambda i: (0, i))] * 2
    else:
        tile = count
        left_specs = [whole(v) for v in [*left, *left_near]]
    return pl.pallas_call(
        functools.partial(
            strip_columns_kernel, len(left), len(right), len(right_near), strip, spans
        ),
        out_shape=[jax.ShapeDtypeStruct((count, length * strip), BF) for _, length in spans],
        grid=(pl.cdiv(count, tile),),
        in_specs=left_specs + [whole(v) for v in right] + [near(v) for v in right_near],
        out_specs=[pl.BlockSpec((tile, length * strip), lambda i: (i, 0)) for _, length in spans],
        cost_estimate=cost(micros),
        name="strip_columns",
    )(*left, *left_near, *right, *right_near)


def close_kv_kernel(count, *refs):
    cos_ref, sin_ref, dk_ref, dv_ref = refs[count:]
    total = refs[0][...].astype(F32)
    for ref in refs[1:count]:
        total = total + ref[...].astype(F32)
    heads = dk_ref.shape[1] // HD
    for h in range(heads):
        cols = slice(h * HD, (h + 1) * HD)
        keys = total[:, 2 * h * HD : (2 * h + 1) * HD]
        dk_ref[:, cols] = rope(keys, cos_ref[...], -sin_ref[...]).astype(BF)
        dv_ref[:, cols] = total[:, (2 * h + 1) * HD : (2 * h + 2) * HD].astype(BF)


def close_kv(terms, cosine, sine):
    rows, width = terms[0].shape
    first = lambda w: pl.BlockSpec((rows, w), lambda i: (0, 0))
    return pl.pallas_call(
        functools.partial(close_kv_kernel, len(terms)),
        out_shape=[jax.ShapeDtypeStruct((rows, width // 2), BF)] * 2,
        grid=(1,),
        in_specs=[first(width)] * len(terms) + [first(HD)] * 2,
        out_specs=[first(width // 2)] * 2,
        cost_estimate=cost(1.5),
        name="close_kv",
    )(*terms, cosine, sine)


def norm_backward(source, scale_rows, gain, upstream):
    weighted = upstream * gain
    average = jnp.mean(weighted * source, axis=1, keepdims=True)
    return scale_rows * weighted - source * scale_rows**3 * average


def after(value, *done):
    return lax.optimization_barrier((value, *done))[0]


def shards(
    tokens,
    cotangent,
    keep_mask,
    doc_lengths,
    block_order,
    gain_attn,
    w_query,
    w_key,
    w_value,
    w_out,
    gain_dense,
    w_gate,
    w_up,
    w_down,
):
    rows, width = tokens.shape
    half = rows // 2
    wide = lax.axis_size("wide")
    group = wide // block_order.shape[0]
    ring = group // 2
    wide_index = lax.axis_index("wide")
    member = wide_index % group
    seq_index = wide_index // group
    side = (wide_index % 2).astype(jnp.int32)
    core = lax.axis_index("narrow") % 2
    strip = width // wide
    turns = wide // 2

    def ordered(mine, other):
        return jnp.where(
            core == 0,
            jnp.concatenate([mine, other], axis=0),
            jnp.concatenate([other, mine], axis=0),
        )

    def own_half(value):
        return lax.dynamic_slice_in_dim(value, core * half, half)

    def other_half(value):
        return lax.dynamic_slice_in_dim(value, (1 - core) * half, half)

    order_row = lax.dynamic_index_in_dim(block_order, seq_index, 0, keepdims=False)
    length_row = lax.dynamic_index_in_dim(doc_lengths, seq_index, 0, keepdims=False)
    doc_ends = jnp.cumsum(length_row)
    places = jnp.stack([member * 2 + core, member * 2 + 1 - core])
    chosen = jnp.sum(
        jnp.where(places[:, None] == jnp.arange(2 * group)[None, :], order_row[None, :], 0), axis=1
    )
    pos = (chosen[:, None] * half + jnp.arange(half, dtype=jnp.int32)[None, :]).reshape(-1)
    low = jnp.max(jnp.where(doc_ends[None, :] <= pos[:, None], doc_ends[None, :], 0), axis=1)
    block_low = low.reshape(2, half)[:, 0] // half
    stored = jnp.sum(
        jnp.where(
            order_row[None, :] == jnp.arange(2 * group)[:, None], jnp.arange(2 * group)[None, :], 0
        ),
        axis=1,
    )
    owner = stored // 2
    slot = (member // 2 - owner // 2) % ring + ring * (owner % 2 != side).astype(jnp.int32)
    spots = slot * 2 + (stored % 2 != core).astype(jnp.int32)
    place = member // 2
    back = (place - (place ^ jnp.arange(ring, dtype=jnp.int32))) % ring
    meta = jnp.concatenate([block_low, chosen, spots, back]).astype(jnp.int32)
    frequency = BASE ** (-(jnp.arange(HD // 2, dtype=F32) * 2.0) / HD)
    angles = pos.astype(F32)[:, None] * frequency[None, :]
    cosine = jnp.cos(angles)
    sine = jnp.sin(angles)
    cosine = jnp.concatenate([cosine, cosine], axis=1)
    sine = jnp.concatenate([-sine, sine], axis=1)
    pos_row = pos[None, :]
    low_row = low[None, :]

    order = np.array([k for stretch in halving(turns) for k in stretch], np.int32)
    turn_row = wide_index // 2 ^ order
    tbl = jnp.stack([2 * turn_row + side, 2 * turn_row + 1 - side]).astype(jnp.int32)
    round_row = (wide_index // 2 - 1 - jnp.arange(turns, dtype=jnp.int32)) % turns
    round_tbl = jnp.stack([2 * round_row + side, 2 * round_row + 1 - side]).astype(jnp.int32)
    core_arr = core.astype(jnp.int32)[None]
    normed_one, both = norm_kv(core_arr, tokens, gain_attn[None, :], w_key, w_value, cosine, sine)
    low_rows, all_rows = slice(0, half), slice(0, rows)

    def together(*values):
        return list(lax.optimization_barrier(values))

    near, far = [[v] for v in both], [[] for v in both]
    query = d_dense = d_inner = input_near = d_dense_strips = None
    for step in range(ring):
        for head in range(len(both)):
            held = near[head][step]
            if step + 1 < ring:
                sent = [wide_swap(held), wide_ring(held, group)]
            elif head == 0:
                sent = [wide_swap(held)]
            else:
                sent = [wide_ring(far[head][0], group, -1)]
            beside = []
            if step == 0 and head == 0:
                beside = [query_proj(normed_one, w_query, cosine, sine)]
            if step == 0 and head == 1:
                keep_rel = jnp.concatenate([own_half(keep_mask), other_half(keep_mask)])[:, None]
                cot_rel = jnp.concatenate([own_half(cotangent), other_half(cotangent)])
                beside = [jnp.where(keep_rel > 0, cot_rel, jnp.zeros_like(cot_rel))]
            if step == 1 and head == 0:
                beside = [inner_grad(d_dense, w_down, 256)]
            if step == 2 and head == 0:
                beside = pack(
                    [normed_one, d_dense],
                    [[(0, low_rows, 1), (1, low_rows, 1)], [(1, all_rows, 0)]],
                    tbl,
                    strip,
                )
            done = together(*sent, *beside)
            far[head].append(done[0])
            if step + 1 < ring:
                near[head].append(done[1])
            if step == 0 and head == 0:
                query = done[-1]
            if step == 0 and head == 1:
                d_dense = done[-1]
            if step == 1 and head == 0:
                d_inner = done[-1]
            if step == 2 and head == 0:
                input_near, d_dense_strips = done[-2:]
    slots = [n + f for n, f in zip(near, far)]
    input_near = wide_swap(after(input_near, *slots[0], *slots[-1]))
    mixed, lse = None, []
    for h, held in enumerate(slots):
        mixed, part = attn_fwd(h, meta, query, pos_row, low_row, held, mixed)
        lse.append(part)

    def reduce_narrow(halves, hold=()):
        own_part, other_part = halves
        got = narrow_swap(other_part, 1)
        held = (own_part.astype(F32) + got.astype(F32)).astype(BF)
        return held, narrow_swap(held, 2)

    def total_of(held, got):
        return held.astype(F32) + got.astype(F32)

    part = project([(mixed, w_out, 0)], "nn", 1024, 4)
    held, got = reduce_narrow((part[0], after(part[1], input_near)))
    mixed_near = wide_swap(mixed)
    input_near_other = narrow_swap(input_near, 1)
    source = own_half(tokens).astype(F32)
    keep_own = own_half(keep_mask).astype(F32)[:, None]
    hidden_one = source + keep_own * total_of(held, got)
    gain_two = gain_dense.astype(F32)
    scale_two = lax.rsqrt(jnp.mean(hidden_one * hidden_one, axis=1, keepdims=True) + EPSILON)
    normed_two = (hidden_one * scale_two * gain_two).astype(BF)
    normed_two_other = narrow_swap(after(normed_two, mixed_near), 1)
    hidden = w_gate.shape[1]
    tile = 256
    first_count = 3 * tile
    inner_a, *dgu_a = gated(
        normed_two, normed_two_other, w_gate, w_up, d_inner, 0, first_count, tile
    )
    inner_a_near = wide_swap(inner_a)
    inner_b, *dgu_b = gated(
        after(normed_two, inner_a),
        normed_two_other,
        w_gate,
        w_up,
        d_inner,
        first_count,
        hidden - first_count,
        tile,
    )
    back = back_dense([*dgu_a, *dgu_b], w_gate, w_up, 512, 0, 1)
    held, got = reduce_narrow((back[0], after(back[1], inner_a_near)))

    def halve(parts, axis, hold=None):
        groups = halving(1 << (len(parts) - 1))
        size = parts[-1].shape[axis]
        received, sent = [], None
        for bit, group in enumerate(groups[:-1]):
            sent = parts[bit]
            if bit:
                total = sent.astype(F32)
                for early, value in enumerate(received):
                    there = [k ^ (1 << early) for k in groups[early]]
                    pick = [
                        lax.slice_in_dim(value, size * there.index(k), size * (there.index(k) + 1), axis=axis)
                        for k in group
                    ]
                    total = total + (pick[0] if len(pick) == 1 else jnp.concatenate(pick, axis)).astype(F32)
                sent = total.astype(BF)
            got = wide_flip(sent, bit)
            received.append(got if hold is None else after(got, hold))
        return received, sent

    def ring_sum(parts):
        carried, first = parts[0], None
        for part in parts[1:]:
            total = part.astype(F32) + wide_ring(carried, wide).astype(F32)
            carried = total.astype(BF)
            first = carried if first is None else first
        return total, first

    def close(parts, received, axis):
        size = parts[-1].shape[axis]
        total = parts[-1].astype(F32)
        for value in received:
            total = total + lax.slice_in_dim(value, 0, size, axis=axis).astype(F32)
        return total

    near_sides = [input_near, input_near_other]
    down_a = strip_columns_grad(
        [after(inner_a, held)],
        [inner_a_near],
        [d_dense_strips],
        near_sides,
        turns,
        strip,
        tile,
        4,
        1,
    )
    inner_b_near = wide_swap(inner_b)
    down_a_got, down_a_mid = halve(down_a, 1)
    dgu_a_near = [wide_swap(after(v, inner_b)) for v in dgu_a]
    dense_parts = project(
        [(after(inner_a, down_a[0], inner_b_near), w_down, 0), (inner_b, w_down, first_count)], "nn", 512, 6
    )
    (normed_two_near,) = pack(
        [after(normed_two, dense_parts[0])], [[(0, low_rows, 1)]], round_tbl, strip
    )
    normed_two_near = wide_swap(normed_two_near)
    down_b = strip_columns_grad(
        [after(inner_b, dense_parts[0])], [inner_b_near], [d_dense_strips], near_sides, turns, strip, tile, 4, 1
    )

    got = after(got, dense_parts[0], down_b[0])
    upstream = own_half(cotangent).astype(F32)
    d_hidden = upstream + norm_backward(hidden_one, scale_two, gain_two, total_of(held, got))
    d_attn = (keep_own * d_hidden).astype(BF)
    d_attn_other = narrow_swap(after(d_attn, dgu_a_near[0], down_a_mid), 1)

    d_mixed = mixed_grad(d_attn, d_attn_other, w_out)
    d_query, d_near, d_far = attn_bwd(
        meta, query, pos_row, low_row, lse, mixed, after(d_mixed, down_a_got[-1]), cosine, sine, slots
    )
    held_out, got_out = reduce_narrow((dense_parts[0], after(dense_parts[1], d_mixed)))
    output_own = (hidden_one + keep_own * total_of(held_out, got_out)).astype(BF)
    output = ordered(output_own, narrow_swap(output_own, 1))

    down_b_got, down_b_mid = halve(down_b, 1, d_query)
    normed_two_near_other = narrow_swap(after(normed_two_near, d_query), 1)
    normed_two_sides = [normed_two_near, normed_two_near_other]
    gate_up_a = strip_rows_grad(
        [after(normed_two, d_query, down_b_mid), normed_two_other], normed_two_sides, dgu_a, dgu_a_near, round_tbl, strip, 8, True
    )
    grad_gate_up_a, gate_up_a_mid = ring_sum(gate_up_a)
    d_far = [wide_swap(v) for v in d_far]
    d_far[0] = after(d_far[0], gate_up_a_mid)
    pairs = [
        (n.astype(F32) + f.astype(F32)).astype(BF) for n, f in zip(d_near[:-1], d_far[:-1])
    ]
    kv_got, kv_mid = halve([*pairs, d_near[-1]], 0)
    d_key, d_value = close_kv([d_near[-1], d_far[-1], *kv_got], cosine, sine)

    dgu_b_near = [wide_swap(after(v, d_query)) for v in dgu_b]
    gate_up_b = strip_rows_grad(
        [after(normed_two, gate_up_a_mid, kv_mid), normed_two_other],
        normed_two_sides,
        dgu_b,
        dgu_b_near,
        round_tbl,
        strip,
        7,
        True,
    )
    d_query_near = wide_swap(after(d_query, pairs[0]))
    grad_gate_up_b, gate_up_b_mid = ring_sum(gate_up_b)
    d_attn_near, d_attn_strips, d_attn_other_strips = pack(
        [after(d_attn, gate_up_a[0]), d_attn_other],
        [[(0, low_rows, 1)], [(0, low_rows, 0)], [(1, low_rows, 0)]],
        tbl,
        strip,
    )
    d_attn_near = wide_swap(after(d_attn_near, pairs[0]))
    d_attn_near_other = narrow_swap(after(d_attn_near, gate_up_b[0]), 1)
    query_part = strip_rows_grad(
        [after(normed_one, gate_up_b[0])], near_sides, [d_query], [d_query_near], tbl, strip, 4
    )
    out_part = strip_columns_grad(
        [after(mixed, query_part[0])],
        [mixed_near],
        [d_attn_strips, d_attn_other_strips],
        [d_attn_near, d_attn_near_other],
        turns,
        strip,
        tile,
        4,
    )

    kv_width = w_key.shape[1]
    held, got = reduce_narrow(
        project([(d_query, w_query, 0), (d_key, w_key, 0), (d_value, w_value, 0)], "nt", 512, 6)
    )
    gain_one = gain_attn.astype(F32)
    scale_one = lax.rsqrt(jnp.mean(source * source, axis=1, keepdims=True) + EPSILON)
    d_normed_one = total_of(held, got)
    grad_own = (d_hidden + norm_backward(source, scale_one, gain_one, d_normed_one)).astype(BF)
    grad_tokens = ordered(grad_own, narrow_swap(grad_own, 1))

    d_key_near = wide_swap(d_key)
    d_value_near = wide_swap(d_value)
    kv_part = strip_rows_grad(
        [after(normed_one, out_part[0])],
        near_sides,
        [d_key, d_value],
        [d_key_near, d_value_near],
        tbl,
        strip,
        4,
    )
    kv_part_got, _ = halve(kv_part, 0)
    query_got, query_mid = halve(query_part, 0, kv_part[0])
    out_got, out_mid = halve(out_part, 1, kv_part[0])
    kv_part_got[-1] = after(kv_part_got[-1], grad_own, output)
    grad_kv = close(kv_part, kv_part_got, 0)
    down_a_got[-1], down_b_got[-1] = after(down_a_got[-1], kv_part[0]), after(down_b_got[-1], kv_part[0])
    grad_down_a = close(down_a, down_a_got, 1)
    grad_down_b = close(down_b, down_b_got, 1)
    grad_query = close(query_part, query_got, 0)
    grad_out = close(out_part, out_got, 1)
    grad_key, grad_value = grad_kv[:, :kv_width], grad_kv[:, kv_width:]
    grad_down = jnp.concatenate([grad_down_a, grad_down_b], axis=0)
    second_count = hidden - first_count
    grad_gate = jnp.concatenate(
        [grad_gate_up_a[:, :first_count], grad_gate_up_b[:, :second_count]], axis=1
    )
    grad_up = jnp.concatenate(
        [grad_gate_up_a[:, first_count:], grad_gate_up_b[:, second_count:]], axis=1
    )

    def strip_rows(weight):
        return lax.dynamic_slice_in_dim(weight, wide_index * strip, strip).astype(F32)

    def gain_grad(pairs, gain):
        local = sum(jnp.sum(strip_rows(w) * g, axis=1) for w, g in pairs)
        return local / lax.dynamic_slice_in_dim(gain, wide_index * strip, strip)

    local = jnp.stack(
        [
            gain_grad([(w_query, grad_query), (w_key, grad_key), (w_value, grad_value)], gain_one),
            gain_grad([(w_gate, grad_gate), (w_up, grad_up)], gain_two),
        ]
    )
    local = local + narrow_swap(local, 1)
    local = local + narrow_swap(local, 2)
    grad_gain_one, grad_gain_two = local[0], local[1]
    return (
        output,
        grad_tokens,
        grad_gain_one,
        grad_query,
        grad_key,
        grad_value,
        grad_out,
        grad_gain_two,
        grad_gate,
        grad_up,
        grad_down,
    )


def solution(mesh):
    placed = (
        P("wide", None),
        P("wide", None),
        P("wide"),
        P(),
        P(),
        P(),
        P(None, "narrow"),
        P(None, "narrow"),
        P(None, "narrow"),
        P("narrow", None),
        P(),
        P(None, "narrow"),
        P(None, "narrow"),
        P("narrow", None),
    )
    return jax.shard_map(
        shards,
        mesh=mesh,
        in_specs=placed,
        out_specs=(
            P("wide", None),
            P("wide", None),
            P("wide"),
            P("wide", "narrow"),
            P("wide", "narrow"),
            P("wide", "narrow"),
            P("narrow", "wide"),
            P("wide"),
            P("wide", "narrow"),
            P("wide", "narrow"),
            P("narrow", "wide"),
        ),
        check_vma=False,
    )
```

```python
import functools

import jax
import jax.numpy as jnp
import numpy as np
from jax import lax
from jax.experimental import pallas as pl
from jax.experimental.pallas import tpu as pltpu
from jax.sharding import PartitionSpec as P

HD = 128
EPSILON = 1e-05
NEGATIVE = -1e30
BASE = 10000.0
LOG2E = 1.4426950408889634
SCORE = HD ** (-0.5) * LOG2E
FACTOR = HD ** (-0.5)
BF = jnp.bfloat16
F32 = jnp.float32
NT = (((1,), (1,)), ((), ()))
TN = (((0,), (0,)), ((), ()))
NN = (((1,), (0,)), ((), ()))
VM = pl.BlockSpec(memory_space=pltpu.VMEM)
SM = pl.BlockSpec(memory_space=pltpu.SMEM)
ANY = pl.BlockSpec(memory_space=pl.ANY)


def dot(a, b, dims=(((1,), (0,)), ((), ()))):
    return lax.dot_general(a, b, dims, preferred_element_type=F32)


def narrow_swap(value, mask):
    pairs = [(n, n ^ mask) for n in range(lax.axis_size("narrow"))]
    return lax.ppermute(value, "narrow", pairs)


def wide_swap(value):
    return lax.ppermute(value, "wide", [(w, w ^ 1) for w in range(lax.axis_size("wide"))])


def wide_ring(value, group, hop=1):
    ring = group // 2
    pairs = []
    for w in range(lax.axis_size("wide")):
        base, member = w // group * group, w % group
        pairs.append((w, base + (member // 2 + hop) % ring * 2 + member % 2))
    return lax.ppermute(value, "wide", pairs)


def wide_flip(value, bit):
    return lax.ppermute(value, "wide", [(w, w ^ (2 << bit)) for w in range(lax.axis_size("wide"))])


def halving(count):
    groups = []
    step = 1
    while step < count:
        groups.append([k for k in range(count) if k % (2 * step) == step])
        step *= 2
    return [*groups, [0]]


def stretches(groups):
    starts, at = [], 0
    for group in groups:
        starts.append((at, len(group)))
        at += len(group)
    return starts


def rope(value, cosine, sine):
    return value * cosine + pltpu.roll(value, HD // 2, 1) * sine


def norm_kv_kernel(core, x_ref, gain_ref, wk_ref, wv_ref, cos_ref, sin_ref, normed_ref, *kv_refs):
    x = x_ref[...].astype(F32)
    scale = lax.rsqrt(jnp.mean(x * x, axis=1, keepdims=True) + EPSILON)
    normed = (x * scale * gain_ref[...].astype(F32)).astype(BF)
    normed_ref[...] = normed
    keys = dot(normed, wk_ref[...])
    values = dot(normed, wv_ref[...])
    for h, ref in enumerate(kv_refs):
        cols = slice(h * HD, (h + 1) * HD)
        ref[:, :HD] = rope(keys[:, cols], cos_ref[...], sin_ref[...]).astype(BF)
        ref[:, HD:] = values[:, cols].astype(BF)


def norm_kv(core, tokens, gain, wk, wv, cosine, sine):
    rows, width = tokens.shape
    half = rows // 2
    heads = wk.shape[1] // HD
    full = lambda w: pl.BlockSpec(w.shape, lambda i, c: (0, 0))
    outs = pl.pallas_call(
        norm_kv_kernel,
        out_shape=[jax.ShapeDtypeStruct((rows, width), BF)]
        + [jax.ShapeDtypeStruct((rows, 2 * HD), BF)] * heads,
        grid_spec=pltpu.PrefetchScalarGridSpec(
            num_scalar_prefetch=1,
            grid=(2,),
            in_specs=[
                pl.BlockSpec((half, width), lambda i, c: (i ^ c[0], 0)),
                full(gain),
                full(wk),
                full(wv),
                pl.BlockSpec((half, HD), lambda i, c: (i, 0)),
                pl.BlockSpec((half, HD), lambda i, c: (i, 0)),
            ],
            out_specs=[pl.BlockSpec((half, width), lambda i, c: (i, 0))]
            + [pl.BlockSpec((half, 2 * HD), lambda i, c: (i, 0))] * heads,
        ),
        cost_estimate=pl.CostEstimate(flops=int(2.9e9), bytes_accessed=0, transcendentals=0),
        name="norm_kv",
    )(core, tokens, gain, wk, wv, cosine, sine)
    return outs[0], outs[1:]


def query_kernel(x_ref, w_ref, cos_ref, sin_ref, out_ref):
    raw = dot(x_ref[...], w_ref[...])
    for h in range(raw.shape[1] // HD):
        cols = slice(h * HD, (h + 1) * HD)
        out_ref[:, cols] = rope(raw[:, cols], cos_ref[...], sin_ref[...]).astype(BF)


def query_proj(x, w, cosine, sine):
    rows, width = x.shape
    half = rows // 2
    return pl.pallas_call(
        query_kernel,
        out_shape=jax.ShapeDtypeStruct((rows, w.shape[1]), BF),
        grid=(2,),
        in_specs=[
            pl.BlockSpec((half, width), lambda i: (i, 0)),
            pl.BlockSpec(w.shape, lambda i: (0, 0)),
            pl.BlockSpec((half, HD), lambda i: (i, 0)),
            pl.BlockSpec((half, HD), lambda i: (i, 0)),
        ],
        out_specs=pl.BlockSpec((half, w.shape[1]), lambda i: (i, 0)),
        cost_estimate=pl.CostEstimate(flops=int(2.9e9), bytes_accessed=0, transcendentals=0),
        name="query_proj",
    )(x, w, cosine, sine)


def fetch_slots(slot_refs, slots, kv_ref, sems):
    rows, width = slot_refs[0].shape
    copies = []
    for at, ref in enumerate(slot_refs):
        head, slot = divmod(at, slots)
        spot = kv_ref.at[pl.ds(slot * rows, rows), pl.ds(head * width, width)]
        copies.append(pltpu.make_async_copy(ref, spot, sems.at[at]))
    for copy in copies:
        copy.start()
    for copy in copies:
        copy.wait()


def allowed(pk, size, span, pos, low):
    key_pos = pk * size + lax.broadcasted_iota(jnp.int32, (size, span), 0)
    return (key_pos <= pos) & (key_pos >= low)


def attn_fwd_kernel(slots, *refs):
    meta, q_ref, pos_ref, low_ref = refs[:4]
    slot_refs = refs[4 : 4 + slots]
    mixed_ref, lse_ref, kv_ref, acc_ref, sems = refs[-5:]
    fetch_slots(slot_refs, slots, kv_ref, sems)
    size = q_ref.shape[0] // 2
    for i in range(2):
        rows = slice(i * size, (i + 1) * size)
        pos = jnp.tile(pos_ref[0:1, rows], (1, 2))
        low = jnp.tile(low_ref[0:1, rows], (1, 2))
        queries = [q_ref[rows, r * HD : (r + 1) * HD] for r in range(2)]
        acc_ref[...] = jnp.zeros_like(acc_ref)

        def body(pk, carry):
            peak, total = carry
            spot = pl.multiple_of(meta[4 + pk] * size, size)
            keys = kv_ref[pl.ds(spot, size), :HD]
            values = kv_ref[pl.ds(spot, size), HD:]
            scores = jnp.concatenate([dot(keys, q, NT) for q in queries], axis=1) * SCORE
            scores = jnp.where(allowed(pk, size, 2 * size, pos, low), scores, NEGATIVE)
            peak_new = jnp.maximum(peak, jnp.max(scores, axis=0, keepdims=True))
            alpha = jnp.exp2(peak - peak_new)
            probs = jnp.exp2(scores - peak_new)
            total = total * alpha + jnp.sum(probs, axis=0, keepdims=True)
            acc_ref[...] = acc_ref[...] * alpha + dot(values, probs.astype(BF), TN)
            return peak_new, total

        start = (jnp.full((1, 2 * size), NEGATIVE, F32), jnp.zeros((1, 2 * size), F32))
        peak, total = lax.fori_loop(meta[i], meta[2 + i] + 1, body, start)
        lse_ref[i : i + 1, :] = peak + jnp.log2(total)
        out = acc_ref[...] * (1.0 / total)
        for r in range(2):
            mixed_ref[rows, r * HD : (r + 1) * HD] = out[:, r * size : (r + 1) * size].T.astype(BF)


def attn_fwd(head, meta, q, pos, low, slots, mixed):
    rows = q.shape[0]
    count = len(slots)
    earlier = [] if mixed is None else [mixed]
    return pl.pallas_call(
        functools.partial(attn_fwd_kernel, count),
        out_shape=(
            jax.ShapeDtypeStruct(q.shape, BF),
            jax.ShapeDtypeStruct((2, rows), F32),
        ),
        grid=(1,),
        in_specs=[
            SM,
            pl.BlockSpec((rows, 2 * HD), lambda i: (0, head)),
            pl.BlockSpec(pos.shape, lambda i: (0, 0)),
            pl.BlockSpec(low.shape, lambda i: (0, 0)),
        ]
        + [ANY] * (count + len(earlier)),
        out_specs=[
            pl.BlockSpec((rows, 2 * HD), lambda i: (0, head)),
            pl.BlockSpec((2, rows), lambda i: (0, 0)),
        ],
        input_output_aliases={4 + count: 0} if earlier else {},
        scratch_shapes=[
            pltpu.VMEM((count * rows, 2 * HD), BF),
            pltpu.VMEM((HD, rows), F32),
            pltpu.SemaphoreType.DMA((count,)),
        ],
        cost_estimate=pl.CostEstimate(flops=int(1e9), bytes_accessed=0, transcendentals=0),
        name="attn_fwd",
    )(meta, q, pos, low, *slots, *earlier)


def attn_bwd_kernel(heads, slots, groups, *refs):
    meta, q_ref, pos_ref, low_ref, dmix_ref, mixed_ref, cos_ref, sin_ref = refs[:8]
    lse_refs = refs[8 : 8 + heads]
    at = 8 + heads
    slot_refs = refs[at : at + heads * slots]
    at += heads * slots
    dq_ref, dkv_refs = refs[at], refs[at + 1 : -4]
    kv_ref, dkv_ref, dq_acc, sems = refs[-4:]
    fetch_slots(slot_refs, slots, kv_ref, sems)
    dkv_ref[...] = jnp.zeros_like(dkv_ref)
    rows_all = q_ref.shape[0]
    size = rows_all // 2
    for i in range(2):
        rows = slice(i * size, (i + 1) * size)
        pos = jnp.tile(pos_ref[0:1, rows], (1, 2))
        low = jnp.tile(low_ref[0:1, rows], (1, 2))
        for g in range(heads):
            cols = [slice((2 * g + r) * HD, (2 * g + r + 1) * HD) for r in range(2)]
            queries = jnp.concatenate([q_ref[rows, c] for c in cols], axis=0)
            grads = jnp.concatenate([dmix_ref[rows, c] for c in cols], axis=0)
            outs = jnp.concatenate([mixed_ref[rows, c] for c in cols], axis=0)
            delta = jnp.sum((grads.astype(F32) * outs.astype(F32)).T, axis=0, keepdims=True)
            lse = lse_refs[g][i : i + 1, :]
            dq_acc[...] = jnp.zeros_like(dq_acc)

            def body(pk, carry):
                spot = pl.multiple_of(meta[4 + pk] * size, size)
                key_cols = slice(2 * g * HD, (2 * g + 1) * HD)
                value_cols = slice((2 * g + 1) * HD, (2 * g + 2) * HD)
                keys = kv_ref[pl.ds(spot, size), key_cols]
                values = kv_ref[pl.ds(spot, size), value_cols]
                scores = dot(keys, queries, NT) * SCORE
                probs = jnp.where(
                    allowed(pk, size, 2 * size, pos, low), jnp.exp2(scores - lse), 0.0
                )
                d_probs = dot(values, grads, NT)
                d_scores = (probs * (d_probs - delta)).astype(BF)
                dkv_ref[pl.ds(spot, size), value_cols] += dot(probs.astype(BF), grads)
                dkv_ref[pl.ds(spot, size), key_cols] += dot(d_scores, queries) * FACTOR
                dq_acc[...] += dot(d_scores, keys, TN)
                return carry

            lax.fori_loop(meta[i], meta[2 + i] + 1, body, 0)
            for r in range(2):
                part = dq_acc[r * size : (r + 1) * size, :] * FACTOR
                dq_ref[rows, cols[r]] = rope(part, cos_ref[rows, :], -sin_ref[rows, :]).astype(BF)
    ring = slots // 2
    for j, ref in enumerate(dkv_refs):
        first = ring * (j // len(groups))
        for place, k in enumerate(groups[j % len(groups)]):
            spot = pl.multiple_of((first + meta[4 + 2 * slots + k]) * rows_all, rows_all)
            ref[place * rows_all : (place + 1) * rows_all, :] = dkv_ref[
                pl.ds(spot, rows_all), :
            ].astype(BF)


def attn_bwd(meta, q, pos, low, lse, mixed, dmix, cosine, sine, slots):
    rows, q_width = q.shape
    heads, count = len(slots), len(slots[0])
    kv_width = heads * 2 * HD
    groups = halving(count // 2)
    outs = pl.pallas_call(
        functools.partial(attn_bwd_kernel, heads, count, groups),
        out_shape=[jax.ShapeDtypeStruct((rows, q_width), BF)]
        + [jax.ShapeDtypeStruct((len(g) * rows, kv_width), BF) for g in groups] * 2,
        in_specs=[SM] + [VM] * (7 + heads) + [ANY] * (heads * count),
        out_specs=[VM] * (1 + 2 * len(groups)),
        scratch_shapes=[
            pltpu.VMEM((count * rows, kv_width), BF),
            pltpu.VMEM((count * rows, kv_width), F32),
            pltpu.VMEM((rows, HD), F32),
            pltpu.SemaphoreType.DMA((heads * count,)),
        ],
        cost_estimate=pl.CostEstimate(flops=int(2e9), bytes_accessed=0, transcendentals=0),
        name="attn_bwd",
    )(meta, q, pos, low, dmix, mixed, cosine, sine, *lse, *[v for head in slots for v in head])
    return outs[0], outs[1 : 1 + len(groups)], outs[1 + len(groups) :]


def cost(micros):
    return pl.CostEstimate(flops=int(micros * 0.3e9), bytes_accessed=0, transcendentals=0)


def split_rows(total, own_ref, other_ref):
    half = own_ref.shape[0]
    own_ref[...] = total[:half].astype(BF)
    other_ref[...] = total[half:].astype(BF)


def project_kernel(spec, *refs):
    total = None
    for a, b, offset, dims in spec:
        left = refs[a][...] if dims is not None else None
        if dims == "nt":
            right, form = refs[b][:, offset : offset + left.shape[1]], NT
        else:
            right, form = refs[b][offset : offset + left.shape[1], :], NN
        term = dot(left, right, form)
        total = term if total is None else total + term
    split_rows(total, refs[-2], refs[-1])


def project(pairs, dims, tile, micros):
    operands, specs, plan, weights = [], [], [], []
    for a, b, offset in pairs:
        operands.append(a)
        specs.append(pl.BlockSpec(a.shape, lambda i: (0, 0)))
        spot = next((at for at, seen in weights if seen is b), None)
        left = len(operands) - 1
        if spot is None:
            spot = len(operands)
            operands.append(b)
            weights.append((spot, b))
            if dims == "nt":
                specs.append(pl.BlockSpec((tile, b.shape[1]), lambda i: (i, 0)))
            else:
                specs.append(pl.BlockSpec((b.shape[0], tile), lambda i: (0, i)))
        plan.append((left, spot, offset, dims))
    rows = pairs[0][0].shape[0]
    width = pairs[0][1].shape[0 if dims == "nt" else 1]
    return pl.pallas_call(
        functools.partial(project_kernel, plan),
        out_shape=[jax.ShapeDtypeStruct((rows // 2, width), BF)] * 2,
        grid=(width // tile,),
        in_specs=specs,
        out_specs=[pl.BlockSpec((rows // 2, tile), lambda i: (0, i))] * 2,
        cost_estimate=cost(micros),
        name="project",
    )(*operands)


def back_dense_kernel(gate_a, up_a, gate_b, up_b, wg_ref, wu_ref, own_ref, other_ref):
    total = None
    offset = 0
    for group in ((gate_a, up_a), (gate_b, up_b)):
        count = group[0].shape[1]
        for ref, w_ref in zip(group, (wg_ref, wu_ref)):
            term = dot(ref[...], w_ref[:, offset : offset + count], NT)
            total = term if total is None else total + term
        offset += count
    split_rows(total, own_ref, other_ref)


def back_dense(grads, w_gate, w_up, tile, part, parts):
    width, hidden = w_gate.shape[0] // parts, w_gate.shape[1]
    rows = grads[0].shape[0]
    ahead = part * (width // tile)
    weight = pl.BlockSpec((tile, hidden), lambda i: (ahead + i, 0))
    return pl.pallas_call(
        back_dense_kernel,
        out_shape=[jax.ShapeDtypeStruct((rows // 2, width), BF)] * 2,
        grid=(width // tile,),
        in_specs=[pl.BlockSpec(v.shape, lambda i: (0, 0)) for v in grads] + [weight, weight],
        out_specs=[pl.BlockSpec((rows // 2, tile), lambda i: (0, i))] * 2,
        cost_estimate=cost(11 / parts),
        name="back_dense",
    )(*grads, w_gate, w_up)


def gated_kernel(own_ref, other_ref, wg_ref, wu_ref, di_ref, inner_ref, dg_ref, du_ref, all_ref):
    @pl.when(pl.program_id(0) == 0)
    def _():
        half = own_ref.shape[0]
        all_ref[:half, :] = own_ref[...]
        all_ref[half:, :] = other_ref[...]

    gate = dot(all_ref[...], wg_ref[...])
    up = dot(all_ref[...], wu_ref[...])
    sigma = 1.0 / (1.0 + jnp.exp(-gate))
    silu = gate * sigma
    d_inner = di_ref[...]
    inner_ref[...] = (silu * up).astype(BF)
    dg_ref[...] = (d_inner * up * sigma * (1.0 + gate * (1.0 - sigma))).astype(BF)
    du_ref[...] = (d_inner * silu).astype(BF)


def gated(own, other, wg, wu, d_inner, first, columns, tile):
    half, width = own.shape
    weight = pl.BlockSpec((width, tile), lambda i: (0, first // tile + i))
    whole = pl.BlockSpec((half, width), lambda i: (0, 0))
    return pl.pallas_call(
        gated_kernel,
        out_shape=[jax.ShapeDtypeStruct((2 * half, columns), BF)] * 3,
        grid=(pl.cdiv(columns, tile),),
        in_specs=[
            whole,
            whole,
            weight,
            weight,
            pl.BlockSpec((2 * half, tile), lambda i: (0, first // tile + i)),
        ],
        out_specs=[pl.BlockSpec((2 * half, tile), lambda i: (0, i))] * 3,
        scratch_shapes=[pltpu.VMEM((2 * half, width), BF)],
        cost_estimate=cost(7.5),
        name="gated",
    )(own, other, wg, wu, d_inner)


def mixed_grad_kernel(own_ref, other_ref, w_ref, out_ref):
    both = jnp.concatenate([own_ref[...], other_ref[...]], axis=0)
    out_ref[...] = dot(both, w_ref[...], NT).astype(BF)


def mixed_grad(own, other, w):
    return pl.pallas_call(
        mixed_grad_kernel,
        out_shape=jax.ShapeDtypeStruct((2 * own.shape[0], w.shape[0]), BF),
        in_specs=[VM] * 3,
        out_specs=VM,
        cost_estimate=cost(4),
        name="mixed_grad",
    )(own, other, w)


def d_inner_kernel(x_ref, w_ref, out_ref):
    out_ref[...] = dot(x_ref[...], w_ref[...], NT)


def inner_grad(x, w, tile):
    rows, width = x.shape
    hidden = w.shape[0]
    return pl.pallas_call(
        d_inner_kernel,
        out_shape=jax.ShapeDtypeStruct((rows, hidden), F32),
        grid=(pl.cdiv(hidden, tile),),
        in_specs=[
            pl.BlockSpec((rows, width), lambda i: (0, 0)),
            pl.BlockSpec((tile, width), lambda i: (i, 0)),
        ],
        out_specs=pl.BlockSpec((rows, tile), lambda i: (0, i)),
        cost_estimate=cost(8),
        name="inner_grad",
    )(x, w)


def pack_kernel(count, plan, strip, tbl, *refs):
    ins, outs = refs[:count], refs[count:]
    for out_ref, pieces in zip(outs, plan):
        column = 0
        for at, rows, row in pieces:
            for k in range(tbl.shape[1]):
                first = pl.multiple_of(tbl[row, k] * strip, 128)
                out_ref[:, column : column + strip] = ins[at][rows, pl.ds(first, strip)]
                column += strip


def pack(values, plan, tbl, strip):
    turns = tbl.shape[1]
    if strip % 128:
        cut = lambda v, rows, at: lax.dynamic_slice_in_dim(v[rows], at * strip, strip, axis=1)
        return [
            jnp.concatenate(
                [cut(values[at], rows, tbl[row, k]) for at, rows, row in pieces for k in range(turns)],
                axis=1,
            )
            for pieces in plan
        ]
    return pl.pallas_call(
        functools.partial(pack_kernel, len(values), plan, strip),
        out_shape=[
            jax.ShapeDtypeStruct(
                (p[0][1].stop - p[0][1].start, len(p) * turns * strip), values[0].dtype
            )
            for p in plan
        ],
        in_specs=[SM] + [VM] * len(values),
        out_specs=[VM] * len(plan),
        cost_estimate=cost(1.5),
        name="pack",
    )(tbl, *values)


def strip_rows_kernel(halves, near, rights, nears, spans, tbl, *refs):
    left = refs[:halves]
    left_near = refs[halves : halves + near]
    right = refs[halves + near : halves + near + rights]
    right_near = refs[halves + near + rights : halves + near + rights + nears]
    outs = refs[halves + near + rights + nears :]
    step = pl.program_id(0)
    join = lambda group: (
        group[0][...] if len(group) == 1 else jnp.concatenate([r[...] for r in group], axis=0)
    )
    mine, theirs = join(left), join(left_near)
    pieces = []
    for r, n in zip(right, right_near):
        planes = range(r.shape[0]) if len(r.shape) == 3 else [None]
        for k in planes:
            a = r[...] if k is None else r[k]
            b = n[...] if k is None else n[k]
            pieces.append((dot(mine, a, TN) + dot(theirs, b, TN)).astype(BF))
    for (start, length), out in zip(spans, outs):

        @pl.when((step >= start) & (step < start + length))
        def _(out=out):
            column = 0
            for piece in pieces:
                out[:, column : column + piece.shape[1]] = piece
                column += piece.shape[1]


def strip_rows_grad(left, left_near, right, right_near, tbl, strip, micros, single=False):
    turns = tbl.shape[1]
    columns = sum(r.shape[-1] * (r.shape[0] if r.ndim == 3 else 1) for r in right)
    spans = [(k, 1) for k in range(turns)] if single else stretches(halving(turns))
    if strip % 128:
        near = jnp.concatenate(left_near, axis=0)
        mine = jnp.concatenate(left, axis=0)
        flat = lambda r: [r] if r.ndim == 2 else [r[k] for k in range(r.shape[0])]
        outs = []
        for start, length in spans:
            group = []
            for k in range(start, start + length):
                a = lax.dynamic_slice_in_dim(mine, tbl[0, k] * strip, strip, axis=1)
                b = near[:, k * strip : (k + 1) * strip]
                group.append(
                    jnp.concatenate(
                        [
                            dot(a, x, TN) + dot(b, y, TN)
                            for r, n in zip(right, right_near)
                            for x, y in zip(flat(r), flat(n))
                        ],
                        axis=1,
                    ).astype(BF)
                )
            outs.append(jnp.concatenate(group, axis=0))
        return outs
    held = lambda start, length: (lambda i, t: (jnp.clip(i - start, 0, length - 1), 0))
    whole = lambda v: pl.BlockSpec(v.shape, lambda i, t: (0,) * v.ndim)
    return pl.pallas_call(
        functools.partial(
            strip_rows_kernel, len(left), len(left_near), len(right), len(right_near), spans
        ),
        out_shape=[jax.ShapeDtypeStruct((length * strip, columns), BF) for _, length in spans],
        grid_spec=pltpu.PrefetchScalarGridSpec(
            num_scalar_prefetch=1,
            grid=(turns,),
            in_specs=[pl.BlockSpec((v.shape[0], strip), lambda i, t: (0, t[0, i])) for v in left]
            + [pl.BlockSpec((v.shape[0], strip), lambda i, t: (0, i)) for v in left_near]
            + [whole(v) for v in [*right, *right_near]],
            out_specs=[pl.BlockSpec((strip, columns), held(*span)) for span in spans],
        ),
        cost_estimate=cost(micros),
        name="strip_rows",
    )(tbl, *left, *left_near, *right, *right_near)


def strip_columns_kernel(parts, halves, near, strip, spans, *refs):
    at = 2 * parts
    right, right_near = refs[at : at + halves], refs[at + halves : at + halves + near]
    outs = refs[at + halves + near :]
    first = 0
    for p in range(parts):
        total = None
        for ref, group in ((refs[p], right), (refs[parts + p], right_near)):
            row = 0
            for r in group:
                term = dot(ref[row : row + r.shape[0], :], r[...], TN)
                total = term if total is None else total + term
                row += r.shape[0]
        for (start, length), out in zip(spans, outs):
            out[first : first + total.shape[0], :] = total[
                :, start * strip : (start + length) * strip
            ].astype(BF)
        first += total.shape[0]


def strip_columns_grad(
    left, left_near, right, right_near, turns, strip, tile, micros, near_at=0, single=False
):
    rows, count = left[0].shape[0], sum(v.shape[1] for v in left)
    if strip * turns % 128:
        raise ValueError(strip)
    spans = [(k, 1) for k in range(turns)] if single else stretches(halving(turns))
    whole = lambda v: pl.BlockSpec(v.shape, lambda i: (0, 0))
    near = lambda v: pl.BlockSpec((v.shape[0], turns * strip), lambda i: (0, near_at))
    if len(left) == 1:
        left_specs = [pl.BlockSpec((rows, tile), lambda i: (0, i))] * 2
    else:
        tile = count
        left_specs = [whole(v) for v in [*left, *left_near]]
    return pl.pallas_call(
        functools.partial(
            strip_columns_kernel, len(left), len(right), len(right_near), strip, spans
        ),
        out_shape=[jax.ShapeDtypeStruct((count, length * strip), BF) for _, length in spans],
        grid=(pl.cdiv(count, tile),),
        in_specs=left_specs + [whole(v) for v in right] + [near(v) for v in right_near],
        out_specs=[pl.BlockSpec((tile, length * strip), lambda i: (i, 0)) for _, length in spans],
        cost_estimate=cost(micros),
        name="strip_columns",
    )(*left, *left_near, *right, *right_near)


def close_kv_kernel(count, *refs):
    cos_ref, sin_ref, dk_ref, dv_ref = refs[count:]
    total = refs[0][...].astype(F32)
    for ref in refs[1:count]:
        total = total + ref[...].astype(F32)
    heads = dk_ref.shape[1] // HD
    for h in range(heads):
        cols = slice(h * HD, (h + 1) * HD)
        keys = total[:, 2 * h * HD : (2 * h + 1) * HD]
        dk_ref[:, cols] = rope(keys, cos_ref[...], -sin_ref[...]).astype(BF)
        dv_ref[:, cols] = total[:, (2 * h + 1) * HD : (2 * h + 2) * HD].astype(BF)


def close_kv(terms, cosine, sine):
    rows, width = terms[0].shape
    first = lambda w: pl.BlockSpec((rows, w), lambda i: (0, 0))
    return pl.pallas_call(
        functools.partial(close_kv_kernel, len(terms)),
        out_shape=[jax.ShapeDtypeStruct((rows, width // 2), BF)] * 2,
        grid=(1,),
        in_specs=[first(width)] * len(terms) + [first(HD)] * 2,
        out_specs=[first(width // 2)] * 2,
        cost_estimate=cost(1.5),
        name="close_kv",
    )(*terms, cosine, sine)


def norm_backward(source, scale_rows, gain, upstream):
    weighted = upstream * gain
    average = jnp.mean(weighted * source, axis=1, keepdims=True)
    return scale_rows * weighted - source * scale_rows**3 * average


def after(value, *done):
    return lax.optimization_barrier((value, *done))[0]


def shards(
    tokens,
    cotangent,
    keep_mask,
    doc_lengths,
    block_order,
    gain_attn,
    w_query,
    w_key,
    w_value,
    w_out,
    gain_dense,
    w_gate,
    w_up,
    w_down,
):
    rows, width = tokens.shape
    half = rows // 2
    wide = lax.axis_size("wide")
    group = wide // block_order.shape[0]
    ring = group // 2
    wide_index = lax.axis_index("wide")
    member = wide_index % group
    seq_index = wide_index // group
    side = (wide_index % 2).astype(jnp.int32)
    core = lax.axis_index("narrow") % 2
    strip = width // wide
    turns = wide // 2

    def ordered(mine, other):
        return jnp.where(
            core == 0,
            jnp.concatenate([mine, other], axis=0),
            jnp.concatenate([other, mine], axis=0),
        )

    def own_half(value):
        return lax.dynamic_slice_in_dim(value, core * half, half)

    def other_half(value):
        return lax.dynamic_slice_in_dim(value, (1 - core) * half, half)

    order_row = lax.dynamic_index_in_dim(block_order, seq_index, 0, keepdims=False)
    length_row = lax.dynamic_index_in_dim(doc_lengths, seq_index, 0, keepdims=False)
    doc_ends = jnp.cumsum(length_row)
    places = jnp.stack([member * 2 + core, member * 2 + 1 - core])
    chosen = jnp.sum(
        jnp.where(places[:, None] == jnp.arange(2 * group)[None, :], order_row[None, :], 0), axis=1
    )
    pos = (chosen[:, None] * half + jnp.arange(half, dtype=jnp.int32)[None, :]).reshape(-1)
    low = jnp.max(jnp.where(doc_ends[None, :] <= pos[:, None], doc_ends[None, :], 0), axis=1)
    block_low = low.reshape(2, half)[:, 0] // half
    stored = jnp.sum(
        jnp.where(
            order_row[None, :] == jnp.arange(2 * group)[:, None], jnp.arange(2 * group)[None, :], 0
        ),
        axis=1,
    )
    owner = stored // 2
    slot = (member // 2 - owner // 2) % ring + ring * (owner % 2 != side).astype(jnp.int32)
    spots = slot * 2 + (stored % 2 != core).astype(jnp.int32)
    place = member // 2
    back = (place - (place ^ jnp.arange(ring, dtype=jnp.int32))) % ring
    meta = jnp.concatenate([block_low, chosen, spots, back]).astype(jnp.int32)
    frequency = BASE ** (-(jnp.arange(HD // 2, dtype=F32) * 2.0) / HD)
    angles = pos.astype(F32)[:, None] * frequency[None, :]
    cosine = jnp.cos(angles)
    sine = jnp.sin(angles)
    cosine = jnp.concatenate([cosine, cosine], axis=1)
    sine = jnp.concatenate([-sine, sine], axis=1)
    pos_row = pos[None, :]
    low_row = low[None, :]

    order = np.array([k for stretch in halving(turns) for k in stretch], np.int32)
    turn_row = wide_index // 2 ^ order
    tbl = jnp.stack([2 * turn_row + side, 2 * turn_row + 1 - side]).astype(jnp.int32)
    round_row = (wide_index // 2 - 1 - jnp.arange(turns, dtype=jnp.int32)) % turns
    round_tbl = jnp.stack([2 * round_row + side, 2 * round_row + 1 - side]).astype(jnp.int32)
    both_tbl = jnp.concatenate([tbl, round_tbl])
    core_arr = core.astype(jnp.int32)[None]
    normed_one, both = norm_kv(core_arr, tokens, gain_attn[None, :], w_key, w_value, cosine, sine)
    low_rows, all_rows = slice(0, half), slice(0, rows)

    def together(*values):
        return list(lax.optimization_barrier(values))

    near, far = [[v] for v in both], [[] for v in both]
    query = d_dense = d_inner = input_near = d_dense_strips = None
    for step in range(ring):
        for head in range(len(both)):
            held = near[head][step]
            if step + 1 < ring:
                sent = [wide_swap(held), wide_ring(held, group)]
            elif head == 0:
                sent = [wide_swap(held)]
            else:
                sent = [wide_ring(far[head][0], group, -1)]
            beside = []
            if step == 0 and head == 0:
                beside = [query_proj(normed_one, w_query, cosine, sine)]
            if step == 0 and head == 1:
                keep_rel = jnp.concatenate([own_half(keep_mask), other_half(keep_mask)])[:, None]
                cot_rel = jnp.concatenate([own_half(cotangent), other_half(cotangent)])
                beside = [jnp.where(keep_rel > 0, cot_rel, jnp.zeros_like(cot_rel))]
            if step == 1 and head == 0:
                beside = [inner_grad(d_dense, w_down, 256)]
            if step == 2 and head == 0:
                beside = pack(
                    [normed_one, d_dense],
                    [[(0, low_rows, 3), (1, low_rows, 1)], [(1, all_rows, 0)]],
                    both_tbl,
                    strip,
                )
            done = together(*sent, *beside)
            far[head].append(done[0])
            if step + 1 < ring:
                near[head].append(done[1])
            if step == 0 and head == 0:
                query = done[-1]
            if step == 0 and head == 1:
                d_dense = done[-1]
            if step == 1 and head == 0:
                d_inner = done[-1]
            if step == 2 and head == 0:
                input_near, d_dense_strips = done[-2:]
    slots = [n + f for n, f in zip(near, far)]
    input_near = wide_swap(after(input_near, *slots[0], *slots[-1]))
    mixed, lse = None, []
    for h, held in enumerate(slots):
        mixed, part = attn_fwd(h, meta, query, pos_row, low_row, held, mixed)
        lse.append(part)

    def reduce_narrow(halves, hold=()):
        own_part, other_part = halves
        got = narrow_swap(other_part, 1)
        held = (own_part.astype(F32) + got.astype(F32)).astype(BF)
        return held, narrow_swap(held, 2)

    def total_of(held, got):
        return held.astype(F32) + got.astype(F32)

    part = project([(mixed, w_out, 0)], "nn", 1024, 4)
    held, got = reduce_narrow((part[0], after(part[1], input_near)))
    mixed_near = wide_swap(mixed)
    input_near_other = narrow_swap(input_near, 1)
    source = own_half(tokens).astype(F32)
    keep_own = own_half(keep_mask).astype(F32)[:, None]
    hidden_one = source + keep_own * total_of(held, got)
    gain_two = gain_dense.astype(F32)
    scale_two = lax.rsqrt(jnp.mean(hidden_one * hidden_one, axis=1, keepdims=True) + EPSILON)
    normed_two = (hidden_one * scale_two * gain_two).astype(BF)
    normed_two_other = narrow_swap(after(normed_two, mixed_near), 1)
    hidden = w_gate.shape[1]
    tile = 256
    first_count = 3 * tile
    inner_a, *dgu_a = gated(
        normed_two, normed_two_other, w_gate, w_up, d_inner, 0, first_count, tile
    )
    inner_a_near = wide_swap(inner_a)
    inner_b, *dgu_b = gated(
        after(normed_two, inner_a),
        normed_two_other,
        w_gate,
        w_up,
        d_inner,
        first_count,
        hidden - first_count,
        tile,
    )
    back = back_dense([*dgu_a, *dgu_b], w_gate, w_up, 512, 0, 1)
    held, got = reduce_narrow((back[0], after(back[1], inner_a_near)))

    def halve(parts, axis, hold=None, first=None):
        groups = halving(1 << (len(parts) - 1))
        size = parts[-1].shape[axis]
        received, sent = [], None
        for bit, group in enumerate(groups[:-1]):
            sent = parts[bit]
            if bit:
                total = sent.astype(F32)
                for early, value in enumerate(received):
                    there = [k ^ (1 << early) for k in groups[early]]
                    pick = [
                        lax.slice_in_dim(value, size * there.index(k), size * (there.index(k) + 1), axis=axis)
                        for k in group
                    ]
                    total = total + (pick[0] if len(pick) == 1 else jnp.concatenate(pick, axis)).astype(F32)
                sent = total.astype(BF)
            got = first if bit == 0 and first is not None else wide_flip(sent, bit)
            received.append(got if hold is None else after(got, hold))
        return received, sent

    def ring_sum(parts, hold=None, last=()):
        carried, first = parts[0], None
        for k, part in enumerate(parts[1:]):
            got = wide_ring(carried, wide)
            if k == 0 and hold is not None:
                got = after(got, hold)
            if k == len(parts) - 2 and last:
                got = after(got, *last)
            total = part.astype(F32) + got.astype(F32)
            carried = total.astype(BF)
            first = carried if first is None else first
        return total, first

    def close(parts, received, axis):
        size = parts[-1].shape[axis]
        total = parts[-1].astype(F32)
        for value in received:
            total = total + lax.slice_in_dim(value, 0, size, axis=axis).astype(F32)
        return total

    near_sides = [input_near, input_near_other]
    down_a = strip_columns_grad(
        [after(inner_a, held)],
        [inner_a_near],
        [d_dense_strips],
        near_sides,
        turns,
        strip,
        tile,
        4,
        1,
    )
    inner_b_near = wide_swap(inner_b)
    down_a_got, down_a_mid = halve(down_a, 1)
    dgu_a_near = [wide_swap(after(v, inner_b)) for v in dgu_a]
    dense_parts = project(
        [(after(inner_a, down_a[0], inner_b_near), w_down, 0), (inner_b, w_down, first_count)], "nn", 512, 6
    )
    (normed_two_near,) = pack(
        [after(normed_two, dense_parts[0])], [[(0, low_rows, 1)]], round_tbl, strip
    )
    normed_two_near = wide_swap(normed_two_near)
    down_b = strip_columns_grad(
        [after(inner_b, dense_parts[0])], [inner_b_near], [d_dense_strips], near_sides, turns, strip, tile, 4, 1
    )

    got = after(got, dense_parts[0], down_b[0])
    upstream = own_half(cotangent).astype(F32)
    d_hidden = upstream + norm_backward(hidden_one, scale_two, gain_two, total_of(held, got))
    d_attn = (keep_own * d_hidden).astype(BF)
    d_attn_other = narrow_swap(after(d_attn, dgu_a_near[0], down_a_mid), 1)

    down_b_first = wide_flip(down_b[0], 0)
    d_mixed = mixed_grad(d_attn, d_attn_other, w_out)
    d_query, d_near, d_far = attn_bwd(
        meta, query, pos_row, low_row, lse, mixed, after(d_mixed, down_a_got[-1]), cosine, sine, slots
    )
    held_out, got_out = reduce_narrow((dense_parts[0], after(dense_parts[1], d_mixed)))
    output_own = (hidden_one + keep_own * total_of(held_out, got_out)).astype(BF)
    output = ordered(output_own, narrow_swap(output_own, 1))

    normed_two_near_other = narrow_swap(after(normed_two_near, d_query), 1)
    normed_two_sides = [normed_two_near, normed_two_near_other]
    gate_up_a = strip_rows_grad(
        [after(normed_two, d_query, down_b_first), normed_two_other], normed_two_sides, dgu_a, dgu_a_near, round_tbl, strip, 8, True
    )
    grad_gate_up_a, gate_up_a_mid = ring_sum(gate_up_a)
    d_far = [wide_swap(v) for v in d_far]
    d_far[0] = after(d_far[0], gate_up_a_mid)
    pairs = [
        (n.astype(F32) + f.astype(F32)).astype(BF) for n, f in zip(d_near[:-1], d_far[:-1])
    ]
    kv_got, kv_mid = halve([*pairs, d_near[-1]], 0)
    d_key, d_value = close_kv([d_near[-1], d_far[-1], *kv_got], cosine, sine)

    down_b_got, _ = halve(down_b, 1, kv_mid, down_b_first)
    dgu_b_near = [wide_swap(after(v, d_query)) for v in dgu_b]
    gate_up_b = strip_rows_grad(
        [after(normed_two, gate_up_a_mid, kv_mid), normed_two_other],
        normed_two_sides,
        dgu_b,
        dgu_b_near,
        round_tbl,
        strip,
        7,
        True,
    )
    d_query_near = wide_swap(after(d_query, pairs[0]))
    grad_gate_up_b, gate_up_b_mid = ring_sum(gate_up_b)
    d_attn_near, d_attn_strips, d_attn_other_strips = pack(
        [after(d_attn, gate_up_a[0]), d_attn_other],
        [[(0, low_rows, 1)], [(0, low_rows, 0)], [(1, low_rows, 0)]],
        round_tbl,
        strip,
    )
    d_attn_near = wide_swap(after(d_attn_near, pairs[0]))
    d_attn_near_other = narrow_swap(after(d_attn_near, gate_up_b[0]), 1)
    query_part = strip_rows_grad(
        [after(normed_one, gate_up_b[0])], near_sides, [d_query], [d_query_near], round_tbl, strip, 4, True
    )
    out_part = strip_columns_grad(
        [after(mixed, query_part[0])],
        [mixed_near],
        [d_attn_strips, d_attn_other_strips],
        [d_attn_near, d_attn_near_other],
        turns,
        strip,
        tile,
        4,
        0,
        True,
    )

    kv_width = w_key.shape[1]
    held, got = reduce_narrow(
        project([(d_query, w_query, 0), (d_key, w_key, 0), (d_value, w_value, 0)], "nt", 512, 6)
    )
    gain_one = gain_attn.astype(F32)
    scale_one = lax.rsqrt(jnp.mean(source * source, axis=1, keepdims=True) + EPSILON)
    d_normed_one = total_of(held, got)
    grad_own = (d_hidden + norm_backward(source, scale_one, gain_one, d_normed_one)).astype(BF)
    grad_tokens = ordered(grad_own, narrow_swap(grad_own, 1))

    d_key_near = wide_swap(d_key)
    d_value_near = wide_swap(d_value)
    kv_part = strip_rows_grad(
        [after(normed_one, out_part[0])],
        near_sides,
        [d_key, d_value],
        [d_key_near, d_value_near],
        round_tbl,
        strip,
        4,
        True,
    )
    grad_kv, _ = ring_sum(kv_part, None, (grad_own, output))
    grad_query, _ = ring_sum(query_part, kv_part[0])
    grad_out, _ = ring_sum(out_part, kv_part[0])
    down_a_got[-1], down_b_got[-1] = after(down_a_got[-1], kv_part[0]), after(down_b_got[-1], kv_part[0])
    grad_down_a = close(down_a, down_a_got, 1)
    grad_down_b = close(down_b, down_b_got, 1)
    grad_key, grad_value = grad_kv[:, :kv_width], grad_kv[:, kv_width:]
    grad_down = jnp.concatenate([grad_down_a, grad_down_b], axis=0)
    second_count = hidden - first_count
    grad_gate = jnp.concatenate(
        [grad_gate_up_a[:, :first_count], grad_gate_up_b[:, :second_count]], axis=1
    )
    grad_up = jnp.concatenate(
        [grad_gate_up_a[:, first_count:], grad_gate_up_b[:, second_count:]], axis=1
    )

    def strip_rows(weight):
        return lax.dynamic_slice_in_dim(weight, wide_index * strip, strip).astype(F32)

    def gain_grad(pairs, gain):
        local = sum(jnp.sum(strip_rows(w) * g, axis=1) for w, g in pairs)
        return local / lax.dynamic_slice_in_dim(gain, wide_index * strip, strip)

    local = jnp.stack(
        [
            gain_grad([(w_query, grad_query), (w_key, grad_key), (w_value, grad_value)], gain_one),
            gain_grad([(w_gate, grad_gate), (w_up, grad_up)], gain_two),
        ]
    )
    local = local + narrow_swap(local, 1)
    local = local + narrow_swap(local, 2)
    grad_gain_one, grad_gain_two = local[0], local[1]
    return (
        output,
        grad_tokens,
        grad_gain_one,
        grad_query,
        grad_key,
        grad_value,
        grad_out,
        grad_gain_two,
        grad_gate,
        grad_up,
        grad_down,
    )


def solution(mesh):
    placed = (
        P("wide", None),
        P("wide", None),
        P("wide"),
        P(),
        P(),
        P(),
        P(None, "narrow"),
        P(None, "narrow"),
        P(None, "narrow"),
        P("narrow", None),
        P(),
        P(None, "narrow"),
        P(None, "narrow"),
        P("narrow", None),
    )
    return jax.shard_map(
        shards,
        mesh=mesh,
        in_specs=placed,
        out_specs=(
            P("wide", None),
            P("wide", None),
            P("wide"),
            P("wide", "narrow"),
            P("wide", "narrow"),
            P("wide", "narrow"),
            P("narrow", "wide"),
            P("wide"),
            P("wide", "narrow"),
            P("wide", "narrow"),
            P("narrow", "wide"),
        ),
        check_vma=False,
    )
```

```python
import functools

import jax
import jax.numpy as jnp
import numpy as np
from jax import lax
from jax.experimental import pallas as pl
from jax.experimental.pallas import tpu as pltpu
from jax.sharding import PartitionSpec as P

HD = 128
EPSILON = 1e-05
NEGATIVE = -1e30
BASE = 10000.0
LOG2E = 1.4426950408889634
SCORE = HD ** (-0.5) * LOG2E
FACTOR = HD ** (-0.5)
BF = jnp.bfloat16
F32 = jnp.float32
NT = (((1,), (1,)), ((), ()))
TN = (((0,), (0,)), ((), ()))
NN = (((1,), (0,)), ((), ()))
VM = pl.BlockSpec(memory_space=pltpu.VMEM)
SM = pl.BlockSpec(memory_space=pltpu.SMEM)
ANY = pl.BlockSpec(memory_space=pl.ANY)


def dot(a, b, dims=(((1,), (0,)), ((), ()))):
    return lax.dot_general(a, b, dims, preferred_element_type=F32)


def narrow_swap(value, mask):
    pairs = [(n, n ^ mask) for n in range(lax.axis_size("narrow"))]
    return lax.ppermute(value, "narrow", pairs)


def wide_swap(value):
    return lax.ppermute(value, "wide", [(w, w ^ 1) for w in range(lax.axis_size("wide"))])


def wide_ring(value, group, hop=1):
    ring = group // 2
    pairs = []
    for w in range(lax.axis_size("wide")):
        base, member = w // group * group, w % group
        pairs.append((w, base + (member // 2 + hop) % ring * 2 + member % 2))
    return lax.ppermute(value, "wide", pairs)


def wide_flip(value, bit):
    return lax.ppermute(value, "wide", [(w, w ^ (2 << bit)) for w in range(lax.axis_size("wide"))])


def halving(count):
    groups = []
    step = 1
    while step < count:
        groups.append([k for k in range(count) if k % (2 * step) == step])
        step *= 2
    return [*groups, [0]]


def stretches(groups):
    starts, at = [], 0
    for group in groups:
        starts.append((at, len(group)))
        at += len(group)
    return starts


def rope(value, cosine, sine):
    return value * cosine + pltpu.roll(value, HD // 2, 1) * sine


def norm_kv_kernel(core, x_ref, gain_ref, wk_ref, wv_ref, cos_ref, sin_ref, normed_ref, *kv_refs):
    x = x_ref[...].astype(F32)
    scale = lax.rsqrt(jnp.mean(x * x, axis=1, keepdims=True) + EPSILON)
    normed = (x * scale * gain_ref[...].astype(F32)).astype(BF)
    normed_ref[...] = normed
    keys = dot(normed, wk_ref[...])
    values = dot(normed, wv_ref[...])
    for h, ref in enumerate(kv_refs):
        cols = slice(h * HD, (h + 1) * HD)
        ref[:, :HD] = rope(keys[:, cols], cos_ref[...], sin_ref[...]).astype(BF)
        ref[:, HD:] = values[:, cols].astype(BF)


def norm_kv(core, tokens, gain, wk, wv, cosine, sine):
    rows, width = tokens.shape
    half = rows // 2
    heads = wk.shape[1] // HD
    full = lambda w: pl.BlockSpec(w.shape, lambda i, c: (0, 0))
    outs = pl.pallas_call(
        norm_kv_kernel,
        out_shape=[jax.ShapeDtypeStruct((rows, width), BF)]
        + [jax.ShapeDtypeStruct((rows, 2 * HD), BF)] * heads,
        grid_spec=pltpu.PrefetchScalarGridSpec(
            num_scalar_prefetch=1,
            grid=(2,),
            in_specs=[
                pl.BlockSpec((half, width), lambda i, c: (i ^ c[0], 0)),
                full(gain),
                full(wk),
                full(wv),
                pl.BlockSpec((half, HD), lambda i, c: (i, 0)),
                pl.BlockSpec((half, HD), lambda i, c: (i, 0)),
            ],
            out_specs=[pl.BlockSpec((half, width), lambda i, c: (i, 0))]
            + [pl.BlockSpec((half, 2 * HD), lambda i, c: (i, 0))] * heads,
        ),
        cost_estimate=pl.CostEstimate(flops=int(2.9e9), bytes_accessed=0, transcendentals=0),
        name="norm_kv",
    )(core, tokens, gain, wk, wv, cosine, sine)
    return outs[0], outs[1:]


def query_kernel(x_ref, w_ref, cos_ref, sin_ref, out_ref):
    raw = dot(x_ref[...], w_ref[...])
    for h in range(raw.shape[1] // HD):
        cols = slice(h * HD, (h + 1) * HD)
        out_ref[:, cols] = rope(raw[:, cols], cos_ref[...], sin_ref[...]).astype(BF)


def query_proj(x, w, cosine, sine):
    rows, width = x.shape
    half = rows // 2
    return pl.pallas_call(
        query_kernel,
        out_shape=jax.ShapeDtypeStruct((rows, w.shape[1]), BF),
        grid=(2,),
        in_specs=[
            pl.BlockSpec((half, width), lambda i: (i, 0)),
            pl.BlockSpec(w.shape, lambda i: (0, 0)),
            pl.BlockSpec((half, HD), lambda i: (i, 0)),
            pl.BlockSpec((half, HD), lambda i: (i, 0)),
        ],
        out_specs=pl.BlockSpec((half, w.shape[1]), lambda i: (i, 0)),
        cost_estimate=pl.CostEstimate(flops=int(2.9e9), bytes_accessed=0, transcendentals=0),
        name="query_proj",
    )(x, w, cosine, sine)


def fetch_slots(slot_refs, slots, kv_ref, sems):
    rows, width = slot_refs[0].shape
    copies = []
    for at, ref in enumerate(slot_refs):
        head, slot = divmod(at, slots)
        spot = kv_ref.at[pl.ds(slot * rows, rows), pl.ds(head * width, width)]
        copies.append(pltpu.make_async_copy(ref, spot, sems.at[at]))
    for copy in copies:
        copy.start()
    for copy in copies:
        copy.wait()


def allowed(pk, size, span, pos, low):
    key_pos = pk * size + lax.broadcasted_iota(jnp.int32, (size, span), 0)
    return (key_pos <= pos) & (key_pos >= low)


def attn_fwd_kernel(slots, *refs):
    meta, q_ref, pos_ref, low_ref = refs[:4]
    slot_refs = refs[4 : 4 + slots]
    mixed_ref, lse_ref, kv_ref, acc_ref, sems = refs[-5:]
    fetch_slots(slot_refs, slots, kv_ref, sems)
    size = q_ref.shape[0] // 2
    for i in range(2):
        rows = slice(i * size, (i + 1) * size)
        pos = jnp.tile(pos_ref[0:1, rows], (1, 2))
        low = jnp.tile(low_ref[0:1, rows], (1, 2))
        queries = [q_ref[rows, r * HD : (r + 1) * HD] for r in range(2)]
        acc_ref[...] = jnp.zeros_like(acc_ref)

        def body(pk, carry):
            peak, total = carry
            spot = pl.multiple_of(meta[4 + pk] * size, size)
            keys = kv_ref[pl.ds(spot, size), :HD]
            values = kv_ref[pl.ds(spot, size), HD:]
            scores = jnp.concatenate([dot(keys, q, NT) for q in queries], axis=1) * SCORE
            scores = jnp.where(allowed(pk, size, 2 * size, pos, low), scores, NEGATIVE)
            peak_new = jnp.maximum(peak, jnp.max(scores, axis=0, keepdims=True))
            alpha = jnp.exp2(peak - peak_new)
            probs = jnp.exp2(scores - peak_new)
            total = total * alpha + jnp.sum(probs, axis=0, keepdims=True)
            acc_ref[...] = acc_ref[...] * alpha + dot(values, probs.astype(BF), TN)
            return peak_new, total

        start = (jnp.full((1, 2 * size), NEGATIVE, F32), jnp.zeros((1, 2 * size), F32))
        peak, total = lax.fori_loop(meta[i], meta[2 + i] + 1, body, start)
        lse_ref[i : i + 1, :] = peak + jnp.log2(total)
        out = acc_ref[...] * (1.0 / total)
        for r in range(2):
            mixed_ref[rows, r * HD : (r + 1) * HD] = out[:, r * size : (r + 1) * size].T.astype(BF)


def attn_fwd(head, meta, q, pos, low, slots, mixed):
    rows = q.shape[0]
    count = len(slots)
    earlier = [] if mixed is None else [mixed]
    return pl.pallas_call(
        functools.partial(attn_fwd_kernel, count),
        out_shape=(
            jax.ShapeDtypeStruct(q.shape, BF),
            jax.ShapeDtypeStruct((2, rows), F32),
        ),
        grid=(1,),
        in_specs=[
            SM,
            pl.BlockSpec((rows, 2 * HD), lambda i: (0, head)),
            pl.BlockSpec(pos.shape, lambda i: (0, 0)),
            pl.BlockSpec(low.shape, lambda i: (0, 0)),
        ]
        + [ANY] * (count + len(earlier)),
        out_specs=[
            pl.BlockSpec((rows, 2 * HD), lambda i: (0, head)),
            pl.BlockSpec((2, rows), lambda i: (0, 0)),
        ],
        input_output_aliases={4 + count: 0} if earlier else {},
        scratch_shapes=[
            pltpu.VMEM((count * rows, 2 * HD), BF),
            pltpu.VMEM((HD, rows), F32),
            pltpu.SemaphoreType.DMA((count,)),
        ],
        cost_estimate=pl.CostEstimate(flops=int(1e9), bytes_accessed=0, transcendentals=0),
        name="attn_fwd",
    )(meta, q, pos, low, *slots, *earlier)


def attn_bwd_kernel(heads, slots, groups, *refs):
    meta, q_ref, pos_ref, low_ref, dmix_ref, mixed_ref, cos_ref, sin_ref = refs[:8]
    lse_refs = refs[8 : 8 + heads]
    at = 8 + heads
    slot_refs = refs[at : at + heads * slots]
    at += heads * slots
    dq_ref, dkv_refs = refs[at], refs[at + 1 : -4]
    kv_ref, dkv_ref, dq_acc, sems = refs[-4:]
    fetch_slots(slot_refs, slots, kv_ref, sems)
    dkv_ref[...] = jnp.zeros_like(dkv_ref)
    rows_all = q_ref.shape[0]
    size = rows_all // 2
    for i in range(2):
        rows = slice(i * size, (i + 1) * size)
        pos = jnp.tile(pos_ref[0:1, rows], (1, 2))
        low = jnp.tile(low_ref[0:1, rows], (1, 2))
        for g in range(heads):
            cols = [slice((2 * g + r) * HD, (2 * g + r + 1) * HD) for r in range(2)]
            queries = jnp.concatenate([q_ref[rows, c] for c in cols], axis=0)
            grads = jnp.concatenate([dmix_ref[rows, c] for c in cols], axis=0)
            outs = jnp.concatenate([mixed_ref[rows, c] for c in cols], axis=0)
            delta = jnp.sum((grads.astype(F32) * outs.astype(F32)).T, axis=0, keepdims=True)
            lse = lse_refs[g][i : i + 1, :]
            dq_acc[...] = jnp.zeros_like(dq_acc)

            def body(pk, carry):
                spot = pl.multiple_of(meta[4 + pk] * size, size)
                key_cols = slice(2 * g * HD, (2 * g + 1) * HD)
                value_cols = slice((2 * g + 1) * HD, (2 * g + 2) * HD)
                keys = kv_ref[pl.ds(spot, size), key_cols]
                values = kv_ref[pl.ds(spot, size), value_cols]
                scores = dot(keys, queries, NT) * SCORE
                probs = jnp.where(
                    allowed(pk, size, 2 * size, pos, low), jnp.exp2(scores - lse), 0.0
                )
                d_probs = dot(values, grads, NT)
                d_scores = (probs * (d_probs - delta)).astype(BF)
                dkv_ref[pl.ds(spot, size), value_cols] += dot(probs.astype(BF), grads)
                dkv_ref[pl.ds(spot, size), key_cols] += dot(d_scores, queries) * FACTOR
                dq_acc[...] += dot(d_scores, keys, TN)
                return carry

            lax.fori_loop(meta[i], meta[2 + i] + 1, body, 0)
            for r in range(2):
                part = dq_acc[r * size : (r + 1) * size, :] * FACTOR
                dq_ref[rows, cols[r]] = rope(part, cos_ref[rows, :], -sin_ref[rows, :]).astype(BF)
    ring = slots // 2
    for j, ref in enumerate(dkv_refs):
        first = ring * (j // len(groups))
        for place, k in enumerate(groups[j % len(groups)]):
            spot = pl.multiple_of((first + meta[4 + 2 * slots + k]) * rows_all, rows_all)
            ref[place * rows_all : (place + 1) * rows_all, :] = dkv_ref[
                pl.ds(spot, rows_all), :
            ].astype(BF)


def attn_bwd(meta, q, pos, low, lse, mixed, dmix, cosine, sine, slots):
    rows, q_width = q.shape
    heads, count = len(slots), len(slots[0])
    kv_width = heads * 2 * HD
    groups = halving(count // 2)
    outs = pl.pallas_call(
        functools.partial(attn_bwd_kernel, heads, count, groups),
        out_shape=[jax.ShapeDtypeStruct((rows, q_width), BF)]
        + [jax.ShapeDtypeStruct((len(g) * rows, kv_width), BF) for g in groups] * 2,
        in_specs=[SM] + [VM] * (7 + heads) + [ANY] * (heads * count),
        out_specs=[VM] * (1 + 2 * len(groups)),
        scratch_shapes=[
            pltpu.VMEM((count * rows, kv_width), BF),
            pltpu.VMEM((count * rows, kv_width), F32),
            pltpu.VMEM((rows, HD), F32),
            pltpu.SemaphoreType.DMA((heads * count,)),
        ],
        cost_estimate=pl.CostEstimate(flops=int(2e9), bytes_accessed=0, transcendentals=0),
        name="attn_bwd",
    )(meta, q, pos, low, dmix, mixed, cosine, sine, *lse, *[v for head in slots for v in head])
    return outs[0], outs[1 : 1 + len(groups)], outs[1 + len(groups) :]


def cost(micros):
    return pl.CostEstimate(flops=int(micros * 0.3e9), bytes_accessed=0, transcendentals=0)


def split_rows(total, own_ref, other_ref):
    half = own_ref.shape[0]
    own_ref[...] = total[:half].astype(BF)
    other_ref[...] = total[half:].astype(BF)


def project_kernel(spec, *refs):
    total = None
    for a, b, offset, dims in spec:
        left = refs[a][...] if dims is not None else None
        if dims == "nt":
            right, form = refs[b][:, offset : offset + left.shape[1]], NT
        else:
            right, form = refs[b][offset : offset + left.shape[1], :], NN
        term = dot(left, right, form)
        total = term if total is None else total + term
    split_rows(total, refs[-2], refs[-1])


def project(pairs, dims, tile, micros):
    operands, specs, plan, weights = [], [], [], []
    for a, b, offset in pairs:
        operands.append(a)
        specs.append(pl.BlockSpec(a.shape, lambda i: (0, 0)))
        spot = next((at for at, seen in weights if seen is b), None)
        left = len(operands) - 1
        if spot is None:
            spot = len(operands)
            operands.append(b)
            weights.append((spot, b))
            if dims == "nt":
                specs.append(pl.BlockSpec((tile, b.shape[1]), lambda i: (i, 0)))
            else:
                specs.append(pl.BlockSpec((b.shape[0], tile), lambda i: (0, i)))
        plan.append((left, spot, offset, dims))
    rows = pairs[0][0].shape[0]
    width = pairs[0][1].shape[0 if dims == "nt" else 1]
    return pl.pallas_call(
        functools.partial(project_kernel, plan),
        out_shape=[jax.ShapeDtypeStruct((rows // 2, width), BF)] * 2,
        grid=(width // tile,),
        in_specs=specs,
        out_specs=[pl.BlockSpec((rows // 2, tile), lambda i: (0, i))] * 2,
        cost_estimate=cost(micros),
        name="project",
    )(*operands)


def back_dense_kernel(gate_a, up_a, gate_b, up_b, wg_ref, wu_ref, own_ref, other_ref):
    total = None
    offset = 0
    for group in ((gate_a, up_a), (gate_b, up_b)):
        count = group[0].shape[1]
        for ref, w_ref in zip(group, (wg_ref, wu_ref)):
            term = dot(ref[...], w_ref[:, offset : offset + count], NT)
            total = term if total is None else total + term
        offset += count
    split_rows(total, own_ref, other_ref)


def back_dense(grads, w_gate, w_up, tile, part, parts):
    width, hidden = w_gate.shape[0] // parts, w_gate.shape[1]
    rows = grads[0].shape[0]
    ahead = part * (width // tile)
    weight = pl.BlockSpec((tile, hidden), lambda i: (ahead + i, 0))
    return pl.pallas_call(
        back_dense_kernel,
        out_shape=[jax.ShapeDtypeStruct((rows // 2, width), BF)] * 2,
        grid=(width // tile,),
        in_specs=[pl.BlockSpec(v.shape, lambda i: (0, 0)) for v in grads] + [weight, weight],
        out_specs=[pl.BlockSpec((rows // 2, tile), lambda i: (0, i))] * 2,
        cost_estimate=cost(11 / parts),
        name="back_dense",
    )(*grads, w_gate, w_up)


def gated_kernel(own_ref, other_ref, wg_ref, wu_ref, di_ref, inner_ref, dg_ref, du_ref, all_ref):
    @pl.when(pl.program_id(0) == 0)
    def _():
        half = own_ref.shape[0]
        all_ref[:half, :] = own_ref[...]
        all_ref[half:, :] = other_ref[...]

    gate = dot(all_ref[...], wg_ref[...])
    up = dot(all_ref[...], wu_ref[...])
    sigma = 1.0 / (1.0 + jnp.exp(-gate))
    silu = gate * sigma
    d_inner = di_ref[...]
    inner_ref[...] = (silu * up).astype(BF)
    dg_ref[...] = (d_inner * up * sigma * (1.0 + gate * (1.0 - sigma))).astype(BF)
    du_ref[...] = (d_inner * silu).astype(BF)


def gated(own, other, wg, wu, d_inner, first, columns, tile):
    half, width = own.shape
    weight = pl.BlockSpec((width, tile), lambda i: (0, first // tile + i))
    whole = pl.BlockSpec((half, width), lambda i: (0, 0))
    return pl.pallas_call(
        gated_kernel,
        out_shape=[jax.ShapeDtypeStruct((2 * half, columns), BF)] * 3,
        grid=(pl.cdiv(columns, tile),),
        in_specs=[
            whole,
            whole,
            weight,
            weight,
            pl.BlockSpec((2 * half, tile), lambda i: (0, first // tile + i)),
        ],
        out_specs=[pl.BlockSpec((2 * half, tile), lambda i: (0, i))] * 3,
        scratch_shapes=[pltpu.VMEM((2 * half, width), BF)],
        cost_estimate=cost(7.5),
        name="gated",
    )(own, other, wg, wu, d_inner)


def mixed_grad_kernel(own_ref, other_ref, w_ref, out_ref):
    both = jnp.concatenate([own_ref[...], other_ref[...]], axis=0)
    out_ref[...] = dot(both, w_ref[...], NT).astype(BF)


def mixed_grad(own, other, w):
    return pl.pallas_call(
        mixed_grad_kernel,
        out_shape=jax.ShapeDtypeStruct((2 * own.shape[0], w.shape[0]), BF),
        in_specs=[VM] * 3,
        out_specs=VM,
        cost_estimate=cost(4),
        name="mixed_grad",
    )(own, other, w)


def d_inner_kernel(x_ref, w_ref, out_ref):
    out_ref[...] = dot(x_ref[...], w_ref[...], NT)


def inner_grad(x, w, tile):
    rows, width = x.shape
    hidden = w.shape[0]
    return pl.pallas_call(
        d_inner_kernel,
        out_shape=jax.ShapeDtypeStruct((rows, hidden), F32),
        grid=(pl.cdiv(hidden, tile),),
        in_specs=[
            pl.BlockSpec((rows, width), lambda i: (0, 0)),
            pl.BlockSpec((tile, width), lambda i: (i, 0)),
        ],
        out_specs=pl.BlockSpec((rows, tile), lambda i: (0, i)),
        cost_estimate=cost(8),
        name="inner_grad",
    )(x, w)


def pack_kernel(count, plan, strip, tbl, *refs):
    ins, outs = refs[:count], refs[count:]
    for out_ref, pieces in zip(outs, plan):
        column = 0
        for at, rows, row in pieces:
            for k in range(tbl.shape[1]):
                first = pl.multiple_of(tbl[row, k] * strip, 128)
                out_ref[:, column : column + strip] = ins[at][rows, pl.ds(first, strip)]
                column += strip


def pack(values, plan, tbl, strip):
    turns = tbl.shape[1]
    if strip % 128:
        cut = lambda v, rows, at: lax.dynamic_slice_in_dim(v[rows], at * strip, strip, axis=1)
        return [
            jnp.concatenate(
                [cut(values[at], rows, tbl[row, k]) for at, rows, row in pieces for k in range(turns)],
                axis=1,
            )
            for pieces in plan
        ]
    return pl.pallas_call(
        functools.partial(pack_kernel, len(values), plan, strip),
        out_shape=[
            jax.ShapeDtypeStruct(
                (p[0][1].stop - p[0][1].start, len(p) * turns * strip), values[0].dtype
            )
            for p in plan
        ],
        in_specs=[SM] + [VM] * len(values),
        out_specs=[VM] * len(plan),
        cost_estimate=cost(1.5),
        name="pack",
    )(tbl, *values)


def strip_rows_kernel(halves, near, rights, nears, spans, tbl, *refs):
    left = refs[:halves]
    left_near = refs[halves : halves + near]
    right = refs[halves + near : halves + near + rights]
    right_near = refs[halves + near + rights : halves + near + rights + nears]
    outs = refs[halves + near + rights + nears :]
    step = pl.program_id(0)
    join = lambda group: (
        group[0][...] if len(group) == 1 else jnp.concatenate([r[...] for r in group], axis=0)
    )
    mine, theirs = join(left), join(left_near)
    pieces = []
    for r, n in zip(right, right_near):
        planes = range(r.shape[0]) if len(r.shape) == 3 else [None]
        for k in planes:
            a = r[...] if k is None else r[k]
            b = n[...] if k is None else n[k]
            pieces.append((dot(mine, a, TN) + dot(theirs, b, TN)).astype(BF))
    for (start, length), out in zip(spans, outs):

        @pl.when((step >= start) & (step < start + length))
        def _(out=out):
            column = 0
            for piece in pieces:
                out[:, column : column + piece.shape[1]] = piece
                column += piece.shape[1]


def strip_rows_grad(left, left_near, right, right_near, tbl, strip, micros, single=False):
    turns = tbl.shape[1]
    columns = sum(r.shape[-1] * (r.shape[0] if r.ndim == 3 else 1) for r in right)
    spans = [(k, 1) for k in range(turns)] if single else stretches(halving(turns))
    if strip % 128:
        near = jnp.concatenate(left_near, axis=0)
        mine = jnp.concatenate(left, axis=0)
        flat = lambda r: [r] if r.ndim == 2 else [r[k] for k in range(r.shape[0])]
        outs = []
        for start, length in spans:
            group = []
            for k in range(start, start + length):
                a = lax.dynamic_slice_in_dim(mine, tbl[0, k] * strip, strip, axis=1)
                b = near[:, k * strip : (k + 1) * strip]
                group.append(
                    jnp.concatenate(
                        [
                            dot(a, x, TN) + dot(b, y, TN)
                            for r, n in zip(right, right_near)
                            for x, y in zip(flat(r), flat(n))
                        ],
                        axis=1,
                    ).astype(BF)
                )
            outs.append(jnp.concatenate(group, axis=0))
        return outs
    held = lambda start, length: (lambda i, t: (jnp.clip(i - start, 0, length - 1), 0))
    whole = lambda v: pl.BlockSpec(v.shape, lambda i, t: (0,) * v.ndim)
    return pl.pallas_call(
        functools.partial(
            strip_rows_kernel, len(left), len(left_near), len(right), len(right_near), spans
        ),
        out_shape=[jax.ShapeDtypeStruct((length * strip, columns), BF) for _, length in spans],
        grid_spec=pltpu.PrefetchScalarGridSpec(
            num_scalar_prefetch=1,
            grid=(turns,),
            in_specs=[pl.BlockSpec((v.shape[0], strip), lambda i, t: (0, t[0, i])) for v in left]
            + [pl.BlockSpec((v.shape[0], strip), lambda i, t: (0, i)) for v in left_near]
            + [whole(v) for v in [*right, *right_near]],
            out_specs=[pl.BlockSpec((strip, columns), held(*span)) for span in spans],
        ),
        cost_estimate=cost(micros),
        name="strip_rows",
    )(tbl, *left, *left_near, *right, *right_near)


def strip_columns_kernel(parts, halves, near, strip, spans, *refs):
    at = 2 * parts
    right, right_near = refs[at : at + halves], refs[at + halves : at + halves + near]
    outs = refs[at + halves + near :]
    first = 0
    for p in range(parts):
        total = None
        for ref, group in ((refs[p], right), (refs[parts + p], right_near)):
            row = 0
            for r in group:
                term = dot(ref[row : row + r.shape[0], :], r[...], TN)
                total = term if total is None else total + term
                row += r.shape[0]
        for (start, length), out in zip(spans, outs):
            out[first : first + total.shape[0], :] = total[
                :, start * strip : (start + length) * strip
            ].astype(BF)
        first += total.shape[0]


def strip_columns_grad(
    left, left_near, right, right_near, turns, strip, tile, micros, near_at=0, single=False
):
    rows, count = left[0].shape[0], sum(v.shape[1] for v in left)
    if strip * turns % 128:
        raise ValueError(strip)
    spans = [(k, 1) for k in range(turns)] if single else stretches(halving(turns))
    whole = lambda v: pl.BlockSpec(v.shape, lambda i: (0, 0))
    near = lambda v: pl.BlockSpec((v.shape[0], turns * strip), lambda i: (0, near_at))
    if len(left) == 1:
        left_specs = [pl.BlockSpec((rows, tile), lambda i: (0, i))] * 2
    else:
        tile = count
        left_specs = [whole(v) for v in [*left, *left_near]]
    return pl.pallas_call(
        functools.partial(
            strip_columns_kernel, len(left), len(right), len(right_near), strip, spans
        ),
        out_shape=[jax.ShapeDtypeStruct((count, length * strip), BF) for _, length in spans],
        grid=(pl.cdiv(count, tile),),
        in_specs=left_specs + [whole(v) for v in right] + [near(v) for v in right_near],
        out_specs=[pl.BlockSpec((tile, length * strip), lambda i: (i, 0)) for _, length in spans],
        cost_estimate=cost(micros),
        name="strip_columns",
    )(*left, *left_near, *right, *right_near)


def close_kv_kernel(count, *refs):
    cos_ref, sin_ref, dk_ref, dv_ref = refs[count:]
    total = refs[0][...].astype(F32)
    for ref in refs[1:count]:
        total = total + ref[...].astype(F32)
    heads = dk_ref.shape[1] // HD
    for h in range(heads):
        cols = slice(h * HD, (h + 1) * HD)
        keys = total[:, 2 * h * HD : (2 * h + 1) * HD]
        dk_ref[:, cols] = rope(keys, cos_ref[...], -sin_ref[...]).astype(BF)
        dv_ref[:, cols] = total[:, (2 * h + 1) * HD : (2 * h + 2) * HD].astype(BF)


def close_kv(terms, cosine, sine):
    rows, width = terms[0].shape
    first = lambda w: pl.BlockSpec((rows, w), lambda i: (0, 0))
    return pl.pallas_call(
        functools.partial(close_kv_kernel, len(terms)),
        out_shape=[jax.ShapeDtypeStruct((rows, width // 2), BF)] * 2,
        grid=(1,),
        in_specs=[first(width)] * len(terms) + [first(HD)] * 2,
        out_specs=[first(width // 2)] * 2,
        cost_estimate=cost(1.5),
        name="close_kv",
    )(*terms, cosine, sine)


def norm_backward(source, scale_rows, gain, upstream):
    weighted = upstream * gain
    average = jnp.mean(weighted * source, axis=1, keepdims=True)
    return scale_rows * weighted - source * scale_rows**3 * average


def after(value, *done):
    return lax.optimization_barrier((value, *done))[0]


def shards(
    tokens,
    cotangent,
    keep_mask,
    doc_lengths,
    block_order,
    gain_attn,
    w_query,
    w_key,
    w_value,
    w_out,
    gain_dense,
    w_gate,
    w_up,
    w_down,
):
    rows, width = tokens.shape
    half = rows // 2
    wide = lax.axis_size("wide")
    group = wide // block_order.shape[0]
    ring = group // 2
    wide_index = lax.axis_index("wide")
    member = wide_index % group
    seq_index = wide_index // group
    side = (wide_index % 2).astype(jnp.int32)
    core = lax.axis_index("narrow") % 2
    strip = width // wide
    turns = wide // 2

    def ordered(mine, other):
        return jnp.where(
            core == 0,
            jnp.concatenate([mine, other], axis=0),
            jnp.concatenate([other, mine], axis=0),
        )

    def own_half(value):
        return lax.dynamic_slice_in_dim(value, core * half, half)

    def other_half(value):
        return lax.dynamic_slice_in_dim(value, (1 - core) * half, half)

    order_row = lax.dynamic_index_in_dim(block_order, seq_index, 0, keepdims=False)
    length_row = lax.dynamic_index_in_dim(doc_lengths, seq_index, 0, keepdims=False)
    doc_ends = jnp.cumsum(length_row)
    places = jnp.stack([member * 2 + core, member * 2 + 1 - core])
    chosen = jnp.sum(
        jnp.where(places[:, None] == jnp.arange(2 * group)[None, :], order_row[None, :], 0), axis=1
    )
    pos = (chosen[:, None] * half + jnp.arange(half, dtype=jnp.int32)[None, :]).reshape(-1)
    low = jnp.max(jnp.where(doc_ends[None, :] <= pos[:, None], doc_ends[None, :], 0), axis=1)
    block_low = low.reshape(2, half)[:, 0] // half
    stored = jnp.sum(
        jnp.where(
            order_row[None, :] == jnp.arange(2 * group)[:, None], jnp.arange(2 * group)[None, :], 0
        ),
        axis=1,
    )
    owner = stored // 2
    slot = (member // 2 - owner // 2) % ring + ring * (owner % 2 != side).astype(jnp.int32)
    spots = slot * 2 + (stored % 2 != core).astype(jnp.int32)
    place = member // 2
    back = (place - (place ^ jnp.arange(ring, dtype=jnp.int32))) % ring
    meta = jnp.concatenate([block_low, chosen, spots, back]).astype(jnp.int32)
    frequency = BASE ** (-(jnp.arange(HD // 2, dtype=F32) * 2.0) / HD)
    angles = pos.astype(F32)[:, None] * frequency[None, :]
    cosine = jnp.cos(angles)
    sine = jnp.sin(angles)
    cosine = jnp.concatenate([cosine, cosine], axis=1)
    sine = jnp.concatenate([-sine, sine], axis=1)
    pos_row = pos[None, :]
    low_row = low[None, :]

    order = np.array([k for stretch in halving(turns) for k in stretch], np.int32)
    turn_row = wide_index // 2 ^ order
    tbl = jnp.stack([2 * turn_row + side, 2 * turn_row + 1 - side]).astype(jnp.int32)
    round_row = (wide_index // 2 - 1 - jnp.arange(turns, dtype=jnp.int32)) % turns
    round_tbl = jnp.stack([2 * round_row + side, 2 * round_row + 1 - side]).astype(jnp.int32)
    core_arr = core.astype(jnp.int32)[None]
    normed_one, both = norm_kv(core_arr, tokens, gain_attn[None, :], w_key, w_value, cosine, sine)
    low_rows, all_rows = slice(0, half), slice(0, rows)

    def together(*values):
        return list(lax.optimization_barrier(values))

    near, far = [[v] for v in both], [[] for v in both]
    query = d_dense = d_inner = input_near = d_dense_strips = None
    for step in range(ring):
        for head in range(len(both)):
            held = near[head][step]
            if step + 1 < ring:
                sent = [wide_swap(held), wide_ring(held, group)]
            elif head == 0:
                sent = [wide_swap(held)]
            else:
                sent = [wide_ring(far[head][0], group, -1)]
            beside = []
            if step == 0 and head == 0:
                beside = [query_proj(normed_one, w_query, cosine, sine)]
            if step == 0 and head == 1:
                keep_rel = jnp.concatenate([own_half(keep_mask), other_half(keep_mask)])[:, None]
                cot_rel = jnp.concatenate([own_half(cotangent), other_half(cotangent)])
                beside = [jnp.where(keep_rel > 0, cot_rel, jnp.zeros_like(cot_rel))]
            if step == 1 and head == 0:
                beside = [inner_grad(d_dense, w_down, 256)]
            if step == 2 and head == 0:
                beside = pack(
                    [normed_one, d_dense],
                    [[(0, low_rows, 1), (1, low_rows, 1)], [(1, all_rows, 0)]],
                    round_tbl,
                    strip,
                )
            done = together(*sent, *beside)
            far[head].append(done[0])
            if step + 1 < ring:
                near[head].append(done[1])
            if step == 0 and head == 0:
                query = done[-1]
            if step == 0 and head == 1:
                d_dense = done[-1]
            if step == 1 and head == 0:
                d_inner = done[-1]
            if step == 2 and head == 0:
                input_near, d_dense_strips = done[-2:]
    slots = [n + f for n, f in zip(near, far)]
    input_near = wide_swap(after(input_near, *slots[0], *slots[-1]))
    mixed, lse = None, []
    for h, held in enumerate(slots):
        mixed, part = attn_fwd(h, meta, query, pos_row, low_row, held, mixed)
        lse.append(part)

    def reduce_narrow(halves, hold=()):
        own_part, other_part = halves
        got = narrow_swap(other_part, 1)
        held = (own_part.astype(F32) + got.astype(F32)).astype(BF)
        return held, narrow_swap(held, 2)

    def total_of(held, got):
        return held.astype(F32) + got.astype(F32)

    part = project([(mixed, w_out, 0)], "nn", 1024, 4)
    held, got = reduce_narrow((part[0], after(part[1], input_near)))
    mixed_near = wide_swap(mixed)
    input_near_other = narrow_swap(input_near, 1)
    source = own_half(tokens).astype(F32)
    keep_own = own_half(keep_mask).astype(F32)[:, None]
    hidden_one = source + keep_own * total_of(held, got)
    gain_two = gain_dense.astype(F32)
    scale_two = lax.rsqrt(jnp.mean(hidden_one * hidden_one, axis=1, keepdims=True) + EPSILON)
    normed_two = (hidden_one * scale_two * gain_two).astype(BF)
    normed_two_other = narrow_swap(after(normed_two, mixed_near), 1)
    hidden = w_gate.shape[1]
    tile = 256
    first_count = 3 * tile
    inner_a, *dgu_a = gated(
        normed_two, normed_two_other, w_gate, w_up, d_inner, 0, first_count, tile
    )
    inner_a_near = wide_swap(inner_a)
    inner_b, *dgu_b = gated(
        after(normed_two, inner_a),
        normed_two_other,
        w_gate,
        w_up,
        d_inner,
        first_count,
        hidden - first_count,
        tile,
    )
    back = back_dense([*dgu_a, *dgu_b], w_gate, w_up, 512, 0, 1)
    held, got = reduce_narrow((back[0], after(back[1], inner_a_near)))

    def halve(parts, axis, hold=None, first=None):
        groups = halving(1 << (len(parts) - 1))
        size = parts[-1].shape[axis]
        received, sent = [], None
        for bit, group in enumerate(groups[:-1]):
            sent = parts[bit]
            if bit:
                total = sent.astype(F32)
                for early, value in enumerate(received):
                    there = [k ^ (1 << early) for k in groups[early]]
                    pick = [
                        lax.slice_in_dim(value, size * there.index(k), size * (there.index(k) + 1), axis=axis)
                        for k in group
                    ]
                    total = total + (pick[0] if len(pick) == 1 else jnp.concatenate(pick, axis)).astype(F32)
                sent = total.astype(BF)
            got = first if bit == 0 and first is not None else wide_flip(sent, bit)
            received.append(got if hold is None else after(got, hold))
        return received, sent

    def ring_hops(parts, last=(), first=None):
        carried, became = parts[0], []
        for k, part in enumerate(parts[1:]):
            got = wide_ring(carried, wide) if first is None or k else first
            bare = got
            if k == len(parts) - 2 and last:
                got = after(got, *last)
            total = part.astype(F32) + got.astype(F32)
            carried = total.astype(BF)
            became.append(carried)
        return total, became, bare

    def ring_sum(parts, hold=None, last=()):
        first = wide_ring(parts[0], wide)
        total, became, _ = ring_hops(parts, last, first if hold is None else after(first, hold))
        return total, became[0]

    def close(parts, received, axis):
        size = parts[-1].shape[axis]
        total = parts[-1].astype(F32)
        for value in received:
            total = total + lax.slice_in_dim(value, 0, size, axis=axis).astype(F32)
        return total

    near_sides = [input_near, input_near_other]
    down_a = strip_columns_grad(
        [after(inner_a, held)],
        [inner_a_near],
        [d_dense_strips],
        near_sides,
        turns,
        strip,
        tile,
        4,
        1,
        True,
    )
    inner_b_near = wide_swap(inner_b)
    down_a_first = wide_ring(down_a[0], wide)
    dgu_a_near = [wide_swap(after(v, inner_b)) for v in dgu_a]
    dense_parts = project(
        [(after(inner_a, down_a[0], inner_b_near), w_down, 0), (inner_b, w_down, first_count)], "nn", 512, 6
    )
    (normed_two_near,) = pack(
        [after(normed_two, dense_parts[0])], [[(0, low_rows, 1)]], round_tbl, strip
    )
    normed_two_near = wide_swap(normed_two_near)
    down_b = strip_columns_grad(
        [after(inner_b, dense_parts[0])], [inner_b_near], [d_dense_strips], near_sides, turns, strip, tile, 4, 1, True
    )

    got = after(got, dense_parts[0], down_b[0])
    down_a_next = (down_a[1].astype(F32) + down_a_first.astype(F32)).astype(BF)
    down_a_second = down_a_early = wide_ring(down_a_next, wide)
    for part in down_a[2:-1]:
        down_a_second = wide_ring((part.astype(F32) + down_a_second.astype(F32)).astype(BF), wide)
    upstream = own_half(cotangent).astype(F32)
    d_hidden = upstream + norm_backward(hidden_one, scale_two, gain_two, total_of(held, got))
    d_attn = (keep_own * d_hidden).astype(BF)
    d_attn_other = narrow_swap(after(d_attn, dgu_a_near[0], down_a_early), 1)

    down_b_first = wide_ring(down_b[0], wide)
    d_mixed = mixed_grad(d_attn, d_attn_other, w_out)
    d_query, d_near, d_far = attn_bwd(
        meta, query, pos_row, low_row, lse, mixed, after(d_mixed, down_a_second), cosine, sine, slots
    )
    held_out, got_out = reduce_narrow((dense_parts[0], after(dense_parts[1], d_mixed)))
    output_own = (hidden_one + keep_own * total_of(held_out, got_out)).astype(BF)
    output = ordered(output_own, narrow_swap(output_own, 1))

    normed_two_near_other = narrow_swap(after(normed_two_near, d_query), 1)
    normed_two_sides = [normed_two_near, normed_two_near_other]
    gate_up_a = strip_rows_grad(
        [after(normed_two, d_query), normed_two_other], normed_two_sides, dgu_a, dgu_a_near, round_tbl, strip, 8, True
    )
    grad_gate_up_a, gate_up_a_mid = ring_sum(gate_up_a)
    d_far = [wide_swap(v) for v in d_far]
    d_far[0] = after(d_far[0], gate_up_a_mid)
    pairs = [
        (n.astype(F32) + f.astype(F32)).astype(BF) for n, f in zip(d_near[:-1], d_far[:-1])
    ]
    kv_got, kv_mid = halve([*pairs, d_near[-1]], 0)
    d_key, d_value = close_kv([d_near[-1], d_far[-1], *kv_got], cosine, sine)

    dgu_b_near = [wide_swap(after(v, d_query)) for v in dgu_b]
    gate_up_b = strip_rows_grad(
        [after(normed_two, gate_up_a_mid, kv_mid), normed_two_other],
        normed_two_sides,
        dgu_b,
        dgu_b_near,
        round_tbl,
        strip,
        7,
        True,
    )
    d_query_near = wide_swap(after(d_query, pairs[0]))
    grad_gate_up_b, gate_up_b_mid = ring_sum(gate_up_b)
    d_attn_near, d_attn_strips, d_attn_other_strips = pack(
        [after(d_attn, gate_up_a[0]), d_attn_other],
        [[(0, low_rows, 1)], [(0, low_rows, 0)], [(1, low_rows, 0)]],
        round_tbl,
        strip,
    )
    d_attn_near = wide_swap(after(d_attn_near, pairs[0]))
    d_attn_near_other = narrow_swap(after(d_attn_near, gate_up_b[0]), 1)
    query_part = strip_rows_grad(
        [after(normed_one, gate_up_b[0])], near_sides, [d_query], [d_query_near], round_tbl, strip, 4, True
    )
    out_part = strip_columns_grad(
        [after(mixed, query_part[0])],
        [mixed_near],
        [d_attn_strips, d_attn_other_strips],
        [d_attn_near, d_attn_near_other],
        turns,
        strip,
        tile,
        4,
        0,
        True,
    )

    kv_width = w_key.shape[1]
    held, got = reduce_narrow(
        project([(d_query, w_query, 0), (d_key, w_key, 0), (d_value, w_value, 0)], "nt", 512, 6)
    )
    gain_one = gain_attn.astype(F32)
    scale_one = lax.rsqrt(jnp.mean(source * source, axis=1, keepdims=True) + EPSILON)
    d_normed_one = total_of(held, got)
    grad_own = (d_hidden + norm_backward(source, scale_one, gain_one, d_normed_one)).astype(BF)
    grad_tokens = ordered(grad_own, narrow_swap(grad_own, 1))

    d_key_near = wide_swap(d_key)
    d_value_near = wide_swap(d_value)
    kv_part = strip_rows_grad(
        [after(normed_one, out_part[0])],
        near_sides,
        [d_key, d_value],
        [d_key_near, d_value_near],
        round_tbl,
        strip,
        4,
        True,
    )
    grad_kv, _ = ring_sum(kv_part, None, (grad_own, output))
    grad_query, _ = ring_sum(query_part, kv_part[0])
    grad_out, _ = ring_sum(out_part, kv_part[0])
    grad_down_a = down_a[-1].astype(F32) + after(down_a_second, d_query).astype(F32)
    grad_down_b, _, _ = ring_hops(down_b, (), after(down_b_first, gate_up_b_mid))
    grad_key, grad_value = grad_kv[:, :kv_width], grad_kv[:, kv_width:]
    grad_down = jnp.concatenate([grad_down_a, grad_down_b], axis=0)
    second_count = hidden - first_count
    grad_gate = jnp.concatenate(
        [grad_gate_up_a[:, :first_count], grad_gate_up_b[:, :second_count]], axis=1
    )
    grad_up = jnp.concatenate(
        [grad_gate_up_a[:, first_count:], grad_gate_up_b[:, second_count:]], axis=1
    )

    def strip_rows(weight):
        return lax.dynamic_slice_in_dim(weight, wide_index * strip, strip).astype(F32)

    def gain_grad(pairs, gain):
        local = sum(jnp.sum(strip_rows(w) * g, axis=1) for w, g in pairs)
        return local / lax.dynamic_slice_in_dim(gain, wide_index * strip, strip)

    local = jnp.stack(
        [
            gain_grad([(w_query, grad_query), (w_key, grad_key), (w_value, grad_value)], gain_one),
            gain_grad([(w_gate, grad_gate), (w_up, grad_up)], gain_two),
        ]
    )
    local = local + narrow_swap(local, 1)
    local = local + narrow_swap(local, 2)
    grad_gain_one, grad_gain_two = local[0], local[1]
    return (
        output,
        grad_tokens,
        grad_gain_one,
        grad_query,
        grad_key,
        grad_value,
        grad_out,
        grad_gain_two,
        grad_gate,
        grad_up,
        grad_down,
    )


def solution(mesh):
    placed = (
        P("wide", None),
        P("wide", None),
        P("wide"),
        P(),
        P(),
        P(),
        P(None, "narrow"),
        P(None, "narrow"),
        P(None, "narrow"),
        P("narrow", None),
        P(),
        P(None, "narrow"),
        P(None, "narrow"),
        P("narrow", None),
    )
    return jax.shard_map(
        shards,
        mesh=mesh,
        in_specs=placed,
        out_specs=(
            P("wide", None),
            P("wide", None),
            P("wide"),
            P("wide", "narrow"),
            P("wide", "narrow"),
            P("wide", "narrow"),
            P("narrow", "wide"),
            P("wide"),
            P("wide", "narrow"),
            P("wide", "narrow"),
            P("narrow", "wide"),
        ),
        check_vma=False,
    )
```

```python
import functools

import jax
import jax.numpy as jnp
import numpy as np
from jax import lax
from jax.experimental import pallas as pl
from jax.experimental.pallas import tpu as pltpu
from jax.sharding import PartitionSpec as P

HD = 128
EPSILON = 1e-05
NEGATIVE = -1e30
BASE = 10000.0
LOG2E = 1.4426950408889634
SCORE = HD ** (-0.5) * LOG2E
FACTOR = HD ** (-0.5)
BF = jnp.bfloat16
F32 = jnp.float32
NT = (((1,), (1,)), ((), ()))
TN = (((0,), (0,)), ((), ()))
NN = (((1,), (0,)), ((), ()))
VM = pl.BlockSpec(memory_space=pltpu.VMEM)
SM = pl.BlockSpec(memory_space=pltpu.SMEM)
ANY = pl.BlockSpec(memory_space=pl.ANY)


def dot(a, b, dims=(((1,), (0,)), ((), ()))):
    return lax.dot_general(a, b, dims, preferred_element_type=F32)


def narrow_swap(value, mask):
    pairs = [(n, n ^ mask) for n in range(lax.axis_size("narrow"))]
    return lax.ppermute(value, "narrow", pairs)


def wide_swap(value):
    return lax.ppermute(value, "wide", [(w, w ^ 1) for w in range(lax.axis_size("wide"))])


def wide_ring(value, group, hop=1):
    ring = group // 2
    pairs = []
    for w in range(lax.axis_size("wide")):
        base, member = w // group * group, w % group
        pairs.append((w, base + (member // 2 + hop) % ring * 2 + member % 2))
    return lax.ppermute(value, "wide", pairs)


def wide_flip(value, bit):
    return lax.ppermute(value, "wide", [(w, w ^ (2 << bit)) for w in range(lax.axis_size("wide"))])


def halving(count):
    groups = []
    step = 1
    while step < count:
        groups.append([k for k in range(count) if k % (2 * step) == step])
        step *= 2
    return [*groups, [0]]


def stretches(groups):
    starts, at = [], 0
    for group in groups:
        starts.append((at, len(group)))
        at += len(group)
    return starts


def rope(value, cosine, sine):
    return value * cosine + pltpu.roll(value, HD // 2, 1) * sine


def norm_kv_kernel(core, x_ref, gain_ref, wk_ref, wv_ref, cos_ref, sin_ref, normed_ref, *kv_refs):
    x = x_ref[...].astype(F32)
    scale = lax.rsqrt(jnp.mean(x * x, axis=1, keepdims=True) + EPSILON)
    normed = (x * scale * gain_ref[...].astype(F32)).astype(BF)
    normed_ref[...] = normed
    keys = dot(normed, wk_ref[...])
    values = dot(normed, wv_ref[...])
    for h, ref in enumerate(kv_refs):
        cols = slice(h * HD, (h + 1) * HD)
        ref[:, :HD] = rope(keys[:, cols], cos_ref[...], sin_ref[...]).astype(BF)
        ref[:, HD:] = values[:, cols].astype(BF)


def norm_kv(core, tokens, gain, wk, wv, cosine, sine):
    rows, width = tokens.shape
    half = rows // 2
    heads = wk.shape[1] // HD
    full = lambda w: pl.BlockSpec(w.shape, lambda i, c: (0, 0))
    outs = pl.pallas_call(
        norm_kv_kernel,
        out_shape=[jax.ShapeDtypeStruct((rows, width), BF)]
        + [jax.ShapeDtypeStruct((rows, 2 * HD), BF)] * heads,
        grid_spec=pltpu.PrefetchScalarGridSpec(
            num_scalar_prefetch=1,
            grid=(2,),
            in_specs=[
                pl.BlockSpec((half, width), lambda i, c: (i ^ c[0], 0)),
                full(gain),
                full(wk),
                full(wv),
                pl.BlockSpec((half, HD), lambda i, c: (i, 0)),
                pl.BlockSpec((half, HD), lambda i, c: (i, 0)),
            ],
            out_specs=[pl.BlockSpec((half, width), lambda i, c: (i, 0))]
            + [pl.BlockSpec((half, 2 * HD), lambda i, c: (i, 0))] * heads,
        ),
        cost_estimate=pl.CostEstimate(flops=int(2.9e9), bytes_accessed=0, transcendentals=0),
        name="norm_kv",
    )(core, tokens, gain, wk, wv, cosine, sine)
    return outs[0], outs[1:]


def query_kernel(x_ref, w_ref, cos_ref, sin_ref, out_ref):
    raw = dot(x_ref[...], w_ref[...])
    for h in range(raw.shape[1] // HD):
        cols = slice(h * HD, (h + 1) * HD)
        out_ref[:, cols] = rope(raw[:, cols], cos_ref[...], sin_ref[...]).astype(BF)


def query_proj(x, w, cosine, sine):
    rows, width = x.shape
    half = rows // 2
    return pl.pallas_call(
        query_kernel,
        out_shape=jax.ShapeDtypeStruct((rows, w.shape[1]), BF),
        grid=(2,),
        in_specs=[
            pl.BlockSpec((half, width), lambda i: (i, 0)),
            pl.BlockSpec(w.shape, lambda i: (0, 0)),
            pl.BlockSpec((half, HD), lambda i: (i, 0)),
            pl.BlockSpec((half, HD), lambda i: (i, 0)),
        ],
        out_specs=pl.BlockSpec((half, w.shape[1]), lambda i: (i, 0)),
        cost_estimate=pl.CostEstimate(flops=int(2.9e9), bytes_accessed=0, transcendentals=0),
        name="query_proj",
    )(x, w, cosine, sine)


def fetch_slots(slot_refs, slots, kv_ref, sems):
    rows, width = slot_refs[0].shape
    copies = []
    for at, ref in enumerate(slot_refs):
        head, slot = divmod(at, slots)
        spot = kv_ref.at[pl.ds(slot * rows, rows), pl.ds(head * width, width)]
        copies.append(pltpu.make_async_copy(ref, spot, sems.at[at]))
    for copy in copies:
        copy.start()
    for copy in copies:
        copy.wait()


def allowed(pk, size, span, pos, low):
    key_pos = pk * size + lax.broadcasted_iota(jnp.int32, (size, span), 0)
    return (key_pos <= pos) & (key_pos >= low)


def attn_fwd_kernel(slots, *refs):
    meta, q_ref, pos_ref, low_ref = refs[:4]
    slot_refs = refs[4 : 4 + slots]
    mixed_ref, lse_ref, kv_ref, acc_ref, sems = refs[-5:]
    fetch_slots(slot_refs, slots, kv_ref, sems)
    size = q_ref.shape[0] // 2
    for i in range(2):
        rows = slice(i * size, (i + 1) * size)
        pos = jnp.tile(pos_ref[0:1, rows], (1, 2))
        low = jnp.tile(low_ref[0:1, rows], (1, 2))
        queries = [q_ref[rows, r * HD : (r + 1) * HD] for r in range(2)]
        acc_ref[...] = jnp.zeros_like(acc_ref)

        def body(pk, carry):
            peak, total = carry
            spot = pl.multiple_of(meta[4 + pk] * size, size)
            keys = kv_ref[pl.ds(spot, size), :HD]
            values = kv_ref[pl.ds(spot, size), HD:]
            scores = jnp.concatenate([dot(keys, q, NT) for q in queries], axis=1) * SCORE
            scores = jnp.where(allowed(pk, size, 2 * size, pos, low), scores, NEGATIVE)
            peak_new = jnp.maximum(peak, jnp.max(scores, axis=0, keepdims=True))
            alpha = jnp.exp2(peak - peak_new)
            probs = jnp.exp2(scores - peak_new)
            total = total * alpha + jnp.sum(probs, axis=0, keepdims=True)
            acc_ref[...] = acc_ref[...] * alpha + dot(values, probs.astype(BF), TN)
            return peak_new, total

        start = (jnp.full((1, 2 * size), NEGATIVE, F32), jnp.zeros((1, 2 * size), F32))
        peak, total = lax.fori_loop(meta[i], meta[2 + i] + 1, body, start)
        lse_ref[i : i + 1, :] = peak + jnp.log2(total)
        out = acc_ref[...] * (1.0 / total)
        for r in range(2):
            mixed_ref[rows, r * HD : (r + 1) * HD] = out[:, r * size : (r + 1) * size].T.astype(BF)


def attn_fwd(head, meta, q, pos, low, slots, mixed):
    rows = q.shape[0]
    count = len(slots)
    earlier = [] if mixed is None else [mixed]
    return pl.pallas_call(
        functools.partial(attn_fwd_kernel, count),
        out_shape=(
            jax.ShapeDtypeStruct(q.shape, BF),
            jax.ShapeDtypeStruct((2, rows), F32),
        ),
        grid=(1,),
        in_specs=[
            SM,
            pl.BlockSpec((rows, 2 * HD), lambda i: (0, head)),
            pl.BlockSpec(pos.shape, lambda i: (0, 0)),
            pl.BlockSpec(low.shape, lambda i: (0, 0)),
        ]
        + [ANY] * (count + len(earlier)),
        out_specs=[
            pl.BlockSpec((rows, 2 * HD), lambda i: (0, head)),
            pl.BlockSpec((2, rows), lambda i: (0, 0)),
        ],
        input_output_aliases={4 + count: 0} if earlier else {},
        scratch_shapes=[
            pltpu.VMEM((count * rows, 2 * HD), BF),
            pltpu.VMEM((HD, rows), F32),
            pltpu.SemaphoreType.DMA((count,)),
        ],
        cost_estimate=pl.CostEstimate(flops=int(1e9), bytes_accessed=0, transcendentals=0),
        name="attn_fwd",
    )(meta, q, pos, low, *slots, *earlier)


def attn_bwd_kernel(heads, slots, groups, *refs):
    meta, q_ref, pos_ref, low_ref, dmix_ref, mixed_ref, cos_ref, sin_ref = refs[:8]
    lse_refs = refs[8 : 8 + heads]
    at = 8 + heads
    slot_refs = refs[at : at + heads * slots]
    at += heads * slots
    dq_ref, dkv_refs = refs[at], refs[at + 1 : -4]
    kv_ref, dkv_ref, dq_acc, sems = refs[-4:]
    fetch_slots(slot_refs, slots, kv_ref, sems)
    dkv_ref[...] = jnp.zeros_like(dkv_ref)
    rows_all = q_ref.shape[0]
    size = rows_all // 2
    for i in range(2):
        rows = slice(i * size, (i + 1) * size)
        pos = jnp.tile(pos_ref[0:1, rows], (1, 2))
        low = jnp.tile(low_ref[0:1, rows], (1, 2))
        for g in range(heads):
            cols = [slice((2 * g + r) * HD, (2 * g + r + 1) * HD) for r in range(2)]
            queries = jnp.concatenate([q_ref[rows, c] for c in cols], axis=0)
            grads = jnp.concatenate([dmix_ref[rows, c] for c in cols], axis=0)
            outs = jnp.concatenate([mixed_ref[rows, c] for c in cols], axis=0)
            delta = jnp.sum((grads.astype(F32) * outs.astype(F32)).T, axis=0, keepdims=True)
            lse = lse_refs[g][i : i + 1, :]
            dq_acc[...] = jnp.zeros_like(dq_acc)

            def body(pk, carry):
                spot = pl.multiple_of(meta[4 + pk] * size, size)
                key_cols = slice(2 * g * HD, (2 * g + 1) * HD)
                value_cols = slice((2 * g + 1) * HD, (2 * g + 2) * HD)
                keys = kv_ref[pl.ds(spot, size), key_cols]
                values = kv_ref[pl.ds(spot, size), value_cols]
                scores = dot(keys, queries, NT) * SCORE
                probs = jnp.where(
                    allowed(pk, size, 2 * size, pos, low), jnp.exp2(scores - lse), 0.0
                )
                d_probs = dot(values, grads, NT)
                d_scores = (probs * (d_probs - delta)).astype(BF)
                dkv_ref[pl.ds(spot, size), value_cols] += dot(probs.astype(BF), grads)
                dkv_ref[pl.ds(spot, size), key_cols] += dot(d_scores, queries) * FACTOR
                dq_acc[...] += dot(d_scores, keys, TN)
                return carry

            lax.fori_loop(meta[i], meta[2 + i] + 1, body, 0)
            for r in range(2):
                part = dq_acc[r * size : (r + 1) * size, :] * FACTOR
                dq_ref[rows, cols[r]] = rope(part, cos_ref[rows, :], -sin_ref[rows, :]).astype(BF)
    ring = slots // 2
    for j, ref in enumerate(dkv_refs):
        first = ring * (j // len(groups))
        for place, k in enumerate(groups[j % len(groups)]):
            spot = pl.multiple_of((first + meta[4 + 2 * slots + k]) * rows_all, rows_all)
            ref[place * rows_all : (place + 1) * rows_all, :] = dkv_ref[
                pl.ds(spot, rows_all), :
            ].astype(BF)


def attn_bwd(meta, q, pos, low, lse, mixed, dmix, cosine, sine, slots):
    rows, q_width = q.shape
    heads, count = len(slots), len(slots[0])
    kv_width = heads * 2 * HD
    groups = halving(count // 2)
    outs = pl.pallas_call(
        functools.partial(attn_bwd_kernel, heads, count, groups),
        out_shape=[jax.ShapeDtypeStruct((rows, q_width), BF)]
        + [jax.ShapeDtypeStruct((len(g) * rows, kv_width), BF) for g in groups] * 2,
        in_specs=[SM] + [VM] * (7 + heads) + [ANY] * (heads * count),
        out_specs=[VM] * (1 + 2 * len(groups)),
        scratch_shapes=[
            pltpu.VMEM((count * rows, kv_width), BF),
            pltpu.VMEM((count * rows, kv_width), F32),
            pltpu.VMEM((rows, HD), F32),
            pltpu.SemaphoreType.DMA((heads * count,)),
        ],
        cost_estimate=pl.CostEstimate(flops=int(2e9), bytes_accessed=0, transcendentals=0),
        name="attn_bwd",
    )(meta, q, pos, low, dmix, mixed, cosine, sine, *lse, *[v for head in slots for v in head])
    return outs[0], outs[1 : 1 + len(groups)], outs[1 + len(groups) :]


def cost(micros):
    return pl.CostEstimate(flops=int(micros * 0.3e9), bytes_accessed=0, transcendentals=0)


def split_rows(total, own_ref, other_ref):
    half = own_ref.shape[0]
    own_ref[...] = total[:half].astype(BF)
    other_ref[...] = total[half:].astype(BF)


def project_kernel(spec, *refs):
    total = None
    for a, b, offset, dims in spec:
        left = refs[a][...] if dims is not None else None
        if dims == "nt":
            right, form = refs[b][:, offset : offset + left.shape[1]], NT
        else:
            right, form = refs[b][offset : offset + left.shape[1], :], NN
        term = dot(left, right, form)
        total = term if total is None else total + term
    split_rows(total, refs[-2], refs[-1])


def project(pairs, dims, tile, micros):
    operands, specs, plan, weights = [], [], [], []
    for a, b, offset in pairs:
        operands.append(a)
        specs.append(pl.BlockSpec(a.shape, lambda i: (0, 0)))
        spot = next((at for at, seen in weights if seen is b), None)
        left = len(operands) - 1
        if spot is None:
            spot = len(operands)
            operands.append(b)
            weights.append((spot, b))
            if dims == "nt":
                specs.append(pl.BlockSpec((tile, b.shape[1]), lambda i: (i, 0)))
            else:
                specs.append(pl.BlockSpec((b.shape[0], tile), lambda i: (0, i)))
        plan.append((left, spot, offset, dims))
    rows = pairs[0][0].shape[0]
    width = pairs[0][1].shape[0 if dims == "nt" else 1]
    return pl.pallas_call(
        functools.partial(project_kernel, plan),
        out_shape=[jax.ShapeDtypeStruct((rows // 2, width), BF)] * 2,
        grid=(width // tile,),
        in_specs=specs,
        out_specs=[pl.BlockSpec((rows // 2, tile), lambda i: (0, i))] * 2,
        cost_estimate=cost(micros),
        name="project",
    )(*operands)


def back_dense_kernel(gate_a, up_a, gate_b, up_b, wg_ref, wu_ref, own_ref, other_ref):
    total = None
    offset = 0
    for group in ((gate_a, up_a), (gate_b, up_b)):
        count = group[0].shape[1]
        for ref, w_ref in zip(group, (wg_ref, wu_ref)):
            term = dot(ref[...], w_ref[:, offset : offset + count], NT)
            total = term if total is None else total + term
        offset += count
    split_rows(total, own_ref, other_ref)


def back_dense(grads, w_gate, w_up, tile, part, parts):
    width, hidden = w_gate.shape[0] // parts, w_gate.shape[1]
    rows = grads[0].shape[0]
    ahead = part * (width // tile)
    weight = pl.BlockSpec((tile, hidden), lambda i: (ahead + i, 0))
    return pl.pallas_call(
        back_dense_kernel,
        out_shape=[jax.ShapeDtypeStruct((rows // 2, width), BF)] * 2,
        grid=(width // tile,),
        in_specs=[pl.BlockSpec(v.shape, lambda i: (0, 0)) for v in grads] + [weight, weight],
        out_specs=[pl.BlockSpec((rows // 2, tile), lambda i: (0, i))] * 2,
        cost_estimate=cost(11 / parts),
        name="back_dense",
    )(*grads, w_gate, w_up)


def gated_kernel(own_ref, other_ref, wg_ref, wu_ref, di_ref, inner_ref, dg_ref, du_ref, all_ref):
    @pl.when(pl.program_id(0) == 0)
    def _():
        half = own_ref.shape[0]
        all_ref[:half, :] = own_ref[...]
        all_ref[half:, :] = other_ref[...]

    gate = dot(all_ref[...], wg_ref[...])
    up = dot(all_ref[...], wu_ref[...])
    sigma = 1.0 / (1.0 + jnp.exp(-gate))
    silu = gate * sigma
    d_inner = di_ref[...]
    inner_ref[...] = (silu * up).astype(BF)
    dg_ref[...] = (d_inner * up * sigma * (1.0 + gate * (1.0 - sigma))).astype(BF)
    du_ref[...] = (d_inner * silu).astype(BF)


def gated(own, other, wg, wu, d_inner, first, columns, tile):
    half, width = own.shape
    weight = pl.BlockSpec((width, tile), lambda i: (0, first // tile + i))
    whole = pl.BlockSpec((half, width), lambda i: (0, 0))
    return pl.pallas_call(
        gated_kernel,
        out_shape=[jax.ShapeDtypeStruct((2 * half, columns), BF)] * 3,
        grid=(pl.cdiv(columns, tile),),
        in_specs=[
            whole,
            whole,
            weight,
            weight,
            pl.BlockSpec((2 * half, tile), lambda i: (0, first // tile + i)),
        ],
        out_specs=[pl.BlockSpec((2 * half, tile), lambda i: (0, i))] * 3,
        scratch_shapes=[pltpu.VMEM((2 * half, width), BF)],
        cost_estimate=cost(7.5),
        name="gated",
    )(own, other, wg, wu, d_inner)


def mixed_grad_kernel(own_ref, other_ref, w_ref, out_ref):
    both = jnp.concatenate([own_ref[...], other_ref[...]], axis=0)
    out_ref[...] = dot(both, w_ref[...], NT).astype(BF)


def mixed_grad(own, other, w):
    return pl.pallas_call(
        mixed_grad_kernel,
        out_shape=jax.ShapeDtypeStruct((2 * own.shape[0], w.shape[0]), BF),
        in_specs=[VM] * 3,
        out_specs=VM,
        cost_estimate=cost(4),
        name="mixed_grad",
    )(own, other, w)


def d_inner_kernel(x_ref, w_ref, out_ref):
    out_ref[...] = dot(x_ref[...], w_ref[...], NT)


def inner_grad(x, w, tile):
    rows, width = x.shape
    hidden = w.shape[0]
    return pl.pallas_call(
        d_inner_kernel,
        out_shape=jax.ShapeDtypeStruct((rows, hidden), F32),
        grid=(pl.cdiv(hidden, tile),),
        in_specs=[
            pl.BlockSpec((rows, width), lambda i: (0, 0)),
            pl.BlockSpec((tile, width), lambda i: (i, 0)),
        ],
        out_specs=pl.BlockSpec((rows, tile), lambda i: (0, i)),
        cost_estimate=cost(8),
        name="inner_grad",
    )(x, w)


def pack_kernel(count, plan, strip, tbl, *refs):
    ins, outs = refs[:count], refs[count:]
    for out_ref, pieces in zip(outs, plan):
        column = 0
        for at, rows, row in pieces:
            for k in range(tbl.shape[1]):
                first = pl.multiple_of(tbl[row, k] * strip, 128)
                out_ref[:, column : column + strip] = ins[at][rows, pl.ds(first, strip)]
                column += strip


def pack(values, plan, tbl, strip):
    turns = tbl.shape[1]
    if strip % 128:
        cut = lambda v, rows, at: lax.dynamic_slice_in_dim(v[rows], at * strip, strip, axis=1)
        return [
            jnp.concatenate(
                [cut(values[at], rows, tbl[row, k]) for at, rows, row in pieces for k in range(turns)],
                axis=1,
            )
            for pieces in plan
        ]
    return pl.pallas_call(
        functools.partial(pack_kernel, len(values), plan, strip),
        out_shape=[
            jax.ShapeDtypeStruct(
                (p[0][1].stop - p[0][1].start, len(p) * turns * strip), values[0].dtype
            )
            for p in plan
        ],
        in_specs=[SM] + [VM] * len(values),
        out_specs=[VM] * len(plan),
        cost_estimate=cost(1.5),
        name="pack",
    )(tbl, *values)


def strip_rows_kernel(halves, near, rights, nears, spans, tbl, *refs):
    left = refs[:halves]
    left_near = refs[halves : halves + near]
    right = refs[halves + near : halves + near + rights]
    right_near = refs[halves + near + rights : halves + near + rights + nears]
    outs = refs[halves + near + rights + nears :]
    step = pl.program_id(0)
    join = lambda group: (
        group[0][...] if len(group) == 1 else jnp.concatenate([r[...] for r in group], axis=0)
    )
    mine, theirs = join(left), join(left_near)
    pieces = []
    for r, n in zip(right, right_near):
        planes = range(r.shape[0]) if len(r.shape) == 3 else [None]
        for k in planes:
            a = r[...] if k is None else r[k]
            b = n[...] if k is None else n[k]
            pieces.append((dot(mine, a, TN) + dot(theirs, b, TN)).astype(BF))
    for (start, length), out in zip(spans, outs):

        @pl.when((step >= start) & (step < start + length))
        def _(out=out):
            column = 0
            for piece in pieces:
                out[:, column : column + piece.shape[1]] = piece
                column += piece.shape[1]


def strip_rows_grad(left, left_near, right, right_near, tbl, strip, micros, single=False):
    turns = tbl.shape[1]
    columns = sum(r.shape[-1] * (r.shape[0] if r.ndim == 3 else 1) for r in right)
    spans = [(k, 1) for k in range(turns)] if single else stretches(halving(turns))
    if strip % 128:
        near = jnp.concatenate(left_near, axis=0)
        mine = jnp.concatenate(left, axis=0)
        flat = lambda r: [r] if r.ndim == 2 else [r[k] for k in range(r.shape[0])]
        outs = []
        for start, length in spans:
            group = []
            for k in range(start, start + length):
                a = lax.dynamic_slice_in_dim(mine, tbl[0, k] * strip, strip, axis=1)
                b = near[:, k * strip : (k + 1) * strip]
                group.append(
                    jnp.concatenate(
                        [
                            dot(a, x, TN) + dot(b, y, TN)
                            for r, n in zip(right, right_near)
                            for x, y in zip(flat(r), flat(n))
                        ],
                        axis=1,
                    ).astype(BF)
                )
            outs.append(jnp.concatenate(group, axis=0))
        return outs
    held = lambda start, length: (lambda i, t: (jnp.clip(i - start, 0, length - 1), 0))
    whole = lambda v: pl.BlockSpec(v.shape, lambda i, t: (0,) * v.ndim)
    return pl.pallas_call(
        functools.partial(
            strip_rows_kernel, len(left), len(left_near), len(right), len(right_near), spans
        ),
        out_shape=[jax.ShapeDtypeStruct((length * strip, columns), BF) for _, length in spans],
        grid_spec=pltpu.PrefetchScalarGridSpec(
            num_scalar_prefetch=1,
            grid=(turns,),
            in_specs=[pl.BlockSpec((v.shape[0], strip), lambda i, t: (0, t[0, i])) for v in left]
            + [pl.BlockSpec((v.shape[0], strip), lambda i, t: (0, i)) for v in left_near]
            + [whole(v) for v in [*right, *right_near]],
            out_specs=[pl.BlockSpec((strip, columns), held(*span)) for span in spans],
        ),
        cost_estimate=cost(micros),
        name="strip_rows",
    )(tbl, *left, *left_near, *right, *right_near)


def strip_columns_kernel(parts, halves, near, strip, spans, *refs):
    at = 2 * parts
    right, right_near = refs[at : at + halves], refs[at + halves : at + halves + near]
    outs = refs[at + halves + near :]
    first = 0
    for p in range(parts):
        total = None
        for ref, group in ((refs[p], right), (refs[parts + p], right_near)):
            row = 0
            for r in group:
                term = dot(ref[row : row + r.shape[0], :], r[...], TN)
                total = term if total is None else total + term
                row += r.shape[0]
        for (start, length), out in zip(spans, outs):
            out[first : first + total.shape[0], :] = total[
                :, start * strip : (start + length) * strip
            ].astype(BF)
        first += total.shape[0]


def strip_columns_grad(
    left, left_near, right, right_near, turns, strip, tile, micros, near_at=0, single=False
):
    rows, count = left[0].shape[0], sum(v.shape[1] for v in left)
    if strip * turns % 128:
        raise ValueError(strip)
    spans = [(k, 1) for k in range(turns)] if single else stretches(halving(turns))
    whole = lambda v: pl.BlockSpec(v.shape, lambda i: (0, 0))
    near = lambda v: pl.BlockSpec((v.shape[0], turns * strip), lambda i: (0, near_at))
    if len(left) == 1:
        left_specs = [pl.BlockSpec((rows, tile), lambda i: (0, i))] * 2
    else:
        tile = count
        left_specs = [whole(v) for v in [*left, *left_near]]
    return pl.pallas_call(
        functools.partial(
            strip_columns_kernel, len(left), len(right), len(right_near), strip, spans
        ),
        out_shape=[jax.ShapeDtypeStruct((count, length * strip), BF) for _, length in spans],
        grid=(pl.cdiv(count, tile),),
        in_specs=left_specs + [whole(v) for v in right] + [near(v) for v in right_near],
        out_specs=[pl.BlockSpec((tile, length * strip), lambda i: (i, 0)) for _, length in spans],
        cost_estimate=cost(micros),
        name="strip_columns",
    )(*left, *left_near, *right, *right_near)


def close_kv_kernel(count, *refs):
    cos_ref, sin_ref, dk_ref, dv_ref = refs[count:]
    total = refs[0][...].astype(F32)
    for ref in refs[1:count]:
        total = total + ref[...].astype(F32)
    heads = dk_ref.shape[1] // HD
    for h in range(heads):
        cols = slice(h * HD, (h + 1) * HD)
        keys = total[:, 2 * h * HD : (2 * h + 1) * HD]
        dk_ref[:, cols] = rope(keys, cos_ref[...], -sin_ref[...]).astype(BF)
        dv_ref[:, cols] = total[:, (2 * h + 1) * HD : (2 * h + 2) * HD].astype(BF)


def close_kv(terms, cosine, sine):
    rows, width = terms[0].shape
    first = lambda w: pl.BlockSpec((rows, w), lambda i: (0, 0))
    return pl.pallas_call(
        functools.partial(close_kv_kernel, len(terms)),
        out_shape=[jax.ShapeDtypeStruct((rows, width // 2), BF)] * 2,
        grid=(1,),
        in_specs=[first(width)] * len(terms) + [first(HD)] * 2,
        out_specs=[first(width // 2)] * 2,
        cost_estimate=cost(1.5),
        name="close_kv",
    )(*terms, cosine, sine)


def norm_backward(source, scale_rows, gain, upstream):
    weighted = upstream * gain
    average = jnp.mean(weighted * source, axis=1, keepdims=True)
    return scale_rows * weighted - source * scale_rows**3 * average


def after(value, *done):
    return lax.optimization_barrier((value, *done))[0]


def shards(
    tokens,
    cotangent,
    keep_mask,
    doc_lengths,
    block_order,
    gain_attn,
    w_query,
    w_key,
    w_value,
    w_out,
    gain_dense,
    w_gate,
    w_up,
    w_down,
):
    rows, width = tokens.shape
    half = rows // 2
    wide = lax.axis_size("wide")
    group = wide // block_order.shape[0]
    ring = group // 2
    wide_index = lax.axis_index("wide")
    member = wide_index % group
    seq_index = wide_index // group
    side = (wide_index % 2).astype(jnp.int32)
    core = lax.axis_index("narrow") % 2
    strip = width // wide
    turns = wide // 2

    def ordered(mine, other):
        return jnp.where(
            core == 0,
            jnp.concatenate([mine, other], axis=0),
            jnp.concatenate([other, mine], axis=0),
        )

    def own_half(value):
        return lax.dynamic_slice_in_dim(value, core * half, half)

    def other_half(value):
        return lax.dynamic_slice_in_dim(value, (1 - core) * half, half)

    order_row = lax.dynamic_index_in_dim(block_order, seq_index, 0, keepdims=False)
    length_row = lax.dynamic_index_in_dim(doc_lengths, seq_index, 0, keepdims=False)
    doc_ends = jnp.cumsum(length_row)
    places = jnp.stack([member * 2 + core, member * 2 + 1 - core])
    chosen = jnp.sum(
        jnp.where(places[:, None] == jnp.arange(2 * group)[None, :], order_row[None, :], 0), axis=1
    )
    pos = (chosen[:, None] * half + jnp.arange(half, dtype=jnp.int32)[None, :]).reshape(-1)
    low = jnp.max(jnp.where(doc_ends[None, :] <= pos[:, None], doc_ends[None, :], 0), axis=1)
    block_low = low.reshape(2, half)[:, 0] // half
    stored = jnp.sum(
        jnp.where(
            order_row[None, :] == jnp.arange(2 * group)[:, None], jnp.arange(2 * group)[None, :], 0
        ),
        axis=1,
    )
    owner = stored // 2
    slot = (member // 2 - owner // 2) % ring + ring * (owner % 2 != side).astype(jnp.int32)
    spots = slot * 2 + (stored % 2 != core).astype(jnp.int32)
    place = member // 2
    back = (place - (place ^ jnp.arange(ring, dtype=jnp.int32))) % ring
    meta = jnp.concatenate([block_low, chosen, spots, back]).astype(jnp.int32)
    frequency = BASE ** (-(jnp.arange(HD // 2, dtype=F32) * 2.0) / HD)
    angles = pos.astype(F32)[:, None] * frequency[None, :]
    cosine = jnp.cos(angles)
    sine = jnp.sin(angles)
    cosine = jnp.concatenate([cosine, cosine], axis=1)
    sine = jnp.concatenate([-sine, sine], axis=1)
    pos_row = pos[None, :]
    low_row = low[None, :]

    order = np.array([k for stretch in halving(turns) for k in stretch], np.int32)
    turn_row = wide_index // 2 ^ order
    tbl = jnp.stack([2 * turn_row + side, 2 * turn_row + 1 - side]).astype(jnp.int32)
    round_row = (wide_index // 2 - 1 - jnp.arange(turns, dtype=jnp.int32)) % turns
    round_tbl = jnp.stack([2 * round_row + side, 2 * round_row + 1 - side]).astype(jnp.int32)
    both_tbl = jnp.concatenate([tbl, round_tbl])
    core_arr = core.astype(jnp.int32)[None]
    normed_one, both = norm_kv(core_arr, tokens, gain_attn[None, :], w_key, w_value, cosine, sine)
    low_rows, all_rows = slice(0, half), slice(0, rows)

    def together(*values):
        return list(lax.optimization_barrier(values))

    near, far = [[v] for v in both], [[] for v in both]
    query = d_dense = d_inner = input_near = d_dense_strips = None
    for step in range(ring):
        for head in range(len(both)):
            held = near[head][step]
            if step + 1 < ring:
                sent = [wide_swap(held), wide_ring(held, group)]
            elif head == 0:
                sent = [wide_swap(held)]
            else:
                sent = [wide_ring(far[head][0], group, -1)]
            beside = []
            if step == 0 and head == 0:
                beside = [query_proj(normed_one, w_query, cosine, sine)]
            if step == 0 and head == 1:
                keep_rel = jnp.concatenate([own_half(keep_mask), other_half(keep_mask)])[:, None]
                cot_rel = jnp.concatenate([own_half(cotangent), other_half(cotangent)])
                beside = [jnp.where(keep_rel > 0, cot_rel, jnp.zeros_like(cot_rel))]
            if step == 1 and head == 0:
                beside = [inner_grad(d_dense, w_down, 256)]
            if step == 2 and head == 0:
                beside = pack(
                    [normed_one, d_dense],
                    [[(0, low_rows, 3), (1, low_rows, 1)], [(1, all_rows, 0)]],
                    both_tbl,
                    strip,
                )
            done = together(*sent, *beside)
            far[head].append(done[0])
            if step + 1 < ring:
                near[head].append(done[1])
            if step == 0 and head == 0:
                query = done[-1]
            if step == 0 and head == 1:
                d_dense = done[-1]
            if step == 1 and head == 0:
                d_inner = done[-1]
            if step == 2 and head == 0:
                input_near, d_dense_strips = done[-2:]
    slots = [n + f for n, f in zip(near, far)]
    input_near = wide_swap(after(input_near, *slots[0], *slots[-1]))
    mixed, lse = None, []
    for h, held in enumerate(slots):
        mixed, part = attn_fwd(h, meta, query, pos_row, low_row, held, mixed)
        lse.append(part)

    def reduce_narrow(halves, hold=()):
        own_part, other_part = halves
        got = narrow_swap(other_part, 1)
        held = (own_part.astype(F32) + got.astype(F32)).astype(BF)
        return held, narrow_swap(held, 2)

    def total_of(held, got):
        return held.astype(F32) + got.astype(F32)

    part = project([(mixed, w_out, 0)], "nn", 1024, 4)
    held, got = reduce_narrow((part[0], after(part[1], input_near)))
    mixed_near = wide_swap(mixed)
    input_near_other = narrow_swap(input_near, 1)
    source = own_half(tokens).astype(F32)
    keep_own = own_half(keep_mask).astype(F32)[:, None]
    hidden_one = source + keep_own * total_of(held, got)
    gain_two = gain_dense.astype(F32)
    scale_two = lax.rsqrt(jnp.mean(hidden_one * hidden_one, axis=1, keepdims=True) + EPSILON)
    normed_two = (hidden_one * scale_two * gain_two).astype(BF)
    normed_two_other = narrow_swap(after(normed_two, mixed_near), 1)
    hidden = w_gate.shape[1]
    tile = 256
    first_count = 3 * tile
    inner_a, *dgu_a = gated(
        normed_two, normed_two_other, w_gate, w_up, d_inner, 0, first_count, tile
    )
    inner_a_near = wide_swap(inner_a)
    inner_b, *dgu_b = gated(
        after(normed_two, inner_a),
        normed_two_other,
        w_gate,
        w_up,
        d_inner,
        first_count,
        hidden - first_count,
        tile,
    )
    back = back_dense([*dgu_a, *dgu_b], w_gate, w_up, 512, 0, 1)
    held, got = reduce_narrow((back[0], after(back[1], inner_a_near)))

    def halve(parts, axis, hold=None, first=None):
        groups = halving(1 << (len(parts) - 1))
        size = parts[-1].shape[axis]
        received, sent = [], None
        for bit, group in enumerate(groups[:-1]):
            sent = parts[bit]
            if bit:
                total = sent.astype(F32)
                for early, value in enumerate(received):
                    there = [k ^ (1 << early) for k in groups[early]]
                    pick = [
                        lax.slice_in_dim(value, size * there.index(k), size * (there.index(k) + 1), axis=axis)
                        for k in group
                    ]
                    total = total + (pick[0] if len(pick) == 1 else jnp.concatenate(pick, axis)).astype(F32)
                sent = total.astype(BF)
            got = first if bit == 0 and first is not None else wide_flip(sent, bit)
            received.append(got if hold is None else after(got, hold))
        return received, sent

    def ring_sum(parts, hold=None, last=()):
        carried, first = parts[0], None
        for k, part in enumerate(parts[1:]):
            got = wide_ring(carried, wide)
            if k == 0 and hold is not None:
                got = after(got, hold)
            if k == len(parts) - 2 and last:
                got = after(got, *last)
            total = part.astype(F32) + got.astype(F32)
            carried = total.astype(BF)
            first = carried if first is None else first
        return total, first

    def close(parts, received, axis):
        size = parts[-1].shape[axis]
        total = parts[-1].astype(F32)
        for value in received:
            total = total + lax.slice_in_dim(value, 0, size, axis=axis).astype(F32)
        return total

    near_sides = [input_near, input_near_other]
    down_a = strip_columns_grad(
        [after(inner_a, held)],
        [inner_a_near],
        [d_dense_strips],
        near_sides,
        turns,
        strip,
        tile,
        4,
        1,
    )
    inner_b_near = wide_swap(inner_b)
    down_a_got, down_a_mid = halve(down_a, 1)
    dgu_a_near = [wide_swap(after(v, inner_b)) for v in dgu_a]
    dense_parts = project(
        [(after(inner_a, down_a[0], inner_b_near), w_down, 0), (inner_b, w_down, first_count)], "nn", 512, 6
    )
    (normed_two_near,) = pack(
        [after(normed_two, dense_parts[0])], [[(0, low_rows, 1)]], round_tbl, strip
    )
    normed_two_near = wide_swap(normed_two_near)
    down_b = strip_columns_grad(
        [after(inner_b, dense_parts[0])], [inner_b_near], [d_dense_strips], near_sides, turns, strip, tile, 4, 1
    )

    got = after(got, dense_parts[0], down_b[0])
    upstream = own_half(cotangent).astype(F32)
    d_hidden = upstream + norm_backward(hidden_one, scale_two, gain_two, total_of(held, got))
    d_attn = (keep_own * d_hidden).astype(BF)
    d_attn_other = narrow_swap(after(d_attn, dgu_a_near[0], down_a_mid), 1)

    down_b_first = wide_flip(down_b[0], 0)
    d_mixed = mixed_grad(d_attn, d_attn_other, w_out)
    d_query, d_near, d_far = attn_bwd(
        meta, query, pos_row, low_row, lse, mixed, after(d_mixed, down_a_got[-1]), cosine, sine, slots
    )
    held_out, got_out = reduce_narrow((dense_parts[0], after(dense_parts[1], d_mixed)))
    output_own = (hidden_one + keep_own * total_of(held_out, got_out)).astype(BF)
    output = ordered(output_own, narrow_swap(output_own, 1))

    normed_two_near_other = narrow_swap(after(normed_two_near, d_query), 1)
    normed_two_sides = [normed_two_near, normed_two_near_other]
    gate_up_a = strip_rows_grad(
        [after(normed_two, d_query, down_b_first), normed_two_other], normed_two_sides, dgu_a, dgu_a_near, round_tbl, strip, 8, True
    )
    grad_gate_up_a, gate_up_a_mid = ring_sum(gate_up_a)
    d_far = [wide_swap(v) for v in d_far]
    d_far[0] = after(d_far[0], gate_up_a_mid)
    pairs = [
        (n.astype(F32) + f.astype(F32)).astype(BF) for n, f in zip(d_near[:-1], d_far[:-1])
    ]
    kv_got, kv_mid = halve([*pairs, d_near[-1]], 0)
    d_key, d_value = close_kv([d_near[-1], d_far[-1], *kv_got], cosine, sine)

    dgu_b_near = [wide_swap(after(v, d_query)) for v in dgu_b]
    gate_up_b = strip_rows_grad(
        [after(normed_two, gate_up_a_mid, kv_mid), normed_two_other],
        normed_two_sides,
        dgu_b,
        dgu_b_near,
        round_tbl,
        strip,
        7,
        True,
    )
    d_query_near = wide_swap(after(d_query, pairs[0]))
    grad_gate_up_b, gate_up_b_mid = ring_sum(gate_up_b)
    d_attn_near, d_attn_strips, d_attn_other_strips = pack(
        [after(d_attn, gate_up_a[0]), d_attn_other],
        [[(0, low_rows, 1)], [(0, low_rows, 0)], [(1, low_rows, 0)]],
        round_tbl,
        strip,
    )
    d_attn_near = wide_swap(after(d_attn_near, pairs[0]))
    d_attn_near_other = narrow_swap(after(d_attn_near, gate_up_b[0]), 1)
    query_part = strip_rows_grad(
        [after(normed_one, gate_up_b[0])], near_sides, [d_query], [d_query_near], round_tbl, strip, 4, True
    )
    out_part = strip_columns_grad(
        [after(mixed, query_part[0])],
        [mixed_near],
        [d_attn_strips, d_attn_other_strips],
        [d_attn_near, d_attn_near_other],
        turns,
        strip,
        tile,
        4,
        0,
        True,
    )

    kv_width = w_key.shape[1]
    held, got = reduce_narrow(
        project([(d_query, w_query, 0), (d_key, w_key, 0), (d_value, w_value, 0)], "nt", 512, 6)
    )
    gain_one = gain_attn.astype(F32)
    scale_one = lax.rsqrt(jnp.mean(source * source, axis=1, keepdims=True) + EPSILON)
    d_normed_one = total_of(held, got)
    grad_own = (d_hidden + norm_backward(source, scale_one, gain_one, d_normed_one)).astype(BF)
    grad_tokens = ordered(grad_own, narrow_swap(grad_own, 1))

    d_key_near = wide_swap(d_key)
    d_value_near = wide_swap(d_value)
    kv_part = strip_rows_grad(
        [after(normed_one, out_part[0])],
        near_sides,
        [d_key, d_value],
        [d_key_near, d_value_near],
        round_tbl,
        strip,
        4,
        True,
    )
    grad_kv, _ = ring_sum(kv_part, None, (grad_own, output))
    grad_query, _ = ring_sum(query_part, kv_part[0])
    grad_out, _ = ring_sum(out_part, kv_part[0])
    down_b_got, _ = halve(down_b, 1, gate_up_b_mid, down_b_first)
    down_a_got[-1], down_b_got[-1] = after(down_a_got[-1], kv_part[0]), after(down_b_got[-1], kv_part[0])
    grad_down_a = close(down_a, down_a_got, 1)
    grad_down_b = close(down_b, down_b_got, 1)
    grad_key, grad_value = grad_kv[:, :kv_width], grad_kv[:, kv_width:]
    grad_down = jnp.concatenate([grad_down_a, grad_down_b], axis=0)
    second_count = hidden - first_count
    grad_gate = jnp.concatenate(
        [grad_gate_up_a[:, :first_count], grad_gate_up_b[:, :second_count]], axis=1
    )
    grad_up = jnp.concatenate(
        [grad_gate_up_a[:, first_count:], grad_gate_up_b[:, second_count:]], axis=1
    )

    def strip_rows(weight):
        return lax.dynamic_slice_in_dim(weight, wide_index * strip, strip).astype(F32)

    def gain_grad(pairs, gain):
        local = sum(jnp.sum(strip_rows(w) * g, axis=1) for w, g in pairs)
        return local / lax.dynamic_slice_in_dim(gain, wide_index * strip, strip)

    local = jnp.stack(
        [
            gain_grad([(w_query, grad_query), (w_key, grad_key), (w_value, grad_value)], gain_one),
            gain_grad([(w_gate, grad_gate), (w_up, grad_up)], gain_two),
        ]
    )
    local = local + narrow_swap(local, 1)
    local = local + narrow_swap(local, 2)
    grad_gain_one, grad_gain_two = local[0], local[1]
    return (
        output,
        grad_tokens,
        grad_gain_one,
        grad_query,
        grad_key,
        grad_value,
        grad_out,
        grad_gain_two,
        grad_gate,
        grad_up,
        grad_down,
    )


def solution(mesh):
    placed = (
        P("wide", None),
        P("wide", None),
        P("wide"),
        P(),
        P(),
        P(),
        P(None, "narrow"),
        P(None, "narrow"),
        P(None, "narrow"),
        P("narrow", None),
        P(),
        P(None, "narrow"),
        P(None, "narrow"),
        P("narrow", None),
    )
    return jax.shard_map(
        shards,
        mesh=mesh,
        in_specs=placed,
        out_specs=(
            P("wide", None),
            P("wide", None),
            P("wide"),
            P("wide", "narrow"),
            P("wide", "narrow"),
            P("wide", "narrow"),
            P("narrow", "wide"),
            P("wide"),
            P("wide", "narrow"),
            P("wide", "narrow"),
            P("narrow", "wide"),
        ),
        check_vma=False,
    )
```

```python
import functools

import jax
import jax.numpy as jnp
import numpy as np
from jax import lax
from jax.experimental import pallas as pl
from jax.experimental.pallas import tpu as pltpu
from jax.sharding import PartitionSpec as P

HD = 128
EPSILON = 1e-05
NEGATIVE = -1e30
BASE = 10000.0
LOG2E = 1.4426950408889634
SCORE = HD ** (-0.5) * LOG2E
FACTOR = HD ** (-0.5)
BF = jnp.bfloat16
F32 = jnp.float32
NT = (((1,), (1,)), ((), ()))
TN = (((0,), (0,)), ((), ()))
NN = (((1,), (0,)), ((), ()))
VM = pl.BlockSpec(memory_space=pltpu.VMEM)
SM = pl.BlockSpec(memory_space=pltpu.SMEM)
ANY = pl.BlockSpec(memory_space=pl.ANY)


def dot(a, b, dims=(((1,), (0,)), ((), ()))):
    return lax.dot_general(a, b, dims, preferred_element_type=F32)


def narrow_swap(value, mask):
    pairs = [(n, n ^ mask) for n in range(lax.axis_size("narrow"))]
    return lax.ppermute(value, "narrow", pairs)


def wide_swap(value):
    return lax.ppermute(value, "wide", [(w, w ^ 1) for w in range(lax.axis_size("wide"))])


def wide_ring(value, group, hop=1):
    ring = group // 2
    pairs = []
    for w in range(lax.axis_size("wide")):
        base, member = w // group * group, w % group
        pairs.append((w, base + (member // 2 + hop) % ring * 2 + member % 2))
    return lax.ppermute(value, "wide", pairs)


def wide_flip(value, bit):
    return lax.ppermute(value, "wide", [(w, w ^ (2 << bit)) for w in range(lax.axis_size("wide"))])


def halving(count):
    groups = []
    step = 1
    while step < count:
        groups.append([k for k in range(count) if k % (2 * step) == step])
        step *= 2
    return [*groups, [0]]


def stretches(groups):
    starts, at = [], 0
    for group in groups:
        starts.append((at, len(group)))
        at += len(group)
    return starts


def rope(value, cosine, sine):
    return value * cosine + pltpu.roll(value, HD // 2, 1) * sine


def norm_kv_kernel(core, x_ref, gain_ref, wk_ref, wv_ref, cos_ref, sin_ref, normed_ref, *kv_refs):
    x = x_ref[...].astype(F32)
    scale = lax.rsqrt(jnp.mean(x * x, axis=1, keepdims=True) + EPSILON)
    normed = (x * scale * gain_ref[...].astype(F32)).astype(BF)
    normed_ref[...] = normed
    keys = dot(normed, wk_ref[...])
    values = dot(normed, wv_ref[...])
    for h, ref in enumerate(kv_refs):
        cols = slice(h * HD, (h + 1) * HD)
        ref[:, :HD] = rope(keys[:, cols], cos_ref[...], sin_ref[...]).astype(BF)
        ref[:, HD:] = values[:, cols].astype(BF)


def norm_kv(core, tokens, gain, wk, wv, cosine, sine):
    rows, width = tokens.shape
    half = rows // 2
    heads = wk.shape[1] // HD
    full = lambda w: pl.BlockSpec(w.shape, lambda i, c: (0, 0))
    outs = pl.pallas_call(
        norm_kv_kernel,
        out_shape=[jax.ShapeDtypeStruct((rows, width), BF)]
        + [jax.ShapeDtypeStruct((rows, 2 * HD), BF)] * heads,
        grid_spec=pltpu.PrefetchScalarGridSpec(
            num_scalar_prefetch=1,
            grid=(2,),
            in_specs=[
                pl.BlockSpec((half, width), lambda i, c: (i ^ c[0], 0)),
                full(gain),
                full(wk),
                full(wv),
                pl.BlockSpec((half, HD), lambda i, c: (i, 0)),
                pl.BlockSpec((half, HD), lambda i, c: (i, 0)),
            ],
            out_specs=[pl.BlockSpec((half, width), lambda i, c: (i, 0))]
            + [pl.BlockSpec((half, 2 * HD), lambda i, c: (i, 0))] * heads,
        ),
        cost_estimate=pl.CostEstimate(flops=int(2.9e9), bytes_accessed=0, transcendentals=0),
        name="norm_kv",
    )(core, tokens, gain, wk, wv, cosine, sine)
    return outs[0], outs[1:]


def query_kernel(x_ref, w_ref, cos_ref, sin_ref, out_ref):
    raw = dot(x_ref[...], w_ref[...])
    for h in range(raw.shape[1] // HD):
        cols = slice(h * HD, (h + 1) * HD)
        out_ref[:, cols] = rope(raw[:, cols], cos_ref[...], sin_ref[...]).astype(BF)


def query_proj(x, w, cosine, sine):
    rows, width = x.shape
    half = rows // 2
    return pl.pallas_call(
        query_kernel,
        out_shape=jax.ShapeDtypeStruct((rows, w.shape[1]), BF),
        grid=(2,),
        in_specs=[
            pl.BlockSpec((half, width), lambda i: (i, 0)),
            pl.BlockSpec(w.shape, lambda i: (0, 0)),
            pl.BlockSpec((half, HD), lambda i: (i, 0)),
            pl.BlockSpec((half, HD), lambda i: (i, 0)),
        ],
        out_specs=pl.BlockSpec((half, w.shape[1]), lambda i: (i, 0)),
        cost_estimate=pl.CostEstimate(flops=int(2.9e9), bytes_accessed=0, transcendentals=0),
        name="query_proj",
    )(x, w, cosine, sine)


def fetch_slots(slot_refs, slots, kv_ref, sems):
    rows, width = slot_refs[0].shape
    copies = []
    for at, ref in enumerate(slot_refs):
        head, slot = divmod(at, slots)
        spot = kv_ref.at[pl.ds(slot * rows, rows), pl.ds(head * width, width)]
        copies.append(pltpu.make_async_copy(ref, spot, sems.at[at]))
    for copy in copies:
        copy.start()
    for copy in copies:
        copy.wait()


def allowed(pk, size, span, pos, low):
    key_pos = pk * size + lax.broadcasted_iota(jnp.int32, (size, span), 0)
    return (key_pos <= pos) & (key_pos >= low)


def attn_fwd_kernel(slots, *refs):
    meta, q_ref, pos_ref, low_ref = refs[:4]
    slot_refs = refs[4 : 4 + slots]
    mixed_ref, lse_ref, kv_ref, acc_ref, sems = refs[-5:]
    fetch_slots(slot_refs, slots, kv_ref, sems)
    size = q_ref.shape[0] // 2
    for i in range(2):
        rows = slice(i * size, (i + 1) * size)
        pos = jnp.tile(pos_ref[0:1, rows], (1, 2))
        low = jnp.tile(low_ref[0:1, rows], (1, 2))
        queries = [q_ref[rows, r * HD : (r + 1) * HD] for r in range(2)]
        acc_ref[...] = jnp.zeros_like(acc_ref)

        def body(pk, carry):
            peak, total = carry
            spot = pl.multiple_of(meta[4 + pk] * size, size)
            keys = kv_ref[pl.ds(spot, size), :HD]
            values = kv_ref[pl.ds(spot, size), HD:]
            scores = jnp.concatenate([dot(keys, q, NT) for q in queries], axis=1) * SCORE
            scores = jnp.where(allowed(pk, size, 2 * size, pos, low), scores, NEGATIVE)
            peak_new = jnp.maximum(peak, jnp.max(scores, axis=0, keepdims=True))
            alpha = jnp.exp2(peak - peak_new)
            probs = jnp.exp2(scores - peak_new)
            total = total * alpha + jnp.sum(probs, axis=0, keepdims=True)
            acc_ref[...] = acc_ref[...] * alpha + dot(values, probs.astype(BF), TN)
            return peak_new, total

        start = (jnp.full((1, 2 * size), NEGATIVE, F32), jnp.zeros((1, 2 * size), F32))
        peak, total = lax.fori_loop(meta[i], meta[2 + i] + 1, body, start)
        lse_ref[i : i + 1, :] = peak + jnp.log2(total)
        out = acc_ref[...] * (1.0 / total)
        for r in range(2):
            mixed_ref[rows, r * HD : (r + 1) * HD] = out[:, r * size : (r + 1) * size].T.astype(BF)


def attn_fwd(head, meta, q, pos, low, slots, mixed):
    rows = q.shape[0]
    count = len(slots)
    earlier = [] if mixed is None else [mixed]
    return pl.pallas_call(
        functools.partial(attn_fwd_kernel, count),
        out_shape=(
            jax.ShapeDtypeStruct(q.shape, BF),
            jax.ShapeDtypeStruct((2, rows), F32),
        ),
        grid=(1,),
        in_specs=[
            SM,
            pl.BlockSpec((rows, 2 * HD), lambda i: (0, head)),
            pl.BlockSpec(pos.shape, lambda i: (0, 0)),
            pl.BlockSpec(low.shape, lambda i: (0, 0)),
        ]
        + [ANY] * (count + len(earlier)),
        out_specs=[
            pl.BlockSpec((rows, 2 * HD), lambda i: (0, head)),
            pl.BlockSpec((2, rows), lambda i: (0, 0)),
        ],
        input_output_aliases={4 + count: 0} if earlier else {},
        scratch_shapes=[
            pltpu.VMEM((count * rows, 2 * HD), BF),
            pltpu.VMEM((HD, rows), F32),
            pltpu.SemaphoreType.DMA((count,)),
        ],
        cost_estimate=pl.CostEstimate(flops=int(1e9), bytes_accessed=0, transcendentals=0),
        name="attn_fwd",
    )(meta, q, pos, low, *slots, *earlier)


def attn_bwd_kernel(heads, slots, groups, *refs):
    meta, q_ref, pos_ref, low_ref, dmix_ref, mixed_ref, cos_ref, sin_ref = refs[:8]
    lse_refs = refs[8 : 8 + heads]
    at = 8 + heads
    slot_refs = refs[at : at + heads * slots]
    at += heads * slots
    dq_ref, dkv_refs = refs[at], refs[at + 1 : -4]
    kv_ref, dkv_ref, dq_acc, sems = refs[-4:]
    fetch_slots(slot_refs, slots, kv_ref, sems)
    dkv_ref[...] = jnp.zeros_like(dkv_ref)
    rows_all = q_ref.shape[0]
    size = rows_all // 2
    for i in range(2):
        rows = slice(i * size, (i + 1) * size)
        pos = jnp.tile(pos_ref[0:1, rows], (1, 2))
        low = jnp.tile(low_ref[0:1, rows], (1, 2))
        for g in range(heads):
            cols = [slice((2 * g + r) * HD, (2 * g + r + 1) * HD) for r in range(2)]
            queries = jnp.concatenate([q_ref[rows, c] for c in cols], axis=0)
            grads = jnp.concatenate([dmix_ref[rows, c] for c in cols], axis=0)
            outs = jnp.concatenate([mixed_ref[rows, c] for c in cols], axis=0)
            delta = jnp.sum((grads.astype(F32) * outs.astype(F32)).T, axis=0, keepdims=True)
            lse = lse_refs[g][i : i + 1, :]
            dq_acc[...] = jnp.zeros_like(dq_acc)

            def body(pk, carry):
                spot = pl.multiple_of(meta[4 + pk] * size, size)
                key_cols = slice(2 * g * HD, (2 * g + 1) * HD)
                value_cols = slice((2 * g + 1) * HD, (2 * g + 2) * HD)
                keys = kv_ref[pl.ds(spot, size), key_cols]
                values = kv_ref[pl.ds(spot, size), value_cols]
                scores = dot(keys, queries, NT) * SCORE
                probs = jnp.where(
                    allowed(pk, size, 2 * size, pos, low), jnp.exp2(scores - lse), 0.0
                )
                d_probs = dot(values, grads, NT)
                d_scores = (probs * (d_probs - delta)).astype(BF)
                dkv_ref[pl.ds(spot, size), value_cols] += dot(probs.astype(BF), grads)
                dkv_ref[pl.ds(spot, size), key_cols] += dot(d_scores, queries) * FACTOR
                dq_acc[...] += dot(d_scores, keys, TN)
                return carry

            lax.fori_loop(meta[i], meta[2 + i] + 1, body, 0)
            for r in range(2):
                part = dq_acc[r * size : (r + 1) * size, :] * FACTOR
                dq_ref[rows, cols[r]] = rope(part, cos_ref[rows, :], -sin_ref[rows, :]).astype(BF)
    ring = slots // 2
    for j, ref in enumerate(dkv_refs):
        first = ring * (j // len(groups))
        for place, k in enumerate(groups[j % len(groups)]):
            spot = pl.multiple_of((first + meta[4 + 2 * slots + k]) * rows_all, rows_all)
            ref[place * rows_all : (place + 1) * rows_all, :] = dkv_ref[
                pl.ds(spot, rows_all), :
            ].astype(BF)


def attn_bwd(meta, q, pos, low, lse, mixed, dmix, cosine, sine, slots):
    rows, q_width = q.shape
    heads, count = len(slots), len(slots[0])
    kv_width = heads * 2 * HD
    groups = halving(count // 2)
    outs = pl.pallas_call(
        functools.partial(attn_bwd_kernel, heads, count, groups),
        out_shape=[jax.ShapeDtypeStruct((rows, q_width), BF)]
        + [jax.ShapeDtypeStruct((len(g) * rows, kv_width), BF) for g in groups] * 2,
        in_specs=[SM] + [VM] * (7 + heads) + [ANY] * (heads * count),
        out_specs=[VM] * (1 + 2 * len(groups)),
        scratch_shapes=[
            pltpu.VMEM((count * rows, kv_width), BF),
            pltpu.VMEM((count * rows, kv_width), F32),
            pltpu.VMEM((rows, HD), F32),
            pltpu.SemaphoreType.DMA((heads * count,)),
        ],
        cost_estimate=pl.CostEstimate(flops=int(2e9), bytes_accessed=0, transcendentals=0),
        name="attn_bwd",
    )(meta, q, pos, low, dmix, mixed, cosine, sine, *lse, *[v for head in slots for v in head])
    return outs[0], outs[1 : 1 + len(groups)], outs[1 + len(groups) :]


def cost(micros):
    return pl.CostEstimate(flops=int(micros * 0.3e9), bytes_accessed=0, transcendentals=0)


def split_rows(total, own_ref, other_ref):
    half = own_ref.shape[0]
    own_ref[...] = total[:half].astype(BF)
    other_ref[...] = total[half:].astype(BF)


def project_kernel(spec, *refs):
    total = None
    for a, b, offset, dims in spec:
        left = refs[a][...] if dims is not None else None
        if dims == "nt":
            right, form = refs[b][:, offset : offset + left.shape[1]], NT
        else:
            right, form = refs[b][offset : offset + left.shape[1], :], NN
        term = dot(left, right, form)
        total = term if total is None else total + term
    split_rows(total, refs[-2], refs[-1])


def project(pairs, dims, tile, micros):
    operands, specs, plan, weights = [], [], [], []
    for a, b, offset in pairs:
        operands.append(a)
        specs.append(pl.BlockSpec(a.shape, lambda i: (0, 0)))
        spot = next((at for at, seen in weights if seen is b), None)
        left = len(operands) - 1
        if spot is None:
            spot = len(operands)
            operands.append(b)
            weights.append((spot, b))
            if dims == "nt":
                specs.append(pl.BlockSpec((tile, b.shape[1]), lambda i: (i, 0)))
            else:
                specs.append(pl.BlockSpec((b.shape[0], tile), lambda i: (0, i)))
        plan.append((left, spot, offset, dims))
    rows = pairs[0][0].shape[0]
    width = pairs[0][1].shape[0 if dims == "nt" else 1]
    return pl.pallas_call(
        functools.partial(project_kernel, plan),
        out_shape=[jax.ShapeDtypeStruct((rows // 2, width), BF)] * 2,
        grid=(width // tile,),
        in_specs=specs,
        out_specs=[pl.BlockSpec((rows // 2, tile), lambda i: (0, i))] * 2,
        cost_estimate=cost(micros),
        name="project",
    )(*operands)


def back_dense_kernel(gate_a, up_a, gate_b, up_b, wg_ref, wu_ref, own_ref, other_ref):
    total = None
    offset = 0
    for group in ((gate_a, up_a), (gate_b, up_b)):
        count = group[0].shape[1]
        for ref, w_ref in zip(group, (wg_ref, wu_ref)):
            term = dot(ref[...], w_ref[:, offset : offset + count], NT)
            total = term if total is None else total + term
        offset += count
    split_rows(total, own_ref, other_ref)


def back_dense(grads, w_gate, w_up, tile, part, parts):
    width, hidden = w_gate.shape[0] // parts, w_gate.shape[1]
    rows = grads[0].shape[0]
    ahead = part * (width // tile)
    weight = pl.BlockSpec((tile, hidden), lambda i: (ahead + i, 0))
    return pl.pallas_call(
        back_dense_kernel,
        out_shape=[jax.ShapeDtypeStruct((rows // 2, width), BF)] * 2,
        grid=(width // tile,),
        in_specs=[pl.BlockSpec(v.shape, lambda i: (0, 0)) for v in grads] + [weight, weight],
        out_specs=[pl.BlockSpec((rows // 2, tile), lambda i: (0, i))] * 2,
        cost_estimate=cost(11 / parts),
        name="back_dense",
    )(*grads, w_gate, w_up)


def gated_kernel(own_ref, other_ref, wg_ref, wu_ref, di_ref, inner_ref, dg_ref, du_ref, all_ref):
    @pl.when(pl.program_id(0) == 0)
    def _():
        half = own_ref.shape[0]
        all_ref[:half, :] = own_ref[...]
        all_ref[half:, :] = other_ref[...]

    gate = dot(all_ref[...], wg_ref[...])
    up = dot(all_ref[...], wu_ref[...])
    sigma = 1.0 / (1.0 + jnp.exp(-gate))
    silu = gate * sigma
    d_inner = di_ref[...]
    inner_ref[...] = (silu * up).astype(BF)
    dg_ref[...] = (d_inner * up * sigma * (1.0 + gate * (1.0 - sigma))).astype(BF)
    du_ref[...] = (d_inner * silu).astype(BF)


def gated(own, other, wg, wu, d_inner, first, columns, tile):
    half, width = own.shape
    weight = pl.BlockSpec((width, tile), lambda i: (0, first // tile + i))
    whole = pl.BlockSpec((half, width), lambda i: (0, 0))
    return pl.pallas_call(
        gated_kernel,
        out_shape=[jax.ShapeDtypeStruct((2 * half, columns), BF)] * 3,
        grid=(pl.cdiv(columns, tile),),
        in_specs=[
            whole,
            whole,
            weight,
            weight,
            pl.BlockSpec((2 * half, tile), lambda i: (0, first // tile + i)),
        ],
        out_specs=[pl.BlockSpec((2 * half, tile), lambda i: (0, i))] * 3,
        scratch_shapes=[pltpu.VMEM((2 * half, width), BF)],
        cost_estimate=cost(7.5),
        name="gated",
    )(own, other, wg, wu, d_inner)


def mixed_grad_kernel(own_ref, other_ref, w_ref, out_ref):
    both = jnp.concatenate([own_ref[...], other_ref[...]], axis=0)
    out_ref[...] = dot(both, w_ref[...], NT).astype(BF)


def mixed_grad(own, other, w):
    return pl.pallas_call(
        mixed_grad_kernel,
        out_shape=jax.ShapeDtypeStruct((2 * own.shape[0], w.shape[0]), BF),
        in_specs=[VM] * 3,
        out_specs=VM,
        cost_estimate=cost(4),
        name="mixed_grad",
    )(own, other, w)


def d_inner_kernel(x_ref, w_ref, out_ref):
    out_ref[...] = dot(x_ref[...], w_ref[...], NT)


def inner_grad(x, w, tile):
    rows, width = x.shape
    hidden = w.shape[0]
    return pl.pallas_call(
        d_inner_kernel,
        out_shape=jax.ShapeDtypeStruct((rows, hidden), F32),
        grid=(pl.cdiv(hidden, tile),),
        in_specs=[
            pl.BlockSpec((rows, width), lambda i: (0, 0)),
            pl.BlockSpec((tile, width), lambda i: (i, 0)),
        ],
        out_specs=pl.BlockSpec((rows, tile), lambda i: (0, i)),
        cost_estimate=cost(8),
        name="inner_grad",
    )(x, w)


def pack_kernel(count, plan, strip, tbl, *refs):
    ins, outs = refs[:count], refs[count:]
    for out_ref, pieces in zip(outs, plan):
        column = 0
        for at, rows, row in pieces:
            for k in range(tbl.shape[1]):
                first = pl.multiple_of(tbl[row, k] * strip, 128)
                out_ref[:, column : column + strip] = ins[at][rows, pl.ds(first, strip)]
                column += strip


def pack(values, plan, tbl, strip):
    turns = tbl.shape[1]
    if strip % 128:
        cut = lambda v, rows, at: lax.dynamic_slice_in_dim(v[rows], at * strip, strip, axis=1)
        return [
            jnp.concatenate(
                [cut(values[at], rows, tbl[row, k]) for at, rows, row in pieces for k in range(turns)],
                axis=1,
            )
            for pieces in plan
        ]
    return pl.pallas_call(
        functools.partial(pack_kernel, len(values), plan, strip),
        out_shape=[
            jax.ShapeDtypeStruct(
                (p[0][1].stop - p[0][1].start, len(p) * turns * strip), values[0].dtype
            )
            for p in plan
        ],
        in_specs=[SM] + [VM] * len(values),
        out_specs=[VM] * len(plan),
        cost_estimate=cost(1.5),
        name="pack",
    )(tbl, *values)


def strip_rows_kernel(halves, near, rights, nears, spans, tbl, *refs):
    left = refs[:halves]
    left_near = refs[halves : halves + near]
    right = refs[halves + near : halves + near + rights]
    right_near = refs[halves + near + rights : halves + near + rights + nears]
    outs = refs[halves + near + rights + nears :]
    step = pl.program_id(0)
    join = lambda group: (
        group[0][...] if len(group) == 1 else jnp.concatenate([r[...] for r in group], axis=0)
    )
    mine, theirs = join(left), join(left_near)
    pieces = []
    for r, n in zip(right, right_near):
        planes = range(r.shape[0]) if len(r.shape) == 3 else [None]
        for k in planes:
            a = r[...] if k is None else r[k]
            b = n[...] if k is None else n[k]
            pieces.append((dot(mine, a, TN) + dot(theirs, b, TN)).astype(BF))
    for (start, length), out in zip(spans, outs):

        @pl.when((step >= start) & (step < start + length))
        def _(out=out):
            column = 0
            for piece in pieces:
                out[:, column : column + piece.shape[1]] = piece
                column += piece.shape[1]


def strip_rows_grad(left, left_near, right, right_near, tbl, strip, micros, single=False):
    turns = tbl.shape[1]
    columns = sum(r.shape[-1] * (r.shape[0] if r.ndim == 3 else 1) for r in right)
    spans = [(k, 1) for k in range(turns)] if single else stretches(halving(turns))
    if strip % 128:
        near = jnp.concatenate(left_near, axis=0)
        mine = jnp.concatenate(left, axis=0)
        flat = lambda r: [r] if r.ndim == 2 else [r[k] for k in range(r.shape[0])]
        outs = []
        for start, length in spans:
            group = []
            for k in range(start, start + length):
                a = lax.dynamic_slice_in_dim(mine, tbl[0, k] * strip, strip, axis=1)
                b = near[:, k * strip : (k + 1) * strip]
                group.append(
                    jnp.concatenate(
                        [
                            dot(a, x, TN) + dot(b, y, TN)
                            for r, n in zip(right, right_near)
                            for x, y in zip(flat(r), flat(n))
                        ],
                        axis=1,
                    ).astype(BF)
                )
            outs.append(jnp.concatenate(group, axis=0))
        return outs
    held = lambda start, length: (lambda i, t: (jnp.clip(i - start, 0, length - 1), 0))
    whole = lambda v: pl.BlockSpec(v.shape, lambda i, t: (0,) * v.ndim)
    return pl.pallas_call(
        functools.partial(
            strip_rows_kernel, len(left), len(left_near), len(right), len(right_near), spans
        ),
        out_shape=[jax.ShapeDtypeStruct((length * strip, columns), BF) for _, length in spans],
        grid_spec=pltpu.PrefetchScalarGridSpec(
            num_scalar_prefetch=1,
            grid=(turns,),
            in_specs=[pl.BlockSpec((v.shape[0], strip), lambda i, t: (0, t[0, i])) for v in left]
            + [pl.BlockSpec((v.shape[0], strip), lambda i, t: (0, i)) for v in left_near]
            + [whole(v) for v in [*right, *right_near]],
            out_specs=[pl.BlockSpec((strip, columns), held(*span)) for span in spans],
        ),
        cost_estimate=cost(micros),
        name="strip_rows",
    )(tbl, *left, *left_near, *right, *right_near)


def strip_columns_kernel(parts, halves, near, strip, spans, *refs):
    at = 2 * parts
    right, right_near = refs[at : at + halves], refs[at + halves : at + halves + near]
    outs = refs[at + halves + near :]
    first = 0
    for p in range(parts):
        total = None
        for ref, group in ((refs[p], right), (refs[parts + p], right_near)):
            row = 0
            for r in group:
                term = dot(ref[row : row + r.shape[0], :], r[...], TN)
                total = term if total is None else total + term
                row += r.shape[0]
        for (start, length), out in zip(spans, outs):
            out[first : first + total.shape[0], :] = total[
                :, start * strip : (start + length) * strip
            ].astype(BF)
        first += total.shape[0]


def strip_columns_grad(left, left_near, right, right_near, turns, strip, tile, micros, near_at=0):
    rows, count = left[0].shape[0], sum(v.shape[1] for v in left)
    if strip * turns % 128:
        raise ValueError(strip)
    spans = stretches(halving(turns))
    whole = lambda v: pl.BlockSpec(v.shape, lambda i: (0, 0))
    near = lambda v: pl.BlockSpec((v.shape[0], turns * strip), lambda i: (0, near_at))
    if len(left) == 1:
        left_specs = [pl.BlockSpec((rows, tile), lambda i: (0, i))] * 2
    else:
        tile = count
        left_specs = [whole(v) for v in [*left, *left_near]]
    return pl.pallas_call(
        functools.partial(
            strip_columns_kernel, len(left), len(right), len(right_near), strip, spans
        ),
        out_shape=[jax.ShapeDtypeStruct((count, length * strip), BF) for _, length in spans],
        grid=(pl.cdiv(count, tile),),
        in_specs=left_specs + [whole(v) for v in right] + [near(v) for v in right_near],
        out_specs=[pl.BlockSpec((tile, length * strip), lambda i: (i, 0)) for _, length in spans],
        cost_estimate=cost(micros),
        name="strip_columns",
    )(*left, *left_near, *right, *right_near)


def close_kv_kernel(count, *refs):
    cos_ref, sin_ref, dk_ref, dv_ref = refs[count:]
    total = refs[0][...].astype(F32)
    for ref in refs[1:count]:
        total = total + ref[...].astype(F32)
    heads = dk_ref.shape[1] // HD
    for h in range(heads):
        cols = slice(h * HD, (h + 1) * HD)
        keys = total[:, 2 * h * HD : (2 * h + 1) * HD]
        dk_ref[:, cols] = rope(keys, cos_ref[...], -sin_ref[...]).astype(BF)
        dv_ref[:, cols] = total[:, (2 * h + 1) * HD : (2 * h + 2) * HD].astype(BF)


def close_kv(terms, cosine, sine):
    rows, width = terms[0].shape
    first = lambda w: pl.BlockSpec((rows, w), lambda i: (0, 0))
    return pl.pallas_call(
        functools.partial(close_kv_kernel, len(terms)),
        out_shape=[jax.ShapeDtypeStruct((rows, width // 2), BF)] * 2,
        grid=(1,),
        in_specs=[first(width)] * len(terms) + [first(HD)] * 2,
        out_specs=[first(width // 2)] * 2,
        cost_estimate=cost(1.5),
        name="close_kv",
    )(*terms, cosine, sine)


def norm_backward(source, scale_rows, gain, upstream):
    weighted = upstream * gain
    average = jnp.mean(weighted * source, axis=1, keepdims=True)
    return scale_rows * weighted - source * scale_rows**3 * average


def after(value, *done):
    return lax.optimization_barrier((value, *done))[0]


def shards(
    tokens,
    cotangent,
    keep_mask,
    doc_lengths,
    block_order,
    gain_attn,
    w_query,
    w_key,
    w_value,
    w_out,
    gain_dense,
    w_gate,
    w_up,
    w_down,
):
    rows, width = tokens.shape
    half = rows // 2
    wide = lax.axis_size("wide")
    group = wide // block_order.shape[0]
    ring = group // 2
    wide_index = lax.axis_index("wide")
    member = wide_index % group
    seq_index = wide_index // group
    side = (wide_index % 2).astype(jnp.int32)
    core = lax.axis_index("narrow") % 2
    strip = width // wide
    turns = wide // 2

    def ordered(mine, other):
        return jnp.where(
            core == 0,
            jnp.concatenate([mine, other], axis=0),
            jnp.concatenate([other, mine], axis=0),
        )

    def own_half(value):
        return lax.dynamic_slice_in_dim(value, core * half, half)

    def other_half(value):
        return lax.dynamic_slice_in_dim(value, (1 - core) * half, half)

    order_row = lax.dynamic_index_in_dim(block_order, seq_index, 0, keepdims=False)
    length_row = lax.dynamic_index_in_dim(doc_lengths, seq_index, 0, keepdims=False)
    doc_ends = jnp.cumsum(length_row)
    places = jnp.stack([member * 2 + core, member * 2 + 1 - core])
    chosen = jnp.sum(
        jnp.where(places[:, None] == jnp.arange(2 * group)[None, :], order_row[None, :], 0), axis=1
    )
    pos = (chosen[:, None] * half + jnp.arange(half, dtype=jnp.int32)[None, :]).reshape(-1)
    low = jnp.max(jnp.where(doc_ends[None, :] <= pos[:, None], doc_ends[None, :], 0), axis=1)
    block_low = low.reshape(2, half)[:, 0] // half
    stored = jnp.sum(
        jnp.where(
            order_row[None, :] == jnp.arange(2 * group)[:, None], jnp.arange(2 * group)[None, :], 0
        ),
        axis=1,
    )
    owner = stored // 2
    slot = (member // 2 - owner // 2) % ring + ring * (owner % 2 != side).astype(jnp.int32)
    spots = slot * 2 + (stored % 2 != core).astype(jnp.int32)
    place = member // 2
    back = (place - (place ^ jnp.arange(ring, dtype=jnp.int32))) % ring
    meta = jnp.concatenate([block_low, chosen, spots, back]).astype(jnp.int32)
    frequency = BASE ** (-(jnp.arange(HD // 2, dtype=F32) * 2.0) / HD)
    angles = pos.astype(F32)[:, None] * frequency[None, :]
    cosine = jnp.cos(angles)
    sine = jnp.sin(angles)
    cosine = jnp.concatenate([cosine, cosine], axis=1)
    sine = jnp.concatenate([-sine, sine], axis=1)
    pos_row = pos[None, :]
    low_row = low[None, :]

    order = np.array([k for stretch in halving(turns) for k in stretch], np.int32)
    turn_row = wide_index // 2 ^ order
    tbl = jnp.stack([2 * turn_row + side, 2 * turn_row + 1 - side]).astype(jnp.int32)
    round_row = (wide_index // 2 - 1 - jnp.arange(turns, dtype=jnp.int32)) % turns
    round_tbl = jnp.stack([2 * round_row + side, 2 * round_row + 1 - side]).astype(jnp.int32)
    core_arr = core.astype(jnp.int32)[None]
    normed_one, both = norm_kv(core_arr, tokens, gain_attn[None, :], w_key, w_value, cosine, sine)
    low_rows, all_rows = slice(0, half), slice(0, rows)

    def together(*values):
        return list(lax.optimization_barrier(values))

    near, far = [[v] for v in both], [[] for v in both]
    query = d_dense = d_inner = input_near = d_dense_strips = None
    for step in range(ring):
        for head in range(len(both)):
            held = near[head][step]
            if step + 1 < ring:
                sent = [wide_swap(held), wide_ring(held, group)]
            elif head == 0:
                sent = [wide_swap(held)]
            else:
                sent = [wide_ring(far[head][0], group, -1)]
            beside = []
            if step == 0 and head == 0:
                beside = [query_proj(normed_one, w_query, cosine, sine)]
            if step == 0 and head == 1:
                keep_rel = jnp.concatenate([own_half(keep_mask), other_half(keep_mask)])[:, None]
                cot_rel = jnp.concatenate([own_half(cotangent), other_half(cotangent)])
                beside = [jnp.where(keep_rel > 0, cot_rel, jnp.zeros_like(cot_rel))]
            if step == 1 and head == 0:
                beside = [inner_grad(d_dense, w_down, 256)]
            if step == 2 and head == 0:
                beside = pack(
                    [normed_one, d_dense],
                    [[(0, low_rows, 1), (1, low_rows, 1)], [(1, all_rows, 0)]],
                    tbl,
                    strip,
                )
            done = together(*sent, *beside)
            far[head].append(done[0])
            if step + 1 < ring:
                near[head].append(done[1])
            if step == 0 and head == 0:
                query = done[-1]
            if step == 0 and head == 1:
                d_dense = done[-1]
            if step == 1 and head == 0:
                d_inner = done[-1]
            if step == 2 and head == 0:
                input_near, d_dense_strips = done[-2:]
    slots = [n + f for n, f in zip(near, far)]
    input_near = wide_swap(after(input_near, *slots[0], *slots[-1]))
    mixed, lse = None, []
    for h, held in enumerate(slots):
        mixed, part = attn_fwd(h, meta, query, pos_row, low_row, held, mixed)
        lse.append(part)

    def reduce_narrow(halves, hold=()):
        own_part, other_part = halves
        got = narrow_swap(other_part, 1)
        held = (own_part.astype(F32) + got.astype(F32)).astype(BF)
        return held, narrow_swap(held, 2)

    def total_of(held, got):
        return held.astype(F32) + got.astype(F32)

    part = project([(mixed, w_out, 0)], "nn", 1024, 4)
    held, got = reduce_narrow((part[0], after(part[1], input_near)))
    mixed_near = wide_swap(mixed)
    input_near_other = narrow_swap(input_near, 1)
    source = own_half(tokens).astype(F32)
    keep_own = own_half(keep_mask).astype(F32)[:, None]
    hidden_one = source + keep_own * total_of(held, got)
    gain_two = gain_dense.astype(F32)
    scale_two = lax.rsqrt(jnp.mean(hidden_one * hidden_one, axis=1, keepdims=True) + EPSILON)
    normed_two = (hidden_one * scale_two * gain_two).astype(BF)
    normed_two_other = narrow_swap(after(normed_two, mixed_near), 1)
    hidden = w_gate.shape[1]
    tile = 256
    first_count = 3 * tile
    inner_a, *dgu_a = gated(
        normed_two, normed_two_other, w_gate, w_up, d_inner, 0, first_count, tile
    )
    inner_a_near = wide_swap(inner_a)
    inner_b, *dgu_b = gated(
        after(normed_two, inner_a),
        normed_two_other,
        w_gate,
        w_up,
        d_inner,
        first_count,
        hidden - first_count,
        tile,
    )
    back = back_dense([*dgu_a, *dgu_b], w_gate, w_up, 512, 0, 1)
    held, got = reduce_narrow((back[0], after(back[1], inner_a_near)))

    def halve(parts, axis, hold=None):
        groups = halving(1 << (len(parts) - 1))
        size = parts[-1].shape[axis]
        received, sent = [], None
        for bit, group in enumerate(groups[:-1]):
            sent = parts[bit]
            if bit:
                total = sent.astype(F32)
                for early, value in enumerate(received):
                    there = [k ^ (1 << early) for k in groups[early]]
                    pick = [
                        lax.slice_in_dim(value, size * there.index(k), size * (there.index(k) + 1), axis=axis)
                        for k in group
                    ]
                    total = total + (pick[0] if len(pick) == 1 else jnp.concatenate(pick, axis)).astype(F32)
                sent = total.astype(BF)
            got = wide_flip(sent, bit)
            received.append(got if hold is None else after(got, hold))
        return received, sent

    def ring_sum(parts):
        carried, first = parts[0], None
        for part in parts[1:]:
            total = part.astype(F32) + wide_ring(carried, wide).astype(F32)
            carried = total.astype(BF)
            first = carried if first is None else first
        return total, first

    def close(parts, received, axis):
        size = parts[-1].shape[axis]
        total = parts[-1].astype(F32)
        for value in received:
            total = total + lax.slice_in_dim(value, 0, size, axis=axis).astype(F32)
        return total

    near_sides = [input_near, input_near_other]
    down_a = strip_columns_grad(
        [after(inner_a, held)],
        [inner_a_near],
        [d_dense_strips],
        near_sides,
        turns,
        strip,
        tile,
        4,
        1,
    )
    inner_b_near = wide_swap(inner_b)
    down_a_got, down_a_mid = halve(down_a, 1)
    dgu_a_near = [wide_swap(after(v, inner_b)) for v in dgu_a]
    dense_parts = project(
        [(after(inner_a, down_a[0], inner_b_near), w_down, 0), (inner_b, w_down, first_count)], "nn", 512, 6
    )
    (normed_two_near,) = pack(
        [after(normed_two, dense_parts[0])], [[(0, low_rows, 1)]], round_tbl, strip
    )
    normed_two_near = wide_swap(normed_two_near)
    down_b = strip_columns_grad(
        [after(inner_b, dense_parts[0])], [inner_b_near], [d_dense_strips], near_sides, turns, strip, tile, 4, 1
    )

    got = after(got, dense_parts[0], down_b[0])
    upstream = own_half(cotangent).astype(F32)
    d_hidden = upstream + norm_backward(hidden_one, scale_two, gain_two, total_of(held, got))
    d_attn = (keep_own * d_hidden).astype(BF)
    d_attn_other = narrow_swap(after(d_attn, dgu_a_near[0], down_a_mid), 1)

    d_mixed = mixed_grad(d_attn, d_attn_other, w_out)
    d_query, d_near, d_far = attn_bwd(
        meta, query, pos_row, low_row, lse, mixed, after(d_mixed, down_a_got[-1]), cosine, sine, slots
    )
    held_out, got_out = reduce_narrow((dense_parts[0], after(dense_parts[1], d_mixed)))
    output_own = (hidden_one + keep_own * total_of(held_out, got_out)).astype(BF)
    output = ordered(output_own, narrow_swap(output_own, 1))

    down_b_got, down_b_mid = halve(down_b, 1, d_query)
    normed_two_near_other = narrow_swap(after(normed_two_near, d_query), 1)
    normed_two_sides = [normed_two_near, normed_two_near_other]
    gate_up_a = strip_rows_grad(
        [after(normed_two, d_query, down_b_mid), normed_two_other], normed_two_sides, dgu_a, dgu_a_near, round_tbl, strip, 8, True
    )
    grad_gate_up_a, gate_up_a_mid = ring_sum(gate_up_a)
    d_far = [wide_swap(v) for v in d_far]
    d_far[0] = after(d_far[0], gate_up_a_mid)
    pairs = [
        (n.astype(F32) + f.astype(F32)).astype(BF) for n, f in zip(d_near[:-1], d_far[:-1])
    ]
    dgu_b_near = [wide_swap(after(v, d_query)) for v in dgu_b]
    kv_got, kv_mid = halve([*pairs, d_near[-1]], 0, dgu_b_near[0])
    d_key, d_value = close_kv([d_near[-1], d_far[-1], *kv_got], cosine, sine)

    gate_up_b = strip_rows_grad(
        [after(normed_two, gate_up_a_mid, kv_mid), normed_two_other],
        normed_two_sides,
        dgu_b,
        dgu_b_near,
        round_tbl,
        strip,
        7,
        True,
    )
    d_query_near = wide_swap(after(d_query, pairs[0]))
    grad_gate_up_b, gate_up_b_mid = ring_sum(gate_up_b)
    d_attn_near, d_attn_strips, d_attn_other_strips = pack(
        [after(d_attn, gate_up_a[0]), d_attn_other],
        [[(0, low_rows, 1)], [(0, low_rows, 0)], [(1, low_rows, 0)]],
        tbl,
        strip,
    )
    d_attn_near = wide_swap(after(d_attn_near, pairs[0]))
    d_attn_near_other = narrow_swap(after(d_attn_near, gate_up_b[0]), 1)
    query_part = strip_rows_grad(
        [after(normed_one, gate_up_b[0])], near_sides, [d_query], [d_query_near], tbl, strip, 4
    )
    out_part = strip_columns_grad(
        [after(mixed, query_part[0])],
        [mixed_near],
        [d_attn_strips, d_attn_other_strips],
        [d_attn_near, d_attn_near_other],
        turns,
        strip,
        tile,
        4,
    )

    kv_width = w_key.shape[1]
    held, got = reduce_narrow(
        project([(d_query, w_query, 0), (d_key, w_key, 0), (d_value, w_value, 0)], "nt", 512, 6)
    )
    gain_one = gain_attn.astype(F32)
    scale_one = lax.rsqrt(jnp.mean(source * source, axis=1, keepdims=True) + EPSILON)
    d_normed_one = total_of(held, got)
    grad_own = (d_hidden + norm_backward(source, scale_one, gain_one, d_normed_one)).astype(BF)
    grad_tokens = ordered(grad_own, narrow_swap(grad_own, 1))

    d_key_near = wide_swap(d_key)
    d_value_near = wide_swap(d_value)
    kv_part = strip_rows_grad(
        [after(normed_one, out_part[0])],
        near_sides,
        [d_key, d_value],
        [d_key_near, d_value_near],
        tbl,
        strip,
        4,
    )
    kv_part_got, _ = halve(kv_part, 0)
    query_got, query_mid = halve(query_part, 0, kv_part[0])
    out_got, out_mid = halve(out_part, 1, kv_part[0])
    kv_part_got[-1] = after(kv_part_got[-1], grad_own, output)
    grad_kv = close(kv_part, kv_part_got, 0)
    down_a_got[-1], down_b_got[-1] = after(down_a_got[-1], kv_part[0]), after(down_b_got[-1], kv_part[0])
    grad_down_a = close(down_a, down_a_got, 1)
    grad_down_b = close(down_b, down_b_got, 1)
    grad_query = close(query_part, query_got, 0)
    grad_out = close(out_part, out_got, 1)
    grad_key, grad_value = grad_kv[:, :kv_width], grad_kv[:, kv_width:]
    grad_down = jnp.concatenate([grad_down_a, grad_down_b], axis=0)
    second_count = hidden - first_count
    grad_gate = jnp.concatenate(
        [grad_gate_up_a[:, :first_count], grad_gate_up_b[:, :second_count]], axis=1
    )
    grad_up = jnp.concatenate(
        [grad_gate_up_a[:, first_count:], grad_gate_up_b[:, second_count:]], axis=1
    )

    def strip_rows(weight):
        return lax.dynamic_slice_in_dim(weight, wide_index * strip, strip).astype(F32)

    def gain_grad(pairs, gain):
        local = sum(jnp.sum(strip_rows(w) * g, axis=1) for w, g in pairs)
        return local / lax.dynamic_slice_in_dim(gain, wide_index * strip, strip)

    local = jnp.stack(
        [
            gain_grad([(w_query, grad_query), (w_key, grad_key), (w_value, grad_value)], gain_one),
            gain_grad([(w_gate, grad_gate), (w_up, grad_up)], gain_two),
        ]
    )
    local = local + narrow_swap(local, 1)
    local = local + narrow_swap(local, 2)
    grad_gain_one, grad_gain_two = local[0], local[1]
    return (
        output,
        grad_tokens,
        grad_gain_one,
        grad_query,
        grad_key,
        grad_value,
        grad_out,
        grad_gain_two,
        grad_gate,
        grad_up,
        grad_down,
    )


def solution(mesh):
    placed = (
        P("wide", None),
        P("wide", None),
        P("wide"),
        P(),
        P(),
        P(),
        P(None, "narrow"),
        P(None, "narrow"),
        P(None, "narrow"),
        P("narrow", None),
        P(),
        P(None, "narrow"),
        P(None, "narrow"),
        P("narrow", None),
    )
    return jax.shard_map(
        shards,
        mesh=mesh,
        in_specs=placed,
        out_specs=(
            P("wide", None),
            P("wide", None),
            P("wide"),
            P("wide", "narrow"),
            P("wide", "narrow"),
            P("wide", "narrow"),
            P("narrow", "wide"),
            P("wide"),
            P("wide", "narrow"),
            P("wide", "narrow"),
            P("narrow", "wide"),
        ),
        check_vma=False,
    )
```
